256 devices in a mesh: seq: 64 (over z, y, core), chan: 4 (over x).
Axes of the slice: x: 4, y: 4, z: 8, core: 2. Of those that a mesh axis runs over, the one named last changes fastest.
Arguments:
- features: bfloat16 [32768, 512], P('seq', 'chan'), may hold values from -600 to 600
- pre_gate: bfloat16 [32768, 512], P('seq', 'chan'), may hold values from -6 to 6
- post_gate: bfloat16 [32768, 512], P('seq', 'chan'), may hold values from -6 to 6
- norm_gain: float32 [512], P('chan'), may hold values from 0.1 to 1.9
- skip_weight: float32 [512], P('chan'), may hold values from -4 to 4
- spectrum: float32 [2, 128, 512, 512], P(None, 'seq', None, 'chan'), may hold values from -6 to 6
Outputs:
- gated_out: bfloat16 [32768, 512], P('seq', 'chan')
The draws below stay inside these ranges and needn't reach their ends.
All inputs are finite; a program needn't handle non-finite values.
Results may differ from the reference program's by a relative error of at most 0.007.
Values may be sent and summed in bfloat16 or wider, within the bound.
A program may use at most 64 MiB of HBM per device.

```python
import math
import jax
import jax.numpy as jnp
import numpy as np
from jax import lax

TOK_DEV = 512
CHANNELS = 512
SEQLEN = 32768
BINS = 65536
STRIDE = 128
N_SEQ = 64


def draw_features(key, part):
    folded = jax.random.fold_in(key, 17)
    base_key, chan_key, token_key = jax.random.split(folded, 3)
    channel_ramp = (jnp.arange(CHANNELS, dtype=jnp.float32) + jax.random.uniform(chan_key, (CHANNELS,))) / CHANNELS
    token_scale = jnp.exp(math.log(10.0) * jax.random.uniform(token_key, (SEQLEN, 1)))
    base_draw = jnp.clip(jax.random.normal(base_key, (SEQLEN, CHANNELS)), -6.0, 6.0)
    chan_scale = jnp.exp(math.log(10.0) * channel_ramp)
    return (base_draw * token_scale * chan_scale).astype(jnp.bfloat16)


def block_scale(stream_key, shape, pieces, least, top_value):
    loudness, own = 1.0, jax.random.fold_in(stream_key, 6)
    for axis_at, shards_of in pieces:
        heights = jnp.exp(jax.random.uniform(jax.random.fold_in(own, axis_at), (shards_of,), jnp.float32, least / len(pieces), top_value / len(pieces)))
        loudness = loudness * jnp.repeat(heights, shape[axis_at] // shards_of).reshape([-1 if axis == axis_at else 1 for axis in range(len(shape))])
    return loudness


def noise(stream_key, dims, scale, bound, cuts=(), held_as=jnp.bfloat16):
    entries = jax.random.normal(stream_key, dims, jnp.float32) * scale
    if len(cuts) > 0:
        entries = block_scale(stream_key, dims, cuts, -0.22, 0.18) * entries
    return jnp.clip(entries, min=-bound, max=bound).astype(held_as)


def setup_inputs(seed: int = 0) -> dict:
    key_list = jax.random.split(jax.random.key(seed), 7)
    features = draw_features(jax.random.fold_in(key_list[6], 71), 0)
    pre_gate = noise(key_list[1], (SEQLEN, CHANNELS), 1.0, 6.0, ((0, 64), (1, 4)))
    post_gate = noise(key_list[2], (SEQLEN, CHANNELS), 1.0, 6.0, ((0, 64), (1, 4)))
    norm_gain = jnp.clip(1.0 + 0.18 * jax.random.normal(key_list[3], (CHANNELS,), jnp.float32), 0.1, 1.9)
    skip_weight = noise(key_list[4], (CHANNELS,), 1.0, 4.0, ((0, 4),), jnp.float32)
    spectrum = noise(key_list[5], (2, STRIDE, TOK_DEV, CHANNELS), 1.0, 6.0, ((1, 64), (3, 4)), jnp.float32)
    return dict(features=features, pre_gate=pre_gate, post_gate=post_gate, norm_gain=norm_gain, skip_weight=skip_weight, spectrum=spectrum)


def reversed_digits(axis_count):
    levels = axis_count.bit_length() - 1
    positions = np.arange(axis_count)
    result = np.zeros(axis_count, np.int64)
    for bit_pos in range(levels):
        result = result + ((positions >> bit_pos & 1) << levels - 1 - bit_pos)
    return result

def convolve_block(packed):
    signal_block, filter_block = packed
    padded = jnp.concatenate([signal_block, jnp.zeros_like(signal_block)], axis=0)
    forward = jnp.fft.fft(padded, axis=0)
    response = filter_block[0] + 1j * filter_block[1]
    return jnp.real(jnp.fft.ifft(forward * response, axis=0))[:SEQLEN]

def reference(features, pre_gate, post_gate, norm_gain, skip_weight, spectrum):
    widened = features.astype(jnp.float32)
    mean_square = lax.optimization_barrier(jnp.mean(widened * widened, axis=1, keepdims=True))
    scaled = widened * lax.rsqrt(mean_square + 1e-06) * norm_gain
    signal = (scaled * pre_gate.astype(jnp.float32)).astype(jnp.bfloat16)
    digit_order = reversed_digits(N_SEQ)
    stride = 2 * N_SEQ
    slots = np.arange(stride)
    low_bins = 2 * digit_order[slots // 2] + slots % 2
    bin_index = (low_bins[:, None] + stride * np.arange(TOK_DEV)[None, :]).reshape(-1)
    inverse = np.argsort(bin_index)
    natural = spectrum.reshape(2, stride * TOK_DEV, CHANNELS)[:, inverse]
    group_size = min(CHANNELS, 64)
    blocks = CHANNELS // group_size
    signal_blocks = signal.astype(jnp.float32).reshape(SEQLEN, blocks, group_size).transpose(1, 0, 2)
    filter_blocks = natural.reshape(2, BINS, blocks, group_size).transpose(2, 0, 1, 3)
    per_block = lax.map(convolve_block, (signal_blocks, filter_blocks))
    convolved = per_block.transpose(1, 0, 2).reshape(SEQLEN, CHANNELS)
    gated = post_gate.astype(jnp.float32) * (convolved + skip_weight * signal.astype(jnp.float32))
    return gated.astype(jnp.bfloat16)
```

```python
import math

import jax
import jax.numpy as jnp
import numpy as np
from jax import lax
from jax.sharding import PartitionSpec as P

CHANNELS = 512
ROW_GROUP = 4


PRECISE = lax.Precision.HIGHEST
FULL_TURN = 2.0 * math.pi


def reversed_digits(count):
    levels = count.bit_length() - 1
    positions = np.arange(count)
    result = np.zeros(count, np.int64)
    for bit_pos in range(levels):
        result = result + ((positions >> bit_pos & 1) << levels - 1 - bit_pos)
    return result


def rotation(numerator, denominator):
    angle = (numerator % denominator).astype(jnp.float32) * (FULL_TURN / denominator)
    return (jnp.cos(angle), jnp.sin(angle))


def mm(spec, left, right):
    return jnp.einsum(spec, left, right, precision=PRECISE, preferred_element_type=jnp.float32)


def local(features, pre_gate, post_gate, norm_gain, skip_weight, spectrum):
    tok_rows, chan_width = features.shape
    seq_count = lax.axis_size("seq")
    stride = 2 * seq_count
    all_bins = stride * tok_rows
    group = chan_width // seq_count
    first_len = stride * ROW_GROUP
    second_len = all_bins // first_len
    half_first = first_len // 2

    spec_rows = spectrum.reshape(2, 2, second_len, ROW_GROUP, chan_width)
    spec_rows = jnp.transpose(spec_rows, (4, 0, 1, 3, 2))
    spec_chan = lax.all_to_all(spec_rows, "seq", 0, 2, tiled=True)
    spec_chan = spec_chan.reshape(group, 2, first_len, second_len)

    widened = features.astype(jnp.float32)
    squares = lax.psum(jnp.sum(widened * widened, axis=1), "chan")
    scaled = widened * lax.rsqrt(squares / CHANNELS + 1e-06)[:, None] * norm_gain
    signal = (scaled * pre_gate.astype(jnp.float32)).astype(jnp.bfloat16)

    sig_chan = lax.all_to_all(signal.T, "seq", 0, 1, tiled=True)
    sig_chan = sig_chan.astype(jnp.float32).reshape(group, half_first, second_len)

    digit_order = reversed_digits(seq_count)
    slots = np.arange(stride)
    low_bins = 2 * digit_order[slots // 2] + slots % 2
    row_bins = (low_bins[:, None] + stride * np.arange(ROW_GROUP)[None, :]).reshape(-1)
    row_bins = jnp.asarray(row_bins.astype(np.int32))

    first_in = jnp.arange(half_first, dtype=jnp.int32)
    cos_first, sin_first = rotation(row_bins[:, None] * first_in[None, :], first_len)
    second_in = jnp.arange(second_len, dtype=jnp.int32)
    cos_twist, sin_twist = rotation(row_bins[:, None] * second_in[None, :], all_bins)
    cos_second, sin_second = rotation(second_in[:, None] * second_in[None, :], second_len)

    part_re = mm("rn,cnm->crm", cos_first, sig_chan)
    part_im = -mm("rn,cnm->crm", sin_first, sig_chan)
    twist_re = part_re * cos_twist + part_im * sin_twist
    twist_im = part_im * cos_twist - part_re * sin_twist
    freq_re = mm("crn,nk->crk", twist_re, cos_second) + mm("crn,nk->crk", twist_im, sin_second)
    freq_im = mm("crn,nk->crk", twist_im, cos_second) - mm("crn,nk->crk", twist_re, sin_second)

    filt_re = spec_chan[:, 0]
    filt_im = spec_chan[:, 1]
    prod_re = freq_re * filt_re - freq_im * filt_im
    prod_im = freq_re * filt_im + freq_im * filt_re

    back_re = mm("crk,kn->crn", prod_re, cos_second) - mm("crk,kn->crn", prod_im, sin_second)
    back_im = mm("crk,kn->crn", prod_im, cos_second) + mm("crk,kn->crn", prod_re, sin_second)
    untwist_re = back_re * cos_twist - back_im * sin_twist
    untwist_im = back_im * cos_twist + back_re * sin_twist
    conv = mm("rn,crm->cnm", cos_first, untwist_re) - mm("rn,crm->cnm", sin_first, untwist_im)
    conv = (conv * (1.0 / all_bins)).reshape(group, seq_count * tok_rows)

    result = lax.all_to_all(conv, "seq", 1, 0, tiled=True).T
    gated = post_gate.astype(jnp.float32) * (result + skip_weight * signal.astype(jnp.float32))
    return gated.astype(jnp.bfloat16)


def solution(mesh):
    return jax.shard_map(
        local,
        mesh=mesh,
        in_specs=(
            P("seq", "chan"),
            P("seq", "chan"),
            P("seq", "chan"),
            P("chan"),
            P("chan"),
            P(None, "seq", None, "chan"),
        ),
        out_specs=P("seq", "chan"),
        check_vma=False,
    )
```

```python
import math

import jax
import jax.numpy as jnp
import numpy as np
from jax import lax
from jax.experimental import pallas as pl
from jax.experimental.pallas import tpu as pltpu
from jax.sharding import PartitionSpec as P

CHANNELS = 512
ROW_GROUP = 4


PRECISE = lax.Precision.HIGHEST
FULL_TURN = 2.0 * math.pi


def reversed_digits(count):
    levels = count.bit_length() - 1
    positions = np.arange(count)
    result = np.zeros(count, np.int64)
    for bit_pos in range(levels):
        result = result + ((positions >> bit_pos & 1) << levels - 1 - bit_pos)
    return result


def rotation(numerator, denominator):
    angle = (numerator % denominator).astype(jnp.float32) * (FULL_TURN / denominator)
    return (jnp.cos(angle), jnp.sin(angle))


def mm(spec, left, right):
    return jnp.einsum(spec, left, right, precision=PRECISE, preferred_element_type=jnp.float32)


def exchange_kernel(src_ref, dst_ref, send_sem, recv_sem, local_sem):
    count = src_ref.shape[0]
    me = lax.axis_index("seq")
    mesh_ids = pl.DeviceIdType.MESH
    barrier = pltpu.get_barrier_semaphore()

    def greet(step, carry):
        peer = lax.rem(me + step, count)
        pl.semaphore_signal(barrier, inc=1, device_id={"seq": peer}, device_id_type=mesh_ids)
        return carry

    lax.fori_loop(1, count, greet, 0)
    pl.semaphore_wait(barrier, count - 1)
    own = pltpu.make_async_copy(src_ref.at[me], dst_ref.at[me], local_sem)
    own.start()

    def remote(step):
        peer = lax.rem(me + step, count)
        return pltpu.make_async_remote_copy(
            src_ref.at[peer],
            dst_ref.at[me],
            send_sem.at[step],
            recv_sem.at[step],
            device_id={"seq": peer},
            device_id_type=mesh_ids,
        )

    def send(step, carry):
        remote(step).start()
        return carry

    lax.fori_loop(1, count, send, 0)

    def finish(step, carry):
        copy = remote(step)
        copy.wait_send()
        copy.wait_recv()
        return carry

    lax.fori_loop(1, count, finish, 0)
    own.wait()


def exchange(blocks, tag):
    count = blocks.shape[0]
    return pl.pallas_call(
        exchange_kernel,
        out_shape=jax.ShapeDtypeStruct(blocks.shape, blocks.dtype),
        in_specs=[pl.BlockSpec(memory_space=pl.ANY)],
        out_specs=pl.BlockSpec(memory_space=pl.ANY),
        scratch_shapes=[
            pltpu.SemaphoreType.DMA((count,)),
            pltpu.SemaphoreType.DMA((count,)),
            pltpu.SemaphoreType.DMA,
        ],
        compiler_params=pltpu.CompilerParams(collective_id=tag, has_side_effects=True),
    )(blocks)


def local(features, pre_gate, post_gate, norm_gain, skip_weight, spectrum):
    tok_rows, chan_width = features.shape
    seq_count = lax.axis_size("seq")
    stride = 2 * seq_count
    all_bins = stride * tok_rows
    group = chan_width // seq_count
    first_len = stride * ROW_GROUP
    second_len = all_bins // first_len
    half_first = first_len // 2

    spec_rows = spectrum.reshape(2, 2, second_len, ROW_GROUP, seq_count, group)
    spec_rows = jnp.transpose(spec_rows, (4, 5, 0, 1, 3, 2)).reshape(seq_count, -1, 128)
    spec_chan = exchange(spec_rows, 0).reshape(seq_count, group, 2, 2, ROW_GROUP, second_len)
    spec_chan = jnp.transpose(spec_chan, (1, 2, 0, 3, 4, 5)).reshape(group, 2, first_len, second_len)

    widened = features.astype(jnp.float32)
    squares = lax.psum(jnp.sum(widened * widened, axis=1), "chan")
    scaled = widened * lax.rsqrt(squares / CHANNELS + 1e-06)[:, None] * norm_gain
    signal = (scaled * pre_gate.astype(jnp.float32)).astype(jnp.bfloat16)

    sig_rows = signal.astype(jnp.float32).reshape(tok_rows, seq_count, group)
    sig_rows = jnp.transpose(sig_rows, (1, 2, 0)).reshape(seq_count, -1, 128)
    sig_chan = exchange(sig_rows, 1).reshape(seq_count, group, tok_rows)
    sig_chan = jnp.transpose(sig_chan, (1, 0, 2)).reshape(group, half_first, second_len)

    digit_order = reversed_digits(seq_count)
    slots = np.arange(stride)
    low_bins = 2 * digit_order[slots // 2] + slots % 2
    row_bins = (low_bins[:, None] + stride * np.arange(ROW_GROUP)[None, :]).reshape(-1)
    row_bins = jnp.asarray(row_bins.astype(np.int32))

    first_in = jnp.arange(half_first, dtype=jnp.int32)
    cos_first, sin_first = rotation(row_bins[:, None] * first_in[None, :], first_len)
    second_in = jnp.arange(second_len, dtype=jnp.int32)
    cos_twist, sin_twist = rotation(row_bins[:, None] * second_in[None, :], all_bins)
    cos_second, sin_second = rotation(second_in[:, None] * second_in[None, :], second_len)

    part_re = mm("rn,cnm->crm", cos_first, sig_chan)
    part_im = -mm("rn,cnm->crm", sin_first, sig_chan)
    twist_re = part_re * cos_twist + part_im * sin_twist
    twist_im = part_im * cos_twist - part_re * sin_twist
    freq_re = mm("crn,nk->crk", twist_re, cos_second) + mm("crn,nk->crk", twist_im, sin_second)
    freq_im = mm("crn,nk->crk", twist_im, cos_second) - mm("crn,nk->crk", twist_re, sin_second)

    filt_re = spec_chan[:, 0]
    filt_im = spec_chan[:, 1]
    prod_re = freq_re * filt_re - freq_im * filt_im
    prod_im = freq_re * filt_im + freq_im * filt_re

    back_re = mm("crk,kn->crn", prod_re, cos_second) - mm("crk,kn->crn", prod_im, sin_second)
    back_im = mm("crk,kn->crn", prod_im, cos_second) + mm("crk,kn->crn", prod_re, sin_second)
    untwist_re = back_re * cos_twist - back_im * sin_twist
    untwist_im = back_im * cos_twist + back_re * sin_twist
    conv = mm("rn,crm->cnm", cos_first, untwist_re) - mm("rn,crm->cnm", sin_first, untwist_im)
    conv = (conv * (1.0 / all_bins)).reshape(group, seq_count, tok_rows)
    conv = jnp.transpose(conv, (1, 0, 2)).reshape(seq_count, -1, 128)
    result = exchange(conv, 2).reshape(seq_count, group, tok_rows)
    result = jnp.transpose(result, (2, 0, 1)).reshape(tok_rows, chan_width)
    gated = post_gate.astype(jnp.float32) * (result + skip_weight * signal.astype(jnp.float32))
    return gated.astype(jnp.bfloat16)


def solution(mesh):
    return jax.shard_map(
        local,
        mesh=mesh,
        in_specs=(
            P("seq", "chan"),
            P("seq", "chan"),
            P("seq", "chan"),
            P("chan"),
            P("chan"),
            P(None, "seq", None, "chan"),
        ),
        out_specs=P("seq", "chan"),
        check_vma=False,
    )
```

```python
import math

import jax
import jax.numpy as jnp
import numpy as np
from jax import lax
from jax.experimental import pallas as pl
from jax.experimental.pallas import tpu as pltpu
from jax.sharding import PartitionSpec as P

CHANNELS = 512
ROW_GROUP = 4
HIGH_DIGIT = 8


PRECISE = lax.Precision.HIGHEST
FULL_TURN = 2.0 * math.pi


def reversed_digits(count):
    levels = count.bit_length() - 1
    positions = np.arange(count)
    result = np.zeros(count, np.int64)
    for bit_pos in range(levels):
        result = result + ((positions >> bit_pos & 1) << levels - 1 - bit_pos)
    return result


def rotation(numerator, denominator):
    angle = (numerator % denominator).astype(jnp.float32) * (FULL_TURN / denominator)
    return (jnp.cos(angle), jnp.sin(angle))


def mm(spec, left, right):
    return jnp.einsum(spec, left, right, precision=PRECISE, preferred_element_type=jnp.float32)


def exchange_kernel(src_ref, dst_ref, mid_ref, send_sem, recv_sem, own_sem):
    high, width = src_ref.shape[0], src_ref.shape[1]
    me = lax.axis_index("seq")
    top, low = me // width, me % width
    mesh_ids = pl.DeviceIdType.MESH
    barrier = pltpu.get_barrier_semaphore()
    for step in range(1, width):
        peer = top * width + lax.rem(low + step, width)
        pl.semaphore_signal(barrier, inc=1, device_id={"seq": peer}, device_id_type=mesh_ids)
    for step in range(1, high):
        peer = lax.rem(top + step, high) * width + low
        pl.semaphore_signal(barrier, inc=1, device_id={"seq": peer}, device_id_type=mesh_ids)
    pl.semaphore_wait(barrier, width + high - 2)

    own = pltpu.make_async_copy(src_ref.at[:, low], mid_ref.at[low], own_sem.at[0])
    own.start()

    def across(step):
        other = lax.rem(low + step, width)
        return pltpu.make_async_remote_copy(
            src_ref.at[:, other],
            mid_ref.at[low],
            send_sem.at[0, step],
            recv_sem.at[0, step],
            device_id={"seq": top * width + other},
            device_id_type=mesh_ids,
        )

    for step in range(1, width):
        across(step).start()
    for step in range(1, width):
        copy = across(step)
        copy.wait_send()
        copy.wait_recv()
    own.wait()

    own = pltpu.make_async_copy(mid_ref.at[:, top], dst_ref.at[top], own_sem.at[1])
    own.start()

    def along(step):
        other = lax.rem(top + step, high)
        return pltpu.make_async_remote_copy(
            mid_ref.at[:, other],
            dst_ref.at[top],
            send_sem.at[1, step],
            recv_sem.at[1, step],
            device_id={"seq": other * width + low},
            device_id_type=mesh_ids,
        )

    for step in range(1, high):
        along(step).start()
    for step in range(1, high):
        copy = along(step)
        copy.wait_send()
        copy.wait_recv()
    own.wait()


def exchange(blocks, tag):
    high, width = blocks.shape[0], blocks.shape[1]
    vmem = pl.BlockSpec(memory_space=pltpu.VMEM)
    return pl.pallas_call(
        exchange_kernel,
        out_shape=jax.ShapeDtypeStruct(blocks.shape, blocks.dtype),
        in_specs=[vmem],
        out_specs=vmem,
        scratch_shapes=[
            pltpu.VMEM((width, high) + blocks.shape[2:], blocks.dtype),
            pltpu.SemaphoreType.DMA((2, max(high, width))),
            pltpu.SemaphoreType.DMA((2, max(high, width))),
            pltpu.SemaphoreType.DMA((2,)),
        ],
        compiler_params=pltpu.CompilerParams(collective_id=tag, has_side_effects=True),
    )(blocks)


def local(features, pre_gate, post_gate, norm_gain, skip_weight, spectrum):
    tok_rows, chan_width = features.shape
    seq_count = lax.axis_size("seq")
    stride = 2 * seq_count
    all_bins = stride * tok_rows
    group = chan_width // seq_count
    first_len = stride * ROW_GROUP
    second_len = all_bins // first_len
    half_first = first_len // 2
    lanes = 128
    own_rows = first_len // seq_count
    tok_tiles = tok_rows // lanes
    high = HIGH_DIGIT
    width = seq_count // high

    spec_rows = spectrum.reshape(2, 2, second_len, ROW_GROUP, seq_count, group)
    spec_rows = jnp.transpose(spec_rows, (4, 0, 5, 1, 3, 2)).reshape(high, width, -1, lanes)
    spec_chan = exchange(spec_rows, 0).reshape(seq_count, 2, group, own_rows, second_len)
    filt_re = spec_chan[:, 0]
    filt_im = spec_chan[:, 1]

    widened = features.astype(jnp.float32)
    squares = lax.psum(jnp.sum(widened * widened, axis=1), "chan")
    scaled = widened * lax.rsqrt(squares / CHANNELS + 1e-06)[:, None] * norm_gain
    signal = (scaled * pre_gate.astype(jnp.float32)).astype(jnp.bfloat16)

    sig_rows = signal.astype(jnp.float32).reshape(tok_tiles, lanes, seq_count, group)
    sig_rows = jnp.transpose(sig_rows, (2, 3, 0, 1)).reshape(high, width, -1, lanes)
    sig_chan = exchange(sig_rows, 1).reshape(seq_count, group, tok_tiles, lanes)

    digit_order = reversed_digits(seq_count)
    slots = np.arange(stride)
    low_bins = 2 * digit_order[slots // 2] + slots % 2
    row_bins = (low_bins[:, None] + stride * np.arange(ROW_GROUP)[None, :]).reshape(-1)
    row_bins = jnp.asarray(row_bins.astype(np.int32))

    first_in = jnp.arange(half_first, dtype=jnp.int32)
    cos_first, sin_first = rotation(row_bins[:, None] * first_in[None, :], first_len)
    second_in = jnp.arange(second_len, dtype=jnp.int32)
    cos_twist, sin_twist = rotation(row_bins[:, None] * second_in[None, :], all_bins)
    cos_twist = cos_twist.reshape(seq_count, 1, own_rows, second_len)
    sin_twist = sin_twist.reshape(seq_count, 1, own_rows, second_len)
    cos_second, sin_second = rotation(second_in[:, None] * second_in[None, :], second_len)

    def rows_of(chan):
        block = sig_chan[:, chan].reshape(half_first, second_len)
        return (mm("rn,nm->rm", cos_first, block), -mm("rn,nm->rm", sin_first, block))

    firsts = [rows_of(chan) for chan in range(group)]
    part_re = jnp.stack([f[0].reshape(seq_count, own_rows, second_len) for f in firsts], axis=1)
    part_im = jnp.stack([f[1].reshape(seq_count, own_rows, second_len) for f in firsts], axis=1)
    twist_re = part_re * cos_twist + part_im * sin_twist
    twist_im = part_im * cos_twist - part_re * sin_twist
    freq_re = mm("scjn,nk->scjk", twist_re, cos_second) + mm("scjn,nk->scjk", twist_im, sin_second)
    freq_im = mm("scjn,nk->scjk", twist_im, cos_second) - mm("scjn,nk->scjk", twist_re, sin_second)

    prod_re = freq_re * filt_re - freq_im * filt_im
    prod_im = freq_re * filt_im + freq_im * filt_re

    back_re = mm("scjk,kn->scjn", prod_re, cos_second) - mm("scjk,kn->scjn", prod_im, sin_second)
    back_im = mm("scjk,kn->scjn", prod_im, cos_second) + mm("scjk,kn->scjn", prod_re, sin_second)
    untwist_re = back_re * cos_twist - back_im * sin_twist
    untwist_im = back_im * cos_twist + back_re * sin_twist

    def out_of(chan):
        w_re = untwist_re[:, chan].reshape(first_len, second_len)
        w_im = untwist_im[:, chan].reshape(first_len, second_len)
        block = mm("rn,rm->nm", cos_first, w_re) - mm("rn,rm->nm", sin_first, w_im)
        return block.reshape(seq_count, tok_tiles, lanes)

    conv = jnp.stack([out_of(chan) for chan in range(group)], axis=1) * (1.0 / all_bins)
    conv = conv.reshape(high, width, -1, lanes)
    result = exchange(conv, 2).reshape(seq_count, group, tok_tiles, lanes)
    result = jnp.transpose(result, (2, 3, 0, 1)).reshape(tok_rows, chan_width)
    gated = post_gate.astype(jnp.float32) * (result + skip_weight * signal.astype(jnp.float32))
    return gated.astype(jnp.bfloat16)


def solution(mesh):
    return jax.shard_map(
        local,
        mesh=mesh,
        in_specs=(
            P("seq", "chan"),
            P("seq", "chan"),
            P("seq", "chan"),
            P("chan"),
            P("chan"),
            P(None, "seq", None, "chan"),
        ),
        out_specs=P("seq", "chan"),
        check_vma=False,
    )
```

```python
import math

import jax
import jax.numpy as jnp
import numpy as np
from jax import lax
from jax.experimental import pallas as pl
from jax.experimental.pallas import tpu as pltpu
from jax.sharding import PartitionSpec as P

CHANNELS = 512
ROW_GROUP = 4
HIGH_DIGIT = 8


PRECISE = lax.Precision.HIGHEST
FULL_TURN = 2.0 * math.pi


def reversed_digits(count):
    levels = count.bit_length() - 1
    positions = np.arange(count)
    result = np.zeros(count, np.int64)
    for bit_pos in range(levels):
        result = result + ((positions >> bit_pos & 1) << levels - 1 - bit_pos)
    return result


def rotation(numerator, denominator):
    angle = (numerator % denominator).astype(jnp.float32) * (FULL_TURN / denominator)
    return (jnp.cos(angle), jnp.sin(angle))


def mm(spec, left, right):
    return jnp.einsum(spec, left, right, precision=PRECISE, preferred_element_type=jnp.float32)


def exchange_kernel(src_ref, dst_ref, send_sem, recv_sem, own_sem):
    count = src_ref.shape[0]
    me = lax.axis_index("seq")
    mesh_ids = pl.DeviceIdType.MESH
    barrier = pltpu.get_barrier_semaphore()

    def greet(step, carry):
        peer = lax.rem(me + step, count)
        pl.semaphore_signal(barrier, inc=1, device_id={"seq": peer}, device_id_type=mesh_ids)
        return carry

    lax.fori_loop(1, count, greet, 0)
    pl.semaphore_wait(barrier, count - 1)
    own = pltpu.make_async_copy(src_ref.at[me], dst_ref.at[me], own_sem)
    own.start()

    def remote(step):
        peer = lax.rem(me + step, count)
        return pltpu.make_async_remote_copy(
            src_ref.at[peer],
            dst_ref.at[me],
            send_sem.at[step],
            recv_sem.at[step],
            device_id={"seq": peer},
            device_id_type=mesh_ids,
        )

    def send(step, carry):
        remote(step).start()
        return carry

    lax.fori_loop(1, count, send, 0)

    def finish(step, carry):
        copy = remote(step)
        copy.wait_send()
        copy.wait_recv()
        return carry

    lax.fori_loop(1, count, finish, 0)
    own.wait()


def exchange(blocks, tag):
    count = blocks.shape[0]
    vmem = pl.BlockSpec(memory_space=pltpu.VMEM)
    return pl.pallas_call(
        exchange_kernel,
        out_shape=jax.ShapeDtypeStruct(blocks.shape, blocks.dtype),
        in_specs=[vmem],
        out_specs=vmem,
        scratch_shapes=[
            pltpu.SemaphoreType.DMA((count,)),
            pltpu.SemaphoreType.DMA((count,)),
            pltpu.SemaphoreType.DMA,
        ],
        compiler_params=pltpu.CompilerParams(collective_id=tag, has_side_effects=True),
    )(blocks)


def local(features, pre_gate, post_gate, norm_gain, skip_weight, spectrum):
    tok_rows, chan_width = features.shape
    seq_count = lax.axis_size("seq")
    stride = 2 * seq_count
    all_bins = stride * tok_rows
    group = chan_width // seq_count
    first_len = stride * ROW_GROUP
    second_len = all_bins // first_len
    half_first = first_len // 2
    lanes = 128
    tok_tiles = tok_rows // lanes

    spec_rows = spectrum.reshape(2, 2, second_len, ROW_GROUP, chan_width)
    spec_rows = jnp.transpose(spec_rows, (4, 0, 1, 3, 2))
    spec_chan = lax.all_to_all(spec_rows, "seq", 0, 2, tiled=True)
    spec_chan = spec_chan.reshape(group, 2, first_len, second_len)

    widened = features.astype(jnp.float32)
    squares = lax.psum(jnp.sum(widened * widened, axis=1), "chan")
    scaled = widened * lax.rsqrt(squares / CHANNELS + 1e-06)[:, None] * norm_gain
    signal = (scaled * pre_gate.astype(jnp.float32)).astype(jnp.bfloat16)

    sig_rows = signal.astype(jnp.float32).reshape(tok_tiles, lanes, seq_count, group)
    sig_rows = jnp.transpose(sig_rows, (2, 3, 0, 1)).reshape(seq_count, -1, lanes)
    sig_chan = exchange(sig_rows, 1).reshape(seq_count, group, tok_tiles, lanes)
    sig_chan = jnp.transpose(sig_chan, (1, 0, 2, 3)).reshape(group, half_first, second_len)

    digit_order = reversed_digits(seq_count)
    slots = np.arange(stride)
    low_bins = 2 * digit_order[slots // 2] + slots % 2
    row_bins = (low_bins[:, None] + stride * np.arange(ROW_GROUP)[None, :]).reshape(-1)
    row_bins = jnp.asarray(row_bins.astype(np.int32))

    first_in = jnp.arange(half_first, dtype=jnp.int32)
    cos_first, sin_first = rotation(row_bins[:, None] * first_in[None, :], first_len)
    second_in = jnp.arange(second_len, dtype=jnp.int32)
    cos_twist, sin_twist = rotation(row_bins[:, None] * second_in[None, :], all_bins)
    cos_second, sin_second = rotation(second_in[:, None] * second_in[None, :], second_len)

    part_re = mm("rn,cnm->crm", cos_first, sig_chan)
    part_im = -mm("rn,cnm->crm", sin_first, sig_chan)
    twist_re = part_re * cos_twist + part_im * sin_twist
    twist_im = part_im * cos_twist - part_re * sin_twist
    freq_re = mm("crn,nk->crk", twist_re, cos_second) + mm("crn,nk->crk", twist_im, sin_second)
    freq_im = mm("crn,nk->crk", twist_im, cos_second) - mm("crn,nk->crk", twist_re, sin_second)

    filt_re = spec_chan[:, 0]
    filt_im = spec_chan[:, 1]
    prod_re = freq_re * filt_re - freq_im * filt_im
    prod_im = freq_re * filt_im + freq_im * filt_re

    back_re = mm("crk,kn->crn", prod_re, cos_second) - mm("crk,kn->crn", prod_im, sin_second)
    back_im = mm("crk,kn->crn", prod_im, cos_second) + mm("crk,kn->crn", prod_re, sin_second)
    untwist_re = back_re * cos_twist - back_im * sin_twist
    untwist_im = back_im * cos_twist + back_re * sin_twist
    conv = mm("rn,crm->cnm", cos_first, untwist_re) - mm("rn,crm->cnm", sin_first, untwist_im)
    conv = (conv * (1.0 / all_bins)).reshape(group, seq_count, tok_tiles, lanes)
    conv = jnp.transpose(conv, (1, 0, 2, 3)).reshape(seq_count, -1, lanes)
    result = exchange(conv, 2).reshape(seq_count, group, tok_tiles, lanes)
    result = jnp.transpose(result, (2, 3, 0, 1)).reshape(tok_rows, chan_width)
    gated = post_gate.astype(jnp.float32) * (result + skip_weight * signal.astype(jnp.float32))
    return gated.astype(jnp.bfloat16)


def solution(mesh):
    return jax.shard_map(
        local,
        mesh=mesh,
        in_specs=(
            P("seq", "chan"),
            P("seq", "chan"),
            P("seq", "chan"),
            P("chan"),
            P("chan"),
            P(None, "seq", None, "chan"),
        ),
        out_specs=P("seq", "chan"),
        check_vma=False,
    )
```

```python
import math

import jax
import jax.numpy as jnp
import numpy as np
from jax import lax
from jax.experimental import pallas as pl
from jax.experimental.pallas import tpu as pltpu
from jax.sharding import PartitionSpec as P

CHANNELS = 512
ROW_GROUP = 4
HIGH_DIGIT = 8


PRECISE = lax.Precision.HIGH
FULL_TURN = 2.0 * math.pi


def reversed_digits(count):
    levels = count.bit_length() - 1
    positions = np.arange(count)
    result = np.zeros(count, np.int64)
    for bit_pos in range(levels):
        result = result + ((positions >> bit_pos & 1) << levels - 1 - bit_pos)
    return result


def rotation(numerator, denominator):
    angle = (numerator % denominator).astype(jnp.float32) * (FULL_TURN / denominator)
    return (jnp.cos(angle), jnp.sin(angle))


def mm(spec, left, right):
    return jnp.einsum(spec, left, right, precision=PRECISE, preferred_element_type=jnp.float32)


def exchange_kernel(src_ref, dst_ref, send_sem, recv_sem, own_sem):
    count = src_ref.shape[0]
    me = lax.axis_index("seq")
    mesh_ids = pl.DeviceIdType.MESH
    barrier = pltpu.get_barrier_semaphore()

    def greet(step, carry):
        peer = lax.rem(me + step, count)
        pl.semaphore_signal(barrier, inc=1, device_id={"seq": peer}, device_id_type=mesh_ids)
        return carry

    lax.fori_loop(1, count, greet, 0)
    pl.semaphore_wait(barrier, count - 1)
    own = pltpu.make_async_copy(src_ref.at[me], dst_ref.at[me], own_sem)
    own.start()

    def remote(step):
        peer = lax.rem(me + step, count)
        return pltpu.make_async_remote_copy(
            src_ref.at[peer],
            dst_ref.at[me],
            send_sem.at[step],
            recv_sem.at[step],
            device_id={"seq": peer},
            device_id_type=mesh_ids,
        )

    def send(step, carry):
        remote(step).start()
        return carry

    lax.fori_loop(1, count, send, 0)

    def finish(step, carry):
        copy = remote(step)
        copy.wait_send()
        copy.wait_recv()
        return carry

    lax.fori_loop(1, count, finish, 0)
    own.wait()


def exchange(blocks, tag):
    count = blocks.shape[0]
    vmem = pl.BlockSpec(memory_space=pltpu.VMEM)
    return pl.pallas_call(
        exchange_kernel,
        out_shape=jax.ShapeDtypeStruct(blocks.shape, blocks.dtype),
        in_specs=[vmem],
        out_specs=vmem,
        scratch_shapes=[
            pltpu.SemaphoreType.DMA((count,)),
            pltpu.SemaphoreType.DMA((count,)),
            pltpu.SemaphoreType.DMA,
        ],
        compiler_params=pltpu.CompilerParams(collective_id=tag, has_side_effects=True),
    )(blocks)


def local(features, pre_gate, post_gate, norm_gain, skip_weight, spectrum):
    tok_rows, chan_width = features.shape
    seq_count = lax.axis_size("seq")
    stride = 2 * seq_count
    all_bins = stride * tok_rows
    group = chan_width // seq_count
    first_len = stride * ROW_GROUP
    second_len = all_bins // first_len
    half_first = first_len // 2
    lanes = 128
    tok_tiles = tok_rows // lanes

    spec_rows = spectrum.reshape(2, 2, second_len, ROW_GROUP, chan_width)
    spec_rows = jnp.transpose(spec_rows, (4, 0, 1, 3, 2))
    spec_chan = lax.all_to_all(spec_rows, "seq", 0, 2, tiled=True)
    spec_chan = spec_chan.reshape(group, 2, first_len, second_len)

    widened = features.astype(jnp.float32)
    squares = lax.psum(jnp.sum(widened * widened, axis=1), "chan")
    scaled = widened * lax.rsqrt(squares / CHANNELS + 1e-06)[:, None] * norm_gain
    signal = (scaled * pre_gate.astype(jnp.float32)).astype(jnp.bfloat16)

    sig_rows = signal.astype(jnp.float32).reshape(tok_tiles, lanes, seq_count, group)
    sig_rows = jnp.transpose(sig_rows, (2, 3, 0, 1)).reshape(seq_count, -1, lanes)
    sig_chan = exchange(sig_rows, 1).reshape(seq_count, group, tok_tiles, lanes)
    sig_chan = jnp.transpose(sig_chan, (1, 0, 2, 3)).reshape(group, half_first, second_len)

    digit_order = reversed_digits(seq_count)
    slots = np.arange(stride)
    low_bins = 2 * digit_order[slots // 2] + slots % 2
    row_bins = (low_bins[:, None] + stride * np.arange(ROW_GROUP)[None, :]).reshape(-1)
    row_bins = jnp.asarray(row_bins.astype(np.int32))

    first_in = jnp.arange(half_first, dtype=jnp.int32)
    cos_first, sin_first = rotation(row_bins[:, None] * first_in[None, :], first_len)
    second_in = jnp.arange(second_len, dtype=jnp.int32)
    cos_twist, sin_twist = rotation(row_bins[:, None] * second_in[None, :], all_bins)
    cos_second, sin_second = rotation(second_in[:, None] * second_in[None, :], second_len)

    part_re = mm("rn,cnm->crm", cos_first, sig_chan)
    part_im = -mm("rn,cnm->crm", sin_first, sig_chan)
    twist_re = part_re * cos_twist + part_im * sin_twist
    twist_im = part_im * cos_twist - part_re * sin_twist
    freq_re = mm("crn,nk->crk", twist_re, cos_second) + mm("crn,nk->crk", twist_im, sin_second)
    freq_im = mm("crn,nk->crk", twist_im, cos_second) - mm("crn,nk->crk", twist_re, sin_second)

    filt_re = spec_chan[:, 0]
    filt_im = spec_chan[:, 1]
    prod_re = freq_re * filt_re - freq_im * filt_im
    prod_im = freq_re * filt_im + freq_im * filt_re

    back_re = mm("crk,kn->crn", prod_re, cos_second) - mm("crk,kn->crn", prod_im, sin_second)
    back_im = mm("crk,kn->crn", prod_im, cos_second) + mm("crk,kn->crn", prod_re, sin_second)
    untwist_re = back_re * cos_twist - back_im * sin_twist
    untwist_im = back_im * cos_twist + back_re * sin_twist
    conv = mm("rn,crm->cnm", cos_first, untwist_re) - mm("rn,crm->cnm", sin_first, untwist_im)
    conv = (conv * (1.0 / all_bins)).reshape(group, seq_count, tok_tiles, lanes)
    conv = jnp.transpose(conv, (1, 0, 2, 3)).reshape(seq_count, -1, lanes)
    result = exchange(conv, 2).reshape(seq_count, group, tok_tiles, lanes)
    result = jnp.transpose(result, (2, 3, 0, 1)).reshape(tok_rows, chan_width)
    gated = post_gate.astype(jnp.float32) * (result + skip_weight * signal.astype(jnp.float32))
    return gated.astype(jnp.bfloat16)


def solution(mesh):
    return jax.shard_map(
        local,
        mesh=mesh,
        in_specs=(
            P("seq", "chan"),
            P("seq", "chan"),
            P("seq", "chan"),
            P("chan"),
            P("chan"),
            P(None, "seq", None, "chan"),
        ),
        out_specs=P("seq", "chan"),
        check_vma=False,
    )
```

```python
import math

import jax
import jax.numpy as jnp
import numpy as np
from jax import lax
from jax.experimental import pallas as pl
from jax.experimental.pallas import tpu as pltpu
from jax.sharding import PartitionSpec as P

CHANNELS = 512
ROW_GROUP = 4
HIGH_DIGIT = 8


PRECISE = lax.Precision.HIGH
FULL_TURN = 2.0 * math.pi


def reversed_digits(count):
    levels = count.bit_length() - 1
    positions = np.arange(count)
    result = np.zeros(count, np.int64)
    for bit_pos in range(levels):
        result = result + ((positions >> bit_pos & 1) << levels - 1 - bit_pos)
    return result


def rotation(numerator, denominator):
    angle = (numerator % denominator).astype(jnp.float32) * (FULL_TURN / denominator)
    return (jnp.cos(angle), jnp.sin(angle))


def mm(spec, left, right):
    return jnp.einsum(spec, left, right, precision=PRECISE, preferred_element_type=jnp.float32)


def exchange_kernel(src_ref, dst_ref, send_sem, recv_sem, own_sem):
    count = src_ref.shape[0]
    me = lax.axis_index("seq")
    mesh_ids = pl.DeviceIdType.MESH
    barrier = pltpu.get_barrier_semaphore()

    def greet(step, carry):
        peer = lax.rem(me + step, count)
        pl.semaphore_signal(barrier, inc=1, device_id={"seq": peer}, device_id_type=mesh_ids)
        return carry

    lax.fori_loop(1, count, greet, 0)
    pl.semaphore_wait(barrier, count - 1)
    own = pltpu.make_async_copy(src_ref.at[me], dst_ref.at[me], own_sem)
    own.start()

    def remote(step):
        peer = lax.rem(me + step, count)
        return pltpu.make_async_remote_copy(
            src_ref.at[peer],
            dst_ref.at[me],
            send_sem.at[step],
            recv_sem.at[step],
            device_id={"seq": peer},
            device_id_type=mesh_ids,
        )

    def send(step, carry):
        remote(step).start()
        return carry

    lax.fori_loop(1, count, send, 0)

    def finish(step, carry):
        copy = remote(step)
        copy.wait_send()
        copy.wait_recv()
        return carry

    lax.fori_loop(1, count, finish, 0)
    own.wait()


def exchange(blocks, tag):
    count = blocks.shape[0]
    vmem = pl.BlockSpec(memory_space=pltpu.VMEM)
    return pl.pallas_call(
        exchange_kernel,
        out_shape=jax.ShapeDtypeStruct(blocks.shape, blocks.dtype),
        in_specs=[vmem],
        out_specs=vmem,
        scratch_shapes=[
            pltpu.SemaphoreType.DMA((count,)),
            pltpu.SemaphoreType.DMA((count,)),
            pltpu.SemaphoreType.DMA,
        ],
        compiler_params=pltpu.CompilerParams(collective_id=tag, has_side_effects=True),
    )(blocks)


def front_kernel(
    feat_ref, gate_ref, gain_ref, spec_ref,
    sig_out, sig_recv, spec_recv,
    sq_mine, sq_recv, sig_send, spec_sems, sig_sems, chan_sems, own_sems,
):
    count = spec_ref.shape[0]
    chans = sq_recv.shape[0]
    me = lax.axis_index("seq")
    mine = lax.axis_index("chan")
    mesh_ids = pl.DeviceIdType.MESH
    barrier = pltpu.get_barrier_semaphore()

    def greet(step, carry):
        peer = lax.rem(me + step, count)
        pl.semaphore_signal(barrier, inc=1, device_id={"seq": peer}, device_id_type=mesh_ids)
        return carry

    lax.fori_loop(1, count, greet, 0)
    for step in range(1, chans):
        peer = lax.rem(mine + step, chans)
        pl.semaphore_signal(barrier, inc=1, device_id={"chan": peer}, device_id_type=mesh_ids)
    pl.semaphore_wait(barrier, count + chans - 2)

    def spec_copy(step):
        peer = lax.rem(me + step, count)
        return pltpu.make_async_remote_copy(
            spec_ref.at[peer],
            spec_recv.at[me],
            spec_sems.at[0, step],
            spec_sems.at[1, step],
            device_id={"seq": peer},
            device_id_type=mesh_ids,
        )

    spec_own = pltpu.make_async_copy(spec_ref.at[me], spec_recv.at[me], own_sems.at[0])
    spec_own.start()

    def spec_send(step, carry):
        spec_copy(step).start()
        return carry

    lax.fori_loop(1, count, spec_send, 0)

    feat = feat_ref[...].astype(jnp.float32)
    part = jnp.sum(feat * feat, axis=0, keepdims=True)
    sq_mine[...] = jnp.broadcast_to(part, sq_mine.shape)

    def chan_copy(step):
        peer = lax.rem(mine + step, chans)
        return pltpu.make_async_remote_copy(
            sq_mine,
            sq_recv.at[mine],
            chan_sems.at[0, step],
            chan_sems.at[1, step],
            device_id={"chan": peer},
            device_id_type=mesh_ids,
        )

    for step in range(1, chans):
        chan_copy(step).start()
    for step in range(1, chans):
        copy = chan_copy(step)
        copy.wait_send()
        copy.wait_recv()
    total = part
    for step in range(1, chans):
        other = lax.rem(mine + step, chans)
        total = total + sq_recv[other][0:1, :]
    scale = lax.rsqrt(total / CHANNELS + 1e-06)
    signal = (feat * scale * gain_ref[...] * gate_ref[...].astype(jnp.float32)).astype(jnp.bfloat16)
    sig_out[...] = signal
    wide = signal.astype(jnp.float32)
    pair = sig_send.shape[1]
    for peer in range(count):
        sig_send[peer] = wide[pair * peer:pair * peer + pair, :]

    def sig_copy(step):
        peer = lax.rem(me + step, count)
        return pltpu.make_async_remote_copy(
            sig_send.at[peer],
            sig_recv.at[me],
            sig_sems.at[0, step],
            sig_sems.at[1, step],
            device_id={"seq": peer},
            device_id_type=mesh_ids,
        )

    sig_own = pltpu.make_async_copy(sig_send.at[me], sig_recv.at[me], own_sems.at[1])
    sig_own.start()

    def sig_start(step, carry):
        sig_copy(step).start()
        return carry

    lax.fori_loop(1, count, sig_start, 0)

    def sig_finish(step, carry):
        copy = sig_copy(step)
        copy.wait_send()
        copy.wait_recv()
        return carry

    lax.fori_loop(1, count, sig_finish, 0)
    sig_own.wait()

    def spec_finish(step, carry):
        copy = spec_copy(step)
        copy.wait_send()
        copy.wait_recv()
        return carry

    lax.fori_loop(1, count, spec_finish, 0)
    spec_own.wait()


def front(feat_t, gate_t, gain_col, spec_rows, chans):
    count = spec_rows.shape[0]
    width, length = feat_t.shape
    pair = width // count
    vmem = pl.BlockSpec(memory_space=pltpu.VMEM)
    return pl.pallas_call(
        front_kernel,
        out_shape=(
            jax.ShapeDtypeStruct((width, length), jnp.bfloat16),
            jax.ShapeDtypeStruct((count, pair, length), jnp.float32),
            jax.ShapeDtypeStruct(spec_rows.shape, spec_rows.dtype),
        ),
        in_specs=[vmem] * 4,
        out_specs=(vmem, vmem, vmem),
        scratch_shapes=[
            pltpu.VMEM((8, length), jnp.float32),
            pltpu.VMEM((chans, 8, length), jnp.float32),
            pltpu.VMEM((count, pair, length), jnp.float32),
            pltpu.SemaphoreType.DMA((2, count)),
            pltpu.SemaphoreType.DMA((2, count)),
            pltpu.SemaphoreType.DMA((2, chans)),
            pltpu.SemaphoreType.DMA((2,)),
        ],
        compiler_params=pltpu.CompilerParams(collective_id=0, has_side_effects=True),
    )(feat_t, gate_t, gain_col, spec_rows)


def local(features, pre_gate, post_gate, norm_gain, skip_weight, spectrum):
    tok_rows, chan_width = features.shape
    seq_count = lax.axis_size("seq")
    chans = lax.axis_size("chan")
    stride = 2 * seq_count
    all_bins = stride * tok_rows
    group = chan_width // seq_count
    first_len = stride * ROW_GROUP
    second_len = all_bins // first_len
    half_first = first_len // 2
    lanes = 128
    tok_tiles = tok_rows // lanes

    spec_rows = spectrum.reshape(2, 2, second_len, ROW_GROUP, chan_width)
    spec_rows = jnp.transpose(spec_rows, (4, 0, 1, 3, 2)).reshape(seq_count, -1, ROW_GROUP * second_len)
    signal_t, sig_chan, spec_chan = front(
        features.T, pre_gate.T, norm_gain.reshape(chan_width, 1), spec_rows, chans
    )
    spec_chan = spec_chan.reshape(seq_count, group, 2, 2, ROW_GROUP * second_len)
    spec_chan = jnp.transpose(spec_chan, (1, 2, 0, 3, 4)).reshape(group, 2, first_len, second_len)
    sig_chan = jnp.transpose(sig_chan, (1, 0, 2)).reshape(group, half_first, second_len)
    signal = signal_t.T

    digit_order = reversed_digits(seq_count)
    slots = np.arange(stride)
    low_bins = 2 * digit_order[slots // 2] + slots % 2
    row_bins = (low_bins[:, None] + stride * np.arange(ROW_GROUP)[None, :]).reshape(-1)
    row_bins = jnp.asarray(row_bins.astype(np.int32))

    first_in = jnp.arange(half_first, dtype=jnp.int32)
    cos_first, sin_first = rotation(row_bins[:, None] * first_in[None, :], first_len)
    second_in = jnp.arange(second_len, dtype=jnp.int32)
    cos_twist, sin_twist = rotation(row_bins[:, None] * second_in[None, :], all_bins)
    cos_second, sin_second = rotation(second_in[:, None] * second_in[None, :], second_len)

    part_re = mm("rn,cnm->crm", cos_first, sig_chan)
    part_im = -mm("rn,cnm->crm", sin_first, sig_chan)
    twist_re = part_re * cos_twist + part_im * sin_twist
    twist_im = part_im * cos_twist - part_re * sin_twist
    freq_re = mm("crn,nk->crk", twist_re, cos_second) + mm("crn,nk->crk", twist_im, sin_second)
    freq_im = mm("crn,nk->crk", twist_im, cos_second) - mm("crn,nk->crk", twist_re, sin_second)

    filt_re = spec_chan[:, 0]
    filt_im = spec_chan[:, 1]
    prod_re = freq_re * filt_re - freq_im * filt_im
    prod_im = freq_re * filt_im + freq_im * filt_re

    back_re = mm("crk,kn->crn", prod_re, cos_second) - mm("crk,kn->crn", prod_im, sin_second)
    back_im = mm("crk,kn->crn", prod_im, cos_second) + mm("crk,kn->crn", prod_re, sin_second)
    untwist_re = back_re * cos_twist - back_im * sin_twist
    untwist_im = back_im * cos_twist + back_re * sin_twist
    conv = mm("rn,crm->cnm", cos_first, untwist_re) - mm("rn,crm->cnm", sin_first, untwist_im)
    conv = (conv * (1.0 / all_bins)).reshape(group, seq_count, tok_tiles, lanes)
    conv = jnp.transpose(conv, (1, 0, 2, 3)).reshape(seq_count, -1, lanes)
    result = exchange(conv, 2).reshape(seq_count, group, tok_tiles, lanes)
    result = jnp.transpose(result, (2, 3, 0, 1)).reshape(tok_rows, chan_width)
    gated = post_gate.astype(jnp.float32) * (result + skip_weight * signal.astype(jnp.float32))
    return gated.astype(jnp.bfloat16)


def solution(mesh):
    return jax.shard_map(
        local,
        mesh=mesh,
        in_specs=(
            P("seq", "chan"),
            P("seq", "chan"),
            P("seq", "chan"),
            P("chan"),
            P("chan"),
            P(None, "seq", None, "chan"),
        ),
        out_specs=P("seq", "chan"),
        check_vma=False,
    )
```

```python
import math

import jax
import jax.numpy as jnp
import numpy as np
from jax import lax
from jax.experimental import pallas as pl
from jax.experimental.pallas import tpu as pltpu
from jax.sharding import PartitionSpec as P

CHANNELS = 512
ROW_GROUP = 4
HIGH_DIGIT = 8


PRECISE = lax.Precision.HIGH
FULL_TURN = 2.0 * math.pi


def reversed_digits(count):
    levels = count.bit_length() - 1
    positions = np.arange(count)
    result = np.zeros(count, np.int64)
    for bit_pos in range(levels):
        result = result + ((positions >> bit_pos & 1) << levels - 1 - bit_pos)
    return result


def rotation(numerator, denominator):
    angle = (numerator % denominator).astype(jnp.float32) * (FULL_TURN / denominator)
    return (jnp.cos(angle), jnp.sin(angle))


def mm(spec, left, right):
    return jnp.einsum(spec, left, right, precision=PRECISE, preferred_element_type=jnp.float32)


def exchange_kernel(src_ref, dst_ref, send_sem, recv_sem, own_sem):
    count = src_ref.shape[0]
    me = lax.axis_index("seq")
    mesh_ids = pl.DeviceIdType.MESH
    barrier = pltpu.get_barrier_semaphore()

    def greet(step, carry):
        peer = lax.rem(me + step, count)
        pl.semaphore_signal(barrier, inc=1, device_id={"seq": peer}, device_id_type=mesh_ids)
        return carry

    lax.fori_loop(1, count, greet, 0)
    pl.semaphore_wait(barrier, count - 1)
    own = pltpu.make_async_copy(src_ref.at[me], dst_ref.at[me], own_sem)
    own.start()

    def remote(step):
        peer = lax.rem(me + step, count)
        return pltpu.make_async_remote_copy(
            src_ref.at[peer],
            dst_ref.at[me],
            send_sem.at[step],
            recv_sem.at[step],
            device_id={"seq": peer},
            device_id_type=mesh_ids,
        )

    def send(step, carry):
        remote(step).start()
        return carry

    lax.fori_loop(1, count, send, 0)

    def finish(step, carry):
        copy = remote(step)
        copy.wait_send()
        copy.wait_recv()
        return carry

    lax.fori_loop(1, count, finish, 0)
    own.wait()


def exchange(blocks, tag):
    count = blocks.shape[0]
    vmem = pl.BlockSpec(memory_space=pltpu.VMEM)
    return pl.pallas_call(
        exchange_kernel,
        out_shape=jax.ShapeDtypeStruct(blocks.shape, blocks.dtype),
        in_specs=[vmem],
        out_specs=vmem,
        scratch_shapes=[
            pltpu.SemaphoreType.DMA((count,)),
            pltpu.SemaphoreType.DMA((count,)),
            pltpu.SemaphoreType.DMA,
        ],
        compiler_params=pltpu.CompilerParams(collective_id=tag, has_side_effects=True),
    )(blocks)


def front_kernel(
    feat_ref, gate_ref, gain_ref, spec_ref,
    sig_out, sig_recv, spec_recv,
    sq_mine, sq_recv, sig_send, spec_sems, sig_sems, chan_sems, own_sems,
):
    count = spec_ref.shape[0]
    chans = sq_recv.shape[0]
    me = lax.axis_index("seq")
    mine = lax.axis_index("chan")
    mesh_ids = pl.DeviceIdType.MESH
    barrier = pltpu.get_barrier_semaphore()

    def greet(step, carry):
        peer = lax.rem(me + step, count)
        pl.semaphore_signal(barrier, inc=1, device_id={"seq": peer}, device_id_type=mesh_ids)
        return carry

    lax.fori_loop(1, count, greet, 0)
    for step in range(1, chans):
        peer = lax.rem(mine + step, chans)
        pl.semaphore_signal(barrier, inc=1, device_id={"chan": peer}, device_id_type=mesh_ids)
    pl.semaphore_wait(barrier, count + chans - 2)

    def spec_copy(step):
        peer = lax.rem(me + step, count)
        return pltpu.make_async_remote_copy(
            spec_ref.at[peer],
            spec_recv.at[me],
            spec_sems.at[0, step],
            spec_sems.at[1, step],
            device_id={"seq": peer},
            device_id_type=mesh_ids,
        )

    spec_own = pltpu.make_async_copy(spec_ref.at[me], spec_recv.at[me], own_sems.at[0])
    spec_own.start()

    def spec_send(step, carry):
        spec_copy(step).start()
        return carry

    lax.fori_loop(1, count, spec_send, 0)

    feat = feat_ref[...].astype(jnp.float32)
    part = jnp.sum(feat * feat, axis=0, keepdims=True)
    sq_mine[...] = jnp.broadcast_to(part, sq_mine.shape)

    def chan_copy(step):
        peer = lax.rem(mine + step, chans)
        return pltpu.make_async_remote_copy(
            sq_mine,
            sq_recv.at[mine],
            chan_sems.at[0, step],
            chan_sems.at[1, step],
            device_id={"chan": peer},
            device_id_type=mesh_ids,
        )

    for step in range(1, chans):
        chan_copy(step).start()
    for step in range(1, chans):
        copy = chan_copy(step)
        copy.wait_send()
        copy.wait_recv()
    total = part
    for step in range(1, chans):
        other = lax.rem(mine + step, chans)
        total = total + sq_recv[other][0:1, :]
    scale = lax.rsqrt(total / CHANNELS + 1e-06)
    signal = (feat * scale * gain_ref[...] * gate_ref[...].astype(jnp.float32)).astype(jnp.bfloat16)
    sig_out[...] = signal
    wide = signal.astype(jnp.float32)
    pair = sig_send.shape[1]
    for peer in range(count):
        sig_send[peer] = wide[pair * peer:pair * peer + pair, :]

    def sig_copy(step):
        peer = lax.rem(me + step, count)
        return pltpu.make_async_remote_copy(
            sig_send.at[peer],
            sig_recv.at[me],
            sig_sems.at[0, step],
            sig_sems.at[1, step],
            device_id={"seq": peer},
            device_id_type=mesh_ids,
        )

    sig_own = pltpu.make_async_copy(sig_send.at[me], sig_recv.at[me], own_sems.at[1])
    sig_own.start()

    def sig_start(step, carry):
        sig_copy(step).start()
        return carry

    lax.fori_loop(1, count, sig_start, 0)

    def sig_finish(step, carry):
        copy = sig_copy(step)
        copy.wait_send()
        copy.wait_recv()
        return carry

    lax.fori_loop(1, count, sig_finish, 0)
    sig_own.wait()

    def spec_finish(step, carry):
        copy = spec_copy(step)
        copy.wait_send()
        copy.wait_recv()
        return carry

    lax.fori_loop(1, count, spec_finish, 0)
    spec_own.wait()


def front(feat_t, gate_t, gain_col, spec_rows, chans):
    count = spec_rows.shape[0]
    width, length = feat_t.shape
    pair = width // count
    vmem = pl.BlockSpec(memory_space=pltpu.VMEM)
    return pl.pallas_call(
        front_kernel,
        out_shape=(
            jax.ShapeDtypeStruct((width, length), jnp.bfloat16),
            jax.ShapeDtypeStruct((count, pair, length), jnp.float32),
            jax.ShapeDtypeStruct(spec_rows.shape, spec_rows.dtype),
        ),
        in_specs=[vmem] * 4,
        out_specs=(vmem, vmem, vmem),
        scratch_shapes=[
            pltpu.VMEM((8, length), jnp.float32),
            pltpu.VMEM((chans, 8, length), jnp.float32),
            pltpu.VMEM((count, pair, length), jnp.float32),
            pltpu.SemaphoreType.DMA((2, count)),
            pltpu.SemaphoreType.DMA((2, count)),
            pltpu.SemaphoreType.DMA((2, chans)),
            pltpu.SemaphoreType.DMA((2,)),
        ],
        compiler_params=pltpu.CompilerParams(collective_id=0, has_side_effects=True),
    )(feat_t, gate_t, gain_col, spec_rows)


def local(features, pre_gate, post_gate, norm_gain, skip_weight, spectrum):
    tok_rows, chan_width = features.shape
    seq_count = lax.axis_size("seq")
    chans = lax.axis_size("chan")
    stride = 2 * seq_count
    all_bins = stride * tok_rows
    group = chan_width // seq_count
    first_len = stride * ROW_GROUP
    second_len = all_bins // first_len
    half_first = first_len // 2
    lanes = 128
    tok_tiles = tok_rows // lanes

    half_group = ROW_GROUP // 2
    spec_rows = spectrum.reshape(2, 2, second_len, half_group, 2, chan_width)
    spec_rows = jnp.transpose(spec_rows, (5, 0, 1, 3, 4, 2)).astype(jnp.bfloat16)
    spec_rows = spec_rows.reshape(seq_count, -1, 2 * second_len)
    signal_t, sig_chan, spec_chan = front(
        features.T, pre_gate.T, norm_gain.reshape(chan_width, 1), spec_rows, chans
    )
    spec_chan = spec_chan.reshape(seq_count, group, 2, -1, 2 * second_len)
    spec_chan = jnp.transpose(spec_chan, (1, 2, 0, 3, 4)).astype(jnp.float32)
    spec_chan = spec_chan.reshape(group, 2, first_len, second_len)
    sig_chan = jnp.transpose(sig_chan, (1, 0, 2)).reshape(group, half_first, second_len)
    signal = signal_t.T

    digit_order = reversed_digits(seq_count)
    slots = np.arange(stride)
    low_bins = 2 * digit_order[slots // 2] + slots % 2
    row_bins = (low_bins[:, None] + stride * np.arange(ROW_GROUP)[None, :]).reshape(-1)
    row_bins = jnp.asarray(row_bins.astype(np.int32))

    first_in = jnp.arange(half_first, dtype=jnp.int32)
    cos_first, sin_first = rotation(row_bins[:, None] * first_in[None, :], first_len)
    second_in = jnp.arange(second_len, dtype=jnp.int32)
    cos_twist, sin_twist = rotation(row_bins[:, None] * second_in[None, :], all_bins)
    cos_second, sin_second = rotation(second_in[:, None] * second_in[None, :], second_len)

    part_re = mm("rn,cnm->crm", cos_first, sig_chan)
    part_im = -mm("rn,cnm->crm", sin_first, sig_chan)
    twist_re = part_re * cos_twist + part_im * sin_twist
    twist_im = part_im * cos_twist - part_re * sin_twist
    freq_re = mm("crn,nk->crk", twist_re, cos_second) + mm("crn,nk->crk", twist_im, sin_second)
    freq_im = mm("crn,nk->crk", twist_im, cos_second) - mm("crn,nk->crk", twist_re, sin_second)

    filt_re = spec_chan[:, 0]
    filt_im = spec_chan[:, 1]
    prod_re = freq_re * filt_re - freq_im * filt_im
    prod_im = freq_re * filt_im + freq_im * filt_re

    back_re = mm("crk,kn->crn", prod_re, cos_second) - mm("crk,kn->crn", prod_im, sin_second)
    back_im = mm("crk,kn->crn", prod_im, cos_second) + mm("crk,kn->crn", prod_re, sin_second)
    untwist_re = back_re * cos_twist - back_im * sin_twist
    untwist_im = back_im * cos_twist + back_re * sin_twist
    conv = mm("rn,crm->cnm", cos_first, untwist_re) - mm("rn,crm->cnm", sin_first, untwist_im)
    conv = (conv * (1.0 / all_bins)).reshape(group, seq_count, tok_tiles, lanes)
    conv = jnp.transpose(conv, (1, 0, 2, 3)).reshape(seq_count, -1, lanes)
    result = exchange(conv, 2).reshape(seq_count, group, tok_tiles, lanes)
    result = jnp.transpose(result, (2, 3, 0, 1)).reshape(tok_rows, chan_width)
    gated = post_gate.astype(jnp.float32) * (result + skip_weight * signal.astype(jnp.float32))
    return gated.astype(jnp.bfloat16)


def solution(mesh):
    return jax.shard_map(
        local,
        mesh=mesh,
        in_specs=(
            P("seq", "chan"),
            P("seq", "chan"),
            P("seq", "chan"),
            P("chan"),
            P("chan"),
            P(None, "seq", None, "chan"),
        ),
        out_specs=P("seq", "chan"),
        check_vma=False,
    )
```

```python
import math

import jax
import jax.numpy as jnp
import numpy as np
from jax import lax
from jax.experimental import pallas as pl
from jax.experimental.pallas import tpu as pltpu
from jax.sharding import PartitionSpec as P

CHANNELS = 512
ROW_GROUP = 4
HIGH_DIGIT = 8


PRECISE = lax.Precision.HIGH
FULL_TURN = 2.0 * math.pi


def reversed_digits(count):
    levels = count.bit_length() - 1
    positions = np.arange(count)
    result = np.zeros(count, np.int64)
    for bit_pos in range(levels):
        result = result + ((positions >> bit_pos & 1) << levels - 1 - bit_pos)
    return result


def rotation(numerator, denominator):
    angle = (numerator % denominator).astype(jnp.float32) * (FULL_TURN / denominator)
    return (jnp.cos(angle), jnp.sin(angle))


def mm(spec, left, right):
    return jnp.einsum(spec, left, right, precision=PRECISE, preferred_element_type=jnp.float32)


def exchange_kernel(src_ref, dst_ref, send_sem, recv_sem, own_sem):
    count = src_ref.shape[0]
    me = lax.axis_index("seq")
    mesh_ids = pl.DeviceIdType.MESH
    barrier = pltpu.get_barrier_semaphore()

    def greet(step, carry):
        peer = lax.rem(me + step, count)
        pl.semaphore_signal(barrier, inc=1, device_id={"seq": peer}, device_id_type=mesh_ids)
        return carry

    lax.fori_loop(1, count, greet, 0)
    pl.semaphore_wait(barrier, count - 1)
    own = pltpu.make_async_copy(src_ref.at[me], dst_ref.at[me], own_sem)
    own.start()

    def remote(step):
        peer = lax.rem(me + step, count)
        return pltpu.make_async_remote_copy(
            src_ref.at[peer],
            dst_ref.at[me],
            send_sem.at[step],
            recv_sem.at[step],
            device_id={"seq": peer},
            device_id_type=mesh_ids,
        )

    def send(step, carry):
        remote(step).start()
        return carry

    lax.fori_loop(1, count, send, 0)

    def finish(step, carry):
        copy = remote(step)
        copy.wait_send()
        copy.wait_recv()
        return carry

    lax.fori_loop(1, count, finish, 0)
    own.wait()


def exchange(blocks, tag):
    count = blocks.shape[0]
    vmem = pl.BlockSpec(memory_space=pltpu.VMEM)
    return pl.pallas_call(
        exchange_kernel,
        out_shape=jax.ShapeDtypeStruct(blocks.shape, blocks.dtype),
        in_specs=[vmem],
        out_specs=vmem,
        scratch_shapes=[
            pltpu.SemaphoreType.DMA((count,)),
            pltpu.SemaphoreType.DMA((count,)),
            pltpu.SemaphoreType.DMA,
        ],
        compiler_params=pltpu.CompilerParams(collective_id=tag, has_side_effects=True),
    )(blocks)


def front_kernel(
    feat_ref, gate_ref, gain_ref, spec_ref,
    sig_out, sig_recv, spec_recv,
    sq_mine, sq_recv, sig_send, spec_sems, sig_sems, chan_sems, own_sems,
):
    count = spec_ref.shape[0]
    chans = sq_recv.shape[0]
    me = lax.axis_index("seq")
    mine = lax.axis_index("chan")
    mesh_ids = pl.DeviceIdType.MESH
    barrier = pltpu.get_barrier_semaphore()

    def greet(step, carry):
        peer = lax.rem(me + step, count)
        pl.semaphore_signal(barrier, inc=1, device_id={"seq": peer}, device_id_type=mesh_ids)
        return carry

    lax.fori_loop(1, count, greet, 0)
    for step in range(1, chans):
        peer = lax.rem(mine + step, chans)
        pl.semaphore_signal(barrier, inc=1, device_id={"chan": peer}, device_id_type=mesh_ids)
    pl.semaphore_wait(barrier, count + chans - 2)

    def spec_copy(step):
        peer = lax.rem(me + step, count)
        return pltpu.make_async_remote_copy(
            spec_ref.at[peer],
            spec_recv.at[me],
            spec_sems.at[0, step],
            spec_sems.at[1, step],
            device_id={"seq": peer},
            device_id_type=mesh_ids,
        )

    spec_own = pltpu.make_async_copy(spec_ref.at[me], spec_recv.at[me], own_sems.at[0])
    spec_own.start()

    def spec_send(step, carry):
        spec_copy(step).start()
        return carry

    lax.fori_loop(1, count, spec_send, 0)

    feat = feat_ref[...].astype(jnp.float32)
    part = jnp.sum(feat * feat, axis=0, keepdims=True)
    sq_mine[...] = jnp.broadcast_to(part, sq_mine.shape)

    def chan_copy(step):
        peer = lax.rem(mine + step, chans)
        return pltpu.make_async_remote_copy(
            sq_mine,
            sq_recv.at[mine],
            chan_sems.at[0, step],
            chan_sems.at[1, step],
            device_id={"chan": peer},
            device_id_type=mesh_ids,
        )

    for step in range(1, chans):
        chan_copy(step).start()
    for step in range(1, chans):
        copy = chan_copy(step)
        copy.wait_send()
        copy.wait_recv()
    total = part
    for step in range(1, chans):
        other = lax.rem(mine + step, chans)
        total = total + sq_recv[other][0:1, :]
    scale = lax.rsqrt(total / CHANNELS + 1e-06)
    signal = (feat * scale * gain_ref[...] * gate_ref[...].astype(jnp.float32)).astype(jnp.bfloat16)
    sig_out[...] = signal
    wide = signal.astype(jnp.float32)
    pair = sig_send.shape[1]
    for peer in range(count):
        sig_send[peer] = wide[pair * peer:pair * peer + pair, :]

    def sig_copy(step):
        peer = lax.rem(me + step, count)
        return pltpu.make_async_remote_copy(
            sig_send.at[peer],
            sig_recv.at[me],
            sig_sems.at[0, step],
            sig_sems.at[1, step],
            device_id={"seq": peer},
            device_id_type=mesh_ids,
        )

    sig_own = pltpu.make_async_copy(sig_send.at[me], sig_recv.at[me], own_sems.at[1])
    sig_own.start()

    def sig_start(step, carry):
        sig_copy(step).start()
        return carry

    lax.fori_loop(1, count, sig_start, 0)

    def sig_finish(step, carry):
        copy = sig_copy(step)
        copy.wait_send()
        copy.wait_recv()
        return carry

    lax.fori_loop(1, count, sig_finish, 0)
    sig_own.wait()

    def spec_finish(step, carry):
        copy = spec_copy(step)
        copy.wait_send()
        copy.wait_recv()
        return carry

    lax.fori_loop(1, count, spec_finish, 0)
    spec_own.wait()


def front(feat_t, gate_t, gain_col, spec_rows, chans):
    count = spec_rows.shape[0]
    width, length = feat_t.shape
    pair = width // count
    vmem = pl.BlockSpec(memory_space=pltpu.VMEM)
    return pl.pallas_call(
        front_kernel,
        out_shape=(
            jax.ShapeDtypeStruct((width, length), jnp.bfloat16),
            jax.ShapeDtypeStruct((count, pair, length), jnp.float32),
            jax.ShapeDtypeStruct(spec_rows.shape, spec_rows.dtype),
        ),
        in_specs=[vmem] * 4,
        out_specs=(vmem, vmem, vmem),
        scratch_shapes=[
            pltpu.VMEM((8, length), jnp.float32),
            pltpu.VMEM((chans, 8, length), jnp.float32),
            pltpu.VMEM((count, pair, length), jnp.float32),
            pltpu.SemaphoreType.DMA((2, count)),
            pltpu.SemaphoreType.DMA((2, count)),
            pltpu.SemaphoreType.DMA((2, chans)),
            pltpu.SemaphoreType.DMA((2,)),
        ],
        compiler_params=pltpu.CompilerParams(collective_id=0, has_side_effects=True),
    )(feat_t, gate_t, gain_col, spec_rows)


def bin_rows(seq_count):
    digit_order = reversed_digits(seq_count)
    stride = 2 * seq_count
    slots = np.arange(stride)
    low_bins = 2 * digit_order[slots // 2] + slots % 2
    return (low_bins[:, None] + stride * np.arange(ROW_GROUP)[None, :]).reshape(-1).astype(np.int32)


def convolve(sig_cols, spec_chan, seq_count, tok_rows):
    group = spec_chan.shape[0]
    first_len, second_len = spec_chan.shape[2], spec_chan.shape[3]
    half_first = first_len // 2
    all_bins = first_len * second_len
    row_bins = jnp.asarray(bin_rows(seq_count))
    first_in = jnp.arange(half_first, dtype=jnp.int32)
    cos_first, sin_first = rotation(row_bins[:, None] * first_in[None, :], first_len)
    second_in = jnp.arange(second_len, dtype=jnp.int32)
    cos_twist, sin_twist = rotation(row_bins[:, None] * second_in[None, :], all_bins)
    cos_second, sin_second = rotation(second_in[:, None] * second_in[None, :], second_len)
    fwd_second = jnp.concatenate(
        [jnp.concatenate([cos_second, -sin_second], 1), jnp.concatenate([sin_second, cos_second], 1)], 0
    )
    inv_second = jnp.concatenate(
        [jnp.concatenate([cos_second, sin_second], 1), jnp.concatenate([-sin_second, cos_second], 1)], 0
    )
    stacked = jnp.concatenate([cos_first, sin_first], 0)
    last = jnp.concatenate([cos_first.T, -sin_first.T], 1) * (1.0 / all_bins)

    both = mm("rn,nm->rm", stacked, sig_cols)
    along_cos, along_sin = both[:first_len], both[first_len:]
    outs_re, outs_im = [], []
    for chan in range(group):
        lanes_of = slice(chan * second_len, (chan + 1) * second_len)
        p_cos, p_sin = along_cos[:, lanes_of], along_sin[:, lanes_of]
        twist_re = p_cos * cos_twist - p_sin * sin_twist
        twist_im = -p_sin * cos_twist - p_cos * sin_twist
        freq = mm("rn,nk->rk", jnp.concatenate([twist_re, twist_im], 1), fwd_second)
        freq_re, freq_im = freq[:, :second_len], freq[:, second_len:]
        filt_re, filt_im = spec_chan[chan, 0], spec_chan[chan, 1]
        prod_re = freq_re * filt_re - freq_im * filt_im
        prod_im = freq_re * filt_im + freq_im * filt_re
        back = mm("rk,kn->rn", jnp.concatenate([prod_re, prod_im], 1), inv_second)
        back_re, back_im = back[:, :second_len], back[:, second_len:]
        outs_re.append(back_re * cos_twist - back_im * sin_twist)
        outs_im.append(back_im * cos_twist + back_re * sin_twist)
    untwisted = jnp.concatenate([jnp.concatenate(outs_re, 1), jnp.concatenate(outs_im, 1)], 0)
    return mm("nr,rm->nm", last, untwisted)


def local(features, pre_gate, post_gate, norm_gain, skip_weight, spectrum):
    tok_rows, chan_width = features.shape
    seq_count = lax.axis_size("seq")
    chans = lax.axis_size("chan")
    stride = 2 * seq_count
    all_bins = stride * tok_rows
    group = chan_width // seq_count
    first_len = stride * ROW_GROUP
    second_len = all_bins // first_len
    half_first = first_len // 2
    lanes = 128
    tok_tiles = tok_rows // lanes

    half_group = ROW_GROUP // 2
    spec_rows = spectrum.reshape(2, 2, second_len, half_group, 2, chan_width)
    spec_rows = jnp.transpose(spec_rows, (5, 0, 1, 3, 4, 2)).astype(jnp.bfloat16)
    spec_rows = spec_rows.reshape(seq_count, -1, 2 * second_len)
    signal_t, sig_chan, spec_chan = front(
        features.T, pre_gate.T, norm_gain.reshape(chan_width, 1), spec_rows, chans
    )
    spec_chan = spec_chan.reshape(seq_count, group, 2, -1, 2 * second_len)
    spec_chan = jnp.transpose(spec_chan, (1, 2, 0, 3, 4)).astype(jnp.float32)
    spec_chan = spec_chan.reshape(group, 2, first_len, second_len)
    sig_cols = sig_chan.reshape(seq_count, group, tok_tiles, lanes)
    sig_cols = jnp.transpose(sig_cols, (0, 2, 1, 3)).reshape(half_first, group * second_len)
    signal = signal_t.T
    conv = convolve(sig_cols, spec_chan, seq_count, tok_rows)
    conv = jnp.transpose(conv.reshape(seq_count, tok_tiles, group, lanes), (0, 2, 1, 3))
    conv = conv.reshape(seq_count, -1, lanes)
    result = exchange(conv, 2).reshape(seq_count, group, tok_tiles, lanes)
    result = jnp.transpose(result, (2, 3, 0, 1)).reshape(tok_rows, chan_width)
    gated = post_gate.astype(jnp.float32) * (result + skip_weight * signal.astype(jnp.float32))
    return gated.astype(jnp.bfloat16)


def solution(mesh):
    return jax.shard_map(
        local,
        mesh=mesh,
        in_specs=(
            P("seq", "chan"),
            P("seq", "chan"),
            P("seq", "chan"),
            P("chan"),
            P("chan"),
            P(None, "seq", None, "chan"),
        ),
        out_specs=P("seq", "chan"),
        check_vma=False,
    )
```

```python
import math

import jax
import jax.numpy as jnp
import numpy as np
from jax import lax
from jax.experimental import pallas as pl
from jax.experimental.pallas import tpu as pltpu
from jax.sharding import PartitionSpec as P

CHANNELS = 512
ROW_GROUP = 4
HIGH_DIGIT = 8


PRECISE = lax.Precision.HIGH
FULL_TURN = 2.0 * math.pi


def reversed_digits(count):
    levels = count.bit_length() - 1
    positions = np.arange(count)
    result = np.zeros(count, np.int64)
    for bit_pos in range(levels):
        result = result + ((positions >> bit_pos & 1) << levels - 1 - bit_pos)
    return result


def rotation(numerator, denominator):
    angle = (numerator % denominator).astype(jnp.float32) * (FULL_TURN / denominator)
    return (jnp.cos(angle), jnp.sin(angle))


def mm(spec, left, right):
    return jnp.einsum(spec, left, right, precision=PRECISE, preferred_element_type=jnp.float32)


def exchange_kernel(src_ref, dst_ref, send_sem, recv_sem, own_sem):
    count = src_ref.shape[0]
    me = lax.axis_index("seq")
    mesh_ids = pl.DeviceIdType.MESH
    barrier = pltpu.get_barrier_semaphore()

    def greet(step, carry):
        peer = lax.rem(me + step, count)
        pl.semaphore_signal(barrier, inc=1, device_id={"seq": peer}, device_id_type=mesh_ids)
        return carry

    lax.fori_loop(1, count, greet, 0, unroll=True)
    pl.semaphore_wait(barrier, count - 1)
    own = pltpu.make_async_copy(src_ref.at[me], dst_ref.at[me], own_sem)
    own.start()

    def remote(step):
        peer = lax.rem(me + step, count)
        return pltpu.make_async_remote_copy(
            src_ref.at[peer],
            dst_ref.at[me],
            send_sem.at[step],
            recv_sem.at[step],
            device_id={"seq": peer},
            device_id_type=mesh_ids,
        )

    def send(step, carry):
        remote(step).start()
        return carry

    lax.fori_loop(1, count, send, 0, unroll=True)

    def finish(step, carry):
        copy = remote(step)
        copy.wait_send()
        copy.wait_recv()
        return carry

    lax.fori_loop(1, count, finish, 0, unroll=True)
    own.wait()


def exchange(blocks, tag):
    count = blocks.shape[0]
    vmem = pl.BlockSpec(memory_space=pltpu.VMEM)
    return pl.pallas_call(
        exchange_kernel,
        out_shape=jax.ShapeDtypeStruct(blocks.shape, blocks.dtype),
        in_specs=[vmem],
        out_specs=vmem,
        scratch_shapes=[
            pltpu.SemaphoreType.DMA((count,)),
            pltpu.SemaphoreType.DMA((count,)),
            pltpu.SemaphoreType.DMA,
        ],
        compiler_params=pltpu.CompilerParams(collective_id=tag, has_side_effects=True),
    )(blocks)


def front_kernel(
    feat_ref, gate_ref, gain_ref, spec_ref,
    sig_out, sig_recv, spec_recv,
    sq_mine, sq_recv, sig_send, spec_sems, sig_sems, chan_sems, own_sems,
):
    count = spec_ref.shape[0]
    chans = sq_recv.shape[0]
    me = lax.axis_index("seq")
    mine = lax.axis_index("chan")
    mesh_ids = pl.DeviceIdType.MESH
    barrier = pltpu.get_barrier_semaphore()

    def greet(step, carry):
        peer = lax.rem(me + step, count)
        pl.semaphore_signal(barrier, inc=1, device_id={"seq": peer}, device_id_type=mesh_ids)
        return carry

    lax.fori_loop(1, count, greet, 0, unroll=True)
    for step in range(1, chans):
        peer = lax.rem(mine + step, chans)
        pl.semaphore_signal(barrier, inc=1, device_id={"chan": peer}, device_id_type=mesh_ids)
    pl.semaphore_wait(barrier, count + chans - 2)

    def spec_copy(step):
        peer = lax.rem(me + step, count)
        return pltpu.make_async_remote_copy(
            spec_ref.at[peer],
            spec_recv.at[me],
            spec_sems.at[0, step],
            spec_sems.at[1, step],
            device_id={"seq": peer},
            device_id_type=mesh_ids,
        )

    spec_own = pltpu.make_async_copy(spec_ref.at[me], spec_recv.at[me], own_sems.at[0])
    spec_own.start()

    def spec_send(step, carry):
        spec_copy(step).start()
        return carry

    lax.fori_loop(1, count, spec_send, 0, unroll=True)

    feat = feat_ref[...].astype(jnp.float32)
    part = jnp.sum(feat * feat, axis=0, keepdims=True)
    sq_mine[...] = jnp.broadcast_to(part, sq_mine.shape)

    def chan_copy(step):
        peer = lax.rem(mine + step, chans)
        return pltpu.make_async_remote_copy(
            sq_mine,
            sq_recv.at[mine],
            chan_sems.at[0, step],
            chan_sems.at[1, step],
            device_id={"chan": peer},
            device_id_type=mesh_ids,
        )

    for step in range(1, chans):
        chan_copy(step).start()
    for step in range(1, chans):
        copy = chan_copy(step)
        copy.wait_send()
        copy.wait_recv()
    total = part
    for step in range(1, chans):
        other = lax.rem(mine + step, chans)
        total = total + sq_recv[other][0:1, :]
    scale = lax.rsqrt(total / CHANNELS + 1e-06)
    signal = (feat * scale * gain_ref[...] * gate_ref[...].astype(jnp.float32)).astype(jnp.bfloat16)
    sig_out[...] = signal
    wide = signal.astype(jnp.float32)
    pair = sig_send.shape[1]
    for peer in range(count):
        sig_send[peer] = wide[pair * peer:pair * peer + pair, :]

    def sig_copy(step):
        peer = lax.rem(me + step, count)
        return pltpu.make_async_remote_copy(
            sig_send.at[peer],
            sig_recv.at[me],
            sig_sems.at[0, step],
            sig_sems.at[1, step],
            device_id={"seq": peer},
            device_id_type=mesh_ids,
        )

    sig_own = pltpu.make_async_copy(sig_send.at[me], sig_recv.at[me], own_sems.at[1])
    sig_own.start()

    def sig_start(step, carry):
        sig_copy(step).start()
        return carry

    lax.fori_loop(1, count, sig_start, 0, unroll=True)

    def sig_finish(step, carry):
        copy = sig_copy(step)
        copy.wait_send()
        copy.wait_recv()
        return carry

    lax.fori_loop(1, count, sig_finish, 0, unroll=True)
    sig_own.wait()

    def spec_finish(step, carry):
        copy = spec_copy(step)
        copy.wait_send()
        copy.wait_recv()
        return carry

    lax.fori_loop(1, count, spec_finish, 0, unroll=True)
    spec_own.wait()


def front(feat_t, gate_t, gain_col, spec_rows, chans):
    count = spec_rows.shape[0]
    width, length = feat_t.shape
    pair = width // count
    vmem = pl.BlockSpec(memory_space=pltpu.VMEM)
    return pl.pallas_call(
        front_kernel,
        out_shape=(
            jax.ShapeDtypeStruct((width, length), jnp.bfloat16),
            jax.ShapeDtypeStruct((count, pair, length), jnp.float32),
            jax.ShapeDtypeStruct(spec_rows.shape, spec_rows.dtype),
        ),
        in_specs=[vmem] * 4,
        out_specs=(vmem, vmem, vmem),
        scratch_shapes=[
            pltpu.VMEM((8, length), jnp.float32),
            pltpu.VMEM((chans, 8, length), jnp.float32),
            pltpu.VMEM((count, pair, length), jnp.float32),
            pltpu.SemaphoreType.DMA((2, count)),
            pltpu.SemaphoreType.DMA((2, count)),
            pltpu.SemaphoreType.DMA((2, chans)),
            pltpu.SemaphoreType.DMA((2,)),
        ],
        compiler_params=pltpu.CompilerParams(collective_id=0, has_side_effects=True),
    )(feat_t, gate_t, gain_col, spec_rows)


def bin_rows(seq_count):
    digit_order = reversed_digits(seq_count)
    stride = 2 * seq_count
    slots = np.arange(stride)
    low_bins = 2 * digit_order[slots // 2] + slots % 2
    return (low_bins[:, None] + stride * np.arange(ROW_GROUP)[None, :]).reshape(-1).astype(np.int32)


def convolve(sig_cols, spec_chan, seq_count, tok_rows):
    group = spec_chan.shape[0]
    first_len, second_len = spec_chan.shape[2], spec_chan.shape[3]
    half_first = first_len // 2
    all_bins = first_len * second_len
    row_bins = jnp.asarray(bin_rows(seq_count))
    first_in = jnp.arange(half_first, dtype=jnp.int32)
    cos_first, sin_first = rotation(row_bins[:, None] * first_in[None, :], first_len)
    second_in = jnp.arange(second_len, dtype=jnp.int32)
    cos_twist, sin_twist = rotation(row_bins[:, None] * second_in[None, :], all_bins)
    cos_second, sin_second = rotation(second_in[:, None] * second_in[None, :], second_len)
    fwd_second = jnp.concatenate(
        [jnp.concatenate([cos_second, -sin_second], 1), jnp.concatenate([sin_second, cos_second], 1)], 0
    )
    inv_second = jnp.concatenate(
        [jnp.concatenate([cos_second, sin_second], 1), jnp.concatenate([-sin_second, cos_second], 1)], 0
    )
    stacked = jnp.concatenate([cos_first, sin_first], 0)
    last = jnp.concatenate([cos_first.T, -sin_first.T], 1) * (1.0 / all_bins)

    both = mm("rn,nm->rm", stacked, sig_cols)
    along_cos, along_sin = both[:first_len], both[first_len:]
    outs_re, outs_im = [], []
    for chan in range(group):
        lanes_of = slice(chan * second_len, (chan + 1) * second_len)
        p_cos, p_sin = along_cos[:, lanes_of], along_sin[:, lanes_of]
        twist_re = p_cos * cos_twist - p_sin * sin_twist
        twist_im = -p_sin * cos_twist - p_cos * sin_twist
        freq = mm("rn,nk->rk", jnp.concatenate([twist_re, twist_im], 1), fwd_second)
        freq_re, freq_im = freq[:, :second_len], freq[:, second_len:]
        filt_re, filt_im = spec_chan[chan, 0], spec_chan[chan, 1]
        prod_re = freq_re * filt_re - freq_im * filt_im
        prod_im = freq_re * filt_im + freq_im * filt_re
        back = mm("rk,kn->rn", jnp.concatenate([prod_re, prod_im], 1), inv_second)
        back_re, back_im = back[:, :second_len], back[:, second_len:]
        outs_re.append(back_re * cos_twist - back_im * sin_twist)
        outs_im.append(back_im * cos_twist + back_re * sin_twist)
    untwisted = jnp.concatenate([jnp.concatenate(outs_re, 1), jnp.concatenate(outs_im, 1)], 0)
    return mm("nr,rm->nm", last, untwisted)


def local(features, pre_gate, post_gate, norm_gain, skip_weight, spectrum):
    tok_rows, chan_width = features.shape
    seq_count = lax.axis_size("seq")
    chans = lax.axis_size("chan")
    stride = 2 * seq_count
    all_bins = stride * tok_rows
    group = chan_width // seq_count
    first_len = stride * ROW_GROUP
    second_len = all_bins // first_len
    half_first = first_len // 2
    lanes = 128
    tok_tiles = tok_rows // lanes

    half_group = ROW_GROUP // 2
    spec_rows = spectrum.reshape(2, 2, second_len, half_group, 2, chan_width)
    spec_rows = jnp.transpose(spec_rows, (5, 0, 1, 3, 4, 2)).astype(jnp.bfloat16)
    spec_rows = spec_rows.reshape(seq_count, -1, 2 * second_len)
    signal_t, sig_chan, spec_chan = front(
        features.T, pre_gate.T, norm_gain.reshape(chan_width, 1), spec_rows, chans
    )
    spec_chan = spec_chan.reshape(seq_count, group, 2, -1, 2 * second_len)
    spec_chan = jnp.transpose(spec_chan, (1, 2, 0, 3, 4)).astype(jnp.float32)
    spec_chan = spec_chan.reshape(group, 2, first_len, second_len)
    sig_cols = sig_chan.reshape(seq_count, group, tok_tiles, lanes)
    sig_cols = jnp.transpose(sig_cols, (0, 2, 1, 3)).reshape(half_first, group * second_len)
    signal = signal_t.T
    conv = convolve(sig_cols, spec_chan, seq_count, tok_rows)
    conv = jnp.transpose(conv.reshape(seq_count, tok_tiles, group, lanes), (0, 2, 1, 3))
    conv = conv.reshape(seq_count, -1, lanes)
    result = exchange(conv, 2).reshape(seq_count, group, tok_tiles, lanes)
    result = jnp.transpose(result, (2, 3, 0, 1)).reshape(tok_rows, chan_width)
    gated = post_gate.astype(jnp.float32) * (result + skip_weight * signal.astype(jnp.float32))
    return gated.astype(jnp.bfloat16)


def solution(mesh):
    return jax.shard_map(
        local,
        mesh=mesh,
        in_specs=(
            P("seq", "chan"),
            P("seq", "chan"),
            P("seq", "chan"),
            P("chan"),
            P("chan"),
            P(None, "seq", None, "chan"),
        ),
        out_specs=P("seq", "chan"),
        check_vma=False,
    )
```

```python
import math

import jax
import jax.numpy as jnp
import numpy as np
from jax import lax
from jax.experimental import pallas as pl
from jax.experimental.pallas import tpu as pltpu
from jax.sharding import PartitionSpec as P

CHANNELS = 512
ROW_GROUP = 4
HIGH_DIGIT = 8


PRECISE = lax.Precision.HIGH
FULL_TURN = 2.0 * math.pi


def reversed_digits(count):
    levels = count.bit_length() - 1
    positions = np.arange(count)
    result = np.zeros(count, np.int64)
    for bit_pos in range(levels):
        result = result + ((positions >> bit_pos & 1) << levels - 1 - bit_pos)
    return result


def rotation(numerator, denominator):
    angle = (numerator % denominator).astype(jnp.float32) * (FULL_TURN / denominator)
    return (jnp.cos(angle), jnp.sin(angle))


def mm(spec, left, right):
    return jnp.einsum(spec, left, right, precision=PRECISE, preferred_element_type=jnp.float32)


def exchange_kernel(src_ref, dst_ref, send_sem, recv_sem, own_sem):
    count = src_ref.shape[0]
    me = lax.axis_index("seq")
    mesh_ids = pl.DeviceIdType.MESH
    barrier = pltpu.get_barrier_semaphore()

    def greet(step, carry):
        peer = lax.rem(me + step, count)
        pl.semaphore_signal(barrier, inc=1, device_id={"seq": peer}, device_id_type=mesh_ids)
        return carry

    lax.fori_loop(1, count, greet, 0, unroll=True)
    pl.semaphore_wait(barrier, count - 1)
    own = pltpu.make_async_copy(src_ref.at[me], dst_ref.at[me], own_sem)
    own.start()

    def remote(step):
        peer = lax.rem(me + step, count)
        return pltpu.make_async_remote_copy(
            src_ref.at[peer],
            dst_ref.at[me],
            send_sem.at[step],
            recv_sem.at[step],
            device_id={"seq": peer},
            device_id_type=mesh_ids,
        )

    def send(step, carry):
        remote(step).start()
        return carry

    lax.fori_loop(1, count, send, 0, unroll=True)

    def finish(step, carry):
        copy = remote(step)
        copy.wait_send()
        copy.wait_recv()
        return carry

    lax.fori_loop(1, count, finish, 0, unroll=True)
    own.wait()


def exchange(blocks, tag):
    count = blocks.shape[0]
    vmem = pl.BlockSpec(memory_space=pltpu.VMEM)
    return pl.pallas_call(
        exchange_kernel,
        out_shape=jax.ShapeDtypeStruct(blocks.shape, blocks.dtype),
        in_specs=[vmem],
        out_specs=vmem,
        scratch_shapes=[
            pltpu.SemaphoreType.DMA((count,)),
            pltpu.SemaphoreType.DMA((count,)),
            pltpu.SemaphoreType.DMA,
        ],
        compiler_params=pltpu.CompilerParams(collective_id=tag, has_side_effects=True),
    )(blocks)


def front_kernel(
    feat_ref, gate_ref, gain_ref, spec_ref,
    sig_out, sig_recv, spec_recv,
    sq_mine, sq_recv, sig_send, spec_sems, sig_sems, chan_sems, own_sems,
):
    count = spec_ref.shape[0]
    chans = sq_recv.shape[0]
    me = lax.axis_index("seq")
    mine = lax.axis_index("chan")
    mesh_ids = pl.DeviceIdType.MESH
    barrier = pltpu.get_barrier_semaphore()

    def greet(step, carry):
        peer = lax.rem(me + step, count)
        pl.semaphore_signal(barrier, inc=1, device_id={"seq": peer}, device_id_type=mesh_ids)
        return carry

    lax.fori_loop(1, count, greet, 0, unroll=True)
    for step in range(1, chans):
        peer = lax.rem(mine + step, chans)
        pl.semaphore_signal(barrier, inc=1, device_id={"chan": peer}, device_id_type=mesh_ids)
    pl.semaphore_wait(barrier, count + chans - 2)

    def spec_copy(step):
        peer = lax.rem(me + step, count)
        return pltpu.make_async_remote_copy(
            spec_ref.at[peer],
            spec_recv.at[me],
            spec_sems.at[0, step],
            spec_sems.at[1, step],
            device_id={"seq": peer},
            device_id_type=mesh_ids,
        )

    spec_own = pltpu.make_async_copy(spec_ref.at[me], spec_recv.at[me], own_sems.at[0])
    spec_own.start()

    def spec_send(step, carry):
        spec_copy(step).start()
        return carry

    lax.fori_loop(1, count, spec_send, 0, unroll=True)

    feat = feat_ref[...].astype(jnp.float32)
    part = jnp.sum(feat * feat, axis=0, keepdims=True)
    sq_mine[...] = jnp.broadcast_to(part, sq_mine.shape)

    def chan_copy(step):
        peer = lax.rem(mine + step, chans)
        return pltpu.make_async_remote_copy(
            sq_mine,
            sq_recv.at[mine],
            chan_sems.at[0, step],
            chan_sems.at[1, step],
            device_id={"chan": peer},
            device_id_type=mesh_ids,
        )

    for step in range(1, chans):
        chan_copy(step).start()
    for step in range(1, chans):
        copy = chan_copy(step)
        copy.wait_send()
        copy.wait_recv()
    total = part
    for step in range(1, chans):
        other = lax.rem(mine + step, chans)
        total = total + sq_recv[other][0:1, :]
    scale = lax.rsqrt(total / CHANNELS + 1e-06)
    signal = (feat * scale * gain_ref[...] * gate_ref[...].astype(jnp.float32)).astype(jnp.bfloat16)
    sig_out[...] = signal
    wide = signal.astype(jnp.float32)
    pair = sig_send.shape[1]
    for peer in range(count):
        sig_send[peer] = wide[pair * peer:pair * peer + pair, :]

    def sig_copy(step):
        peer = lax.rem(me + step, count)
        return pltpu.make_async_remote_copy(
            sig_send.at[peer],
            sig_recv.at[me],
            sig_sems.at[0, step],
            sig_sems.at[1, step],
            device_id={"seq": peer},
            device_id_type=mesh_ids,
        )

    sig_own = pltpu.make_async_copy(sig_send.at[me], sig_recv.at[me], own_sems.at[1])
    sig_own.start()

    def sig_start(step, carry):
        sig_copy(step).start()
        return carry

    lax.fori_loop(1, count, sig_start, 0, unroll=True)

    def sig_finish(step, carry):
        copy = sig_copy(step)
        copy.wait_send()
        copy.wait_recv()
        return carry

    lax.fori_loop(1, count, sig_finish, 0, unroll=True)
    sig_own.wait()

    def spec_finish(step, carry):
        copy = spec_copy(step)
        copy.wait_send()
        copy.wait_recv()
        return carry

    lax.fori_loop(1, count, spec_finish, 0, unroll=True)
    spec_own.wait()


def front(feat_t, gate_t, gain_col, spec_rows, chans):
    count = spec_rows.shape[0]
    width, length = feat_t.shape
    pair = width // count
    vmem = pl.BlockSpec(memory_space=pltpu.VMEM)
    return pl.pallas_call(
        front_kernel,
        out_shape=(
            jax.ShapeDtypeStruct((width, length), jnp.bfloat16),
            jax.ShapeDtypeStruct((count, pair, length), jnp.float32),
            jax.ShapeDtypeStruct(spec_rows.shape, spec_rows.dtype),
        ),
        in_specs=[vmem] * 4,
        out_specs=(vmem, vmem, vmem),
        scratch_shapes=[
            pltpu.VMEM((8, length), jnp.float32),
            pltpu.VMEM((chans, 8, length), jnp.float32),
            pltpu.VMEM((count, pair, length), jnp.float32),
            pltpu.SemaphoreType.DMA((2, count)),
            pltpu.SemaphoreType.DMA((2, count)),
            pltpu.SemaphoreType.DMA((2, chans)),
            pltpu.SemaphoreType.DMA((2,)),
        ],
        compiler_params=pltpu.CompilerParams(collective_id=0, has_side_effects=True),
    )(feat_t, gate_t, gain_col, spec_rows)


def bin_rows(seq_count):
    digit_order = reversed_digits(seq_count)
    stride = 2 * seq_count
    slots = np.arange(stride)
    low_bins = 2 * digit_order[slots // 2] + slots % 2
    return (low_bins[:, None] + stride * np.arange(ROW_GROUP)[None, :]).reshape(-1).astype(np.int32)


def convolve(sig_cols, spec_chan, seq_count, tok_rows):
    group = spec_chan.shape[0]
    first_len, second_len = spec_chan.shape[2], spec_chan.shape[3]
    half_first = first_len // 2
    all_bins = first_len * second_len
    row_bins = bin_rows(seq_count).astype(np.int64)
    first_in = np.arange(half_first)
    first_turn = (row_bins[:, None] * first_in[None, :]) % first_len * (2.0 * np.pi / first_len)
    stacked_np = np.concatenate([np.cos(first_turn), np.sin(first_turn)], 0)
    stacked = jnp.asarray(stacked_np.astype(np.float32))
    signs = np.concatenate([np.ones(first_len), -np.ones(first_len)]) / all_bins
    twist_turn = (row_bins[:, None] * np.arange(second_len)[None, :]) % all_bins * (2.0 * np.pi / all_bins)
    cos_twist = jnp.asarray(np.cos(twist_turn).astype(np.float32))
    sin_twist = jnp.asarray(np.sin(twist_turn).astype(np.float32))
    second_in = jnp.arange(second_len, dtype=jnp.int32)
    cos_second, sin_second = rotation(second_in[:, None] * second_in[None, :], second_len)
    fwd_second = jnp.concatenate(
        [jnp.concatenate([cos_second, -sin_second], 1), jnp.concatenate([sin_second, cos_second], 1)], 0
    )
    inv_second = jnp.concatenate(
        [jnp.concatenate([cos_second, sin_second], 1), jnp.concatenate([-sin_second, cos_second], 1)], 0
    )
    last = stacked * jnp.asarray(signs.astype(np.float32))[:, None]

    both = mm("rn,nm->rm", stacked, sig_cols)
    along_cos, along_sin = both[:first_len], both[first_len:]
    outs_re, outs_im = [], []
    for chan in range(group):
        lanes_of = slice(chan * second_len, (chan + 1) * second_len)
        p_cos, p_sin = along_cos[:, lanes_of], along_sin[:, lanes_of]
        twist_re = p_cos * cos_twist - p_sin * sin_twist
        twist_im = -p_sin * cos_twist - p_cos * sin_twist
        freq = mm("rn,nk->rk", jnp.concatenate([twist_re, twist_im], 1), fwd_second)
        freq_re, freq_im = freq[:, :second_len], freq[:, second_len:]
        filt_re, filt_im = spec_chan[chan, 0], spec_chan[chan, 1]
        prod_re = freq_re * filt_re - freq_im * filt_im
        prod_im = freq_re * filt_im + freq_im * filt_re
        back = mm("rk,kn->rn", jnp.concatenate([prod_re, prod_im], 1), inv_second)
        back_re, back_im = back[:, :second_len], back[:, second_len:]
        outs_re.append(back_re * cos_twist - back_im * sin_twist)
        outs_im.append(back_im * cos_twist + back_re * sin_twist)
    untwisted = jnp.concatenate([jnp.concatenate(outs_re, 1), jnp.concatenate(outs_im, 1)], 0)
    return mm("rn,rm->nm", last, untwisted)


def local(features, pre_gate, post_gate, norm_gain, skip_weight, spectrum):
    tok_rows, chan_width = features.shape
    seq_count = lax.axis_size("seq")
    chans = lax.axis_size("chan")
    stride = 2 * seq_count
    all_bins = stride * tok_rows
    group = chan_width // seq_count
    first_len = stride * ROW_GROUP
    second_len = all_bins // first_len
    half_first = first_len // 2
    lanes = 128
    tok_tiles = tok_rows // lanes

    half_group = ROW_GROUP // 2
    spec_rows = spectrum.reshape(2, 2, second_len, half_group, 2, chan_width)
    spec_rows = jnp.transpose(spec_rows, (5, 0, 1, 3, 4, 2)).astype(jnp.bfloat16)
    spec_rows = spec_rows.reshape(seq_count, -1, 2 * second_len)
    signal_t, sig_chan, spec_chan = front(
        features.T, pre_gate.T, norm_gain.reshape(chan_width, 1), spec_rows, chans
    )
    spec_chan = spec_chan.reshape(seq_count, group, 2, -1, 2 * second_len)
    spec_chan = jnp.transpose(spec_chan, (1, 2, 0, 3, 4)).astype(jnp.float32)
    spec_chan = spec_chan.reshape(group, 2, first_len, second_len)
    sig_cols = sig_chan.reshape(seq_count, group, tok_tiles, lanes)
    sig_cols = jnp.transpose(sig_cols, (0, 2, 1, 3)).reshape(half_first, group * second_len)
    signal = signal_t.T
    conv = convolve(sig_cols, spec_chan, seq_count, tok_rows)
    conv = jnp.transpose(conv.reshape(seq_count, tok_tiles, group, lanes), (0, 2, 1, 3))
    conv = conv.reshape(seq_count, -1, lanes)
    result = exchange(conv, 2).reshape(seq_count, group, tok_tiles, lanes)
    result = jnp.transpose(result, (2, 3, 0, 1)).reshape(tok_rows, chan_width)
    gated = post_gate.astype(jnp.float32) * (result + skip_weight * signal.astype(jnp.float32))
    return gated.astype(jnp.bfloat16)


def solution(mesh):
    return jax.shard_map(
        local,
        mesh=mesh,
        in_specs=(
            P("seq", "chan"),
            P("seq", "chan"),
            P("seq", "chan"),
            P("chan"),
            P("chan"),
            P(None, "seq", None, "chan"),
        ),
        out_specs=P("seq", "chan"),
        check_vma=False,
    )
```

```python
import math

import jax
import jax.numpy as jnp
import numpy as np
from jax import lax
from jax.experimental import pallas as pl
from jax.experimental.pallas import tpu as pltpu
from jax.sharding import PartitionSpec as P

CHANNELS = 512
ROW_GROUP = 4
HIGH_DIGIT = 8


PRECISE = lax.Precision.HIGH
FULL_TURN = 2.0 * math.pi


def reversed_digits(count):
    levels = count.bit_length() - 1
    positions = np.arange(count)
    result = np.zeros(count, np.int64)
    for bit_pos in range(levels):
        result = result + ((positions >> bit_pos & 1) << levels - 1 - bit_pos)
    return result


def rotation(numerator, denominator):
    angle = (numerator % denominator).astype(jnp.float32) * (FULL_TURN / denominator)
    return (jnp.cos(angle), jnp.sin(angle))


def mm(spec, left, right):
    return jnp.einsum(spec, left, right, precision=PRECISE, preferred_element_type=jnp.float32)


def exchange_kernel(src_ref, dst_ref, send_sem, recv_sem, own_sem):
    count = src_ref.shape[0]
    me = lax.axis_index("seq")
    mesh_ids = pl.DeviceIdType.MESH
    barrier = pltpu.get_barrier_semaphore()

    def greet(step, carry):
        peer = lax.rem(me + step, count)
        pl.semaphore_signal(barrier, inc=1, device_id={"seq": peer}, device_id_type=mesh_ids)
        return carry

    lax.fori_loop(1, count, greet, 0, unroll=True)
    pl.semaphore_wait(barrier, count - 1)
    own = pltpu.make_async_copy(src_ref.at[me], dst_ref.at[me], own_sem)
    own.start()

    def remote(step):
        peer = lax.rem(me + step, count)
        return pltpu.make_async_remote_copy(
            src_ref.at[peer],
            dst_ref.at[me],
            send_sem.at[step],
            recv_sem.at[step],
            device_id={"seq": peer},
            device_id_type=mesh_ids,
        )

    def send(step, carry):
        remote(step).start()
        return carry

    lax.fori_loop(1, count, send, 0, unroll=True)

    def finish(step, carry):
        copy = remote(step)
        copy.wait_send()
        copy.wait_recv()
        return carry

    lax.fori_loop(1, count, finish, 0, unroll=True)
    own.wait()


def exchange(blocks, tag):
    count = blocks.shape[0]
    vmem = pl.BlockSpec(memory_space=pltpu.VMEM)
    return pl.pallas_call(
        exchange_kernel,
        out_shape=jax.ShapeDtypeStruct(blocks.shape, blocks.dtype),
        in_specs=[vmem],
        out_specs=vmem,
        scratch_shapes=[
            pltpu.SemaphoreType.DMA((count,)),
            pltpu.SemaphoreType.DMA((count,)),
            pltpu.SemaphoreType.DMA,
        ],
        compiler_params=pltpu.CompilerParams(collective_id=tag, has_side_effects=True),
    )(blocks)


def front_kernel(
    feat_ref, gate_ref, gain_ref, spec_ref,
    sig_out, sig_recv, spec_recv,
    sq_mine, sq_recv, sig_send, spec_sems, sig_sems, chan_sems, own_sems,
):
    count = spec_ref.shape[0]
    chans = sq_recv.shape[0]
    me = lax.axis_index("seq")
    mine = lax.axis_index("chan")
    mesh_ids = pl.DeviceIdType.MESH
    barrier = pltpu.get_barrier_semaphore()

    def greet(step, carry):
        peer = lax.rem(me + step, count)
        pl.semaphore_signal(barrier, inc=1, device_id={"seq": peer}, device_id_type=mesh_ids)
        return carry

    lax.fori_loop(1, count, greet, 0, unroll=True)
    for step in range(1, chans):
        peer = lax.rem(mine + step, chans)
        pl.semaphore_signal(barrier, inc=1, device_id={"chan": peer}, device_id_type=mesh_ids)
    pl.semaphore_wait(barrier, count + chans - 2)

    def spec_copy(step):
        peer = lax.rem(me + step, count)
        return pltpu.make_async_remote_copy(
            spec_ref.at[peer],
            spec_recv.at[me],
            spec_sems.at[0, step],
            spec_sems.at[1, step],
            device_id={"seq": peer},
            device_id_type=mesh_ids,
        )

    spec_own = pltpu.make_async_copy(spec_ref.at[me], spec_recv.at[me], own_sems.at[0])
    spec_own.start()

    def spec_send(step, carry):
        spec_copy(step).start()
        return carry

    lax.fori_loop(1, count, spec_send, 0, unroll=True)

    feat = feat_ref[...].astype(jnp.float32)
    part = jnp.sum(jnp.transpose(feat * feat), axis=0, keepdims=True)
    sq_mine[...] = jnp.broadcast_to(part, sq_mine.shape)

    def chan_copy(step):
        peer = lax.rem(mine + step, chans)
        return pltpu.make_async_remote_copy(
            sq_mine,
            sq_recv.at[mine],
            chan_sems.at[0, step],
            chan_sems.at[1, step],
            device_id={"chan": peer},
            device_id_type=mesh_ids,
        )

    for step in range(1, chans):
        chan_copy(step).start()
    for step in range(1, chans):
        copy = chan_copy(step)
        copy.wait_send()
        copy.wait_recv()
    total = part
    for step in range(1, chans):
        other = lax.rem(mine + step, chans)
        total = total + sq_recv[other][0:1, :]
    scale = lax.rsqrt(total / CHANNELS + 1e-06)
    scale = jnp.transpose(jnp.broadcast_to(scale, (8, scale.shape[1])))[:, 0:1]
    signal = (feat * scale * gain_ref[...] * gate_ref[...].astype(jnp.float32)).astype(jnp.bfloat16)
    sig_out[...] = signal
    wide = jnp.transpose(signal.astype(jnp.float32))
    pair = sig_send.shape[1]
    for peer in range(count):
        sig_send[peer] = wide[pair * peer:pair * peer + pair, :]

    def sig_copy(step):
        peer = lax.rem(me + step, count)
        return pltpu.make_async_remote_copy(
            sig_send.at[peer],
            sig_recv.at[me],
            sig_sems.at[0, step],
            sig_sems.at[1, step],
            device_id={"seq": peer},
            device_id_type=mesh_ids,
        )

    sig_own = pltpu.make_async_copy(sig_send.at[me], sig_recv.at[me], own_sems.at[1])
    sig_own.start()

    def sig_start(step, carry):
        sig_copy(step).start()
        return carry

    lax.fori_loop(1, count, sig_start, 0, unroll=True)

    def sig_finish(step, carry):
        copy = sig_copy(step)
        copy.wait_send()
        copy.wait_recv()
        return carry

    lax.fori_loop(1, count, sig_finish, 0, unroll=True)
    sig_own.wait()

    def spec_finish(step, carry):
        copy = spec_copy(step)
        copy.wait_send()
        copy.wait_recv()
        return carry

    lax.fori_loop(1, count, spec_finish, 0, unroll=True)
    spec_own.wait()


def front(feat, gate, gain_row, spec_rows, chans):
    count = spec_rows.shape[0]
    length, width = feat.shape
    pair = width // count
    vmem = pl.BlockSpec(memory_space=pltpu.VMEM)
    return pl.pallas_call(
        front_kernel,
        out_shape=(
            jax.ShapeDtypeStruct((length, width), jnp.bfloat16),
            jax.ShapeDtypeStruct((count, pair, length), jnp.float32),
            jax.ShapeDtypeStruct(spec_rows.shape, spec_rows.dtype),
        ),
        in_specs=[vmem] * 4,
        out_specs=(vmem, vmem, vmem),
        scratch_shapes=[
            pltpu.VMEM((8, length), jnp.float32),
            pltpu.VMEM((chans, 8, length), jnp.float32),
            pltpu.VMEM((count, pair, length), jnp.float32),
            pltpu.SemaphoreType.DMA((2, count)),
            pltpu.SemaphoreType.DMA((2, count)),
            pltpu.SemaphoreType.DMA((2, chans)),
            pltpu.SemaphoreType.DMA((2,)),
        ],
        compiler_params=pltpu.CompilerParams(collective_id=0, has_side_effects=True),
    )(feat, gate, gain_row, spec_rows)


def bin_rows(seq_count):
    digit_order = reversed_digits(seq_count)
    stride = 2 * seq_count
    slots = np.arange(stride)
    low_bins = 2 * digit_order[slots // 2] + slots % 2
    return (low_bins[:, None] + stride * np.arange(ROW_GROUP)[None, :]).reshape(-1).astype(np.int32)


def convolve(sig_cols, spec_chan, seq_count, tok_rows):
    group = spec_chan.shape[0]
    first_len, second_len = spec_chan.shape[2], spec_chan.shape[3]
    half_first = first_len // 2
    all_bins = first_len * second_len
    row_bins = bin_rows(seq_count).astype(np.int64)
    first_in = np.arange(half_first)
    first_turn = (row_bins[:, None] * first_in[None, :]) % first_len * (2.0 * np.pi / first_len)
    stacked_np = np.concatenate([np.cos(first_turn), np.sin(first_turn)], 0)
    stacked = jnp.asarray(stacked_np.astype(np.float32))
    signs = np.concatenate([np.ones(first_len), -np.ones(first_len)]) / all_bins
    twist_turn = (row_bins[:, None] * np.arange(second_len)[None, :]) % all_bins * (2.0 * np.pi / all_bins)
    cos_twist = jnp.asarray(np.cos(twist_turn).astype(np.float32))
    sin_twist = jnp.asarray(np.sin(twist_turn).astype(np.float32))
    second_in = jnp.arange(second_len, dtype=jnp.int32)
    cos_second, sin_second = rotation(second_in[:, None] * second_in[None, :], second_len)
    fwd_second = jnp.concatenate(
        [jnp.concatenate([cos_second, -sin_second], 1), jnp.concatenate([sin_second, cos_second], 1)], 0
    )
    inv_second = jnp.concatenate(
        [jnp.concatenate([cos_second, sin_second], 1), jnp.concatenate([-sin_second, cos_second], 1)], 0
    )
    last = stacked * jnp.asarray(signs.astype(np.float32))[:, None]

    both = mm("rn,nm->rm", stacked, sig_cols)
    along_cos, along_sin = both[:first_len], both[first_len:]
    outs_re, outs_im = [], []
    for chan in range(group):
        lanes_of = slice(chan * second_len, (chan + 1) * second_len)
        p_cos, p_sin = along_cos[:, lanes_of], along_sin[:, lanes_of]
        twist_re = p_cos * cos_twist - p_sin * sin_twist
        twist_im = -p_sin * cos_twist - p_cos * sin_twist
        freq = mm("rn,nk->rk", jnp.concatenate([twist_re, twist_im], 1), fwd_second)
        freq_re, freq_im = freq[:, :second_len], freq[:, second_len:]
        filt_re, filt_im = spec_chan[chan, 0], spec_chan[chan, 1]
        prod_re = freq_re * filt_re - freq_im * filt_im
        prod_im = freq_re * filt_im + freq_im * filt_re
        back = mm("rk,kn->rn", jnp.concatenate([prod_re, prod_im], 1), inv_second)
        back_re, back_im = back[:, :second_len], back[:, second_len:]
        outs_re.append(back_re * cos_twist - back_im * sin_twist)
        outs_im.append(back_im * cos_twist + back_re * sin_twist)
    untwisted = jnp.concatenate([jnp.concatenate(outs_re, 1), jnp.concatenate(outs_im, 1)], 0)
    return mm("rn,rm->nm", last, untwisted)


def local(features, pre_gate, post_gate, norm_gain, skip_weight, spectrum):
    tok_rows, chan_width = features.shape
    seq_count = lax.axis_size("seq")
    chans = lax.axis_size("chan")
    stride = 2 * seq_count
    all_bins = stride * tok_rows
    group = chan_width // seq_count
    first_len = stride * ROW_GROUP
    second_len = all_bins // first_len
    half_first = first_len // 2
    lanes = 128
    tok_tiles = tok_rows // lanes

    half_group = ROW_GROUP // 2
    spec_rows = spectrum.reshape(2, 2, second_len, half_group, 2, chan_width)
    spec_rows = jnp.transpose(spec_rows, (5, 0, 1, 3, 4, 2)).astype(jnp.bfloat16)
    spec_rows = spec_rows.reshape(seq_count, -1, 2 * second_len)
    signal, sig_chan, spec_chan = front(
        features, pre_gate, norm_gain.reshape(1, chan_width), spec_rows, chans
    )
    spec_chan = spec_chan.reshape(seq_count, group, 2, -1, 2 * second_len)
    spec_chan = jnp.transpose(spec_chan, (1, 2, 0, 3, 4)).astype(jnp.float32)
    spec_chan = spec_chan.reshape(group, 2, first_len, second_len)
    sig_cols = sig_chan.reshape(seq_count, group, tok_tiles, lanes)
    sig_cols = jnp.transpose(sig_cols, (0, 2, 1, 3)).reshape(half_first, group * second_len)
    conv = convolve(sig_cols, spec_chan, seq_count, tok_rows)
    conv = jnp.transpose(conv.reshape(seq_count, tok_tiles, group, lanes), (0, 2, 1, 3))
    conv = conv.reshape(seq_count, -1, lanes)
    result = exchange(conv, 2).reshape(seq_count, group, tok_tiles, lanes)
    result = jnp.transpose(result, (2, 3, 0, 1)).reshape(tok_rows, chan_width)
    gated = post_gate.astype(jnp.float32) * (result + skip_weight * signal.astype(jnp.float32))
    return gated.astype(jnp.bfloat16)


def solution(mesh):
    return jax.shard_map(
        local,
        mesh=mesh,
        in_specs=(
            P("seq", "chan"),
            P("seq", "chan"),
            P("seq", "chan"),
            P("chan"),
            P("chan"),
            P(None, "seq", None, "chan"),
        ),
        out_specs=P("seq", "chan"),
        check_vma=False,
    )
```

```python
import math

import jax
import jax.numpy as jnp
import numpy as np
from jax import lax
from jax.experimental import pallas as pl
from jax.experimental.pallas import tpu as pltpu
from jax.sharding import PartitionSpec as P

CHANNELS = 512
ROW_GROUP = 4
HIGH_DIGIT = 8


PRECISE = lax.Precision.HIGH
FULL_TURN = 2.0 * math.pi


def reversed_digits(count):
    levels = count.bit_length() - 1
    positions = np.arange(count)
    result = np.zeros(count, np.int64)
    for bit_pos in range(levels):
        result = result + ((positions >> bit_pos & 1) << levels - 1 - bit_pos)
    return result


def rotation(numerator, denominator):
    angle = (numerator % denominator).astype(jnp.float32) * (FULL_TURN / denominator)
    return (jnp.cos(angle), jnp.sin(angle))


def mm(spec, left, right):
    return jnp.einsum(spec, left, right, precision=PRECISE, preferred_element_type=jnp.float32)


def exchange_kernel(src_ref, dst_ref, send_sem, recv_sem, own_sem):
    count = src_ref.shape[0]
    me = lax.axis_index("seq")
    mesh_ids = pl.DeviceIdType.MESH
    barrier = pltpu.get_barrier_semaphore()

    def greet(step, carry):
        peer = lax.rem(me + step, count)
        pl.semaphore_signal(barrier, inc=1, device_id={"seq": peer}, device_id_type=mesh_ids)
        return carry

    lax.fori_loop(1, count, greet, 0, unroll=True)
    pl.semaphore_wait(barrier, count - 1)
    own = pltpu.make_async_copy(src_ref.at[me], dst_ref.at[me], own_sem)
    own.start()

    def remote(step):
        peer = lax.rem(me + step, count)
        return pltpu.make_async_remote_copy(
            src_ref.at[peer],
            dst_ref.at[me],
            send_sem.at[step],
            recv_sem.at[step],
            device_id={"seq": peer},
            device_id_type=mesh_ids,
        )

    def send(step, carry):
        remote(step).start()
        return carry

    lax.fori_loop(1, count, send, 0, unroll=True)

    def finish(step, carry):
        copy = remote(step)
        copy.wait_send()
        copy.wait_recv()
        return carry

    lax.fori_loop(1, count, finish, 0, unroll=True)
    own.wait()


def exchange(blocks, tag):
    count = blocks.shape[0]
    vmem = pl.BlockSpec(memory_space=pltpu.VMEM)
    return pl.pallas_call(
        exchange_kernel,
        out_shape=jax.ShapeDtypeStruct(blocks.shape, blocks.dtype),
        in_specs=[vmem],
        out_specs=vmem,
        scratch_shapes=[
            pltpu.SemaphoreType.DMA((count,)),
            pltpu.SemaphoreType.DMA((count,)),
            pltpu.SemaphoreType.DMA,
        ],
        compiler_params=pltpu.CompilerParams(collective_id=tag, has_side_effects=True),
    )(blocks)


def front_kernel(
    feat_ref, gate_ref, gain_ref, spec_ref,
    sig_out, sig_recv, spec_recv,
    sq_mine, sq_recv, sig_turn, sig_send, spec_sems, sig_sems, chan_sems, own_sems,
):
    count = spec_ref.shape[0]
    chans = sq_recv.shape[0]
    me = lax.axis_index("seq")
    mine = lax.axis_index("chan")
    mesh_ids = pl.DeviceIdType.MESH
    barrier = pltpu.get_barrier_semaphore()

    def greet(step, carry):
        peer = lax.rem(me + step, count)
        pl.semaphore_signal(barrier, inc=1, device_id={"seq": peer}, device_id_type=mesh_ids)
        return carry

    lax.fori_loop(1, count, greet, 0, unroll=True)
    for step in range(1, chans):
        peer = lax.rem(mine + step, chans)
        pl.semaphore_signal(barrier, inc=1, device_id={"chan": peer}, device_id_type=mesh_ids)
    pl.semaphore_wait(barrier, count + chans - 2)

    def spec_copy(step):
        peer = lax.rem(me + step, count)
        return pltpu.make_async_remote_copy(
            spec_ref.at[peer],
            spec_recv.at[me],
            spec_sems.at[0, step],
            spec_sems.at[1, step],
            device_id={"seq": peer},
            device_id_type=mesh_ids,
        )

    spec_own = pltpu.make_async_copy(spec_ref.at[me], spec_recv.at[me], own_sems.at[0])
    spec_own.start()

    def spec_send(step, carry):
        spec_copy(step).start()
        return carry

    lax.fori_loop(1, count, spec_send, 0, unroll=True)

    feat = feat_ref[...].astype(jnp.float32)
    part = jnp.sum(jnp.transpose(feat * feat), axis=0, keepdims=True)
    sq_mine[...] = jnp.broadcast_to(part, sq_mine.shape)

    def chan_copy(step):
        peer = lax.rem(mine + step, chans)
        return pltpu.make_async_remote_copy(
            sq_mine,
            sq_recv.at[mine],
            chan_sems.at[0, step],
            chan_sems.at[1, step],
            device_id={"chan": peer},
            device_id_type=mesh_ids,
        )

    for step in range(1, chans):
        chan_copy(step).start()
    for step in range(1, chans):
        copy = chan_copy(step)
        copy.wait_send()
        copy.wait_recv()
    total = part
    for step in range(1, chans):
        other = lax.rem(mine + step, chans)
        total = total + sq_recv[other][0:1, :]
    scale = lax.rsqrt(total / CHANNELS + 1e-06)
    scale = jnp.transpose(jnp.broadcast_to(scale, (8, scale.shape[1])))[:, 0:1]
    signal = (feat * scale * gain_ref[...] * gate_ref[...].astype(jnp.float32)).astype(jnp.bfloat16)
    sig_out[...] = signal
    wide = signal.astype(jnp.float32)
    lanes = wide.shape[1]
    pair = lanes // count
    tiles = wide.shape[0] // lanes
    chunk = pair * tiles
    for tile in range(tiles):
        sig_turn[...] = jnp.transpose(wide[lanes * tile:lanes * (tile + 1), :])
        for chan in range(pair):
            rows = sig_turn[pl.ds(chan, count, stride=pair), :]
            sig_send[pl.ds(tiles * chan + tile, count, stride=chunk), :] = rows

    def sig_rows(peer):
        return sig_send.at[pl.ds(pl.multiple_of(peer * chunk, chunk), chunk)]

    def sig_copy(step):
        peer = lax.rem(me + step, count)
        return pltpu.make_async_remote_copy(
            sig_rows(peer),
            sig_recv.at[me],
            sig_sems.at[0, step],
            sig_sems.at[1, step],
            device_id={"seq": peer},
            device_id_type=mesh_ids,
        )

    sig_own = pltpu.make_async_copy(sig_rows(me), sig_recv.at[me], own_sems.at[1])
    sig_own.start()

    def sig_start(step, carry):
        sig_copy(step).start()
        return carry

    lax.fori_loop(1, count, sig_start, 0, unroll=True)

    def sig_finish(step, carry):
        copy = sig_copy(step)
        copy.wait_send()
        copy.wait_recv()
        return carry

    lax.fori_loop(1, count, sig_finish, 0, unroll=True)
    sig_own.wait()

    def spec_finish(step, carry):
        copy = spec_copy(step)
        copy.wait_send()
        copy.wait_recv()
        return carry

    lax.fori_loop(1, count, spec_finish, 0, unroll=True)
    spec_own.wait()


def front(feat, gate, gain_row, spec_rows, chans):
    count = spec_rows.shape[0]
    length, width = feat.shape
    pair = width // count
    vmem = pl.BlockSpec(memory_space=pltpu.VMEM)
    return pl.pallas_call(
        front_kernel,
        out_shape=(
            jax.ShapeDtypeStruct((length, width), jnp.bfloat16),
            jax.ShapeDtypeStruct((count, pair * length // 128, 128), jnp.float32),
            jax.ShapeDtypeStruct(spec_rows.shape, spec_rows.dtype),
        ),
        in_specs=[vmem] * 4,
        out_specs=(vmem, vmem, vmem),
        scratch_shapes=[
            pltpu.VMEM((8, length), jnp.float32),
            pltpu.VMEM((chans, 8, length), jnp.float32),
            pltpu.VMEM((128, 128), jnp.float32),
            pltpu.VMEM((count * pair * length // 128, 128), jnp.float32),
            pltpu.SemaphoreType.DMA((2, count)),
            pltpu.SemaphoreType.DMA((2, count)),
            pltpu.SemaphoreType.DMA((2, chans)),
            pltpu.SemaphoreType.DMA((2,)),
        ],
        compiler_params=pltpu.CompilerParams(collective_id=0, has_side_effects=True),
    )(feat, gate, gain_row, spec_rows)


def bin_rows(seq_count):
    digit_order = reversed_digits(seq_count)
    stride = 2 * seq_count
    slots = np.arange(stride)
    low_bins = 2 * digit_order[slots // 2] + slots % 2
    return (low_bins[:, None] + stride * np.arange(ROW_GROUP)[None, :]).reshape(-1).astype(np.int32)


def convolve(sig_cols, spec_chan, seq_count, tok_rows):
    group = spec_chan.shape[0]
    first_len, second_len = spec_chan.shape[2], spec_chan.shape[3]
    half_first = first_len // 2
    all_bins = first_len * second_len
    row_bins = bin_rows(seq_count).astype(np.int64)
    first_in = np.arange(half_first)
    first_turn = (row_bins[:, None] * first_in[None, :]) % first_len * (2.0 * np.pi / first_len)
    stacked_np = np.concatenate([np.cos(first_turn), np.sin(first_turn)], 0)
    stacked = jnp.asarray(stacked_np.astype(np.float32))
    signs = np.concatenate([np.ones(first_len), -np.ones(first_len)]) / all_bins
    twist_turn = (row_bins[:, None] * np.arange(second_len)[None, :]) % all_bins * (2.0 * np.pi / all_bins)
    cos_twist = jnp.asarray(np.cos(twist_turn).astype(np.float32))
    sin_twist = jnp.asarray(np.sin(twist_turn).astype(np.float32))
    second_in = jnp.arange(second_len, dtype=jnp.int32)
    cos_second, sin_second = rotation(second_in[:, None] * second_in[None, :], second_len)
    fwd_second = jnp.concatenate(
        [jnp.concatenate([cos_second, -sin_second], 1), jnp.concatenate([sin_second, cos_second], 1)], 0
    )
    inv_second = jnp.concatenate(
        [jnp.concatenate([cos_second, sin_second], 1), jnp.concatenate([-sin_second, cos_second], 1)], 0
    )
    last = stacked * jnp.asarray(signs.astype(np.float32))[:, None]

    both = mm("rn,nm->rm", stacked, sig_cols)
    along_cos, along_sin = both[:first_len], both[first_len:]
    outs_re, outs_im = [], []
    for chan in range(group):
        lanes_of = slice(chan * second_len, (chan + 1) * second_len)
        p_cos, p_sin = along_cos[:, lanes_of], along_sin[:, lanes_of]
        twist_re = p_cos * cos_twist - p_sin * sin_twist
        twist_im = -p_sin * cos_twist - p_cos * sin_twist
        freq = mm("rn,nk->rk", jnp.concatenate([twist_re, twist_im], 1), fwd_second)
        freq_re, freq_im = freq[:, :second_len], freq[:, second_len:]
        filt_re, filt_im = spec_chan[chan, 0], spec_chan[chan, 1]
        prod_re = freq_re * filt_re - freq_im * filt_im
        prod_im = freq_re * filt_im + freq_im * filt_re
        back = mm("rk,kn->rn", jnp.concatenate([prod_re, prod_im], 1), inv_second)
        back_re, back_im = back[:, :second_len], back[:, second_len:]
        outs_re.append(back_re * cos_twist - back_im * sin_twist)
        outs_im.append(back_im * cos_twist + back_re * sin_twist)
    untwisted = jnp.concatenate([jnp.concatenate(outs_re, 1), jnp.concatenate(outs_im, 1)], 0)
    return mm("rn,rm->nm", last, untwisted)


def local(features, pre_gate, post_gate, norm_gain, skip_weight, spectrum):
    tok_rows, chan_width = features.shape
    seq_count = lax.axis_size("seq")
    chans = lax.axis_size("chan")
    stride = 2 * seq_count
    all_bins = stride * tok_rows
    group = chan_width // seq_count
    first_len = stride * ROW_GROUP
    second_len = all_bins // first_len
    half_first = first_len // 2
    lanes = 128
    tok_tiles = tok_rows // lanes

    half_group = ROW_GROUP // 2
    spec_rows = spectrum.reshape(2, 2, second_len, half_group, 2, chan_width)
    spec_rows = jnp.transpose(spec_rows, (5, 0, 1, 3, 4, 2)).astype(jnp.bfloat16)
    spec_rows = spec_rows.reshape(seq_count, -1, 2 * second_len)
    signal, sig_chan, spec_chan = front(
        features, pre_gate, norm_gain.reshape(1, chan_width), spec_rows, chans
    )
    spec_chan = spec_chan.reshape(seq_count, group, 2, -1, 2 * second_len)
    spec_chan = jnp.transpose(spec_chan, (1, 2, 0, 3, 4)).astype(jnp.float32)
    spec_chan = spec_chan.reshape(group, 2, first_len, second_len)
    sig_cols = sig_chan.reshape(seq_count, group, tok_tiles, lanes)
    sig_cols = jnp.transpose(sig_cols, (0, 2, 1, 3)).reshape(half_first, group * second_len)
    conv = convolve(sig_cols, spec_chan, seq_count, tok_rows)
    conv = jnp.transpose(conv.reshape(seq_count, tok_tiles, group, lanes), (0, 2, 1, 3))
    conv = conv.reshape(seq_count, -1, lanes)
    result = exchange(conv, 2).reshape(seq_count, group, tok_tiles, lanes)
    result = jnp.transpose(result, (2, 3, 0, 1)).reshape(tok_rows, chan_width)
    gated = post_gate.astype(jnp.float32) * (result + skip_weight * signal.astype(jnp.float32))
    return gated.astype(jnp.bfloat16)


def solution(mesh):
    return jax.shard_map(
        local,
        mesh=mesh,
        in_specs=(
            P("seq", "chan"),
            P("seq", "chan"),
            P("seq", "chan"),
            P("chan"),
            P("chan"),
            P(None, "seq", None, "chan"),
        ),
        out_specs=P("seq", "chan"),
        check_vma=False,
    )
```

```python
import math

import jax
import jax.numpy as jnp
import numpy as np
from jax import lax
from jax.experimental import pallas as pl
from jax.experimental.pallas import tpu as pltpu
from jax.sharding import PartitionSpec as P

CHANNELS = 512
ROW_GROUP = 4
HIGH_DIGIT = 8


PRECISE = lax.Precision.HIGH
FULL_TURN = 2.0 * math.pi


def reversed_digits(count):
    levels = count.bit_length() - 1
    positions = np.arange(count)
    result = np.zeros(count, np.int64)
    for bit_pos in range(levels):
        result = result + ((positions >> bit_pos & 1) << levels - 1 - bit_pos)
    return result


def rotation(numerator, denominator):
    angle = (numerator % denominator).astype(jnp.float32) * (FULL_TURN / denominator)
    return (jnp.cos(angle), jnp.sin(angle))


def mm(spec, left, right):
    return jnp.einsum(spec, left, right, precision=PRECISE, preferred_element_type=jnp.float32)


def exchange_kernel(src_ref, dst_ref, send_sem, recv_sem, own_sem):
    count = src_ref.shape[0]
    me = lax.axis_index("seq")
    mesh_ids = pl.DeviceIdType.MESH
    barrier = pltpu.get_barrier_semaphore()

    def greet(step, carry):
        peer = lax.rem(me + step, count)
        pl.semaphore_signal(barrier, inc=1, device_id={"seq": peer}, device_id_type=mesh_ids)
        return carry

    lax.fori_loop(1, count, greet, 0, unroll=True)
    pl.semaphore_wait(barrier, count - 1)
    own = pltpu.make_async_copy(src_ref.at[me], dst_ref.at[me], own_sem)
    own.start()

    def remote(step):
        peer = lax.rem(me + step, count)
        return pltpu.make_async_remote_copy(
            src_ref.at[peer],
            dst_ref.at[me],
            send_sem.at[step],
            recv_sem.at[step],
            device_id={"seq": peer},
            device_id_type=mesh_ids,
        )

    def send(step, carry):
        remote(step).start()
        return carry

    lax.fori_loop(1, count, send, 0, unroll=True)

    def finish(step, carry):
        copy = remote(step)
        copy.wait_send()
        copy.wait_recv()
        return carry

    lax.fori_loop(1, count, finish, 0, unroll=True)
    own.wait()


def exchange(blocks, tag):
    count = blocks.shape[0]
    vmem = pl.BlockSpec(memory_space=pltpu.VMEM)
    return pl.pallas_call(
        exchange_kernel,
        out_shape=jax.ShapeDtypeStruct(blocks.shape, blocks.dtype),
        in_specs=[vmem],
        out_specs=vmem,
        scratch_shapes=[
            pltpu.SemaphoreType.DMA((count,)),
            pltpu.SemaphoreType.DMA((count,)),
            pltpu.SemaphoreType.DMA,
        ],
        compiler_params=pltpu.CompilerParams(collective_id=tag, has_side_effects=True),
    )(blocks)


def front_kernel(
    feat_ref, gate_ref, gain_ref, spec_ref,
    sig_out, sig_recv, spec_recv,
    sq_mine, sq_recv, sig_turn, sig_send, spec_sems, sig_sems, chan_sems, own_sems,
):
    count = spec_ref.shape[0]
    chans = sq_recv.shape[0]
    me = lax.axis_index("seq")
    mine = lax.axis_index("chan")
    mesh_ids = pl.DeviceIdType.MESH
    barrier = pltpu.get_barrier_semaphore()

    def greet(step, carry):
        peer = lax.rem(me + step, count)
        pl.semaphore_signal(barrier, inc=1, device_id={"seq": peer}, device_id_type=mesh_ids)
        return carry

    lax.fori_loop(1, count, greet, 0, unroll=True)
    for step in range(1, chans):
        peer = lax.rem(mine + step, chans)
        pl.semaphore_signal(barrier, inc=1, device_id={"chan": peer}, device_id_type=mesh_ids)
    pl.semaphore_wait(barrier, count + chans - 2)

    def spec_copy(step):
        peer = lax.rem(me + step, count)
        return pltpu.make_async_remote_copy(
            spec_ref.at[peer],
            spec_recv.at[me],
            spec_sems.at[0, step],
            spec_sems.at[1, step],
            device_id={"seq": peer},
            device_id_type=mesh_ids,
        )

    spec_own = pltpu.make_async_copy(spec_ref.at[me], spec_recv.at[me], own_sems.at[0])
    spec_own.start()

    def spec_send(step, carry):
        spec_copy(step).start()
        return carry

    lax.fori_loop(1, count, spec_send, 0, unroll=True)

    feat = feat_ref[...].astype(jnp.float32)
    part = jnp.sum(jnp.transpose(feat * feat), axis=0, keepdims=True)
    sq_mine[...] = jnp.broadcast_to(part, sq_mine.shape)

    def chan_copy(step):
        peer = lax.rem(mine + step, chans)
        return pltpu.make_async_remote_copy(
            sq_mine,
            sq_recv.at[mine],
            chan_sems.at[0, step],
            chan_sems.at[1, step],
            device_id={"chan": peer},
            device_id_type=mesh_ids,
        )

    for step in range(1, chans):
        chan_copy(step).start()
    for step in range(1, chans):
        copy = chan_copy(step)
        copy.wait_send()
        copy.wait_recv()
    total = part
    for step in range(1, chans):
        other = lax.rem(mine + step, chans)
        total = total + sq_recv[other][0:1, :]
    scale = lax.rsqrt(total / CHANNELS + 1e-06)
    scale = jnp.transpose(jnp.broadcast_to(scale, (8, scale.shape[1])))[:, 0:1]
    signal = (feat * scale * gain_ref[...] * gate_ref[...].astype(jnp.float32)).astype(jnp.bfloat16)
    sig_out[...] = signal
    wide = signal.astype(jnp.float32)
    lanes = wide.shape[1]
    pair = lanes // count
    tiles = wide.shape[0] // lanes
    chunk = pair * tiles
    for tile in range(tiles):
        sig_turn[...] = jnp.transpose(wide[lanes * tile:lanes * (tile + 1), :])
        for chan in range(pair):
            rows = sig_turn[pl.ds(chan, count, stride=pair), :]
            sig_send[pl.ds(tiles * chan + tile, count, stride=chunk), :] = rows

    def sig_rows(peer):
        return sig_send.at[pl.ds(pl.multiple_of(peer * chunk, chunk), chunk)]

    def sig_copy(step):
        peer = lax.rem(me + step, count)
        return pltpu.make_async_remote_copy(
            sig_rows(peer),
            sig_recv.at[me],
            sig_sems.at[0, step],
            sig_sems.at[1, step],
            device_id={"seq": peer},
            device_id_type=mesh_ids,
        )

    sig_own = pltpu.make_async_copy(sig_rows(me), sig_recv.at[me], own_sems.at[1])
    sig_own.start()

    def sig_start(step, carry):
        sig_copy(step).start()
        return carry

    lax.fori_loop(1, count, sig_start, 0, unroll=True)

    def sig_finish(step, carry):
        copy = sig_copy(step)
        copy.wait_send()
        copy.wait_recv()
        return carry

    lax.fori_loop(1, count, sig_finish, 0, unroll=True)
    sig_own.wait()

    def spec_finish(step, carry):
        copy = spec_copy(step)
        copy.wait_send()
        copy.wait_recv()
        return carry

    lax.fori_loop(1, count, spec_finish, 0, unroll=True)
    spec_own.wait()


def front(feat, gate, gain_row, spec_rows, chans):
    count = spec_rows.shape[0]
    length, width = feat.shape
    pair = width // count
    vmem = pl.BlockSpec(memory_space=pltpu.VMEM)
    return pl.pallas_call(
        front_kernel,
        out_shape=(
            jax.ShapeDtypeStruct((length, width), jnp.bfloat16),
            jax.ShapeDtypeStruct((count, pair * length // 128, 128), jnp.float32),
            jax.ShapeDtypeStruct(spec_rows.shape, spec_rows.dtype),
        ),
        in_specs=[vmem] * 4,
        out_specs=(vmem, vmem, vmem),
        scratch_shapes=[
            pltpu.VMEM((8, length), jnp.float32),
            pltpu.VMEM((chans, 8, length), jnp.float32),
            pltpu.VMEM((128, 128), jnp.float32),
            pltpu.VMEM((count * pair * length // 128, 128), jnp.float32),
            pltpu.SemaphoreType.DMA((2, count)),
            pltpu.SemaphoreType.DMA((2, count)),
            pltpu.SemaphoreType.DMA((2, chans)),
            pltpu.SemaphoreType.DMA((2,)),
        ],
        compiler_params=pltpu.CompilerParams(collective_id=0, has_side_effects=True),
    )(feat, gate, gain_row, spec_rows)


def bin_rows(seq_count):
    digit_order = reversed_digits(seq_count)
    stride = 2 * seq_count
    slots = np.arange(stride)
    low_bins = 2 * digit_order[slots // 2] + slots % 2
    return (low_bins[:, None] + stride * np.arange(ROW_GROUP)[None, :]).reshape(-1).astype(np.int32)


def convolve(sig_cols, spec_chan, seq_count, tok_rows):
    group = spec_chan.shape[0]
    first_len, second_len = spec_chan.shape[2], spec_chan.shape[3]
    half_first = first_len // 2
    all_bins = first_len * second_len
    row_bins = bin_rows(seq_count).astype(np.int64)
    first_in = np.arange(half_first)
    first_turn = (row_bins[:, None] * first_in[None, :]) % first_len * (2.0 * np.pi / first_len)
    stacked_np = np.concatenate([np.cos(first_turn), np.sin(first_turn)], 0)
    stacked = jnp.asarray(stacked_np.astype(np.float32))
    signs = np.concatenate([np.ones(first_len), -np.ones(first_len)]) / all_bins
    twist_turn = (row_bins[:, None] * np.arange(second_len)[None, :]) % all_bins * (2.0 * np.pi / all_bins)
    cos_twist = jnp.asarray(np.cos(twist_turn).astype(np.float32))
    sin_twist = jnp.asarray(np.sin(twist_turn).astype(np.float32))
    second_in = jnp.arange(second_len, dtype=jnp.int32)
    cos_second, sin_second = rotation(second_in[:, None] * second_in[None, :], second_len)
    fwd_second = jnp.concatenate(
        [jnp.concatenate([cos_second, -sin_second], 1), jnp.concatenate([sin_second, cos_second], 1)], 0
    )
    inv_second = jnp.concatenate(
        [jnp.concatenate([cos_second, sin_second], 1), jnp.concatenate([-sin_second, cos_second], 1)], 0
    )
    last = stacked * jnp.asarray(signs.astype(np.float32))[:, None]

    both = mm("rn,nm->rm", stacked, sig_cols)
    along_cos, along_sin = both[:first_len], both[first_len:]
    outs_re, outs_im = [], []
    for chan in range(group):
        lanes_of = slice(chan * second_len, (chan + 1) * second_len)
        p_cos, p_sin = along_cos[:, lanes_of], along_sin[:, lanes_of]
        twist_re = p_cos * cos_twist - p_sin * sin_twist
        twist_im = -p_sin * cos_twist - p_cos * sin_twist
        freq = mm("rn,nk->rk", jnp.concatenate([twist_re, twist_im], 1), fwd_second)
        freq_re, freq_im = freq[:, :second_len], freq[:, second_len:]
        filt_re, filt_im = spec_chan[chan, 0], spec_chan[chan, 1]
        prod_re = freq_re * filt_re - freq_im * filt_im
        prod_im = freq_re * filt_im + freq_im * filt_re
        back = mm("rk,kn->rn", jnp.concatenate([prod_re, prod_im], 1), inv_second)
        back_re, back_im = back[:, :second_len], back[:, second_len:]
        outs_re.append(back_re * cos_twist - back_im * sin_twist)
        outs_im.append(back_im * cos_twist + back_re * sin_twist)
    untwisted = jnp.concatenate([jnp.concatenate(outs_re, 1), jnp.concatenate(outs_im, 1)], 0)
    return mm("rn,rm->nm", last, untwisted)


def split(value):
    high = value.astype(jnp.bfloat16)
    return high, (value - high.astype(jnp.float32)).astype(jnp.bfloat16)


def dot3(left, right):
    l_hi, l_lo = left if isinstance(left, tuple) else split(left)
    r_hi, r_lo = right if isinstance(right, tuple) else split(right)
    out = jnp.dot(l_hi, r_hi, preferred_element_type=jnp.float32)
    out = out + jnp.dot(l_hi, r_lo, preferred_element_type=jnp.float32)
    return out + jnp.dot(l_lo, r_hi, preferred_element_type=jnp.float32)


def whole_kernel(
    feat_ref, gate_ref, gain_ref, spec_ref,
    st_hi, st_lo, tc_ref, ts_ref, fa_hi, fa_lo, fb_hi, fb_lo, ia_hi, ia_lo, ib_hi, ib_lo,
    lc_hi, lc_lo, ls_hi, ls_lo,
    sig_out, res_recv,
    sq_mine, sq_recv, sig_turn, sig_send, sig_recv, spec_recv, cols, conv_one, conv_send,
    spec_sems, sig_sems, res_sems, chan_sems, own_sems,
):
    count = spec_ref.shape[0]
    chans = sq_recv.shape[0]
    me = lax.axis_index("seq")
    mine = lax.axis_index("chan")
    mesh_ids = pl.DeviceIdType.MESH
    barrier = pltpu.get_barrier_semaphore()

    def greet(step, carry):
        peer = lax.rem(me + step, count)
        pl.semaphore_signal(barrier, inc=1, device_id={"seq": peer}, device_id_type=mesh_ids)
        return carry

    lax.fori_loop(1, count, greet, 0)
    for step in range(1, chans):
        peer = lax.rem(mine + step, chans)
        pl.semaphore_signal(barrier, inc=1, device_id={"chan": peer}, device_id_type=mesh_ids)
    pl.semaphore_wait(barrier, count + chans - 2)

    def seq_copy(source, target, sems, step):
        peer = lax.rem(me + step, count)
        return pltpu.make_async_remote_copy(
            source(peer), target, sems.at[0, step], sems.at[1, step],
            device_id={"seq": peer}, device_id_type=mesh_ids,
        )

    def start_all(source, target, sems):
        def body(step, carry):
            seq_copy(source, target, sems, step).start()
            return carry
        lax.fori_loop(1, count, body, 0)

    def finish_all(source, target, sems):
        def body(step, carry):
            copy = seq_copy(source, target, sems, step)
            copy.wait_send()
            copy.wait_recv()
            return carry
        lax.fori_loop(1, count, body, 0)

    spec_src = lambda peer: spec_ref.at[peer]
    spec_own = pltpu.make_async_copy(spec_ref.at[me], spec_recv.at[me], own_sems.at[0])
    spec_own.start()
    start_all(spec_src, spec_recv.at[me], spec_sems)

    feat = feat_ref[...].astype(jnp.float32)
    part = jnp.sum(jnp.transpose(feat * feat), axis=0, keepdims=True)
    sq_mine[...] = jnp.broadcast_to(part, sq_mine.shape)

    def chan_copy(step):
        peer = lax.rem(mine + step, chans)
        return pltpu.make_async_remote_copy(
            sq_mine, sq_recv.at[mine], chan_sems.at[0, step], chan_sems.at[1, step],
            device_id={"chan": peer}, device_id_type=mesh_ids,
        )

    for step in range(1, chans):
        chan_copy(step).start()
    for step in range(1, chans):
        copy = chan_copy(step)
        copy.wait_send()
        copy.wait_recv()
    total = part
    for step in range(1, chans):
        other = lax.rem(mine + step, chans)
        total = total + sq_recv[other][0:1, :]
    scale = lax.rsqrt(total / CHANNELS + 1e-06)
    scale = jnp.transpose(jnp.broadcast_to(scale, (8, scale.shape[1])))[:, 0:1]
    signal = (feat * scale * gain_ref[...] * gate_ref[...].astype(jnp.float32)).astype(jnp.bfloat16)
    sig_out[...] = signal
    wide = signal.astype(jnp.float32)
    lanes = wide.shape[1]
    pair = lanes // count
    tiles = wide.shape[0] // lanes
    chunk = pair * tiles
    for tile in range(tiles):
        sig_turn[...] = jnp.transpose(wide[lanes * tile:lanes * (tile + 1), :])
        for chan in range(pair):
            rows = sig_turn[pl.ds(chan, count, stride=pair), :]
            sig_send[pl.ds(tiles * chan + tile, count, stride=chunk), :] = rows

    def rows_of(buffer):
        return lambda peer: buffer.at[pl.ds(pl.multiple_of(peer * chunk, chunk), chunk)]

    sig_own = pltpu.make_async_copy(rows_of(sig_send)(me), rows_of(sig_recv)(me), own_sems.at[1])
    sig_own.start()
    start_all(rows_of(sig_send), rows_of(sig_recv)(me), sig_sems)
    finish_all(rows_of(sig_send), rows_of(sig_recv)(me), sig_sems)
    sig_own.wait()

    for chan in range(pair):
        for tile in range(tiles):
            rows = sig_recv[pl.ds(tiles * chan + tile, count, stride=chunk), :]
            cols[chan, pl.ds(tile, count, stride=tiles), :] = rows

    first_len = tc_ref.shape[0]
    boths = []
    for chan in range(pair):
        signal_cols = cols[chan].astype(jnp.bfloat16)
        both = jnp.dot(st_hi[...], signal_cols, preferred_element_type=jnp.float32)
        boths.append(both + jnp.dot(st_lo[...], signal_cols, preferred_element_type=jnp.float32))

    finish_all(spec_src, spec_recv.at[me], spec_sems)
    spec_own.wait()

    cos_twist, sin_twist = tc_ref[...], ts_ref[...]
    own_rows = first_len // count
    for chan in range(pair):
        p_cos = boths[chan][:first_len]
        p_sin = boths[chan][first_len:]
        twist_re = p_cos * cos_twist - p_sin * sin_twist
        twist_im = -p_sin * cos_twist - p_cos * sin_twist
        freq = dot3(twist_re, (fa_hi[...], fa_lo[...])) + dot3(twist_im, (fb_hi[...], fb_lo[...]))
        freq_re, freq_im = freq[:, :lanes], freq[:, lanes:]
        filt = []
        for part_of in range(2):
            block = spec_recv[:, pl.ds((2 * chan + part_of) * own_rows, own_rows), :]
            filt.append(block.astype(jnp.float32).reshape(first_len, lanes))
        filt_re, filt_im = filt
        prod_re = freq_re * filt_re - freq_im * filt_im
        prod_im = freq_re * filt_im + freq_im * filt_re
        back = dot3(prod_re, (ia_hi[...], ia_lo[...])) + dot3(prod_im, (ib_hi[...], ib_lo[...]))
        back_re, back_im = back[:, :lanes], back[:, lanes:]
        untwist_re = back_re * cos_twist - back_im * sin_twist
        untwist_im = back_im * cos_twist + back_re * sin_twist
        conv_one[...] = dot3((lc_hi[...], lc_lo[...]), untwist_re) + dot3((ls_hi[...], ls_lo[...]), untwist_im)
        for tile in range(tiles):
            rows = conv_one[pl.ds(tile, count, stride=tiles), :]
            conv_send[pl.ds(tiles * chan + tile, count, stride=chunk), :] = rows

    res_src = rows_of(conv_send)
    res_own = pltpu.make_async_copy(res_src(me), res_recv.at[me], own_sems.at[2])
    res_own.start()
    start_all(res_src, res_recv.at[me], res_sems)
    finish_all(res_src, res_recv.at[me], res_sems)
    res_own.wait()


def whole(features, pre_gate, gain_row, spec_rows, tables, chans):
    count = spec_rows.shape[0]
    length, width = features.shape
    pair = width // count
    lanes = 128
    chunk = pair * length // lanes
    vmem = pl.BlockSpec(memory_space=pltpu.VMEM)
    operands = (features, pre_gate, gain_row, spec_rows) + tuple(tables)
    return pl.pallas_call(
        whole_kernel,
        out_shape=(
            jax.ShapeDtypeStruct((length, width), jnp.bfloat16),
            jax.ShapeDtypeStruct((count, chunk, lanes), jnp.float32),
        ),
        in_specs=[vmem] * len(operands),
        out_specs=(vmem, vmem),
        scratch_shapes=[
            pltpu.VMEM((8, length), jnp.float32),
            pltpu.VMEM((chans, 8, length), jnp.float32),
            pltpu.VMEM((lanes, lanes), jnp.float32),
            pltpu.VMEM((count * chunk, lanes), jnp.float32),
            pltpu.VMEM((count * chunk, lanes), jnp.float32),
            pltpu.VMEM(spec_rows.shape, spec_rows.dtype),
            pltpu.VMEM((pair, count * chunk // pair, lanes), jnp.float32),
            pltpu.VMEM((count * chunk // pair, lanes), jnp.float32),
            pltpu.VMEM((count * chunk, lanes), jnp.float32),
            pltpu.SemaphoreType.DMA((2, count)),
            pltpu.SemaphoreType.DMA((2, count)),
            pltpu.SemaphoreType.DMA((2, count)),
            pltpu.SemaphoreType.DMA((2, chans)),
            pltpu.SemaphoreType.DMA((3,)),
        ],
        compiler_params=pltpu.CompilerParams(
            collective_id=0, has_side_effects=True, vmem_limit_bytes=48 * 1024 * 1024
        ),
    )(*operands)


def dft_tables(seq_count, tok_rows):
    stride = 2 * seq_count
    first_len = stride * ROW_GROUP
    all_bins = stride * tok_rows
    second_len = all_bins // first_len
    half_first = first_len // 2
    row_bins = bin_rows(seq_count).astype(np.int64)
    first_turn = (row_bins[:, None] * np.arange(half_first)[None, :]) % first_len * (2.0 * np.pi / first_len)
    cos_first, sin_first = np.cos(first_turn), np.sin(first_turn)
    twist_turn = (row_bins[:, None] * np.arange(second_len)[None, :]) % all_bins * (2.0 * np.pi / all_bins)
    second_in = np.arange(second_len)
    second_turn = (second_in[:, None] * second_in[None, :]) % second_len * (2.0 * np.pi / second_len)
    cos_second, sin_second = np.cos(second_turn), np.sin(second_turn)

    def pair_of(array):
        array = array.astype(np.float32)
        high = array.astype(jnp.bfloat16)
        return [jnp.asarray(high), jnp.asarray((array - high.astype(np.float32)).astype(jnp.bfloat16))]

    tables = pair_of(np.concatenate([cos_first, sin_first], 0))
    tables += [jnp.asarray(np.cos(twist_turn).astype(np.float32)), jnp.asarray(np.sin(twist_turn).astype(np.float32))]
    tables += pair_of(np.concatenate([cos_second, -sin_second], 1))
    tables += pair_of(np.concatenate([sin_second, cos_second], 1))
    tables += pair_of(np.concatenate([cos_second, sin_second], 1))
    tables += pair_of(np.concatenate([-sin_second, cos_second], 1))
    tables += pair_of(cos_first.T / all_bins)
    tables += pair_of(-sin_first.T / all_bins)
    return tables


def local(features, pre_gate, post_gate, norm_gain, skip_weight, spectrum):
    tok_rows, chan_width = features.shape
    seq_count = lax.axis_size("seq")
    chans = lax.axis_size("chan")
    group = chan_width // seq_count
    second_len = tok_rows // ROW_GROUP
    lanes = 128
    tok_tiles = tok_rows // lanes

    spec_rows = spectrum.reshape(2, 2, second_len, ROW_GROUP, chan_width)
    spec_rows = jnp.transpose(spec_rows, (4, 0, 1, 3, 2)).astype(jnp.bfloat16)
    spec_rows = spec_rows.reshape(seq_count, -1, second_len)
    signal, result = whole(
        features, pre_gate, norm_gain.reshape(1, chan_width), spec_rows,
        dft_tables(seq_count, tok_rows), chans,
    )
    result = result.reshape(seq_count, group, tok_tiles, lanes)
    result = jnp.transpose(result, (2, 3, 0, 1)).reshape(tok_rows, chan_width)
    gated = post_gate.astype(jnp.float32) * (result + skip_weight * signal.astype(jnp.float32))
    return gated.astype(jnp.bfloat16)


def solution(mesh):
    return jax.shard_map(
        local,
        mesh=mesh,
        in_specs=(
            P("seq", "chan"),
            P("seq", "chan"),
            P("seq", "chan"),
            P("chan"),
            P("chan"),
            P(None, "seq", None, "chan"),
        ),
        out_specs=P("seq", "chan"),
        check_vma=False,
    )
```

```python
import math

import jax
import jax.numpy as jnp
import numpy as np
from jax import lax
from jax.experimental import pallas as pl
from jax.experimental.pallas import tpu as pltpu
from jax.sharding import PartitionSpec as P

CHANNELS = 512
ROW_GROUP = 4
TABLE_NAMES = ("st_hi", "st_lo", "tc", "ts", "fa_hi", "fa_lo", "fb_hi", "fb_lo", "ia_hi", "ia_lo", "ib_hi", "ib_lo",
               "lc_hi", "lc_lo", "ls_hi", "ls_lo")
HIGH_DIGIT = 8


PRECISE = lax.Precision.HIGH
FULL_TURN = 2.0 * math.pi


def reversed_digits(count):
    levels = count.bit_length() - 1
    positions = np.arange(count)
    result = np.zeros(count, np.int64)
    for bit_pos in range(levels):
        result = result + ((positions >> bit_pos & 1) << levels - 1 - bit_pos)
    return result


def rotation(numerator, denominator):
    angle = (numerator % denominator).astype(jnp.float32) * (FULL_TURN / denominator)
    return (jnp.cos(angle), jnp.sin(angle))


def mm(spec, left, right):
    return jnp.einsum(spec, left, right, precision=PRECISE, preferred_element_type=jnp.float32)


def exchange_kernel(src_ref, dst_ref, send_sem, recv_sem, own_sem):
    count = src_ref.shape[0]
    me = lax.axis_index("seq")
    mesh_ids = pl.DeviceIdType.MESH
    barrier = pltpu.get_barrier_semaphore()

    def greet(step, carry):
        peer = lax.rem(me + step, count)
        pl.semaphore_signal(barrier, inc=1, device_id={"seq": peer}, device_id_type=mesh_ids)
        return carry

    lax.fori_loop(1, count, greet, 0, unroll=True)
    pl.semaphore_wait(barrier, count - 1)
    own = pltpu.make_async_copy(src_ref.at[me], dst_ref.at[me], own_sem)
    own.start()

    def remote(step):
        peer = lax.rem(me + step, count)
        return pltpu.make_async_remote_copy(
            src_ref.at[peer],
            dst_ref.at[me],
            send_sem.at[step],
            recv_sem.at[step],
            device_id={"seq": peer},
            device_id_type=mesh_ids,
        )

    def send(step, carry):
        remote(step).start()
        return carry

    lax.fori_loop(1, count, send, 0, unroll=True)

    def finish(step, carry):
        copy = remote(step)
        copy.wait_send()
        copy.wait_recv()
        return carry

    lax.fori_loop(1, count, finish, 0, unroll=True)
    own.wait()


def exchange(blocks, tag):
    count = blocks.shape[0]
    vmem = pl.BlockSpec(memory_space=pltpu.VMEM)
    return pl.pallas_call(
        exchange_kernel,
        out_shape=jax.ShapeDtypeStruct(blocks.shape, blocks.dtype),
        in_specs=[vmem],
        out_specs=vmem,
        scratch_shapes=[
            pltpu.SemaphoreType.DMA((count,)),
            pltpu.SemaphoreType.DMA((count,)),
            pltpu.SemaphoreType.DMA,
        ],
        compiler_params=pltpu.CompilerParams(collective_id=tag, has_side_effects=True),
    )(blocks)


def front_kernel(
    feat_ref, gate_ref, gain_ref, spec_ref,
    sig_out, sig_recv, spec_recv,
    sq_mine, sq_recv, sig_turn, sig_send, spec_sems, sig_sems, chan_sems, own_sems,
):
    count = spec_ref.shape[0]
    chans = sq_recv.shape[0]
    me = lax.axis_index("seq")
    mine = lax.axis_index("chan")
    mesh_ids = pl.DeviceIdType.MESH
    barrier = pltpu.get_barrier_semaphore()

    def greet(step, carry):
        peer = lax.rem(me + step, count)
        pl.semaphore_signal(barrier, inc=1, device_id={"seq": peer}, device_id_type=mesh_ids)
        return carry

    lax.fori_loop(1, count, greet, 0, unroll=True)
    for step in range(1, chans):
        peer = lax.rem(mine + step, chans)
        pl.semaphore_signal(barrier, inc=1, device_id={"chan": peer}, device_id_type=mesh_ids)
    pl.semaphore_wait(barrier, count + chans - 2)

    def spec_copy(step):
        peer = lax.rem(me + step, count)
        return pltpu.make_async_remote_copy(
            spec_ref.at[peer],
            spec_recv.at[me],
            spec_sems.at[0, step],
            spec_sems.at[1, step],
            device_id={"seq": peer},
            device_id_type=mesh_ids,
        )

    spec_own = pltpu.make_async_copy(spec_ref.at[me], spec_recv.at[me], own_sems.at[0])
    spec_own.start()

    def spec_send(step, carry):
        spec_copy(step).start()
        return carry

    lax.fori_loop(1, count, spec_send, 0, unroll=True)

    feat = feat_ref[...].astype(jnp.float32)
    part = jnp.sum(jnp.transpose(feat * feat), axis=0, keepdims=True)
    sq_mine[...] = jnp.broadcast_to(part, sq_mine.shape)

    def chan_copy(step):
        peer = lax.rem(mine + step, chans)
        return pltpu.make_async_remote_copy(
            sq_mine,
            sq_recv.at[mine],
            chan_sems.at[0, step],
            chan_sems.at[1, step],
            device_id={"chan": peer},
            device_id_type=mesh_ids,
        )

    for step in range(1, chans):
        chan_copy(step).start()
    for step in range(1, chans):
        copy = chan_copy(step)
        copy.wait_send()
        copy.wait_recv()
    total = part
    for step in range(1, chans):
        other = lax.rem(mine + step, chans)
        total = total + sq_recv[other][0:1, :]
    scale = lax.rsqrt(total / CHANNELS + 1e-06)
    scale = jnp.transpose(jnp.broadcast_to(scale, (8, scale.shape[1])))[:, 0:1]
    signal = (feat * scale * gain_ref[...] * gate_ref[...].astype(jnp.float32)).astype(jnp.bfloat16)
    sig_out[...] = signal
    wide = signal.astype(jnp.float32)
    lanes = wide.shape[1]
    pair = lanes // count
    tiles = wide.shape[0] // lanes
    chunk = pair * tiles
    for tile in range(tiles):
        sig_turn[...] = jnp.transpose(wide[lanes * tile:lanes * (tile + 1), :])
        for chan in range(pair):
            rows = sig_turn[pl.ds(chan, count, stride=pair), :]
            sig_send[pl.ds(tiles * chan + tile, count, stride=chunk), :] = rows

    def sig_rows(peer):
        return sig_send.at[pl.ds(pl.multiple_of(peer * chunk, chunk), chunk)]

    def sig_copy(step):
        peer = lax.rem(me + step, count)
        return pltpu.make_async_remote_copy(
            sig_rows(peer),
            sig_recv.at[me],
            sig_sems.at[0, step],
            sig_sems.at[1, step],
            device_id={"seq": peer},
            device_id_type=mesh_ids,
        )

    sig_own = pltpu.make_async_copy(sig_rows(me), sig_recv.at[me], own_sems.at[1])
    sig_own.start()

    def sig_start(step, carry):
        sig_copy(step).start()
        return carry

    lax.fori_loop(1, count, sig_start, 0, unroll=True)

    def sig_finish(step, carry):
        copy = sig_copy(step)
        copy.wait_send()
        copy.wait_recv()
        return carry

    lax.fori_loop(1, count, sig_finish, 0, unroll=True)
    sig_own.wait()

    def spec_finish(step, carry):
        copy = spec_copy(step)
        copy.wait_send()
        copy.wait_recv()
        return carry

    lax.fori_loop(1, count, spec_finish, 0, unroll=True)
    spec_own.wait()


def front(feat, gate, gain_row, spec_rows, chans):
    count = spec_rows.shape[0]
    length, width = feat.shape
    pair = width // count
    vmem = pl.BlockSpec(memory_space=pltpu.VMEM)
    return pl.pallas_call(
        front_kernel,
        out_shape=(
            jax.ShapeDtypeStruct((length, width), jnp.bfloat16),
            jax.ShapeDtypeStruct((count, pair * length // 128, 128), jnp.float32),
            jax.ShapeDtypeStruct(spec_rows.shape, spec_rows.dtype),
        ),
        in_specs=[vmem] * 4,
        out_specs=(vmem, vmem, vmem),
        scratch_shapes=[
            pltpu.VMEM((8, length), jnp.float32),
            pltpu.VMEM((chans, 8, length), jnp.float32),
            pltpu.VMEM((128, 128), jnp.float32),
            pltpu.VMEM((count * pair * length // 128, 128), jnp.float32),
            pltpu.SemaphoreType.DMA((2, count)),
            pltpu.SemaphoreType.DMA((2, count)),
            pltpu.SemaphoreType.DMA((2, chans)),
            pltpu.SemaphoreType.DMA((2,)),
        ],
        compiler_params=pltpu.CompilerParams(collective_id=0, has_side_effects=True),
    )(feat, gate, gain_row, spec_rows)


def bin_rows(seq_count):
    digit_order = reversed_digits(seq_count)
    stride = 2 * seq_count
    slots = np.arange(stride)
    low_bins = 2 * digit_order[slots // 2] + slots % 2
    return (low_bins[:, None] + stride * np.arange(ROW_GROUP)[None, :]).reshape(-1).astype(np.int32)


def convolve(sig_cols, spec_chan, seq_count, tok_rows):
    group = spec_chan.shape[0]
    first_len, second_len = spec_chan.shape[2], spec_chan.shape[3]
    half_first = first_len // 2
    all_bins = first_len * second_len
    row_bins = bin_rows(seq_count).astype(np.int64)
    first_in = np.arange(half_first)
    first_turn = (row_bins[:, None] * first_in[None, :]) % first_len * (2.0 * np.pi / first_len)
    stacked_np = np.concatenate([np.cos(first_turn), np.sin(first_turn)], 0)
    stacked = jnp.asarray(stacked_np.astype(np.float32))
    signs = np.concatenate([np.ones(first_len), -np.ones(first_len)]) / all_bins
    twist_turn = (row_bins[:, None] * np.arange(second_len)[None, :]) % all_bins * (2.0 * np.pi / all_bins)
    cos_twist = jnp.asarray(np.cos(twist_turn).astype(np.float32))
    sin_twist = jnp.asarray(np.sin(twist_turn).astype(np.float32))
    second_in = jnp.arange(second_len, dtype=jnp.int32)
    cos_second, sin_second = rotation(second_in[:, None] * second_in[None, :], second_len)
    fwd_second = jnp.concatenate(
        [jnp.concatenate([cos_second, -sin_second], 1), jnp.concatenate([sin_second, cos_second], 1)], 0
    )
    inv_second = jnp.concatenate(
        [jnp.concatenate([cos_second, sin_second], 1), jnp.concatenate([-sin_second, cos_second], 1)], 0
    )
    last = stacked * jnp.asarray(signs.astype(np.float32))[:, None]

    both = mm("rn,nm->rm", stacked, sig_cols)
    along_cos, along_sin = both[:first_len], both[first_len:]
    outs_re, outs_im = [], []
    for chan in range(group):
        lanes_of = slice(chan * second_len, (chan + 1) * second_len)
        p_cos, p_sin = along_cos[:, lanes_of], along_sin[:, lanes_of]
        twist_re = p_cos * cos_twist - p_sin * sin_twist
        twist_im = -p_sin * cos_twist - p_cos * sin_twist
        freq = mm("rn,nk->rk", jnp.concatenate([twist_re, twist_im], 1), fwd_second)
        freq_re, freq_im = freq[:, :second_len], freq[:, second_len:]
        filt_re, filt_im = spec_chan[chan, 0], spec_chan[chan, 1]
        prod_re = freq_re * filt_re - freq_im * filt_im
        prod_im = freq_re * filt_im + freq_im * filt_re
        back = mm("rk,kn->rn", jnp.concatenate([prod_re, prod_im], 1), inv_second)
        back_re, back_im = back[:, :second_len], back[:, second_len:]
        outs_re.append(back_re * cos_twist - back_im * sin_twist)
        outs_im.append(back_im * cos_twist + back_re * sin_twist)
    untwisted = jnp.concatenate([jnp.concatenate(outs_re, 1), jnp.concatenate(outs_im, 1)], 0)
    return mm("rn,rm->nm", last, untwisted)


def split(value):
    high = value.astype(jnp.bfloat16)
    return high, (value - high.astype(jnp.float32)).astype(jnp.bfloat16)


def dot3(left, right):
    l_hi, l_lo = left if isinstance(left, tuple) else split(left)
    r_hi, r_lo = right if isinstance(right, tuple) else split(right)
    out = jnp.dot(l_hi, r_hi, preferred_element_type=jnp.float32)
    out = out + jnp.dot(l_hi, r_lo, preferred_element_type=jnp.float32)
    return out + jnp.dot(l_lo, r_hi, preferred_element_type=jnp.float32)


def whole_kernel(feat_ref, gate_ref, gain_ref, spec_ref, *refs):
    table_count = len(TABLE_NAMES)
    held = refs[:table_count]
    sig_out, res_recv = refs[table_count:table_count + 2]
    (sq_mine, sq_recv, sig_turn, sig_send, sig_recv, spec_recv, cols, conv_one, conv_send,
     spec_sems, sig_sems, res_sems, chan_sems, own_sems, table_sems) = refs[table_count + 2:table_count + 17]
    tables = refs[table_count + 17:]
    loads = [pltpu.make_async_copy(held[k], tables[k], table_sems.at[k]) for k in range(table_count)]
    for load in loads:
        load.start()
    (st_hi, st_lo, tc_ref, ts_ref, fa_hi, fa_lo, fb_hi, fb_lo, ia_hi, ia_lo, ib_hi, ib_lo,
     lc_hi, lc_lo, ls_hi, ls_lo) = tables
    count = spec_ref.shape[0]
    chans = sq_recv.shape[0]
    me = lax.axis_index("seq")
    mine = lax.axis_index("chan")
    mesh_ids = pl.DeviceIdType.MESH
    barrier = pltpu.get_barrier_semaphore()

    def greet(step, carry):
        peer = lax.rem(me + step, count)
        pl.semaphore_signal(barrier, inc=1, device_id={"seq": peer}, device_id_type=mesh_ids)
        return carry

    lax.fori_loop(1, count, greet, 0)
    for step in range(1, chans):
        peer = lax.rem(mine + step, chans)
        pl.semaphore_signal(barrier, inc=1, device_id={"chan": peer}, device_id_type=mesh_ids)
    pl.semaphore_wait(barrier, count + chans - 2)

    def seq_copy(source, target, sems, step):
        peer = lax.rem(me + step, count)
        return pltpu.make_async_remote_copy(
            source(peer), target, sems.at[0, step], sems.at[1, step],
            device_id={"seq": peer}, device_id_type=mesh_ids,
        )

    def start_all(source, target, sems):
        def body(step, carry):
            seq_copy(source, target, sems, step).start()
            return carry
        lax.fori_loop(1, count, body, 0)

    def finish_all(source, target, sems):
        def body(step, carry):
            copy = seq_copy(source, target, sems, step)
            copy.wait_send()
            copy.wait_recv()
            return carry
        lax.fori_loop(1, count, body, 0)

    spec_src = lambda peer: spec_ref.at[peer]
    spec_own = pltpu.make_async_copy(spec_ref.at[me], spec_recv.at[me], own_sems.at[0])
    spec_own.start()
    start_all(spec_src, spec_recv.at[me], spec_sems)

    feat = feat_ref[...].astype(jnp.float32)
    part = jnp.sum(jnp.transpose(feat * feat), axis=0, keepdims=True)
    sq_mine[...] = jnp.broadcast_to(part, sq_mine.shape)

    def chan_copy(step):
        peer = lax.rem(mine + step, chans)
        return pltpu.make_async_remote_copy(
            sq_mine, sq_recv.at[mine], chan_sems.at[0, step], chan_sems.at[1, step],
            device_id={"chan": peer}, device_id_type=mesh_ids,
        )

    for step in range(1, chans):
        chan_copy(step).start()
    for step in range(1, chans):
        copy = chan_copy(step)
        copy.wait_send()
        copy.wait_recv()
    total = part
    for step in range(1, chans):
        other = lax.rem(mine + step, chans)
        total = total + sq_recv[other][0:1, :]
    scale = lax.rsqrt(total / CHANNELS + 1e-06)
    scale = jnp.transpose(jnp.broadcast_to(scale, (8, scale.shape[1])))[:, 0:1]
    signal = (feat * scale * gain_ref[...] * gate_ref[...].astype(jnp.float32)).astype(jnp.bfloat16)
    sig_out[...] = signal
    wide = signal.astype(jnp.float32)
    lanes = wide.shape[1]
    pair = lanes // count
    tiles = wide.shape[0] // lanes
    chunk = pair * tiles
    for tile in range(tiles):
        sig_turn[...] = jnp.transpose(wide[lanes * tile:lanes * (tile + 1), :])
        for chan in range(pair):
            rows = sig_turn[pl.ds(chan, count, stride=pair), :]
            sig_send[pl.ds(tiles * chan + tile, count, stride=chunk), :] = rows

    def rows_of(buffer):
        return lambda peer: buffer.at[pl.ds(pl.multiple_of(peer * chunk, chunk), chunk)]

    sig_own = pltpu.make_async_copy(rows_of(sig_send)(me), rows_of(sig_recv)(me), own_sems.at[1])
    sig_own.start()
    start_all(rows_of(sig_send), rows_of(sig_recv)(me), sig_sems)
    finish_all(rows_of(sig_send), rows_of(sig_recv)(me), sig_sems)
    sig_own.wait()

    for chan in range(pair):
        for tile in range(tiles):
            rows = sig_recv[pl.ds(tiles * chan + tile, count, stride=chunk), :]
            cols[chan, pl.ds(tile, count, stride=tiles), :] = rows

    first_len = tc_ref.shape[0]
    for load in loads:
        load.wait()
    boths = []
    for chan in range(pair):
        signal_cols = cols[chan].astype(jnp.bfloat16)
        both = jnp.dot(st_hi[...], signal_cols, preferred_element_type=jnp.float32)
        boths.append(both + jnp.dot(st_lo[...], signal_cols, preferred_element_type=jnp.float32))

    finish_all(spec_src, spec_recv.at[me], spec_sems)
    spec_own.wait()

    cos_twist, sin_twist = tc_ref[...], ts_ref[...]
    own_rows = first_len // count
    for chan in range(pair):
        p_cos = boths[chan][:first_len]
        p_sin = boths[chan][first_len:]
        twist_re = p_cos * cos_twist - p_sin * sin_twist
        twist_im = -p_sin * cos_twist - p_cos * sin_twist
        freq = dot3(twist_re, (fa_hi[...], fa_lo[...])) + dot3(twist_im, (fb_hi[...], fb_lo[...]))
        freq_re, freq_im = freq[:, :lanes], freq[:, lanes:]
        filt = []
        for part_of in range(2):
            block = spec_recv[:, pl.ds((2 * chan + part_of) * own_rows, own_rows), :]
            filt.append(block.astype(jnp.float32).reshape(first_len, lanes))
        filt_re, filt_im = filt
        prod_re = freq_re * filt_re - freq_im * filt_im
        prod_im = freq_re * filt_im + freq_im * filt_re
        back = dot3(prod_re, (ia_hi[...], ia_lo[...])) + dot3(prod_im, (ib_hi[...], ib_lo[...]))
        back_re, back_im = back[:, :lanes], back[:, lanes:]
        untwist_re = back_re * cos_twist - back_im * sin_twist
        untwist_im = back_im * cos_twist + back_re * sin_twist
        conv_one[...] = dot3((lc_hi[...], lc_lo[...]), untwist_re) + dot3((ls_hi[...], ls_lo[...]), untwist_im)
        for tile in range(tiles):
            rows = conv_one[pl.ds(tile, count, stride=tiles), :]
            conv_send[pl.ds(tiles * chan + tile, count, stride=chunk), :] = rows

    res_src = rows_of(conv_send)
    res_own = pltpu.make_async_copy(res_src(me), res_recv.at[me], own_sems.at[2])
    res_own.start()
    start_all(res_src, res_recv.at[me], res_sems)
    finish_all(res_src, res_recv.at[me], res_sems)
    res_own.wait()


def whole(features, pre_gate, gain_row, spec_rows, tables, chans):
    count = spec_rows.shape[0]
    length, width = features.shape
    pair = width // count
    lanes = 128
    chunk = pair * length // lanes
    vmem = pl.BlockSpec(memory_space=pltpu.VMEM)
    operands = (features, pre_gate, gain_row, spec_rows) + tuple(tables)
    hbm = pl.BlockSpec(memory_space=pl.ANY)
    return pl.pallas_call(
        whole_kernel,
        out_shape=(
            jax.ShapeDtypeStruct((length, width), jnp.bfloat16),
            jax.ShapeDtypeStruct((count, chunk, lanes), jnp.float32),
        ),
        in_specs=[vmem] * 4 + [hbm] * len(tables),
        out_specs=(vmem, vmem),
        scratch_shapes=[
            pltpu.VMEM((8, length), jnp.float32),
            pltpu.VMEM((chans, 8, length), jnp.float32),
            pltpu.VMEM((lanes, lanes), jnp.float32),
            pltpu.VMEM((count * chunk, lanes), jnp.float32),
            pltpu.VMEM((count * chunk, lanes), jnp.float32),
            pltpu.VMEM(spec_rows.shape, spec_rows.dtype),
            pltpu.VMEM((pair, count * chunk // pair, lanes), jnp.float32),
            pltpu.VMEM((count * chunk // pair, lanes), jnp.float32),
            pltpu.VMEM((count * chunk, lanes), jnp.float32),
            pltpu.SemaphoreType.DMA((2, count)),
            pltpu.SemaphoreType.DMA((2, count)),
            pltpu.SemaphoreType.DMA((2, count)),
            pltpu.SemaphoreType.DMA((2, chans)),
            pltpu.SemaphoreType.DMA((3,)),
            pltpu.SemaphoreType.DMA((len(tables),)),
        ]
        + [pltpu.VMEM(table.shape, table.dtype) for table in tables],
        compiler_params=pltpu.CompilerParams(
            collective_id=0, has_side_effects=True, vmem_limit_bytes=48 * 1024 * 1024
        ),
    )(*operands)


def dft_tables(seq_count, tok_rows):
    stride = 2 * seq_count
    first_len = stride * ROW_GROUP
    all_bins = stride * tok_rows
    second_len = all_bins // first_len
    half_first = first_len // 2
    row_bins = bin_rows(seq_count).astype(np.int64)
    first_turn = (row_bins[:, None] * np.arange(half_first)[None, :]) % first_len * (2.0 * np.pi / first_len)
    cos_first, sin_first = np.cos(first_turn), np.sin(first_turn)
    twist_turn = (row_bins[:, None] * np.arange(second_len)[None, :]) % all_bins * (2.0 * np.pi / all_bins)
    second_in = np.arange(second_len)
    second_turn = (second_in[:, None] * second_in[None, :]) % second_len * (2.0 * np.pi / second_len)
    cos_second, sin_second = np.cos(second_turn), np.sin(second_turn)

    def pair_of(array):
        array = array.astype(np.float32)
        high = array.astype(jnp.bfloat16)
        return [jnp.asarray(high), jnp.asarray((array - high.astype(np.float32)).astype(jnp.bfloat16))]

    tables = pair_of(np.concatenate([cos_first, sin_first], 0))
    tables += [jnp.asarray(np.cos(twist_turn).astype(np.float32)), jnp.asarray(np.sin(twist_turn).astype(np.float32))]
    tables += pair_of(np.concatenate([cos_second, -sin_second], 1))
    tables += pair_of(np.concatenate([sin_second, cos_second], 1))
    tables += pair_of(np.concatenate([cos_second, sin_second], 1))
    tables += pair_of(np.concatenate([-sin_second, cos_second], 1))
    tables += pair_of(cos_first.T / all_bins)
    tables += pair_of(-sin_first.T / all_bins)
    return tables


def local(features, pre_gate, post_gate, norm_gain, skip_weight, spectrum):
    tok_rows, chan_width = features.shape
    seq_count = lax.axis_size("seq")
    chans = lax.axis_size("chan")
    group = chan_width // seq_count
    second_len = tok_rows // ROW_GROUP
    lanes = 128
    tok_tiles = tok_rows // lanes

    spec_rows = spectrum.reshape(2, 2, second_len, ROW_GROUP, chan_width)
    spec_rows = jnp.transpose(spec_rows, (4, 0, 1, 3, 2)).astype(jnp.bfloat16)
    spec_rows = spec_rows.reshape(seq_count, -1, second_len)
    signal, result = whole(
        features, pre_gate, norm_gain.reshape(1, chan_width), spec_rows,
        dft_tables(seq_count, tok_rows), chans,
    )
    result = result.reshape(seq_count, group, tok_tiles, lanes)
    result = jnp.transpose(result, (2, 3, 0, 1)).reshape(tok_rows, chan_width)
    gated = post_gate.astype(jnp.float32) * (result + skip_weight * signal.astype(jnp.float32))
    return gated.astype(jnp.bfloat16)


def solution(mesh):
    return jax.shard_map(
        local,
        mesh=mesh,
        in_specs=(
            P("seq", "chan"),
            P("seq", "chan"),
            P("seq", "chan"),
            P("chan"),
            P("chan"),
            P(None, "seq", None, "chan"),
        ),
        out_specs=P("seq", "chan"),
        check_vma=False,
    )
```

```python
import math

import jax
import jax.numpy as jnp
import numpy as np
from jax import lax
from jax.experimental import pallas as pl
from jax.experimental.pallas import tpu as pltpu
from jax.sharding import PartitionSpec as P

CHANNELS = 512
ROW_GROUP = 4
TABLE_NAMES = ("st_hi", "st_lo", "tc", "ts", "fa_hi", "fa_lo", "fb_hi", "fb_lo", "ia_hi", "ia_lo", "ib_hi", "ib_lo",
               "lc_hi", "lc_lo", "ls_hi", "ls_lo")
HIGH_DIGIT = 8


PRECISE = lax.Precision.HIGH
FULL_TURN = 2.0 * math.pi


def reversed_digits(count):
    levels = count.bit_length() - 1
    positions = np.arange(count)
    result = np.zeros(count, np.int64)
    for bit_pos in range(levels):
        result = result + ((positions >> bit_pos & 1) << levels - 1 - bit_pos)
    return result


def rotation(numerator, denominator):
    angle = (numerator % denominator).astype(jnp.float32) * (FULL_TURN / denominator)
    return (jnp.cos(angle), jnp.sin(angle))


def mm(spec, left, right):
    return jnp.einsum(spec, left, right, precision=PRECISE, preferred_element_type=jnp.float32)


def exchange_kernel(src_ref, dst_ref, send_sem, recv_sem, own_sem):
    count = src_ref.shape[0]
    me = lax.axis_index("seq")
    mesh_ids = pl.DeviceIdType.MESH
    barrier = pltpu.get_barrier_semaphore()

    def greet(step, carry):
        peer = lax.rem(me + step, count)
        pl.semaphore_signal(barrier, inc=1, device_id={"seq": peer}, device_id_type=mesh_ids)
        return carry

    lax.fori_loop(1, count, greet, 0, unroll=True)
    pl.semaphore_wait(barrier, count - 1)
    own = pltpu.make_async_copy(src_ref.at[me], dst_ref.at[me], own_sem)
    own.start()

    def remote(step):
        peer = lax.rem(me + step, count)
        return pltpu.make_async_remote_copy(
            src_ref.at[peer],
            dst_ref.at[me],
            send_sem.at[step],
            recv_sem.at[step],
            device_id={"seq": peer},
            device_id_type=mesh_ids,
        )

    def send(step, carry):
        remote(step).start()
        return carry

    lax.fori_loop(1, count, send, 0, unroll=True)

    def finish(step, carry):
        copy = remote(step)
        copy.wait_send()
        copy.wait_recv()
        return carry

    lax.fori_loop(1, count, finish, 0, unroll=True)
    own.wait()


def exchange(blocks, tag):
    count = blocks.shape[0]
    vmem = pl.BlockSpec(memory_space=pltpu.VMEM)
    return pl.pallas_call(
        exchange_kernel,
        out_shape=jax.ShapeDtypeStruct(blocks.shape, blocks.dtype),
        in_specs=[vmem],
        out_specs=vmem,
        scratch_shapes=[
            pltpu.SemaphoreType.DMA((count,)),
            pltpu.SemaphoreType.DMA((count,)),
            pltpu.SemaphoreType.DMA,
        ],
        compiler_params=pltpu.CompilerParams(collective_id=tag, has_side_effects=True),
    )(blocks)


def front_kernel(
    feat_ref, gate_ref, gain_ref, spec_ref,
    sig_out, sig_recv, spec_recv,
    sq_mine, sq_recv, sig_turn, sig_send, spec_sems, sig_sems, chan_sems, own_sems,
):
    count = spec_ref.shape[0]
    chans = sq_recv.shape[0]
    me = lax.axis_index("seq")
    mine = lax.axis_index("chan")
    mesh_ids = pl.DeviceIdType.MESH
    barrier = pltpu.get_barrier_semaphore()

    def greet(step, carry):
        peer = lax.rem(me + step, count)
        pl.semaphore_signal(barrier, inc=1, device_id={"seq": peer}, device_id_type=mesh_ids)
        return carry

    lax.fori_loop(1, count, greet, 0, unroll=True)
    for step in range(1, chans):
        peer = lax.rem(mine + step, chans)
        pl.semaphore_signal(barrier, inc=1, device_id={"chan": peer}, device_id_type=mesh_ids)
    pl.semaphore_wait(barrier, count + chans - 2)

    def spec_copy(step):
        peer = lax.rem(me + step, count)
        return pltpu.make_async_remote_copy(
            spec_ref.at[peer],
            spec_recv.at[me],
            spec_sems.at[0, step],
            spec_sems.at[1, step],
            device_id={"seq": peer},
            device_id_type=mesh_ids,
        )

    spec_own = pltpu.make_async_copy(spec_ref.at[me], spec_recv.at[me], own_sems.at[0])
    spec_own.start()

    def spec_send(step, carry):
        spec_copy(step).start()
        return carry

    lax.fori_loop(1, count, spec_send, 0, unroll=True)

    feat = feat_ref[...].astype(jnp.float32)
    part = jnp.sum(jnp.transpose(feat * feat), axis=0, keepdims=True)
    sq_mine[...] = jnp.broadcast_to(part, sq_mine.shape)

    def chan_copy(step):
        peer = lax.rem(mine + step, chans)
        return pltpu.make_async_remote_copy(
            sq_mine,
            sq_recv.at[mine],
            chan_sems.at[0, step],
            chan_sems.at[1, step],
            device_id={"chan": peer},
            device_id_type=mesh_ids,
        )

    for step in range(1, chans):
        chan_copy(step).start()
    for step in range(1, chans):
        copy = chan_copy(step)
        copy.wait_send()
        copy.wait_recv()
    total = part
    for step in range(1, chans):
        other = lax.rem(mine + step, chans)
        total = total + sq_recv[other][0:1, :]
    scale = lax.rsqrt(total / CHANNELS + 1e-06)
    scale = jnp.transpose(jnp.broadcast_to(scale, (8, scale.shape[1])))[:, 0:1]
    signal = (feat * scale * gain_ref[...] * gate_ref[...].astype(jnp.float32)).astype(jnp.bfloat16)
    sig_out[...] = signal
    wide = signal.astype(jnp.float32)
    lanes = wide.shape[1]
    pair = lanes // count
    tiles = wide.shape[0] // lanes
    chunk = pair * tiles
    for tile in range(tiles):
        sig_turn[...] = jnp.transpose(wide[lanes * tile:lanes * (tile + 1), :])
        for chan in range(pair):
            rows = sig_turn[pl.ds(chan, count, stride=pair), :]
            sig_send[pl.ds(tiles * chan + tile, count, stride=chunk), :] = rows

    def sig_rows(peer):
        return sig_send.at[pl.ds(pl.multiple_of(peer * chunk, chunk), chunk)]

    def sig_copy(step):
        peer = lax.rem(me + step, count)
        return pltpu.make_async_remote_copy(
            sig_rows(peer),
            sig_recv.at[me],
            sig_sems.at[0, step],
            sig_sems.at[1, step],
            device_id={"seq": peer},
            device_id_type=mesh_ids,
        )

    sig_own = pltpu.make_async_copy(sig_rows(me), sig_recv.at[me], own_sems.at[1])
    sig_own.start()

    def sig_start(step, carry):
        sig_copy(step).start()
        return carry

    lax.fori_loop(1, count, sig_start, 0, unroll=True)

    def sig_finish(step, carry):
        copy = sig_copy(step)
        copy.wait_send()
        copy.wait_recv()
        return carry

    lax.fori_loop(1, count, sig_finish, 0, unroll=True)
    sig_own.wait()

    def spec_finish(step, carry):
        copy = spec_copy(step)
        copy.wait_send()
        copy.wait_recv()
        return carry

    lax.fori_loop(1, count, spec_finish, 0, unroll=True)
    spec_own.wait()


def front(feat, gate, gain_row, spec_rows, chans):
    count = spec_rows.shape[0]
    length, width = feat.shape
    pair = width // count
    vmem = pl.BlockSpec(memory_space=pltpu.VMEM)
    return pl.pallas_call(
        front_kernel,
        out_shape=(
            jax.ShapeDtypeStruct((length, width), jnp.bfloat16),
            jax.ShapeDtypeStruct((count, pair * length // 128, 128), jnp.float32),
            jax.ShapeDtypeStruct(spec_rows.shape, spec_rows.dtype),
        ),
        in_specs=[vmem] * 4,
        out_specs=(vmem, vmem, vmem),
        scratch_shapes=[
            pltpu.VMEM((8, length), jnp.float32),
            pltpu.VMEM((chans, 8, length), jnp.float32),
            pltpu.VMEM((128, 128), jnp.float32),
            pltpu.VMEM((count * pair * length // 128, 128), jnp.float32),
            pltpu.SemaphoreType.DMA((2, count)),
            pltpu.SemaphoreType.DMA((2, count)),
            pltpu.SemaphoreType.DMA((2, chans)),
            pltpu.SemaphoreType.DMA((2,)),
        ],
        compiler_params=pltpu.CompilerParams(collective_id=0, has_side_effects=True),
    )(feat, gate, gain_row, spec_rows)


def bin_rows(seq_count):
    digit_order = reversed_digits(seq_count)
    stride = 2 * seq_count
    slots = np.arange(stride)
    low_bins = 2 * digit_order[slots // 2] + slots % 2
    return (low_bins[:, None] + stride * np.arange(ROW_GROUP)[None, :]).reshape(-1).astype(np.int32)


def convolve(sig_cols, spec_chan, seq_count, tok_rows):
    group = spec_chan.shape[0]
    first_len, second_len = spec_chan.shape[2], spec_chan.shape[3]
    half_first = first_len // 2
    all_bins = first_len * second_len
    row_bins = bin_rows(seq_count).astype(np.int64)
    first_in = np.arange(half_first)
    first_turn = (row_bins[:, None] * first_in[None, :]) % first_len * (2.0 * np.pi / first_len)
    stacked_np = np.concatenate([np.cos(first_turn), np.sin(first_turn)], 0)
    stacked = jnp.asarray(stacked_np.astype(np.float32))
    signs = np.concatenate([np.ones(first_len), -np.ones(first_len)]) / all_bins
    twist_turn = (row_bins[:, None] * np.arange(second_len)[None, :]) % all_bins * (2.0 * np.pi / all_bins)
    cos_twist = jnp.asarray(np.cos(twist_turn).astype(np.float32))
    sin_twist = jnp.asarray(np.sin(twist_turn).astype(np.float32))
    second_in = jnp.arange(second_len, dtype=jnp.int32)
    cos_second, sin_second = rotation(second_in[:, None] * second_in[None, :], second_len)
    fwd_second = jnp.concatenate(
        [jnp.concatenate([cos_second, -sin_second], 1), jnp.concatenate([sin_second, cos_second], 1)], 0
    )
    inv_second = jnp.concatenate(
        [jnp.concatenate([cos_second, sin_second], 1), jnp.concatenate([-sin_second, cos_second], 1)], 0
    )
    last = stacked * jnp.asarray(signs.astype(np.float32))[:, None]

    both = mm("rn,nm->rm", stacked, sig_cols)
    along_cos, along_sin = both[:first_len], both[first_len:]
    outs_re, outs_im = [], []
    for chan in range(group):
        lanes_of = slice(chan * second_len, (chan + 1) * second_len)
        p_cos, p_sin = along_cos[:, lanes_of], along_sin[:, lanes_of]
        twist_re = p_cos * cos_twist - p_sin * sin_twist
        twist_im = -p_sin * cos_twist - p_cos * sin_twist
        freq = mm("rn,nk->rk", jnp.concatenate([twist_re, twist_im], 1), fwd_second)
        freq_re, freq_im = freq[:, :second_len], freq[:, second_len:]
        filt_re, filt_im = spec_chan[chan, 0], spec_chan[chan, 1]
        prod_re = freq_re * filt_re - freq_im * filt_im
        prod_im = freq_re * filt_im + freq_im * filt_re
        back = mm("rk,kn->rn", jnp.concatenate([prod_re, prod_im], 1), inv_second)
        back_re, back_im = back[:, :second_len], back[:, second_len:]
        outs_re.append(back_re * cos_twist - back_im * sin_twist)
        outs_im.append(back_im * cos_twist + back_re * sin_twist)
    untwisted = jnp.concatenate([jnp.concatenate(outs_re, 1), jnp.concatenate(outs_im, 1)], 0)
    return mm("rn,rm->nm", last, untwisted)


def split(value):
    high = value.astype(jnp.bfloat16)
    return high, (value - high.astype(jnp.float32)).astype(jnp.bfloat16)


def dot3(left, right):
    l_hi, l_lo = left if isinstance(left, tuple) else split(left)
    r_hi, r_lo = right if isinstance(right, tuple) else split(right)
    out = jnp.dot(l_hi, r_hi, preferred_element_type=jnp.float32)
    out = out + jnp.dot(l_hi, r_lo, preferred_element_type=jnp.float32)
    return out + jnp.dot(l_lo, r_hi, preferred_element_type=jnp.float32)


def whole_kernel(*refs):
    table_count = len(TABLE_NAMES) + 4
    held = refs[:table_count]
    sig_out, res_recv = refs[table_count:table_count + 2]
    (sq_mine, sq_recv, sig_turn, sig_send, sig_recv, spec_recv, cols, conv_one, conv_send,
     spec_sems, sig_sems, res_sems, chan_sems, own_sems, table_sems) = refs[table_count + 2:table_count + 17]
    tables = refs[table_count + 17:]
    loads = [pltpu.make_async_copy(held[k], tables[k], table_sems.at[k]) for k in range(table_count)]
    for load in loads:
        load.start()
    for load in loads[:4]:
        load.wait()
    loads = loads[4:]
    feat_ref, gate_ref, gain_ref, spec_ref = tables[:4]
    tables = tables[4:]
    (st_hi, st_lo, tc_ref, ts_ref, fa_hi, fa_lo, fb_hi, fb_lo, ia_hi, ia_lo, ib_hi, ib_lo,
     lc_hi, lc_lo, ls_hi, ls_lo) = tables
    count = spec_ref.shape[0]
    chans = sq_recv.shape[0]
    me = lax.axis_index("seq")
    mine = lax.axis_index("chan")
    mesh_ids = pl.DeviceIdType.MESH
    barrier = pltpu.get_barrier_semaphore()

    def greet(step, carry):
        peer = lax.rem(me + step, count)
        pl.semaphore_signal(barrier, inc=1, device_id={"seq": peer}, device_id_type=mesh_ids)
        return carry

    lax.fori_loop(1, count, greet, 0)
    for step in range(1, chans):
        peer = lax.rem(mine + step, chans)
        pl.semaphore_signal(barrier, inc=1, device_id={"chan": peer}, device_id_type=mesh_ids)
    pl.semaphore_wait(barrier, count + chans - 2)

    def seq_copy(source, target, sems, step):
        peer = lax.rem(me + step, count)
        return pltpu.make_async_remote_copy(
            source(peer), target, sems.at[0, step], sems.at[1, step],
            device_id={"seq": peer}, device_id_type=mesh_ids,
        )

    def start_all(source, target, sems):
        def body(step, carry):
            seq_copy(source, target, sems, step).start()
            return carry
        lax.fori_loop(1, count, body, 0)

    def finish_all(source, target, sems):
        def body(step, carry):
            copy = seq_copy(source, target, sems, step)
            copy.wait_send()
            copy.wait_recv()
            return carry
        lax.fori_loop(1, count, body, 0)

    spec_src = lambda peer: spec_ref.at[peer]
    spec_own = pltpu.make_async_copy(spec_ref.at[me], spec_recv.at[me], own_sems.at[0])
    spec_own.start()
    start_all(spec_src, spec_recv.at[me], spec_sems)

    feat = feat_ref[...].astype(jnp.float32)
    part = jnp.sum(jnp.transpose(feat * feat), axis=0, keepdims=True)
    sq_mine[...] = jnp.broadcast_to(part, sq_mine.shape)

    def chan_copy(step):
        peer = lax.rem(mine + step, chans)
        return pltpu.make_async_remote_copy(
            sq_mine, sq_recv.at[mine], chan_sems.at[0, step], chan_sems.at[1, step],
            device_id={"chan": peer}, device_id_type=mesh_ids,
        )

    for step in range(1, chans):
        chan_copy(step).start()
    for step in range(1, chans):
        copy = chan_copy(step)
        copy.wait_send()
        copy.wait_recv()
    total = part
    for step in range(1, chans):
        other = lax.rem(mine + step, chans)
        total = total + sq_recv[other][0:1, :]
    scale = lax.rsqrt(total / CHANNELS + 1e-06)
    scale = jnp.transpose(jnp.broadcast_to(scale, (8, scale.shape[1])))[:, 0:1]
    signal = (feat * scale * gain_ref[...] * gate_ref[...].astype(jnp.float32)).astype(jnp.bfloat16)
    sig_out[...] = signal
    wide = signal.astype(jnp.float32)
    lanes = wide.shape[1]
    pair = lanes // count
    tiles = wide.shape[0] // lanes
    chunk = pair * tiles
    for tile in range(tiles):
        sig_turn[...] = jnp.transpose(wide[lanes * tile:lanes * (tile + 1), :])
        for chan in range(pair):
            rows = sig_turn[pl.ds(chan, count, stride=pair), :]
            sig_send[pl.ds(tiles * chan + tile, count, stride=chunk), :] = rows

    def rows_of(buffer):
        return lambda peer: buffer.at[pl.ds(pl.multiple_of(peer * chunk, chunk), chunk)]

    sig_own = pltpu.make_async_copy(rows_of(sig_send)(me), rows_of(sig_recv)(me), own_sems.at[1])
    sig_own.start()
    start_all(rows_of(sig_send), rows_of(sig_recv)(me), sig_sems)
    finish_all(rows_of(sig_send), rows_of(sig_recv)(me), sig_sems)
    sig_own.wait()

    for chan in range(pair):
        for tile in range(tiles):
            rows = sig_recv[pl.ds(tiles * chan + tile, count, stride=chunk), :]
            cols[chan, pl.ds(tile, count, stride=tiles), :] = rows

    first_len = tc_ref.shape[0]
    for load in loads:
        load.wait()
    boths = []
    for chan in range(pair):
        signal_cols = cols[chan].astype(jnp.bfloat16)
        both = jnp.dot(st_hi[...], signal_cols, preferred_element_type=jnp.float32)
        boths.append(both + jnp.dot(st_lo[...], signal_cols, preferred_element_type=jnp.float32))

    finish_all(spec_src, spec_recv.at[me], spec_sems)
    spec_own.wait()

    cos_twist, sin_twist = tc_ref[...], ts_ref[...]
    own_rows = first_len // count
    for chan in range(pair):
        p_cos = boths[chan][:first_len]
        p_sin = boths[chan][first_len:]
        twist_re = p_cos * cos_twist - p_sin * sin_twist
        twist_im = -p_sin * cos_twist - p_cos * sin_twist
        freq = dot3(twist_re, (fa_hi[...], fa_lo[...])) + dot3(twist_im, (fb_hi[...], fb_lo[...]))
        freq_re, freq_im = freq[:, :lanes], freq[:, lanes:]
        filt = []
        for part_of in range(2):
            block = spec_recv[:, pl.ds((2 * chan + part_of) * own_rows, own_rows), :]
            filt.append(block.astype(jnp.float32).reshape(first_len, lanes))
        filt_re, filt_im = filt
        prod_re = freq_re * filt_re - freq_im * filt_im
        prod_im = freq_re * filt_im + freq_im * filt_re
        back = dot3(prod_re, (ia_hi[...], ia_lo[...])) + dot3(prod_im, (ib_hi[...], ib_lo[...]))
        back_re, back_im = back[:, :lanes], back[:, lanes:]
        untwist_re = back_re * cos_twist - back_im * sin_twist
        untwist_im = back_im * cos_twist + back_re * sin_twist
        conv_one[...] = dot3((lc_hi[...], lc_lo[...]), untwist_re) + dot3((ls_hi[...], ls_lo[...]), untwist_im)
        for tile in range(tiles):
            rows = conv_one[pl.ds(tile, count, stride=tiles), :]
            conv_send[pl.ds(tiles * chan + tile, count, stride=chunk), :] = rows

    res_src = rows_of(conv_send)
    res_own = pltpu.make_async_copy(res_src(me), res_recv.at[me], own_sems.at[2])
    res_own.start()
    start_all(res_src, res_recv.at[me], res_sems)
    finish_all(res_src, res_recv.at[me], res_sems)
    res_own.wait()


def whole(features, pre_gate, gain_row, spec_rows, tables, chans):
    count = spec_rows.shape[0]
    length, width = features.shape
    pair = width // count
    lanes = 128
    chunk = pair * length // lanes
    vmem = pl.BlockSpec(memory_space=pltpu.VMEM)
    operands = (features, pre_gate, gain_row, spec_rows) + tuple(tables)
    hbm = pl.BlockSpec(memory_space=pl.ANY)
    return pl.pallas_call(
        whole_kernel,
        out_shape=(
            jax.ShapeDtypeStruct((length, width), jnp.bfloat16),
            jax.ShapeDtypeStruct((count, chunk, lanes), jnp.float32),
        ),
        in_specs=[hbm] * len(operands),
        out_specs=(vmem, vmem),
        scratch_shapes=[
            pltpu.VMEM((8, length), jnp.float32),
            pltpu.VMEM((chans, 8, length), jnp.float32),
            pltpu.VMEM((lanes, lanes), jnp.float32),
            pltpu.VMEM((count * chunk, lanes), jnp.float32),
            pltpu.VMEM((count * chunk, lanes), jnp.float32),
            pltpu.VMEM(spec_rows.shape, spec_rows.dtype),
            pltpu.VMEM((pair, count * chunk // pair, lanes), jnp.float32),
            pltpu.VMEM((count * chunk // pair, lanes), jnp.float32),
            pltpu.VMEM((count * chunk, lanes), jnp.float32),
            pltpu.SemaphoreType.DMA((2, count)),
            pltpu.SemaphoreType.DMA((2, count)),
            pltpu.SemaphoreType.DMA((2, count)),
            pltpu.SemaphoreType.DMA((2, chans)),
            pltpu.SemaphoreType.DMA((3,)),
            pltpu.SemaphoreType.DMA((len(operands),)),
        ]
        + [pltpu.VMEM(table.shape, table.dtype) for table in operands],
        compiler_params=pltpu.CompilerParams(
            collective_id=0, has_side_effects=True, vmem_limit_bytes=67043328
        ),
    )(*operands)


def dft_tables(seq_count, tok_rows):
    stride = 2 * seq_count
    first_len = stride * ROW_GROUP
    all_bins = stride * tok_rows
    second_len = all_bins // first_len
    half_first = first_len // 2
    row_bins = bin_rows(seq_count).astype(np.int64)
    first_turn = (row_bins[:, None] * np.arange(half_first)[None, :]) % first_len * (2.0 * np.pi / first_len)
    cos_first, sin_first = np.cos(first_turn), np.sin(first_turn)
    twist_turn = (row_bins[:, None] * np.arange(second_len)[None, :]) % all_bins * (2.0 * np.pi / all_bins)
    second_in = np.arange(second_len)
    second_turn = (second_in[:, None] * second_in[None, :]) % second_len * (2.0 * np.pi / second_len)
    cos_second, sin_second = np.cos(second_turn), np.sin(second_turn)

    def pair_of(array):
        array = array.astype(np.float32)
        high = array.astype(jnp.bfloat16)
        return [jnp.asarray(high), jnp.asarray((array - high.astype(np.float32)).astype(jnp.bfloat16))]

    tables = pair_of(np.concatenate([cos_first, sin_first], 0))
    tables += [jnp.asarray(np.cos(twist_turn).astype(np.float32)), jnp.asarray(np.sin(twist_turn).astype(np.float32))]
    tables += pair_of(np.concatenate([cos_second, -sin_second], 1))
    tables += pair_of(np.concatenate([sin_second, cos_second], 1))
    tables += pair_of(np.concatenate([cos_second, sin_second], 1))
    tables += pair_of(np.concatenate([-sin_second, cos_second], 1))
    tables += pair_of(cos_first.T / all_bins)
    tables += pair_of(-sin_first.T / all_bins)
    return tables


def local(features, pre_gate, post_gate, norm_gain, skip_weight, spectrum):
    tok_rows, chan_width = features.shape
    seq_count = lax.axis_size("seq")
    chans = lax.axis_size("chan")
    group = chan_width // seq_count
    second_len = tok_rows // ROW_GROUP
    lanes = 128
    tok_tiles = tok_rows // lanes

    spec_rows = spectrum.reshape(2, 2, second_len, ROW_GROUP, chan_width)
    spec_rows = jnp.transpose(spec_rows, (4, 0, 1, 3, 2)).astype(jnp.bfloat16)
    spec_rows = spec_rows.reshape(seq_count, -1, second_len)
    signal, result = whole(
        features, pre_gate, norm_gain.reshape(1, chan_width), spec_rows,
        dft_tables(seq_count, tok_rows), chans,
    )
    result = result.reshape(seq_count, group, tok_tiles, lanes)
    result = jnp.transpose(result, (2, 3, 0, 1)).reshape(tok_rows, chan_width)
    gated = post_gate.astype(jnp.float32) * (result + skip_weight * signal.astype(jnp.float32))
    return gated.astype(jnp.bfloat16)


def solution(mesh):
    return jax.shard_map(
        local,
        mesh=mesh,
        in_specs=(
            P("seq", "chan"),
            P("seq", "chan"),
            P("seq", "chan"),
            P("chan"),
            P("chan"),
            P(None, "seq", None, "chan"),
        ),
        out_specs=P("seq", "chan"),
        check_vma=False,
    )
```

```python
import math

import jax
import jax.numpy as jnp
import numpy as np
from jax import lax
from jax.experimental import pallas as pl
from jax.experimental.pallas import tpu as pltpu
from jax.sharding import PartitionSpec as P

CHANNELS = 512
ROW_GROUP = 4
TABLE_NAMES = ("st_hi", "st_lo", "tc", "ts", "fa_hi", "fa_lo", "fb_hi", "fb_lo", "ia_hi", "ia_lo", "ib_hi", "ib_lo",
               "lc_hi", "lc_lo", "ls_hi", "ls_lo")
HIGH_DIGIT = 8


PRECISE = lax.Precision.HIGH
FULL_TURN = 2.0 * math.pi


def reversed_digits(count):
    levels = count.bit_length() - 1
    positions = np.arange(count)
    result = np.zeros(count, np.int64)
    for bit_pos in range(levels):
        result = result + ((positions >> bit_pos & 1) << levels - 1 - bit_pos)
    return result


def rotation(numerator, denominator):
    angle = (numerator % denominator).astype(jnp.float32) * (FULL_TURN / denominator)
    return (jnp.cos(angle), jnp.sin(angle))


def mm(spec, left, right):
    return jnp.einsum(spec, left, right, precision=PRECISE, preferred_element_type=jnp.float32)


def exchange_kernel(src_ref, dst_ref, send_sem, recv_sem, own_sem):
    count = src_ref.shape[0]
    me = lax.axis_index("seq")
    mesh_ids = pl.DeviceIdType.MESH
    barrier = pltpu.get_barrier_semaphore()

    def greet(step, carry):
        peer = lax.rem(me + step, count)
        pl.semaphore_signal(barrier, inc=1, device_id={"seq": peer}, device_id_type=mesh_ids)
        return carry

    lax.fori_loop(1, count, greet, 0, unroll=True)
    pl.semaphore_wait(barrier, count - 1)
    own = pltpu.make_async_copy(src_ref.at[me], dst_ref.at[me], own_sem)
    own.start()

    def remote(step):
        peer = lax.rem(me + step, count)
        return pltpu.make_async_remote_copy(
            src_ref.at[peer],
            dst_ref.at[me],
            send_sem.at[step],
            recv_sem.at[step],
            device_id={"seq": peer},
            device_id_type=mesh_ids,
        )

    def send(step, carry):
        remote(step).start()
        return carry

    lax.fori_loop(1, count, send, 0, unroll=True)

    def finish(step, carry):
        copy = remote(step)
        copy.wait_send()
        copy.wait_recv()
        return carry

    lax.fori_loop(1, count, finish, 0, unroll=True)
    own.wait()


def exchange(blocks, tag):
    count = blocks.shape[0]
    vmem = pl.BlockSpec(memory_space=pltpu.VMEM)
    return pl.pallas_call(
        exchange_kernel,
        out_shape=jax.ShapeDtypeStruct(blocks.shape, blocks.dtype),
        in_specs=[vmem],
        out_specs=vmem,
        scratch_shapes=[
            pltpu.SemaphoreType.DMA((count,)),
            pltpu.SemaphoreType.DMA((count,)),
            pltpu.SemaphoreType.DMA,
        ],
        compiler_params=pltpu.CompilerParams(collective_id=tag, has_side_effects=True),
    )(blocks)


def front_kernel(
    feat_ref, gate_ref, gain_ref, spec_ref,
    sig_out, sig_recv, spec_recv,
    sq_mine, sq_recv, sig_turn, sig_send, spec_sems, sig_sems, chan_sems, own_sems,
):
    count = spec_ref.shape[0]
    chans = sq_recv.shape[0]
    me = lax.axis_index("seq")
    mine = lax.axis_index("chan")
    mesh_ids = pl.DeviceIdType.MESH
    barrier = pltpu.get_barrier_semaphore()

    def greet(step, carry):
        peer = lax.rem(me + step, count)
        pl.semaphore_signal(barrier, inc=1, device_id={"seq": peer}, device_id_type=mesh_ids)
        return carry

    lax.fori_loop(1, count, greet, 0, unroll=True)
    for step in range(1, chans):
        peer = lax.rem(mine + step, chans)
        pl.semaphore_signal(barrier, inc=1, device_id={"chan": peer}, device_id_type=mesh_ids)
    pl.semaphore_wait(barrier, count + chans - 2)

    def spec_copy(step):
        peer = lax.rem(me + step, count)
        return pltpu.make_async_remote_copy(
            spec_ref.at[peer],
            spec_recv.at[me],
            spec_sems.at[0, step],
            spec_sems.at[1, step],
            device_id={"seq": peer},
            device_id_type=mesh_ids,
        )

    spec_own = pltpu.make_async_copy(spec_ref.at[me], spec_recv.at[me], own_sems.at[0])
    spec_own.start()

    def spec_send(step, carry):
        spec_copy(step).start()
        return carry

    lax.fori_loop(1, count, spec_send, 0, unroll=True)

    feat = feat_ref[...].astype(jnp.float32)
    part = jnp.sum(jnp.transpose(feat * feat), axis=0, keepdims=True)
    sq_mine[...] = jnp.broadcast_to(part, sq_mine.shape)

    def chan_copy(step):
        peer = lax.rem(mine + step, chans)
        return pltpu.make_async_remote_copy(
            sq_mine,
            sq_recv.at[mine],
            chan_sems.at[0, step],
            chan_sems.at[1, step],
            device_id={"chan": peer},
            device_id_type=mesh_ids,
        )

    for step in range(1, chans):
        chan_copy(step).start()
    for step in range(1, chans):
        copy = chan_copy(step)
        copy.wait_send()
        copy.wait_recv()
    total = part
    for step in range(1, chans):
        other = lax.rem(mine + step, chans)
        total = total + sq_recv[other][0:1, :]
    scale = lax.rsqrt(total / CHANNELS + 1e-06)
    scale = jnp.transpose(jnp.broadcast_to(scale, (8, scale.shape[1])))[:, 0:1]
    signal = (feat * scale * gain_ref[...] * gate_ref[...].astype(jnp.float32)).astype(jnp.bfloat16)
    sig_out[...] = signal
    wide = signal.astype(jnp.float32)
    lanes = wide.shape[1]
    pair = lanes // count
    tiles = wide.shape[0] // lanes
    chunk = pair * tiles
    for tile in range(tiles):
        sig_turn[...] = jnp.transpose(wide[lanes * tile:lanes * (tile + 1), :])
        for chan in range(pair):
            rows = sig_turn[pl.ds(chan, count, stride=pair), :]
            sig_send[pl.ds(tiles * chan + tile, count, stride=chunk), :] = rows

    def sig_rows(peer):
        return sig_send.at[pl.ds(pl.multiple_of(peer * chunk, chunk), chunk)]

    def sig_copy(step):
        peer = lax.rem(me + step, count)
        return pltpu.make_async_remote_copy(
            sig_rows(peer),
            sig_recv.at[me],
            sig_sems.at[0, step],
            sig_sems.at[1, step],
            device_id={"seq": peer},
            device_id_type=mesh_ids,
        )

    sig_own = pltpu.make_async_copy(sig_rows(me), sig_recv.at[me], own_sems.at[1])
    sig_own.start()

    def sig_start(step, carry):
        sig_copy(step).start()
        return carry

    lax.fori_loop(1, count, sig_start, 0, unroll=True)

    def sig_finish(step, carry):
        copy = sig_copy(step)
        copy.wait_send()
        copy.wait_recv()
        return carry

    lax.fori_loop(1, count, sig_finish, 0, unroll=True)
    sig_own.wait()

    def spec_finish(step, carry):
        copy = spec_copy(step)
        copy.wait_send()
        copy.wait_recv()
        return carry

    lax.fori_loop(1, count, spec_finish, 0, unroll=True)
    spec_own.wait()


def front(feat, gate, gain_row, spec_rows, chans):
    count = spec_rows.shape[0]
    length, width = feat.shape
    pair = width // count
    vmem = pl.BlockSpec(memory_space=pltpu.VMEM)
    return pl.pallas_call(
        front_kernel,
        out_shape=(
            jax.ShapeDtypeStruct((length, width), jnp.bfloat16),
            jax.ShapeDtypeStruct((count, pair * length // 128, 128), jnp.float32),
            jax.ShapeDtypeStruct(spec_rows.shape, spec_rows.dtype),
        ),
        in_specs=[vmem] * 4,
        out_specs=(vmem, vmem, vmem),
        scratch_shapes=[
            pltpu.VMEM((8, length), jnp.float32),
            pltpu.VMEM((chans, 8, length), jnp.float32),
            pltpu.VMEM((128, 128), jnp.float32),
            pltpu.VMEM((count * pair * length // 128, 128), jnp.float32),
            pltpu.SemaphoreType.DMA((2, count)),
            pltpu.SemaphoreType.DMA((2, count)),
            pltpu.SemaphoreType.DMA((2, chans)),
            pltpu.SemaphoreType.DMA((2,)),
        ],
        compiler_params=pltpu.CompilerParams(collective_id=0, has_side_effects=True),
    )(feat, gate, gain_row, spec_rows)


def bin_rows(seq_count):
    digit_order = reversed_digits(seq_count)
    stride = 2 * seq_count
    slots = np.arange(stride)
    low_bins = 2 * digit_order[slots // 2] + slots % 2
    return (low_bins[:, None] + stride * np.arange(ROW_GROUP)[None, :]).reshape(-1).astype(np.int32)


def convolve(sig_cols, spec_chan, seq_count, tok_rows):
    group = spec_chan.shape[0]
    first_len, second_len = spec_chan.shape[2], spec_chan.shape[3]
    half_first = first_len // 2
    all_bins = first_len * second_len
    row_bins = bin_rows(seq_count).astype(np.int64)
    first_in = np.arange(half_first)
    first_turn = (row_bins[:, None] * first_in[None, :]) % first_len * (2.0 * np.pi / first_len)
    stacked_np = np.concatenate([np.cos(first_turn), np.sin(first_turn)], 0)
    stacked = jnp.asarray(stacked_np.astype(np.float32))
    signs = np.concatenate([np.ones(first_len), -np.ones(first_len)]) / all_bins
    twist_turn = (row_bins[:, None] * np.arange(second_len)[None, :]) % all_bins * (2.0 * np.pi / all_bins)
    cos_twist = jnp.asarray(np.cos(twist_turn).astype(np.float32))
    sin_twist = jnp.asarray(np.sin(twist_turn).astype(np.float32))
    second_in = jnp.arange(second_len, dtype=jnp.int32)
    cos_second, sin_second = rotation(second_in[:, None] * second_in[None, :], second_len)
    fwd_second = jnp.concatenate(
        [jnp.concatenate([cos_second, -sin_second], 1), jnp.concatenate([sin_second, cos_second], 1)], 0
    )
    inv_second = jnp.concatenate(
        [jnp.concatenate([cos_second, sin_second], 1), jnp.concatenate([-sin_second, cos_second], 1)], 0
    )
    last = stacked * jnp.asarray(signs.astype(np.float32))[:, None]

    both = mm("rn,nm->rm", stacked, sig_cols)
    along_cos, along_sin = both[:first_len], both[first_len:]
    outs_re, outs_im = [], []
    for chan in range(group):
        lanes_of = slice(chan * second_len, (chan + 1) * second_len)
        p_cos, p_sin = along_cos[:, lanes_of], along_sin[:, lanes_of]
        twist_re = p_cos * cos_twist - p_sin * sin_twist
        twist_im = -p_sin * cos_twist - p_cos * sin_twist
        freq = mm("rn,nk->rk", jnp.concatenate([twist_re, twist_im], 1), fwd_second)
        freq_re, freq_im = freq[:, :second_len], freq[:, second_len:]
        filt_re, filt_im = spec_chan[chan, 0], spec_chan[chan, 1]
        prod_re = freq_re * filt_re - freq_im * filt_im
        prod_im = freq_re * filt_im + freq_im * filt_re
        back = mm("rk,kn->rn", jnp.concatenate([prod_re, prod_im], 1), inv_second)
        back_re, back_im = back[:, :second_len], back[:, second_len:]
        outs_re.append(back_re * cos_twist - back_im * sin_twist)
        outs_im.append(back_im * cos_twist + back_re * sin_twist)
    untwisted = jnp.concatenate([jnp.concatenate(outs_re, 1), jnp.concatenate(outs_im, 1)], 0)
    return mm("rn,rm->nm", last, untwisted)


def split(value):
    high = value.astype(jnp.bfloat16)
    return high, (value - high.astype(jnp.float32)).astype(jnp.bfloat16)


def dot3(left, right):
    l_hi, l_lo = left if isinstance(left, tuple) else split(left)
    r_hi, r_lo = right if isinstance(right, tuple) else split(right)
    out = jnp.dot(l_hi, r_hi, preferred_element_type=jnp.float32)
    out = out + jnp.dot(l_hi, r_lo, preferred_element_type=jnp.float32)
    return out + jnp.dot(l_lo, r_hi, preferred_element_type=jnp.float32)


def whole_kernel(*refs):
    table_count = len(TABLE_NAMES) + 4
    held = refs[:table_count]
    sig_out, res_recv = refs[table_count:table_count + 2]
    (sq_mine, sq_recv, sig_turn, sig_send, sig_recv, spec_recv, cols, conv_one, conv_send,
     spec_sems, sig_sems, res_sems, chan_sems, own_sems, table_sems) = refs[table_count + 2:table_count + 17]
    tables = refs[table_count + 17:]
    loads = [pltpu.make_async_copy(held[k], tables[k], table_sems.at[k]) for k in range(table_count)]
    for load in loads:
        load.start()
    for load in loads[:4]:
        load.wait()
    loads = loads[4:]
    feat_ref, gate_ref, gain_ref, spec_ref = tables[:4]
    tables = tables[4:]
    (st_hi, st_lo, tc_ref, ts_ref, fa_hi, fa_lo, fb_hi, fb_lo, ia_hi, ia_lo, ib_hi, ib_lo,
     lc_hi, lc_lo, ls_hi, ls_lo) = tables
    count = spec_ref.shape[0]
    chans = sq_recv.shape[0]
    me = lax.axis_index("seq")
    mine = lax.axis_index("chan")
    mesh_ids = pl.DeviceIdType.MESH
    barrier = pltpu.get_barrier_semaphore()

    def greet(step, carry):
        peer = lax.rem(me + step, count)
        pl.semaphore_signal(barrier, inc=1, device_id={"seq": peer}, device_id_type=mesh_ids)
        return carry

    lax.fori_loop(1, count, greet, 0)
    for step in range(1, chans):
        peer = lax.rem(mine + step, chans)
        pl.semaphore_signal(barrier, inc=1, device_id={"chan": peer}, device_id_type=mesh_ids)
    pl.semaphore_wait(barrier, count + chans - 2)

    def seq_copy(source, target, sems, step):
        peer = lax.rem(me + step, count)
        return pltpu.make_async_remote_copy(
            source(peer), target, sems.at[0, step], sems.at[1, step],
            device_id={"seq": peer}, device_id_type=mesh_ids,
        )

    def start_all(source, target, sems):
        def body(step, carry):
            seq_copy(source, target, sems, step).start()
            return carry
        lax.fori_loop(1, count, body, 0)

    def finish_all(source, target, sems):
        def body(step, carry):
            copy = seq_copy(source, target, sems, step)
            copy.wait_send()
            copy.wait_recv()
            return carry
        lax.fori_loop(1, count, body, 0)

    spec_src = lambda peer: spec_ref.at[peer]
    spec_own = pltpu.make_async_copy(spec_ref.at[me], spec_recv.at[me], own_sems.at[0])
    spec_own.start()
    start_all(spec_src, spec_recv.at[me], spec_sems)

    feat = feat_ref[...].astype(jnp.float32)
    part = jnp.sum(jnp.transpose(feat * feat), axis=0, keepdims=True)
    sq_mine[...] = jnp.broadcast_to(part, sq_mine.shape)

    def chan_copy(step):
        peer = lax.rem(mine + step, chans)
        return pltpu.make_async_remote_copy(
            sq_mine, sq_recv.at[mine], chan_sems.at[0, step], chan_sems.at[1, step],
            device_id={"chan": peer}, device_id_type=mesh_ids,
        )

    for step in range(1, chans):
        chan_copy(step).start()
    for step in range(1, chans):
        copy = chan_copy(step)
        copy.wait_send()
        copy.wait_recv()
    total = part
    for step in range(1, chans):
        other = lax.rem(mine + step, chans)
        total = total + sq_recv[other][0:1, :]
    scale = lax.rsqrt(total / CHANNELS + 1e-06)
    scale = jnp.transpose(jnp.broadcast_to(scale, (8, scale.shape[1])))[:, 0:1]
    signal = (feat * scale * gain_ref[...] * gate_ref[...].astype(jnp.float32)).astype(jnp.bfloat16)
    sig_out[...] = signal
    wide = signal.astype(jnp.float32)
    lanes = wide.shape[1]
    pair = lanes // count
    tiles = wide.shape[0] // lanes
    chunk = pair * tiles
    for tile in range(tiles):
        sig_turn[...] = jnp.transpose(wide[lanes * tile:lanes * (tile + 1), :])
        for chan in range(pair):
            rows = sig_turn[pl.ds(chan, count, stride=pair), :]
            sig_send[pl.ds(tiles * chan + tile, count, stride=chunk), :] = rows

    def rows_of(buffer):
        return lambda peer: buffer.at[pl.ds(pl.multiple_of(peer * chunk, chunk), chunk)]

    sig_own = pltpu.make_async_copy(rows_of(sig_send)(me), rows_of(sig_recv)(me), own_sems.at[1])
    sig_own.start()
    start_all(rows_of(sig_send), rows_of(sig_recv)(me), sig_sems)
    finish_all(rows_of(sig_send), rows_of(sig_recv)(me), sig_sems)
    sig_own.wait()

    for chan in range(pair):
        for tile in range(tiles):
            rows = sig_recv[pl.ds(tiles * chan + tile, count, stride=chunk), :]
            cols[chan, pl.ds(tile, count, stride=tiles), :] = rows

    first_len = tc_ref.shape[0]
    for load in loads:
        load.wait()
    boths = []
    for chan in range(pair):
        signal_cols = cols[chan].astype(jnp.bfloat16)
        both = jnp.dot(st_hi[...], signal_cols, preferred_element_type=jnp.float32)
        boths.append(both + jnp.dot(st_lo[...], signal_cols, preferred_element_type=jnp.float32))

    cos_twist, sin_twist = tc_ref[...], ts_ref[...]
    own_rows = first_len // count
    freqs = []
    for chan in range(pair):
        p_cos = boths[chan][:first_len]
        p_sin = boths[chan][first_len:]
        twist_re = p_cos * cos_twist - p_sin * sin_twist
        twist_im = -p_sin * cos_twist - p_cos * sin_twist
        freqs.append(dot3(twist_re, (fa_hi[...], fa_lo[...])) + dot3(twist_im, (fb_hi[...], fb_lo[...])))

    finish_all(spec_src, spec_recv.at[me], spec_sems)
    spec_own.wait()

    for chan in range(pair):
        freq = freqs[chan]
        freq_re, freq_im = freq[:, :lanes], freq[:, lanes:]
        filt = []
        for part_of in range(2):
            block = spec_recv[:, pl.ds((2 * chan + part_of) * own_rows, own_rows), :]
            filt.append(block.astype(jnp.float32).reshape(first_len, lanes))
        filt_re, filt_im = filt
        prod_re = freq_re * filt_re - freq_im * filt_im
        prod_im = freq_re * filt_im + freq_im * filt_re
        back = dot3(prod_re, (ia_hi[...], ia_lo[...])) + dot3(prod_im, (ib_hi[...], ib_lo[...]))
        back_re, back_im = back[:, :lanes], back[:, lanes:]
        untwist_re = back_re * cos_twist - back_im * sin_twist
        untwist_im = back_im * cos_twist + back_re * sin_twist
        conv_one[...] = dot3((lc_hi[...], lc_lo[...]), untwist_re) + dot3((ls_hi[...], ls_lo[...]), untwist_im)
        for tile in range(tiles):
            rows = conv_one[pl.ds(tile, count, stride=tiles), :]
            conv_send[pl.ds(tiles * chan + tile, count, stride=chunk), :] = rows

    res_src = rows_of(conv_send)
    res_own = pltpu.make_async_copy(res_src(me), res_recv.at[me], own_sems.at[2])
    res_own.start()
    start_all(res_src, res_recv.at[me], res_sems)
    finish_all(res_src, res_recv.at[me], res_sems)
    res_own.wait()


def whole(features, pre_gate, gain_row, spec_rows, tables, chans):
    count = spec_rows.shape[0]
    length, width = features.shape
    pair = width // count
    lanes = 128
    chunk = pair * length // lanes
    vmem = pl.BlockSpec(memory_space=pltpu.VMEM)
    operands = (features, pre_gate, gain_row, spec_rows) + tuple(tables)
    hbm = pl.BlockSpec(memory_space=pl.ANY)
    return pl.pallas_call(
        whole_kernel,
        out_shape=(
            jax.ShapeDtypeStruct((length, width), jnp.bfloat16),
            jax.ShapeDtypeStruct((count, chunk, lanes), jnp.float32),
        ),
        in_specs=[hbm] * len(operands),
        out_specs=(vmem, vmem),
        scratch_shapes=[
            pltpu.VMEM((8, length), jnp.float32),
            pltpu.VMEM((chans, 8, length), jnp.float32),
            pltpu.VMEM((lanes, lanes), jnp.float32),
            pltpu.VMEM((count * chunk, lanes), jnp.float32),
            pltpu.VMEM((count * chunk, lanes), jnp.float32),
            pltpu.VMEM(spec_rows.shape, spec_rows.dtype),
            pltpu.VMEM((pair, count * chunk // pair, lanes), jnp.float32),
            pltpu.VMEM((count * chunk // pair, lanes), jnp.float32),
            pltpu.VMEM((count * chunk, lanes), jnp.float32),
            pltpu.SemaphoreType.DMA((2, count)),
            pltpu.SemaphoreType.DMA((2, count)),
            pltpu.SemaphoreType.DMA((2, count)),
            pltpu.SemaphoreType.DMA((2, chans)),
            pltpu.SemaphoreType.DMA((3,)),
            pltpu.SemaphoreType.DMA((len(operands),)),
        ]
        + [pltpu.VMEM(table.shape, table.dtype) for table in operands],
        compiler_params=pltpu.CompilerParams(
            collective_id=0, has_side_effects=True, vmem_limit_bytes=67043328
        ),
    )(*operands)


def dft_tables(seq_count, tok_rows):
    stride = 2 * seq_count
    first_len = stride * ROW_GROUP
    all_bins = stride * tok_rows
    second_len = all_bins // first_len
    half_first = first_len // 2
    row_bins = bin_rows(seq_count).astype(np.int64)
    first_turn = (row_bins[:, None] * np.arange(half_first)[None, :]) % first_len * (2.0 * np.pi / first_len)
    cos_first, sin_first = np.cos(first_turn), np.sin(first_turn)
    twist_turn = (row_bins[:, None] * np.arange(second_len)[None, :]) % all_bins * (2.0 * np.pi / all_bins)
    second_in = np.arange(second_len)
    second_turn = (second_in[:, None] * second_in[None, :]) % second_len * (2.0 * np.pi / second_len)
    cos_second, sin_second = np.cos(second_turn), np.sin(second_turn)

    def pair_of(array):
        array = array.astype(np.float32)
        high = array.astype(jnp.bfloat16)
        return [jnp.asarray(high), jnp.asarray((array - high.astype(np.float32)).astype(jnp.bfloat16))]

    tables = pair_of(np.concatenate([cos_first, sin_first], 0))
    tables += [jnp.asarray(np.cos(twist_turn).astype(np.float32)), jnp.asarray(np.sin(twist_turn).astype(np.float32))]
    tables += pair_of(np.concatenate([cos_second, -sin_second], 1))
    tables += pair_of(np.concatenate([sin_second, cos_second], 1))
    tables += pair_of(np.concatenate([cos_second, sin_second], 1))
    tables += pair_of(np.concatenate([-sin_second, cos_second], 1))
    tables += pair_of(cos_first.T / all_bins)
    tables += pair_of(-sin_first.T / all_bins)
    return tables


def local(features, pre_gate, post_gate, norm_gain, skip_weight, spectrum):
    tok_rows, chan_width = features.shape
    seq_count = lax.axis_size("seq")
    chans = lax.axis_size("chan")
    group = chan_width // seq_count
    second_len = tok_rows // ROW_GROUP
    lanes = 128
    tok_tiles = tok_rows // lanes

    spec_rows = spectrum.reshape(2, 2, second_len, ROW_GROUP, chan_width)
    spec_rows = jnp.transpose(spec_rows, (4, 0, 1, 3, 2)).astype(jnp.bfloat16)
    spec_rows = spec_rows.reshape(seq_count, -1, second_len)
    signal, result = whole(
        features, pre_gate, norm_gain.reshape(1, chan_width), spec_rows,
        dft_tables(seq_count, tok_rows), chans,
    )
    result = result.reshape(seq_count, group, tok_tiles, lanes)
    result = jnp.transpose(result, (2, 3, 0, 1)).reshape(tok_rows, chan_width)
    gated = post_gate.astype(jnp.float32) * (result + skip_weight * signal.astype(jnp.float32))
    return gated.astype(jnp.bfloat16)


def solution(mesh):
    return jax.shard_map(
        local,
        mesh=mesh,
        in_specs=(
            P("seq", "chan"),
            P("seq", "chan"),
            P("seq", "chan"),
            P("chan"),
            P("chan"),
            P(None, "seq", None, "chan"),
        ),
        out_specs=P("seq", "chan"),
        check_vma=False,
    )
```

```python
import math

import jax
import jax.numpy as jnp
import numpy as np
from jax import lax
from jax.experimental import pallas as pl
from jax.experimental.pallas import tpu as pltpu
from jax.sharding import PartitionSpec as P

CHANNELS = 512
ROW_GROUP = 4
TABLE_NAMES = ("st_hi", "st_lo", "tc", "ts", "fa_hi", "fa_lo", "fb_hi", "fb_lo", "ia_hi", "ia_lo", "ib_hi", "ib_lo",
               "lc_hi", "lc_lo", "ls_hi", "ls_lo")
HIGH_DIGIT = 8


PRECISE = lax.Precision.HIGH
FULL_TURN = 2.0 * math.pi


def reversed_digits(count):
    levels = count.bit_length() - 1
    positions = np.arange(count)
    result = np.zeros(count, np.int64)
    for bit_pos in range(levels):
        result = result + ((positions >> bit_pos & 1) << levels - 1 - bit_pos)
    return result


def rotation(numerator, denominator):
    angle = (numerator % denominator).astype(jnp.float32) * (FULL_TURN / denominator)
    return (jnp.cos(angle), jnp.sin(angle))


def mm(spec, left, right):
    return jnp.einsum(spec, left, right, precision=PRECISE, preferred_element_type=jnp.float32)


def exchange_kernel(src_ref, dst_ref, send_sem, recv_sem, own_sem):
    count = src_ref.shape[0]
    me = lax.axis_index("seq")
    mesh_ids = pl.DeviceIdType.MESH
    barrier = pltpu.get_barrier_semaphore()

    def greet(step, carry):
        peer = lax.rem(me + step, count)
        pl.semaphore_signal(barrier, inc=1, device_id={"seq": peer}, device_id_type=mesh_ids)
        return carry

    lax.fori_loop(1, count, greet, 0, unroll=True)
    pl.semaphore_wait(barrier, count - 1)
    own = pltpu.make_async_copy(src_ref.at[me], dst_ref.at[me], own_sem)
    own.start()

    def remote(step):
        peer = lax.rem(me + step, count)
        return pltpu.make_async_remote_copy(
            src_ref.at[peer],
            dst_ref.at[me],
            send_sem.at[step],
            recv_sem.at[step],
            device_id={"seq": peer},
            device_id_type=mesh_ids,
        )

    def send(step, carry):
        remote(step).start()
        return carry

    lax.fori_loop(1, count, send, 0, unroll=True)

    def finish(step, carry):
        copy = remote(step)
        copy.wait_send()
        copy.wait_recv()
        return carry

    lax.fori_loop(1, count, finish, 0, unroll=True)
    own.wait()


def exchange(blocks, tag):
    count = blocks.shape[0]
    vmem = pl.BlockSpec(memory_space=pltpu.VMEM)
    return pl.pallas_call(
        exchange_kernel,
        out_shape=jax.ShapeDtypeStruct(blocks.shape, blocks.dtype),
        in_specs=[vmem],
        out_specs=vmem,
        scratch_shapes=[
            pltpu.SemaphoreType.DMA((count,)),
            pltpu.SemaphoreType.DMA((count,)),
            pltpu.SemaphoreType.DMA,
        ],
        compiler_params=pltpu.CompilerParams(collective_id=tag, has_side_effects=True),
    )(blocks)


def front_kernel(
    feat_ref, gate_ref, gain_ref, spec_ref,
    sig_out, sig_recv, spec_recv,
    sq_mine, sq_recv, sig_turn, sig_send, spec_sems, sig_sems, chan_sems, own_sems,
):
    count = spec_ref.shape[0]
    chans = sq_recv.shape[0]
    me = lax.axis_index("seq")
    mine = lax.axis_index("chan")
    mesh_ids = pl.DeviceIdType.MESH
    barrier = pltpu.get_barrier_semaphore()

    def greet(step, carry):
        peer = lax.rem(me + step, count)
        pl.semaphore_signal(barrier, inc=1, device_id={"seq": peer}, device_id_type=mesh_ids)
        return carry

    lax.fori_loop(1, count, greet, 0, unroll=True)
    for step in range(1, chans):
        peer = lax.rem(mine + step, chans)
        pl.semaphore_signal(barrier, inc=1, device_id={"chan": peer}, device_id_type=mesh_ids)
    pl.semaphore_wait(barrier, count + chans - 2)

    def spec_copy(step):
        peer = lax.rem(me + step, count)
        return pltpu.make_async_remote_copy(
            spec_ref.at[peer],
            spec_recv.at[me],
            spec_sems.at[0, step],
            spec_sems.at[1, step],
            device_id={"seq": peer},
            device_id_type=mesh_ids,
        )

    spec_own = pltpu.make_async_copy(spec_ref.at[me], spec_recv.at[me], own_sems.at[0])
    spec_own.start()

    def spec_send(step, carry):
        spec_copy(step).start()
        return carry

    lax.fori_loop(1, count, spec_send, 0, unroll=True)

    feat = feat_ref[...].astype(jnp.float32)
    part = jnp.sum(jnp.transpose(feat * feat), axis=0, keepdims=True)
    sq_mine[...] = jnp.broadcast_to(part, sq_mine.shape)

    def chan_copy(step):
        peer = lax.rem(mine + step, chans)
        return pltpu.make_async_remote_copy(
            sq_mine,
            sq_recv.at[mine],
            chan_sems.at[0, step],
            chan_sems.at[1, step],
            device_id={"chan": peer},
            device_id_type=mesh_ids,
        )

    for step in range(1, chans):
        chan_copy(step).start()
    for step in range(1, chans):
        copy = chan_copy(step)
        copy.wait_send()
        copy.wait_recv()
    total = part
    for step in range(1, chans):
        other = lax.rem(mine + step, chans)
        total = total + sq_recv[other][0:1, :]
    scale = lax.rsqrt(total / CHANNELS + 1e-06)
    scale = jnp.transpose(jnp.broadcast_to(scale, (8, scale.shape[1])))[:, 0:1]
    signal = (feat * scale * gain_ref[...] * gate_ref[...].astype(jnp.float32)).astype(jnp.bfloat16)
    sig_out[...] = signal
    wide = signal.astype(jnp.float32)
    lanes = wide.shape[1]
    pair = lanes // count
    tiles = wide.shape[0] // lanes
    chunk = pair * tiles
    for tile in range(tiles):
        sig_turn[...] = jnp.transpose(wide[lanes * tile:lanes * (tile + 1), :])
        for chan in range(pair):
            rows = sig_turn[pl.ds(chan, count, stride=pair), :]
            sig_send[pl.ds(tiles * chan + tile, count, stride=chunk), :] = rows

    def sig_rows(peer):
        return sig_send.at[pl.ds(pl.multiple_of(peer * chunk, chunk), chunk)]

    def sig_copy(step):
        peer = lax.rem(me + step, count)
        return pltpu.make_async_remote_copy(
            sig_rows(peer),
            sig_recv.at[me],
            sig_sems.at[0, step],
            sig_sems.at[1, step],
            device_id={"seq": peer},
            device_id_type=mesh_ids,
        )

    sig_own = pltpu.make_async_copy(sig_rows(me), sig_recv.at[me], own_sems.at[1])
    sig_own.start()

    def sig_start(step, carry):
        sig_copy(step).start()
        return carry

    lax.fori_loop(1, count, sig_start, 0, unroll=True)

    def sig_finish(step, carry):
        copy = sig_copy(step)
        copy.wait_send()
        copy.wait_recv()
        return carry

    lax.fori_loop(1, count, sig_finish, 0, unroll=True)
    sig_own.wait()

    def spec_finish(step, carry):
        copy = spec_copy(step)
        copy.wait_send()
        copy.wait_recv()
        return carry

    lax.fori_loop(1, count, spec_finish, 0, unroll=True)
    spec_own.wait()


def front(feat, gate, gain_row, spec_rows, chans):
    count = spec_rows.shape[0]
    length, width = feat.shape
    pair = width // count
    vmem = pl.BlockSpec(memory_space=pltpu.VMEM)
    return pl.pallas_call(
        front_kernel,
        out_shape=(
            jax.ShapeDtypeStruct((length, width), jnp.bfloat16),
            jax.ShapeDtypeStruct((count, pair * length // 128, 128), jnp.float32),
            jax.ShapeDtypeStruct(spec_rows.shape, spec_rows.dtype),
        ),
        in_specs=[vmem] * 4,
        out_specs=(vmem, vmem, vmem),
        scratch_shapes=[
            pltpu.VMEM((8, length), jnp.float32),
            pltpu.VMEM((chans, 8, length), jnp.float32),
            pltpu.VMEM((128, 128), jnp.float32),
            pltpu.VMEM((count * pair * length // 128, 128), jnp.float32),
            pltpu.SemaphoreType.DMA((2, count)),
            pltpu.SemaphoreType.DMA((2, count)),
            pltpu.SemaphoreType.DMA((2, chans)),
            pltpu.SemaphoreType.DMA((2,)),
        ],
        compiler_params=pltpu.CompilerParams(collective_id=0, has_side_effects=True),
    )(feat, gate, gain_row, spec_rows)


def bin_rows(seq_count):
    digit_order = reversed_digits(seq_count)
    stride = 2 * seq_count
    slots = np.arange(stride)
    low_bins = 2 * digit_order[slots // 2] + slots % 2
    return (low_bins[:, None] + stride * np.arange(ROW_GROUP)[None, :]).reshape(-1).astype(np.int32)


def convolve(sig_cols, spec_chan, seq_count, tok_rows):
    group = spec_chan.shape[0]
    first_len, second_len = spec_chan.shape[2], spec_chan.shape[3]
    half_first = first_len // 2
    all_bins = first_len * second_len
    row_bins = bin_rows(seq_count).astype(np.int64)
    first_in = np.arange(half_first)
    first_turn = (row_bins[:, None] * first_in[None, :]) % first_len * (2.0 * np.pi / first_len)
    stacked_np = np.concatenate([np.cos(first_turn), np.sin(first_turn)], 0)
    stacked = jnp.asarray(stacked_np.astype(np.float32))
    signs = np.concatenate([np.ones(first_len), -np.ones(first_len)]) / all_bins
    twist_turn = (row_bins[:, None] * np.arange(second_len)[None, :]) % all_bins * (2.0 * np.pi / all_bins)
    cos_twist = jnp.asarray(np.cos(twist_turn).astype(np.float32))
    sin_twist = jnp.asarray(np.sin(twist_turn).astype(np.float32))
    second_in = jnp.arange(second_len, dtype=jnp.int32)
    cos_second, sin_second = rotation(second_in[:, None] * second_in[None, :], second_len)
    fwd_second = jnp.concatenate(
        [jnp.concatenate([cos_second, -sin_second], 1), jnp.concatenate([sin_second, cos_second], 1)], 0
    )
    inv_second = jnp.concatenate(
        [jnp.concatenate([cos_second, sin_second], 1), jnp.concatenate([-sin_second, cos_second], 1)], 0
    )
    last = stacked * jnp.asarray(signs.astype(np.float32))[:, None]

    both = mm("rn,nm->rm", stacked, sig_cols)
    along_cos, along_sin = both[:first_len], both[first_len:]
    outs_re, outs_im = [], []
    for chan in range(group):
        lanes_of = slice(chan * second_len, (chan + 1) * second_len)
        p_cos, p_sin = along_cos[:, lanes_of], along_sin[:, lanes_of]
        twist_re = p_cos * cos_twist - p_sin * sin_twist
        twist_im = -p_sin * cos_twist - p_cos * sin_twist
        freq = mm("rn,nk->rk", jnp.concatenate([twist_re, twist_im], 1), fwd_second)
        freq_re, freq_im = freq[:, :second_len], freq[:, second_len:]
        filt_re, filt_im = spec_chan[chan, 0], spec_chan[chan, 1]
        prod_re = freq_re * filt_re - freq_im * filt_im
        prod_im = freq_re * filt_im + freq_im * filt_re
        back = mm("rk,kn->rn", jnp.concatenate([prod_re, prod_im], 1), inv_second)
        back_re, back_im = back[:, :second_len], back[:, second_len:]
        outs_re.append(back_re * cos_twist - back_im * sin_twist)
        outs_im.append(back_im * cos_twist + back_re * sin_twist)
    untwisted = jnp.concatenate([jnp.concatenate(outs_re, 1), jnp.concatenate(outs_im, 1)], 0)
    return mm("rn,rm->nm", last, untwisted)


def split(value):
    high = value.astype(jnp.bfloat16)
    return high, (value - high.astype(jnp.float32)).astype(jnp.bfloat16)


def dot3(left, right):
    if isinstance(left, tuple):
        d_hi, d_lo = split(right)
        out = jnp.dot(left[0], d_hi, preferred_element_type=jnp.float32)
        return out + jnp.dot(left[0], d_lo, preferred_element_type=jnp.float32)
    d_hi, d_lo = split(left)
    out = jnp.dot(d_hi, right[0], preferred_element_type=jnp.float32)
    return out + jnp.dot(d_lo, right[0], preferred_element_type=jnp.float32)


def whole_kernel(*refs):
    table_count = len(TABLE_NAMES) + 4
    held = refs[:table_count]
    sig_out, res_recv = refs[table_count:table_count + 2]
    (sq_mine, sq_recv, sig_turn, sig_send, sig_recv, spec_recv, cols, conv_one, conv_send,
     spec_sems, sig_sems, res_sems, chan_sems, own_sems, table_sems) = refs[table_count + 2:table_count + 17]
    tables = refs[table_count + 17:]
    loads = [pltpu.make_async_copy(held[k], tables[k], table_sems.at[k]) for k in range(table_count)]
    for load in loads:
        load.start()
    for load in loads[:4]:
        load.wait()
    loads = loads[4:]
    feat_ref, gate_ref, gain_ref, spec_ref = tables[:4]
    tables = tables[4:]
    (st_hi, st_lo, tc_ref, ts_ref, fa_hi, fa_lo, fb_hi, fb_lo, ia_hi, ia_lo, ib_hi, ib_lo,
     lc_hi, lc_lo, ls_hi, ls_lo) = tables
    count = spec_ref.shape[0]
    chans = sq_recv.shape[0]
    me = lax.axis_index("seq")
    mine = lax.axis_index("chan")
    mesh_ids = pl.DeviceIdType.MESH
    barrier = pltpu.get_barrier_semaphore()

    def greet(step, carry):
        peer = lax.rem(me + step, count)
        pl.semaphore_signal(barrier, inc=1, device_id={"seq": peer}, device_id_type=mesh_ids)
        return carry

    lax.fori_loop(1, count, greet, 0)
    for step in range(1, chans):
        peer = lax.rem(mine + step, chans)
        pl.semaphore_signal(barrier, inc=1, device_id={"chan": peer}, device_id_type=mesh_ids)
    pl.semaphore_wait(barrier, count + chans - 2)

    def seq_copy(source, target, sems, step):
        peer = lax.rem(me + step, count)
        return pltpu.make_async_remote_copy(
            source(peer), target, sems.at[0, step], sems.at[1, step],
            device_id={"seq": peer}, device_id_type=mesh_ids,
        )

    def start_all(source, target, sems):
        def body(step, carry):
            seq_copy(source, target, sems, step).start()
            return carry
        lax.fori_loop(1, count, body, 0)

    def finish_all(source, target, sems):
        def body(step, carry):
            copy = seq_copy(source, target, sems, step)
            copy.wait_send()
            copy.wait_recv()
            return carry
        lax.fori_loop(1, count, body, 0)

    spec_src = lambda peer: spec_ref.at[peer]
    spec_own = pltpu.make_async_copy(spec_ref.at[me], spec_recv.at[me], own_sems.at[0])
    spec_own.start()
    start_all(spec_src, spec_recv.at[me], spec_sems)

    feat = feat_ref[...].astype(jnp.float32)
    part = jnp.sum(jnp.transpose(feat * feat), axis=0, keepdims=True)
    sq_mine[...] = jnp.broadcast_to(part, sq_mine.shape)

    def chan_copy(step):
        peer = lax.rem(mine + step, chans)
        return pltpu.make_async_remote_copy(
            sq_mine, sq_recv.at[mine], chan_sems.at[0, step], chan_sems.at[1, step],
            device_id={"chan": peer}, device_id_type=mesh_ids,
        )

    for step in range(1, chans):
        chan_copy(step).start()
    for step in range(1, chans):
        copy = chan_copy(step)
        copy.wait_send()
        copy.wait_recv()
    total = part
    for step in range(1, chans):
        other = lax.rem(mine + step, chans)
        total = total + sq_recv[other][0:1, :]
    scale = lax.rsqrt(total / CHANNELS + 1e-06)
    scale = jnp.transpose(jnp.broadcast_to(scale, (8, scale.shape[1])))[:, 0:1]
    signal = (feat * scale * gain_ref[...] * gate_ref[...].astype(jnp.float32)).astype(jnp.bfloat16)
    sig_out[...] = signal
    wide = signal.astype(jnp.float32)
    lanes = wide.shape[1]
    pair = lanes // count
    tiles = wide.shape[0] // lanes
    chunk = pair * tiles
    for tile in range(tiles):
        sig_turn[...] = jnp.transpose(wide[lanes * tile:lanes * (tile + 1), :])
        for chan in range(pair):
            rows = sig_turn[pl.ds(chan, count, stride=pair), :]
            sig_send[pl.ds(tiles * chan + tile, count, stride=chunk), :] = rows

    def rows_of(buffer):
        return lambda peer: buffer.at[pl.ds(pl.multiple_of(peer * chunk, chunk), chunk)]

    sig_own = pltpu.make_async_copy(rows_of(sig_send)(me), rows_of(sig_recv)(me), own_sems.at[1])
    sig_own.start()
    start_all(rows_of(sig_send), rows_of(sig_recv)(me), sig_sems)
    finish_all(rows_of(sig_send), rows_of(sig_recv)(me), sig_sems)
    sig_own.wait()

    for chan in range(pair):
        for tile in range(tiles):
            rows = sig_recv[pl.ds(tiles * chan + tile, count, stride=chunk), :]
            cols[chan, pl.ds(tile, count, stride=tiles), :] = rows

    first_len = tc_ref.shape[0]
    for load in loads:
        load.wait()
    boths = []
    for chan in range(pair):
        signal_cols = cols[chan].astype(jnp.bfloat16)
        boths.append(jnp.dot(st_hi[...], signal_cols, preferred_element_type=jnp.float32))

    cos_twist, sin_twist = tc_ref[...], ts_ref[...]
    own_rows = first_len // count
    freqs = []
    for chan in range(pair):
        p_cos = boths[chan][:first_len]
        p_sin = boths[chan][first_len:]
        twist_re = p_cos * cos_twist - p_sin * sin_twist
        twist_im = -p_sin * cos_twist - p_cos * sin_twist
        freqs.append(dot3(twist_re, (fa_hi[...], fa_lo[...])) + dot3(twist_im, (fb_hi[...], fb_lo[...])))

    finish_all(spec_src, spec_recv.at[me], spec_sems)
    spec_own.wait()

    for chan in range(pair):
        freq = freqs[chan]
        freq_re, freq_im = freq[:, :lanes], freq[:, lanes:]
        filt = []
        for part_of in range(2):
            block = spec_recv[:, pl.ds((2 * chan + part_of) * own_rows, own_rows), :]
            filt.append(block.astype(jnp.float32).reshape(first_len, lanes))
        filt_re, filt_im = filt
        prod_re = freq_re * filt_re - freq_im * filt_im
        prod_im = freq_re * filt_im + freq_im * filt_re
        back = dot3(prod_re, (ia_hi[...], ia_lo[...])) + dot3(prod_im, (ib_hi[...], ib_lo[...]))
        back_re, back_im = back[:, :lanes], back[:, lanes:]
        untwist_re = back_re * cos_twist - back_im * sin_twist
        untwist_im = back_im * cos_twist + back_re * sin_twist
        conv_one[...] = dot3((lc_hi[...], lc_lo[...]), untwist_re) + dot3((ls_hi[...], ls_lo[...]), untwist_im)
        for tile in range(tiles):
            rows = conv_one[pl.ds(tile, count, stride=tiles), :]
            conv_send[pl.ds(tiles * chan + tile, count, stride=chunk), :] = rows

    res_src = rows_of(conv_send)
    res_own = pltpu.make_async_copy(res_src(me), res_recv.at[me], own_sems.at[2])
    res_own.start()
    start_all(res_src, res_recv.at[me], res_sems)
    finish_all(res_src, res_recv.at[me], res_sems)
    res_own.wait()


def whole(features, pre_gate, gain_row, spec_rows, tables, chans):
    count = spec_rows.shape[0]
    length, width = features.shape
    pair = width // count
    lanes = 128
    chunk = pair * length // lanes
    vmem = pl.BlockSpec(memory_space=pltpu.VMEM)
    operands = (features, pre_gate, gain_row, spec_rows) + tuple(tables)
    hbm = pl.BlockSpec(memory_space=pl.ANY)
    return pl.pallas_call(
        whole_kernel,
        out_shape=(
            jax.ShapeDtypeStruct((length, width), jnp.bfloat16),
            jax.ShapeDtypeStruct((count, chunk, lanes), jnp.float32),
        ),
        in_specs=[hbm] * len(operands),
        out_specs=(vmem, vmem),
        scratch_shapes=[
            pltpu.VMEM((8, length), jnp.float32),
            pltpu.VMEM((chans, 8, length), jnp.float32),
            pltpu.VMEM((lanes, lanes), jnp.float32),
            pltpu.VMEM((count * chunk, lanes), jnp.float32),
            pltpu.VMEM((count * chunk, lanes), jnp.float32),
            pltpu.VMEM(spec_rows.shape, spec_rows.dtype),
            pltpu.VMEM((pair, count * chunk // pair, lanes), jnp.float32),
            pltpu.VMEM((count * chunk // pair, lanes), jnp.float32),
            pltpu.VMEM((count * chunk, lanes), jnp.float32),
            pltpu.SemaphoreType.DMA((2, count)),
            pltpu.SemaphoreType.DMA((2, count)),
            pltpu.SemaphoreType.DMA((2, count)),
            pltpu.SemaphoreType.DMA((2, chans)),
            pltpu.SemaphoreType.DMA((3,)),
            pltpu.SemaphoreType.DMA((len(operands),)),
        ]
        + [pltpu.VMEM(table.shape, table.dtype) for table in operands],
        compiler_params=pltpu.CompilerParams(
            collective_id=0, has_side_effects=True, vmem_limit_bytes=67043328
        ),
    )(*operands)


def dft_tables(seq_count, tok_rows):
    stride = 2 * seq_count
    first_len = stride * ROW_GROUP
    all_bins = stride * tok_rows
    second_len = all_bins // first_len
    half_first = first_len // 2
    row_bins = bin_rows(seq_count).astype(np.int64)
    first_turn = (row_bins[:, None] * np.arange(half_first)[None, :]) % first_len * (2.0 * np.pi / first_len)
    cos_first, sin_first = np.cos(first_turn), np.sin(first_turn)
    twist_turn = (row_bins[:, None] * np.arange(second_len)[None, :]) % all_bins * (2.0 * np.pi / all_bins)
    second_in = np.arange(second_len)
    second_turn = (second_in[:, None] * second_in[None, :]) % second_len * (2.0 * np.pi / second_len)
    cos_second, sin_second = np.cos(second_turn), np.sin(second_turn)

    def pair_of(array):
        array = array.astype(np.float32)
        high = array.astype(jnp.bfloat16)
        return [jnp.asarray(high), jnp.asarray((array - high.astype(np.float32)).astype(jnp.bfloat16))]

    tables = pair_of(np.concatenate([cos_first, sin_first], 0))
    tables += [jnp.asarray(np.cos(twist_turn).astype(np.float32)), jnp.asarray(np.sin(twist_turn).astype(np.float32))]
    tables += pair_of(np.concatenate([cos_second, -sin_second], 1))
    tables += pair_of(np.concatenate([sin_second, cos_second], 1))
    tables += pair_of(np.concatenate([cos_second, sin_second], 1))
    tables += pair_of(np.concatenate([-sin_second, cos_second], 1))
    tables += pair_of(cos_first.T / all_bins)
    tables += pair_of(-sin_first.T / all_bins)
    return tables


def local(features, pre_gate, post_gate, norm_gain, skip_weight, spectrum):
    tok_rows, chan_width = features.shape
    seq_count = lax.axis_size("seq")
    chans = lax.axis_size("chan")
    group = chan_width // seq_count
    second_len = tok_rows // ROW_GROUP
    lanes = 128
    tok_tiles = tok_rows // lanes

    spec_rows = spectrum.reshape(2, 2, second_len, ROW_GROUP, chan_width)
    spec_rows = jnp.transpose(spec_rows, (4, 0, 1, 3, 2)).astype(jnp.bfloat16)
    spec_rows = spec_rows.reshape(seq_count, -1, second_len)
    signal, result = whole(
        features, pre_gate, norm_gain.reshape(1, chan_width), spec_rows,
        dft_tables(seq_count, tok_rows), chans,
    )
    result = result.reshape(seq_count, group, tok_tiles, lanes)
    result = jnp.transpose(result, (2, 3, 0, 1)).reshape(tok_rows, chan_width)
    gated = post_gate.astype(jnp.float32) * (result + skip_weight * signal.astype(jnp.float32))
    return gated.astype(jnp.bfloat16)


def solution(mesh):
    return jax.shard_map(
        local,
        mesh=mesh,
        in_specs=(
            P("seq", "chan"),
            P("seq", "chan"),
            P("seq", "chan"),
            P("chan"),
            P("chan"),
            P(None, "seq", None, "chan"),
        ),
        out_specs=P("seq", "chan"),
        check_vma=False,
    )
```

```python
import math

import jax
import jax.numpy as jnp
import numpy as np
from jax import lax
from jax.experimental import pallas as pl
from jax.experimental.pallas import tpu as pltpu
from jax.sharding import PartitionSpec as P

CHANNELS = 512
ROW_GROUP = 4
TABLE_NAMES = ("st_hi", "st_lo", "tc", "ts", "fa_hi", "fa_lo", "fb_hi", "fb_lo", "ia_hi", "ia_lo", "ib_hi", "ib_lo",
               "lc_hi", "lc_lo", "ls_hi", "ls_lo")
HIGH_DIGIT = 8


PRECISE = lax.Precision.HIGH
FULL_TURN = 2.0 * math.pi


def reversed_digits(count):
    levels = count.bit_length() - 1
    positions = np.arange(count)
    result = np.zeros(count, np.int64)
    for bit_pos in range(levels):
        result = result + ((positions >> bit_pos & 1) << levels - 1 - bit_pos)
    return result


def rotation(numerator, denominator):
    angle = (numerator % denominator).astype(jnp.float32) * (FULL_TURN / denominator)
    return (jnp.cos(angle), jnp.sin(angle))


def mm(spec, left, right):
    return jnp.einsum(spec, left, right, precision=PRECISE, preferred_element_type=jnp.float32)


def bin_rows(seq_count):
    digit_order = reversed_digits(seq_count)
    stride = 2 * seq_count
    slots = np.arange(stride)
    low_bins = 2 * digit_order[slots // 2] + slots % 2
    return (low_bins[:, None] + stride * np.arange(ROW_GROUP)[None, :]).reshape(-1).astype(np.int32)


def split(value):
    high = value.astype(jnp.bfloat16)
    return high, (value - high.astype(jnp.float32)).astype(jnp.bfloat16)


def dot3(left, right):
    if isinstance(left, tuple):
        d_hi, d_lo = split(right)
        out = jnp.dot(left[0], d_hi, preferred_element_type=jnp.float32)
        return out + jnp.dot(left[0], d_lo, preferred_element_type=jnp.float32)
    d_hi, d_lo = split(left)
    out = jnp.dot(d_hi, right[0], preferred_element_type=jnp.float32)
    return out + jnp.dot(d_lo, right[0], preferred_element_type=jnp.float32)


def whole_kernel(*refs):
    table_count = len(TABLE_NAMES) + 4
    held = refs[:table_count]
    sig_out, res_recv = refs[table_count:table_count + 2]
    (sq_mine, sq_recv, sig_turn, sig_send, sig_recv, spec_recv, cols, conv_one, conv_send,
     spec_sems, sig_sems, res_sems, chan_sems, own_sems, table_sems) = refs[table_count + 2:table_count + 17]
    tables = refs[table_count + 17:]
    loads = [pltpu.make_async_copy(held[k], tables[k], table_sems.at[k]) for k in range(table_count)]
    for load in loads:
        load.start()
    for load in loads[:4]:
        load.wait()
    loads = loads[4:]
    feat_ref, gate_ref, gain_ref, spec_ref = tables[:4]
    tables = tables[4:]
    (st_hi, st_lo, tc_ref, ts_ref, fa_hi, fa_lo, fb_hi, fb_lo, ia_hi, ia_lo, ib_hi, ib_lo,
     lc_hi, lc_lo, ls_hi, ls_lo) = tables
    count = spec_ref.shape[0]
    chans = sq_recv.shape[0]
    me = lax.axis_index("seq")
    mine = lax.axis_index("chan")
    mesh_ids = pl.DeviceIdType.MESH
    barrier = pltpu.get_barrier_semaphore()

    def greet(step, carry):
        peer = lax.rem(me + step, count)
        pl.semaphore_signal(barrier, inc=1, device_id={"seq": peer}, device_id_type=mesh_ids)
        return carry

    lax.fori_loop(1, count, greet, 0)
    for step in range(1, chans):
        peer = lax.rem(mine + step, chans)
        pl.semaphore_signal(barrier, inc=1, device_id={"chan": peer}, device_id_type=mesh_ids)
    feat = feat_ref[...].astype(jnp.float32)
    part = jnp.sum(jnp.transpose(feat * feat), axis=0, keepdims=True)
    sq_mine[...] = jnp.broadcast_to(part, sq_mine.shape)
    pl.semaphore_wait(barrier, count + chans - 2)

    def seq_copy(source, target, sems, step):
        peer = lax.rem(me + step, count)
        return pltpu.make_async_remote_copy(
            source(peer), target, sems.at[0, step], sems.at[1, step],
            device_id={"seq": peer}, device_id_type=mesh_ids,
        )

    def start_all(source, target, sems):
        def body(step, carry):
            seq_copy(source, target, sems, step).start()
            return carry
        lax.fori_loop(1, count, body, 0)

    def finish_all(source, target, sems):
        def body(step, carry):
            copy = seq_copy(source, target, sems, step)
            copy.wait_send()
            copy.wait_recv()
            return carry
        lax.fori_loop(1, count, body, 0)


    def chan_copy(step):
        peer = lax.rem(mine + step, chans)
        return pltpu.make_async_remote_copy(
            sq_mine, sq_recv.at[mine], chan_sems.at[0, step], chan_sems.at[1, step],
            device_id={"chan": peer}, device_id_type=mesh_ids,
        )

    for step in range(1, chans):
        chan_copy(step).start()
    spec_src = lambda peer: spec_ref.at[peer]
    spec_own = pltpu.make_async_copy(spec_ref.at[me], spec_recv.at[me], own_sems.at[0])
    spec_own.start()
    start_all(spec_src, spec_recv.at[me], spec_sems)
    for step in range(1, chans):
        copy = chan_copy(step)
        copy.wait_send()
        copy.wait_recv()
    total = part
    for step in range(1, chans):
        other = lax.rem(mine + step, chans)
        total = total + sq_recv[other][0:1, :]
    scale = lax.rsqrt(total / CHANNELS + 1e-06)
    scale = jnp.transpose(jnp.broadcast_to(scale, (8, scale.shape[1])))[:, 0:1]
    signal = (feat * scale * gain_ref[...] * gate_ref[...].astype(jnp.float32)).astype(jnp.bfloat16)
    sig_out[...] = signal
    wide = signal.astype(jnp.float32)
    lanes = wide.shape[1]
    pair = lanes // count
    tiles = wide.shape[0] // lanes
    chunk = pair * tiles
    for tile in range(tiles):
        sig_turn[...] = jnp.transpose(wide[lanes * tile:lanes * (tile + 1), :])
        for chan in range(pair):
            rows = sig_turn[pl.ds(chan, count, stride=pair), :]
            sig_send[pl.ds(tiles * chan + tile, count, stride=chunk), :] = rows

    def rows_of(buffer):
        return lambda peer: buffer.at[pl.ds(pl.multiple_of(peer * chunk, chunk), chunk)]

    sig_own = pltpu.make_async_copy(rows_of(sig_send)(me), rows_of(sig_recv)(me), own_sems.at[1])
    sig_own.start()
    start_all(rows_of(sig_send), rows_of(sig_recv)(me), sig_sems)
    finish_all(rows_of(sig_send), rows_of(sig_recv)(me), sig_sems)
    sig_own.wait()

    for chan in range(pair):
        for tile in range(tiles):
            rows = sig_recv[pl.ds(tiles * chan + tile, count, stride=chunk), :]
            cols[chan, pl.ds(tile, count, stride=tiles), :] = rows

    first_len = tc_ref.shape[0]
    for load in loads:
        load.wait()
    boths = []
    for chan in range(pair):
        signal_cols = cols[chan].astype(jnp.bfloat16)
        boths.append(jnp.dot(st_hi[...], signal_cols, preferred_element_type=jnp.float32))

    cos_twist, sin_twist = tc_ref[...], ts_ref[...]
    own_rows = first_len // count
    freqs = []
    for chan in range(pair):
        p_cos = boths[chan][:first_len]
        p_sin = boths[chan][first_len:]
        twist_re = p_cos * cos_twist - p_sin * sin_twist
        twist_im = -p_sin * cos_twist - p_cos * sin_twist
        freqs.append(dot3(twist_re, (fa_hi[...], fa_lo[...])) + dot3(twist_im, (fb_hi[...], fb_lo[...])))

    finish_all(spec_src, spec_recv.at[me], spec_sems)
    spec_own.wait()

    for chan in range(pair):
        freq = freqs[chan]
        freq_re, freq_im = freq[:, :lanes], freq[:, lanes:]
        filt = []
        for part_of in range(2):
            block = spec_recv[:, pl.ds((2 * chan + part_of) * own_rows, own_rows), :]
            filt.append(block.astype(jnp.float32).reshape(first_len, lanes))
        filt_re, filt_im = filt
        prod_re = freq_re * filt_re - freq_im * filt_im
        prod_im = freq_re * filt_im + freq_im * filt_re
        back = dot3(prod_re, (ia_hi[...], ia_lo[...])) + dot3(prod_im, (ib_hi[...], ib_lo[...]))
        back_re, back_im = back[:, :lanes], back[:, lanes:]
        untwist_re = back_re * cos_twist - back_im * sin_twist
        untwist_im = back_im * cos_twist + back_re * sin_twist
        conv_one[...] = dot3((lc_hi[...], lc_lo[...]), untwist_re) + dot3((ls_hi[...], ls_lo[...]), untwist_im)
        for tile in range(tiles):
            rows = conv_one[pl.ds(tile, count, stride=tiles), :]
            conv_send[pl.ds(tiles * chan + tile, count, stride=chunk), :] = rows

    res_src = rows_of(conv_send)
    res_own = pltpu.make_async_copy(res_src(me), res_recv.at[me], own_sems.at[2])
    res_own.start()
    start_all(res_src, res_recv.at[me], res_sems)
    finish_all(res_src, res_recv.at[me], res_sems)
    res_own.wait()


def whole(features, pre_gate, gain_row, spec_rows, tables, chans):
    count = spec_rows.shape[0]
    length, width = features.shape
    pair = width // count
    lanes = 128
    chunk = pair * length // lanes
    vmem = pl.BlockSpec(memory_space=pltpu.VMEM)
    operands = (features, pre_gate, gain_row, spec_rows) + tuple(tables)
    hbm = pl.BlockSpec(memory_space=pl.ANY)
    return pl.pallas_call(
        whole_kernel,
        out_shape=(
            jax.ShapeDtypeStruct((length, width), jnp.bfloat16),
            jax.ShapeDtypeStruct((count, chunk, lanes), jnp.float32),
        ),
        in_specs=[hbm] * len(operands),
        out_specs=(vmem, vmem),
        scratch_shapes=[
            pltpu.VMEM((8, length), jnp.float32),
            pltpu.VMEM((chans, 8, length), jnp.float32),
            pltpu.VMEM((lanes, lanes), jnp.float32),
            pltpu.VMEM((count * chunk, lanes), jnp.float32),
            pltpu.VMEM((count * chunk, lanes), jnp.float32),
            pltpu.VMEM(spec_rows.shape, spec_rows.dtype),
            pltpu.VMEM((pair, count * chunk // pair, lanes), jnp.float32),
            pltpu.VMEM((count * chunk // pair, lanes), jnp.float32),
            pltpu.VMEM((count * chunk, lanes), jnp.float32),
            pltpu.SemaphoreType.DMA((2, count)),
            pltpu.SemaphoreType.DMA((2, count)),
            pltpu.SemaphoreType.DMA((2, count)),
            pltpu.SemaphoreType.DMA((2, chans)),
            pltpu.SemaphoreType.DMA((3,)),
            pltpu.SemaphoreType.DMA((len(operands),)),
        ]
        + [pltpu.VMEM(table.shape, table.dtype) for table in operands],
        compiler_params=pltpu.CompilerParams(
            collective_id=0, has_side_effects=True, vmem_limit_bytes=67043328
        ),
    )(*operands)


def dft_tables(seq_count, tok_rows):
    stride = 2 * seq_count
    first_len = stride * ROW_GROUP
    all_bins = stride * tok_rows
    second_len = all_bins // first_len
    half_first = first_len // 2
    row_bins = bin_rows(seq_count).astype(np.int64)
    first_turn = (row_bins[:, None] * np.arange(half_first)[None, :]) % first_len * (2.0 * np.pi / first_len)
    cos_first, sin_first = np.cos(first_turn), np.sin(first_turn)
    twist_turn = (row_bins[:, None] * np.arange(second_len)[None, :]) % all_bins * (2.0 * np.pi / all_bins)
    second_in = np.arange(second_len)
    second_turn = (second_in[:, None] * second_in[None, :]) % second_len * (2.0 * np.pi / second_len)
    cos_second, sin_second = np.cos(second_turn), np.sin(second_turn)

    def pair_of(array):
        array = array.astype(np.float32)
        high = array.astype(jnp.bfloat16)
        return [jnp.asarray(high), jnp.asarray((array - high.astype(np.float32)).astype(jnp.bfloat16))]

    tables = pair_of(np.concatenate([cos_first, sin_first], 0))
    tables += [jnp.asarray(np.cos(twist_turn).astype(np.float32)), jnp.asarray(np.sin(twist_turn).astype(np.float32))]
    tables += pair_of(np.concatenate([cos_second, -sin_second], 1))
    tables += pair_of(np.concatenate([sin_second, cos_second], 1))
    tables += pair_of(np.concatenate([cos_second, sin_second], 1))
    tables += pair_of(np.concatenate([-sin_second, cos_second], 1))
    tables += pair_of(cos_first.T / all_bins)
    tables += pair_of(-sin_first.T / all_bins)
    return tables


def local(features, pre_gate, post_gate, norm_gain, skip_weight, spectrum):
    tok_rows, chan_width = features.shape
    seq_count = lax.axis_size("seq")
    chans = lax.axis_size("chan")
    group = chan_width // seq_count
    second_len = tok_rows // ROW_GROUP
    lanes = 128
    tok_tiles = tok_rows // lanes

    spec_rows = spectrum.reshape(2, 2, second_len, ROW_GROUP, chan_width)
    spec_rows = jnp.transpose(spec_rows, (4, 0, 1, 3, 2)).astype(jnp.bfloat16)
    spec_rows = spec_rows.reshape(seq_count, -1, second_len)
    signal, result = whole(
        features, pre_gate, norm_gain.reshape(1, chan_width), spec_rows,
        dft_tables(seq_count, tok_rows), chans,
    )
    result = result.reshape(seq_count, group, tok_tiles, lanes)
    result = jnp.transpose(result, (2, 3, 0, 1)).reshape(tok_rows, chan_width)
    gated = post_gate.astype(jnp.float32) * (result + skip_weight * signal.astype(jnp.float32))
    return gated.astype(jnp.bfloat16)


def solution(mesh):
    return jax.shard_map(
        local,
        mesh=mesh,
        in_specs=(
            P("seq", "chan"),
            P("seq", "chan"),
            P("seq", "chan"),
            P("chan"),
            P("chan"),
            P(None, "seq", None, "chan"),
        ),
        out_specs=P("seq", "chan"),
        check_vma=False,
    )
```

```python
import math

import jax
import jax.numpy as jnp
import numpy as np
from jax import lax
from jax.experimental import pallas as pl
from jax.experimental.pallas import tpu as pltpu
from jax.sharding import PartitionSpec as P

CHANNELS = 512
ROW_GROUP = 4
TABLE_NAMES = ("st_hi", "st_lo", "tc", "ts", "fa_hi", "fa_lo", "fb_hi", "fb_lo", "ia_hi", "ia_lo", "ib_hi", "ib_lo",
               "lc_hi", "lc_lo", "ls_hi", "ls_lo")
HIGH_DIGIT = 8


PRECISE = lax.Precision.HIGH
FULL_TURN = 2.0 * math.pi


def reversed_digits(count):
    levels = count.bit_length() - 1
    positions = np.arange(count)
    result = np.zeros(count, np.int64)
    for bit_pos in range(levels):
        result = result + ((positions >> bit_pos & 1) << levels - 1 - bit_pos)
    return result


def rotation(numerator, denominator):
    angle = (numerator % denominator).astype(jnp.float32) * (FULL_TURN / denominator)
    return (jnp.cos(angle), jnp.sin(angle))


def mm(spec, left, right):
    return jnp.einsum(spec, left, right, precision=PRECISE, preferred_element_type=jnp.float32)


def bin_rows(seq_count):
    digit_order = reversed_digits(seq_count)
    stride = 2 * seq_count
    slots = np.arange(stride)
    low_bins = 2 * digit_order[slots // 2] + slots % 2
    return (low_bins[:, None] + stride * np.arange(ROW_GROUP)[None, :]).reshape(-1).astype(np.int32)


def split(value):
    high = value.astype(jnp.bfloat16)
    return high, (value - high.astype(jnp.float32)).astype(jnp.bfloat16)


def dot3(left, right):
    if isinstance(left, tuple):
        d_hi, d_lo = split(right)
        out = jnp.dot(left[0], d_hi, preferred_element_type=jnp.float32)
        return out + jnp.dot(left[0], d_lo, preferred_element_type=jnp.float32)
    d_hi, d_lo = split(left)
    out = jnp.dot(d_hi, right[0], preferred_element_type=jnp.float32)
    return out + jnp.dot(d_lo, right[0], preferred_element_type=jnp.float32)


def whole_kernel(*refs):
    table_count = len(TABLE_NAMES) + 6
    held = refs[:table_count]
    gated_out = refs[table_count]
    (sq_mine, sq_recv, sig_turn, sig_send, sig_recv, spec_recv, cols, conv_one, conv_send, res_recv,
     spec_sems, sig_sems, res_sems, chan_sems, own_sems, table_sems) = refs[table_count + 1:table_count + 17]
    tables = refs[table_count + 17:]
    loads = [pltpu.make_async_copy(held[k], tables[k], table_sems.at[k]) for k in range(table_count)]
    for load in loads:
        load.start()
    for load in loads[:6]:
        load.wait()
    loads = loads[6:]
    feat_ref, gate_ref, gain_ref, spec_ref, post_ref, skip_ref = tables[:6]
    tables = tables[6:]
    (st_hi, st_lo, tc_ref, ts_ref, fa_hi, fa_lo, fb_hi, fb_lo, ia_hi, ia_lo, ib_hi, ib_lo,
     lc_hi, lc_lo, ls_hi, ls_lo) = tables
    count = spec_ref.shape[0]
    chans = sq_recv.shape[0]
    me = lax.axis_index("seq")
    mine = lax.axis_index("chan")
    mesh_ids = pl.DeviceIdType.MESH
    barrier = pltpu.get_barrier_semaphore()

    def greet(step, carry):
        peer = lax.rem(me + step, count)
        pl.semaphore_signal(barrier, inc=1, device_id={"seq": peer}, device_id_type=mesh_ids)
        return carry

    lax.fori_loop(1, count, greet, 0)
    for step in range(1, chans):
        peer = lax.rem(mine + step, chans)
        pl.semaphore_signal(barrier, inc=1, device_id={"chan": peer}, device_id_type=mesh_ids)
    feat = feat_ref[...].astype(jnp.float32)
    part = jnp.sum(jnp.transpose(feat * feat), axis=0, keepdims=True)
    sq_mine[...] = jnp.broadcast_to(part, sq_mine.shape)
    pl.semaphore_wait(barrier, count + chans - 2)

    def seq_copy(source, target, sems, step):
        peer = lax.rem(me + step, count)
        return pltpu.make_async_remote_copy(
            source(peer), target, sems.at[0, step], sems.at[1, step],
            device_id={"seq": peer}, device_id_type=mesh_ids,
        )

    def start_all(source, target, sems):
        def body(step, carry):
            seq_copy(source, target, sems, step).start()
            return carry
        lax.fori_loop(1, count, body, 0)

    def finish_all(source, target, sems):
        def body(step, carry):
            copy = seq_copy(source, target, sems, step)
            copy.wait_send()
            copy.wait_recv()
            return carry
        lax.fori_loop(1, count, body, 0)


    def chan_copy(step):
        peer = lax.rem(mine + step, chans)
        return pltpu.make_async_remote_copy(
            sq_mine, sq_recv.at[mine], chan_sems.at[0, step], chan_sems.at[1, step],
            device_id={"chan": peer}, device_id_type=mesh_ids,
        )

    for step in range(1, chans):
        chan_copy(step).start()
    spec_src = lambda peer: spec_ref.at[peer]
    spec_own = pltpu.make_async_copy(spec_ref.at[me], spec_recv.at[me], own_sems.at[0])
    spec_own.start()
    start_all(spec_src, spec_recv.at[me], spec_sems)
    for step in range(1, chans):
        copy = chan_copy(step)
        copy.wait_send()
        copy.wait_recv()
    total = part
    for step in range(1, chans):
        other = lax.rem(mine + step, chans)
        total = total + sq_recv[other][0:1, :]
    scale = lax.rsqrt(total / CHANNELS + 1e-06)
    scale = jnp.transpose(jnp.broadcast_to(scale, (8, scale.shape[1])))[:, 0:1]
    signal = (feat * scale * gain_ref[...] * gate_ref[...].astype(jnp.float32)).astype(jnp.bfloat16)
    wide = signal.astype(jnp.float32)
    lanes = wide.shape[1]
    pair = lanes // count
    tiles = wide.shape[0] // lanes
    chunk = pair * tiles
    for tile in range(tiles):
        sig_turn[...] = jnp.transpose(wide[lanes * tile:lanes * (tile + 1), :])
        for chan in range(pair):
            rows = sig_turn[pl.ds(chan, count, stride=pair), :]
            sig_send[pl.ds(tiles * chan + tile, count, stride=chunk), :] = rows

    def rows_of(buffer):
        return lambda peer: buffer.at[pl.ds(pl.multiple_of(peer * chunk, chunk), chunk)]

    sig_own = pltpu.make_async_copy(rows_of(sig_send)(me), rows_of(sig_recv)(me), own_sems.at[1])
    sig_own.start()
    start_all(rows_of(sig_send), rows_of(sig_recv)(me), sig_sems)
    finish_all(rows_of(sig_send), rows_of(sig_recv)(me), sig_sems)
    sig_own.wait()

    for chan in range(pair):
        for tile in range(tiles):
            rows = sig_recv[pl.ds(tiles * chan + tile, count, stride=chunk), :]
            cols[chan, pl.ds(tile, count, stride=tiles), :] = rows

    first_len = tc_ref.shape[0]
    for load in loads:
        load.wait()
    boths = []
    for chan in range(pair):
        signal_cols = cols[chan].astype(jnp.bfloat16)
        boths.append(jnp.dot(st_hi[...], signal_cols, preferred_element_type=jnp.float32))

    cos_twist, sin_twist = tc_ref[...], ts_ref[...]
    own_rows = first_len // count
    freqs = []
    for chan in range(pair):
        p_cos = boths[chan][:first_len]
        p_sin = boths[chan][first_len:]
        twist_re = p_cos * cos_twist - p_sin * sin_twist
        twist_im = -p_sin * cos_twist - p_cos * sin_twist
        freqs.append(dot3(twist_re, (fa_hi[...], fa_lo[...])) + dot3(twist_im, (fb_hi[...], fb_lo[...])))

    finish_all(spec_src, spec_recv.at[me], spec_sems)
    spec_own.wait()

    for chan in range(pair):
        freq = freqs[chan]
        freq_re, freq_im = freq[:, :lanes], freq[:, lanes:]
        filt = []
        for part_of in range(2):
            block = spec_recv[:, pl.ds((2 * chan + part_of) * own_rows, own_rows), :]
            filt.append(block.astype(jnp.float32).reshape(first_len, lanes))
        filt_re, filt_im = filt
        prod_re = freq_re * filt_re - freq_im * filt_im
        prod_im = freq_re * filt_im + freq_im * filt_re
        back = dot3(prod_re, (ia_hi[...], ia_lo[...])) + dot3(prod_im, (ib_hi[...], ib_lo[...]))
        back_re, back_im = back[:, :lanes], back[:, lanes:]
        untwist_re = back_re * cos_twist - back_im * sin_twist
        untwist_im = back_im * cos_twist + back_re * sin_twist
        conv_one[...] = dot3((lc_hi[...], lc_lo[...]), untwist_re) + dot3((ls_hi[...], ls_lo[...]), untwist_im)
        for tile in range(tiles):
            rows = conv_one[pl.ds(tile, count, stride=tiles), :]
            conv_send[pl.ds(tiles * chan + tile, count, stride=chunk), :] = rows

    res_src = rows_of(conv_send)
    res_dst = rows_of(res_recv)(me)
    res_own = pltpu.make_async_copy(res_src(me), res_dst, own_sems.at[2])
    res_own.start()
    start_all(res_src, res_dst, res_sems)
    finish_all(res_src, res_dst, res_sems)
    res_own.wait()

    skip = skip_ref[...]
    for tile in range(tiles):
        for chan in range(pair):
            sig_turn[pl.ds(chan, count, stride=pair), :] = res_recv[pl.ds(tiles * chan + tile, count, stride=chunk), :]
        block = jnp.transpose(sig_turn[...])
        these = slice(lanes * tile, lanes * (tile + 1))
        direct = signal[these, :].astype(jnp.float32)
        gated = post_ref[these, :].astype(jnp.float32) * (block + skip * direct)
        gated_out[these, :] = gated.astype(gated_out.dtype)


def whole(features, pre_gate, gain_row, spec_rows, post_gate, skip_row, tables, chans):
    count = spec_rows.shape[0]
    length, width = features.shape
    pair = width // count
    lanes = 128
    chunk = pair * length // lanes
    vmem = pl.BlockSpec(memory_space=pltpu.VMEM)
    operands = (features, pre_gate, gain_row, spec_rows, post_gate, skip_row) + tuple(tables)
    hbm = pl.BlockSpec(memory_space=pl.ANY)
    return pl.pallas_call(
        whole_kernel,
        out_shape=jax.ShapeDtypeStruct((length, width), jnp.bfloat16),
        in_specs=[hbm] * len(operands),
        out_specs=vmem,
        scratch_shapes=[
            pltpu.VMEM((8, length), jnp.float32),
            pltpu.VMEM((chans, 8, length), jnp.float32),
            pltpu.VMEM((lanes, lanes), jnp.float32),
            pltpu.VMEM((count * chunk, lanes), jnp.float32),
            pltpu.VMEM((count * chunk, lanes), jnp.float32),
            pltpu.VMEM(spec_rows.shape, spec_rows.dtype),
            pltpu.VMEM((pair, count * chunk // pair, lanes), jnp.float32),
            pltpu.VMEM((count * chunk // pair, lanes), jnp.float32),
            pltpu.VMEM((count * chunk, lanes), jnp.float32),
            pltpu.VMEM((count * chunk, lanes), jnp.float32),
            pltpu.SemaphoreType.DMA((2, count)),
            pltpu.SemaphoreType.DMA((2, count)),
            pltpu.SemaphoreType.DMA((2, count)),
            pltpu.SemaphoreType.DMA((2, chans)),
            pltpu.SemaphoreType.DMA((3,)),
            pltpu.SemaphoreType.DMA((len(operands),)),
        ]
        + [pltpu.VMEM(table.shape, table.dtype) for table in operands],
        compiler_params=pltpu.CompilerParams(
            collective_id=0, has_side_effects=True, vmem_limit_bytes=67043328
        ),
    )(*operands)


def dft_tables(seq_count, tok_rows):
    stride = 2 * seq_count
    first_len = stride * ROW_GROUP
    all_bins = stride * tok_rows
    second_len = all_bins // first_len
    half_first = first_len // 2
    row_bins = bin_rows(seq_count).astype(np.int64)
    first_turn = (row_bins[:, None] * np.arange(half_first)[None, :]) % first_len * (2.0 * np.pi / first_len)
    cos_first, sin_first = np.cos(first_turn), np.sin(first_turn)
    twist_turn = (row_bins[:, None] * np.arange(second_len)[None, :]) % all_bins * (2.0 * np.pi / all_bins)
    second_in = np.arange(second_len)
    second_turn = (second_in[:, None] * second_in[None, :]) % second_len * (2.0 * np.pi / second_len)
    cos_second, sin_second = np.cos(second_turn), np.sin(second_turn)

    def pair_of(array):
        array = array.astype(np.float32)
        high = array.astype(jnp.bfloat16)
        return [jnp.asarray(high), jnp.asarray((array - high.astype(np.float32)).astype(jnp.bfloat16))]

    tables = pair_of(np.concatenate([cos_first, sin_first], 0))
    tables += [jnp.asarray(np.cos(twist_turn).astype(np.float32)), jnp.asarray(np.sin(twist_turn).astype(np.float32))]
    tables += pair_of(np.concatenate([cos_second, -sin_second], 1))
    tables += pair_of(np.concatenate([sin_second, cos_second], 1))
    tables += pair_of(np.concatenate([cos_second, sin_second], 1))
    tables += pair_of(np.concatenate([-sin_second, cos_second], 1))
    tables += pair_of(cos_first.T / all_bins)
    tables += pair_of(-sin_first.T / all_bins)
    return tables


def local(features, pre_gate, post_gate, norm_gain, skip_weight, spectrum):
    tok_rows, chan_width = features.shape
    seq_count = lax.axis_size("seq")
    chans = lax.axis_size("chan")
    group = chan_width // seq_count
    second_len = tok_rows // ROW_GROUP
    lanes = 128
    tok_tiles = tok_rows // lanes

    spec_rows = spectrum.reshape(2, 2, second_len, ROW_GROUP, chan_width)
    spec_rows = jnp.transpose(spec_rows, (4, 0, 1, 3, 2)).astype(jnp.bfloat16)
    spec_rows = spec_rows.reshape(seq_count, -1, second_len)
    return whole(
        features, pre_gate, norm_gain.reshape(1, chan_width), spec_rows,
        post_gate, skip_weight.reshape(1, chan_width), dft_tables(seq_count, tok_rows), chans,
    )


def solution(mesh):
    return jax.shard_map(
        local,
        mesh=mesh,
        in_specs=(
            P("seq", "chan"),
            P("seq", "chan"),
            P("seq", "chan"),
            P("chan"),
            P("chan"),
            P(None, "seq", None, "chan"),
        ),
        out_specs=P("seq", "chan"),
        check_vma=False,
    )
```

```python
import math

import jax
import jax.numpy as jnp
import numpy as np
from jax import lax
from jax.experimental import pallas as pl
from jax.experimental.pallas import tpu as pltpu
from jax.sharding import PartitionSpec as P

CHANNELS = 512
ROW_GROUP = 4
TABLE_NAMES = ("st_hi", "st_lo", "tc", "ts", "fa_hi", "fa_lo", "fb_hi", "fb_lo", "ia_hi", "ia_lo", "ib_hi", "ib_lo",
               "lc_hi", "lc_lo", "ls_hi", "ls_lo")
HIGH_DIGIT = 8


PRECISE = lax.Precision.HIGH
FULL_TURN = 2.0 * math.pi


def reversed_digits(count):
    levels = count.bit_length() - 1
    positions = np.arange(count)
    result = np.zeros(count, np.int64)
    for bit_pos in range(levels):
        result = result + ((positions >> bit_pos & 1) << levels - 1 - bit_pos)
    return result


def rotation(numerator, denominator):
    angle = (numerator % denominator).astype(jnp.float32) * (FULL_TURN / denominator)
    return (jnp.cos(angle), jnp.sin(angle))


def mm(spec, left, right):
    return jnp.einsum(spec, left, right, precision=PRECISE, preferred_element_type=jnp.float32)


def bin_rows(seq_count):
    digit_order = reversed_digits(seq_count)
    stride = 2 * seq_count
    slots = np.arange(stride)
    low_bins = 2 * digit_order[slots // 2] + slots % 2
    return (low_bins[:, None] + stride * np.arange(ROW_GROUP)[None, :]).reshape(-1).astype(np.int32)


def split(value):
    high = value.astype(jnp.bfloat16)
    return high, (value - high.astype(jnp.float32)).astype(jnp.bfloat16)


def dot3(left, right):
    if isinstance(left, tuple):
        d_hi, d_lo = split(right)
        out = jnp.dot(left[0], d_hi, preferred_element_type=jnp.float32)
        return out + jnp.dot(left[0], d_lo, preferred_element_type=jnp.float32)
    d_hi, d_lo = split(left)
    out = jnp.dot(d_hi, right[0], preferred_element_type=jnp.float32)
    return out + jnp.dot(d_lo, right[0], preferred_element_type=jnp.float32)


def whole_kernel(*refs):
    table_count = len(TABLE_NAMES) + 6
    held = refs[:table_count]
    gated_out = refs[table_count]
    (sq_mine, sq_recv, sig_turn, sig_send, sig_recv, spec_recv, cols, conv_one, conv_send, res_recv,
     spec_sems, sig_sems, res_sems, chan_sems, own_sems, table_sems) = refs[table_count + 1:table_count + 17]
    tables = refs[table_count + 17:]
    loads = [pltpu.make_async_copy(held[k], tables[k], table_sems.at[k]) for k in range(table_count)]
    for load in loads:
        load.start()
    inputs = loads[:6]
    loads = loads[6:]
    feat_ref, gate_ref, gain_ref, spec_ref, post_ref, skip_ref = tables[:6]
    tables = tables[6:]
    (st_hi, st_lo, tc_ref, ts_ref, fa_hi, fa_lo, fb_hi, fb_lo, ia_hi, ia_lo, ib_hi, ib_lo,
     lc_hi, lc_lo, ls_hi, ls_lo) = tables
    count = spec_ref.shape[0]
    chans = sq_recv.shape[0]
    me = lax.axis_index("seq")
    mine = lax.axis_index("chan")
    mesh_ids = pl.DeviceIdType.MESH
    barrier = pltpu.get_barrier_semaphore()

    def greet(step, carry):
        peer = lax.rem(me + step, count)
        pl.semaphore_signal(barrier, inc=1, device_id={"seq": peer}, device_id_type=mesh_ids)
        return carry

    lax.fori_loop(1, count, greet, 0)
    for step in range(1, chans):
        peer = lax.rem(mine + step, chans)
        pl.semaphore_signal(barrier, inc=1, device_id={"chan": peer}, device_id_type=mesh_ids)
    inputs[0].wait()
    feat = feat_ref[...].astype(jnp.float32)
    part = jnp.sum(jnp.transpose(feat * feat), axis=0, keepdims=True)
    sq_mine[...] = jnp.broadcast_to(part, sq_mine.shape)
    pl.semaphore_wait(barrier, count + chans - 2)

    def seq_copy(source, target, sems, step):
        peer = lax.rem(me + step, count)
        return pltpu.make_async_remote_copy(
            source(peer), target, sems.at[0, step], sems.at[1, step],
            device_id={"seq": peer}, device_id_type=mesh_ids,
        )

    def start_all(source, target, sems):
        def body(step, carry):
            seq_copy(source, target, sems, step).start()
            return carry
        lax.fori_loop(1, count, body, 0)

    def finish_all(source, target, sems):
        def body(step, carry):
            copy = seq_copy(source, target, sems, step)
            copy.wait_send()
            copy.wait_recv()
            return carry
        lax.fori_loop(1, count, body, 0)


    def chan_copy(step):
        peer = lax.rem(mine + step, chans)
        return pltpu.make_async_remote_copy(
            sq_mine, sq_recv.at[mine], chan_sems.at[0, step], chan_sems.at[1, step],
            device_id={"chan": peer}, device_id_type=mesh_ids,
        )

    for step in range(1, chans):
        chan_copy(step).start()
    inputs[3].wait()
    spec_src = lambda peer: spec_ref.at[peer]
    spec_own = pltpu.make_async_copy(spec_ref.at[me], spec_recv.at[me], own_sems.at[0])
    spec_own.start()
    start_all(spec_src, spec_recv.at[me], spec_sems)
    for step in range(1, chans):
        copy = chan_copy(step)
        copy.wait_send()
        copy.wait_recv()
    total = part
    for step in range(1, chans):
        other = lax.rem(mine + step, chans)
        total = total + sq_recv[other][0:1, :]
    inputs[1].wait()
    inputs[2].wait()
    scale = lax.rsqrt(total / CHANNELS + 1e-06)
    scale = jnp.transpose(jnp.broadcast_to(scale, (8, scale.shape[1])))[:, 0:1]
    signal = (feat * scale * gain_ref[...] * gate_ref[...].astype(jnp.float32)).astype(jnp.bfloat16)
    wide = signal.astype(jnp.float32)
    lanes = wide.shape[1]
    pair = lanes // count
    tiles = wide.shape[0] // lanes
    chunk = pair * tiles
    for tile in range(tiles):
        sig_turn[...] = jnp.transpose(wide[lanes * tile:lanes * (tile + 1), :])
        for chan in range(pair):
            rows = sig_turn[pl.ds(chan, count, stride=pair), :]
            sig_send[pl.ds(tiles * chan + tile, count, stride=chunk), :] = rows

    def rows_of(buffer):
        return lambda peer: buffer.at[pl.ds(pl.multiple_of(peer * chunk, chunk), chunk)]

    sig_own = pltpu.make_async_copy(rows_of(sig_send)(me), rows_of(sig_recv)(me), own_sems.at[1])
    sig_own.start()
    start_all(rows_of(sig_send), rows_of(sig_recv)(me), sig_sems)
    finish_all(rows_of(sig_send), rows_of(sig_recv)(me), sig_sems)
    sig_own.wait()

    for chan in range(pair):
        for tile in range(tiles):
            rows = sig_recv[pl.ds(tiles * chan + tile, count, stride=chunk), :]
            cols[chan, pl.ds(tile, count, stride=tiles), :] = rows

    first_len = tc_ref.shape[0]
    for load in loads:
        load.wait()
    boths = []
    for chan in range(pair):
        signal_cols = cols[chan].astype(jnp.bfloat16)
        boths.append(jnp.dot(st_hi[...], signal_cols, preferred_element_type=jnp.float32))

    cos_twist, sin_twist = tc_ref[...], ts_ref[...]
    own_rows = first_len // count
    freqs = []
    for chan in range(pair):
        p_cos = boths[chan][:first_len]
        p_sin = boths[chan][first_len:]
        twist_re = p_cos * cos_twist - p_sin * sin_twist
        twist_im = -p_sin * cos_twist - p_cos * sin_twist
        freqs.append(dot3(twist_re, (fa_hi[...], fa_lo[...])) + dot3(twist_im, (fb_hi[...], fb_lo[...])))

    finish_all(spec_src, spec_recv.at[me], spec_sems)
    spec_own.wait()

    for chan in range(pair):
        freq = freqs[chan]
        freq_re, freq_im = freq[:, :lanes], freq[:, lanes:]
        filt = []
        for part_of in range(2):
            block = spec_recv[:, pl.ds((2 * chan + part_of) * own_rows, own_rows), :]
            filt.append(block.astype(jnp.float32).reshape(first_len, lanes))
        filt_re, filt_im = filt
        prod_re = freq_re * filt_re - freq_im * filt_im
        prod_im = freq_re * filt_im + freq_im * filt_re
        back = dot3(prod_re, (ia_hi[...], ia_lo[...])) + dot3(prod_im, (ib_hi[...], ib_lo[...]))
        back_re, back_im = back[:, :lanes], back[:, lanes:]
        untwist_re = back_re * cos_twist - back_im * sin_twist
        untwist_im = back_im * cos_twist + back_re * sin_twist
        conv_one[...] = dot3((lc_hi[...], lc_lo[...]), untwist_re) + dot3((ls_hi[...], ls_lo[...]), untwist_im)
        for tile in range(tiles):
            rows = conv_one[pl.ds(tile, count, stride=tiles), :]
            conv_send[pl.ds(tiles * chan + tile, count, stride=chunk), :] = rows

    res_src = rows_of(conv_send)
    res_dst = rows_of(res_recv)(me)
    res_own = pltpu.make_async_copy(res_src(me), res_dst, own_sems.at[2])
    res_own.start()
    start_all(res_src, res_dst, res_sems)
    finish_all(res_src, res_dst, res_sems)
    res_own.wait()

    inputs[4].wait()
    inputs[5].wait()
    skip = skip_ref[...]
    for tile in range(tiles):
        for chan in range(pair):
            sig_turn[pl.ds(chan, count, stride=pair), :] = res_recv[pl.ds(tiles * chan + tile, count, stride=chunk), :]
        block = jnp.transpose(sig_turn[...])
        these = slice(lanes * tile, lanes * (tile + 1))
        direct = signal[these, :].astype(jnp.float32)
        gated = post_ref[these, :].astype(jnp.float32) * (block + skip * direct)
        gated_out[these, :] = gated.astype(gated_out.dtype)


def whole(features, pre_gate, gain_row, spec_rows, post_gate, skip_row, tables, chans):
    count = spec_rows.shape[0]
    length, width = features.shape
    pair = width // count
    lanes = 128
    chunk = pair * length // lanes
    vmem = pl.BlockSpec(memory_space=pltpu.VMEM)
    operands = (features, pre_gate, gain_row, spec_rows, post_gate, skip_row) + tuple(tables)
    hbm = pl.BlockSpec(memory_space=pl.ANY)
    return pl.pallas_call(
        whole_kernel,
        out_shape=jax.ShapeDtypeStruct((length, width), jnp.bfloat16),
        in_specs=[hbm] * len(operands),
        out_specs=vmem,
        scratch_shapes=[
            pltpu.VMEM((8, length), jnp.float32),
            pltpu.VMEM((chans, 8, length), jnp.float32),
            pltpu.VMEM((lanes, lanes), jnp.float32),
            pltpu.VMEM((count * chunk, lanes), jnp.float32),
            pltpu.VMEM((count * chunk, lanes), jnp.float32),
            pltpu.VMEM(spec_rows.shape, spec_rows.dtype),
            pltpu.VMEM((pair, count * chunk // pair, lanes), jnp.float32),
            pltpu.VMEM((count * chunk // pair, lanes), jnp.float32),
            pltpu.VMEM((count * chunk, lanes), jnp.float32),
            pltpu.VMEM((count * chunk, lanes), jnp.float32),
            pltpu.SemaphoreType.DMA((2, count)),
            pltpu.SemaphoreType.DMA((2, count)),
            pltpu.SemaphoreType.DMA((2, count)),
            pltpu.SemaphoreType.DMA((2, chans)),
            pltpu.SemaphoreType.DMA((3,)),
            pltpu.SemaphoreType.DMA((len(operands),)),
        ]
        + [pltpu.VMEM(table.shape, table.dtype) for table in operands],
        compiler_params=pltpu.CompilerParams(
            collective_id=0, has_side_effects=True, vmem_limit_bytes=67043328
        ),
    )(*operands)


def dft_tables(seq_count, tok_rows):
    stride = 2 * seq_count
    first_len = stride * ROW_GROUP
    all_bins = stride * tok_rows
    second_len = all_bins // first_len
    half_first = first_len // 2
    row_bins = bin_rows(seq_count).astype(np.int64)
    first_turn = (row_bins[:, None] * np.arange(half_first)[None, :]) % first_len * (2.0 * np.pi / first_len)
    cos_first, sin_first = np.cos(first_turn), np.sin(first_turn)
    twist_turn = (row_bins[:, None] * np.arange(second_len)[None, :]) % all_bins * (2.0 * np.pi / all_bins)
    second_in = np.arange(second_len)
    second_turn = (second_in[:, None] * second_in[None, :]) % second_len * (2.0 * np.pi / second_len)
    cos_second, sin_second = np.cos(second_turn), np.sin(second_turn)

    def pair_of(array):
        array = array.astype(np.float32)
        high = array.astype(jnp.bfloat16)
        return [jnp.asarray(high), jnp.asarray((array - high.astype(np.float32)).astype(jnp.bfloat16))]

    tables = pair_of(np.concatenate([cos_first, sin_first], 0))
    tables += [jnp.asarray(np.cos(twist_turn).astype(np.float32)), jnp.asarray(np.sin(twist_turn).astype(np.float32))]
    tables += pair_of(np.concatenate([cos_second, -sin_second], 1))
    tables += pair_of(np.concatenate([sin_second, cos_second], 1))
    tables += pair_of(np.concatenate([cos_second, sin_second], 1))
    tables += pair_of(np.concatenate([-sin_second, cos_second], 1))
    tables += pair_of(cos_first.T / all_bins)
    tables += pair_of(-sin_first.T / all_bins)
    return tables


def local(features, pre_gate, post_gate, norm_gain, skip_weight, spectrum):
    tok_rows, chan_width = features.shape
    seq_count = lax.axis_size("seq")
    chans = lax.axis_size("chan")
    group = chan_width // seq_count
    second_len = tok_rows // ROW_GROUP
    lanes = 128
    tok_tiles = tok_rows // lanes

    spec_rows = spectrum.reshape(2, 2, second_len, ROW_GROUP, chan_width)
    spec_rows = jnp.transpose(spec_rows, (4, 0, 1, 3, 2)).astype(jnp.bfloat16)
    spec_rows = spec_rows.reshape(seq_count, -1, second_len)
    return whole(
        features, pre_gate, norm_gain.reshape(1, chan_width), spec_rows,
        post_gate, skip_weight.reshape(1, chan_width), dft_tables(seq_count, tok_rows), chans,
    )


def solution(mesh):
    return jax.shard_map(
        local,
        mesh=mesh,
        in_specs=(
            P("seq", "chan"),
            P("seq", "chan"),
            P("seq", "chan"),
            P("chan"),
            P("chan"),
            P(None, "seq", None, "chan"),
        ),
        out_specs=P("seq", "chan"),
        check_vma=False,
    )
```

```python
import math

import jax
import jax.numpy as jnp
import numpy as np
from jax import lax
from jax.experimental import pallas as pl
from jax.experimental.pallas import tpu as pltpu
from jax.sharding import PartitionSpec as P

CHANNELS = 512
ROW_GROUP = 4
TABLE_NAMES = ("st_hi", "st_lo", "tc", "ts", "fa_hi", "fa_lo", "fb_hi", "fb_lo", "ia_hi", "ia_lo", "ib_hi", "ib_lo",
               "lc_hi", "lc_lo", "ls_hi", "ls_lo")
HIGH_DIGIT = 8


PRECISE = lax.Precision.HIGH
FULL_TURN = 2.0 * math.pi


def reversed_digits(count):
    levels = count.bit_length() - 1
    positions = np.arange(count)
    result = np.zeros(count, np.int64)
    for bit_pos in range(levels):
        result = result + ((positions >> bit_pos & 1) << levels - 1 - bit_pos)
    return result


def rotation(numerator, denominator):
    angle = (numerator % denominator).astype(jnp.float32) * (FULL_TURN / denominator)
    return (jnp.cos(angle), jnp.sin(angle))


def mm(spec, left, right):
    return jnp.einsum(spec, left, right, precision=PRECISE, preferred_element_type=jnp.float32)


def bin_rows(seq_count):
    digit_order = reversed_digits(seq_count)
    stride = 2 * seq_count
    slots = np.arange(stride)
    low_bins = 2 * digit_order[slots // 2] + slots % 2
    return (low_bins[:, None] + stride * np.arange(ROW_GROUP)[None, :]).reshape(-1).astype(np.int32)


def split(value):
    high = value.astype(jnp.bfloat16)
    return high, (value - high.astype(jnp.float32)).astype(jnp.bfloat16)


def dot3(left, right):
    if isinstance(left, tuple):
        d_hi, d_lo = split(right)
        out = jnp.dot(left[0], d_hi, preferred_element_type=jnp.float32)
        return out + jnp.dot(left[0], d_lo, preferred_element_type=jnp.float32)
    d_hi, d_lo = split(left)
    out = jnp.dot(d_hi, right[0], preferred_element_type=jnp.float32)
    return out + jnp.dot(d_lo, right[0], preferred_element_type=jnp.float32)


def whole_kernel(*refs):
    table_count = len(TABLE_NAMES) + 6
    held = refs[:table_count]
    gated_out = refs[table_count]
    (sq_mine, sq_recv, sig_turn, sig_send, sig_recv, spec_recv, cols, conv_one, conv_send, res_recv,
     spec_sems, sig_sems, res_sems, chan_sems, own_sems, table_sems) = refs[table_count + 1:table_count + 17]
    tables = refs[table_count + 17:]
    loads = [pltpu.make_async_copy(held[k], tables[k], table_sems.at[k]) for k in range(table_count)]
    for load in loads:
        load.start()
    inputs = loads[:6]
    loads = loads[6:]
    feat_ref, gate_ref, gain_ref, spec_ref, post_ref, skip_ref = tables[:6]
    tables = tables[6:]
    (st_hi, st_lo, tc_ref, ts_ref, fa_hi, fa_lo, fb_hi, fb_lo, ia_hi, ia_lo, ib_hi, ib_lo,
     lc_hi, lc_lo, ls_hi, ls_lo) = tables
    count = spec_ref.shape[0]
    chans = sq_recv.shape[0]
    me = lax.axis_index("seq")
    mine = lax.axis_index("chan")
    mesh_ids = pl.DeviceIdType.MESH
    barrier = pltpu.get_barrier_semaphore()

    def greet(step, carry):
        peer = lax.rem(me + step, count)
        pl.semaphore_signal(barrier, inc=1, device_id={"seq": peer}, device_id_type=mesh_ids)
        return carry

    lax.fori_loop(1, count, greet, 0)
    for step in range(1, chans):
        peer = lax.rem(mine + step, chans)
        pl.semaphore_signal(barrier, inc=1, device_id={"chan": peer}, device_id_type=mesh_ids)
    inputs[0].wait()
    feat = feat_ref[...].astype(jnp.float32)
    part = jnp.sum(jnp.transpose(feat * feat), axis=0, keepdims=True)
    sq_mine[...] = jnp.broadcast_to(part, sq_mine.shape)
    pl.semaphore_wait(barrier, count + chans - 2)

    def seq_copy(source, target, sems, step):
        peer = lax.rem(me + step, count)
        return pltpu.make_async_remote_copy(
            source(peer), target, sems.at[0, step], sems.at[1, step],
            device_id={"seq": peer}, device_id_type=mesh_ids,
        )

    def start_all(source, target, sems):
        def body(step, carry):
            seq_copy(source, target, sems, step).start()
            return carry
        lax.fori_loop(1, count, body, 0)

    def finish_all(source, target, sems):
        def body(step, carry):
            copy = seq_copy(source, target, sems, step)
            copy.wait_send()
            copy.wait_recv()
            return carry
        lax.fori_loop(1, count, body, 0)


    def chan_copy(step):
        peer = lax.rem(mine + step, chans)
        return pltpu.make_async_remote_copy(
            sq_mine, sq_recv.at[mine], chan_sems.at[0, step], chan_sems.at[1, step],
            device_id={"chan": peer}, device_id_type=mesh_ids,
        )

    for step in range(1, chans):
        chan_copy(step).start()
    for step in range(1, chans):
        copy = chan_copy(step)
        copy.wait_send()
        copy.wait_recv()
    total = part
    for step in range(1, chans):
        other = lax.rem(mine + step, chans)
        total = total + sq_recv[other][0:1, :]
    inputs[1].wait()
    inputs[2].wait()
    scale = lax.rsqrt(total / CHANNELS + 1e-06)
    scale = jnp.transpose(jnp.broadcast_to(scale, (8, scale.shape[1])))[:, 0:1]
    signal = (feat * scale * gain_ref[...] * gate_ref[...].astype(jnp.float32)).astype(jnp.bfloat16)
    wide = signal.astype(jnp.float32)
    lanes = wide.shape[1]
    pair = lanes // count
    tiles = wide.shape[0] // lanes
    chunk = pair * tiles
    for tile in range(tiles):
        sig_turn[...] = jnp.transpose(wide[lanes * tile:lanes * (tile + 1), :])
        for chan in range(pair):
            rows = sig_turn[pl.ds(chan, count, stride=pair), :]
            sig_send[pl.ds(tiles * chan + tile, count, stride=chunk), :] = rows

    def rows_of(buffer):
        return lambda peer: buffer.at[pl.ds(pl.multiple_of(peer * chunk, chunk), chunk)]

    sig_own = pltpu.make_async_copy(rows_of(sig_send)(me), rows_of(sig_recv)(me), own_sems.at[1])
    sig_own.start()
    start_all(rows_of(sig_send), rows_of(sig_recv)(me), sig_sems)
    inputs[3].wait()
    spec_src = lambda peer: spec_ref.at[peer]
    spec_own = pltpu.make_async_copy(spec_ref.at[me], spec_recv.at[me], own_sems.at[0])
    spec_own.start()
    start_all(spec_src, spec_recv.at[me], spec_sems)
    finish_all(rows_of(sig_send), rows_of(sig_recv)(me), sig_sems)
    sig_own.wait()

    for chan in range(pair):
        for tile in range(tiles):
            rows = sig_recv[pl.ds(tiles * chan + tile, count, stride=chunk), :]
            cols[chan, pl.ds(tile, count, stride=tiles), :] = rows

    first_len = tc_ref.shape[0]
    for load in loads:
        load.wait()
    boths = []
    for chan in range(pair):
        signal_cols = cols[chan].astype(jnp.bfloat16)
        boths.append(jnp.dot(st_hi[...], signal_cols, preferred_element_type=jnp.float32))

    cos_twist, sin_twist = tc_ref[...], ts_ref[...]
    own_rows = first_len // count
    freqs = []
    for chan in range(pair):
        p_cos = boths[chan][:first_len]
        p_sin = boths[chan][first_len:]
        twist_re = p_cos * cos_twist - p_sin * sin_twist
        twist_im = -p_sin * cos_twist - p_cos * sin_twist
        freqs.append(dot3(twist_re, (fa_hi[...], fa_lo[...])) + dot3(twist_im, (fb_hi[...], fb_lo[...])))

    finish_all(spec_src, spec_recv.at[me], spec_sems)
    spec_own.wait()

    for chan in range(pair):
        freq = freqs[chan]
        freq_re, freq_im = freq[:, :lanes], freq[:, lanes:]
        filt = []
        for part_of in range(2):
            block = spec_recv[:, pl.ds((2 * chan + part_of) * own_rows, own_rows), :]
            filt.append(block.astype(jnp.float32).reshape(first_len, lanes))
        filt_re, filt_im = filt
        prod_re = freq_re * filt_re - freq_im * filt_im
        prod_im = freq_re * filt_im + freq_im * filt_re
        back = dot3(prod_re, (ia_hi[...], ia_lo[...])) + dot3(prod_im, (ib_hi[...], ib_lo[...]))
        back_re, back_im = back[:, :lanes], back[:, lanes:]
        untwist_re = back_re * cos_twist - back_im * sin_twist
        untwist_im = back_im * cos_twist + back_re * sin_twist
        conv_one[...] = dot3((lc_hi[...], lc_lo[...]), untwist_re) + dot3((ls_hi[...], ls_lo[...]), untwist_im)
        for tile in range(tiles):
            rows = conv_one[pl.ds(tile, count, stride=tiles), :]
            conv_send[pl.ds(tiles * chan + tile, count, stride=chunk), :] = rows

    res_src = rows_of(conv_send)
    res_dst = rows_of(res_recv)(me)
    res_own = pltpu.make_async_copy(res_src(me), res_dst, own_sems.at[2])
    res_own.start()
    start_all(res_src, res_dst, res_sems)
    finish_all(res_src, res_dst, res_sems)
    res_own.wait()

    inputs[4].wait()
    inputs[5].wait()
    skip = skip_ref[...]
    for tile in range(tiles):
        for chan in range(pair):
            sig_turn[pl.ds(chan, count, stride=pair), :] = res_recv[pl.ds(tiles * chan + tile, count, stride=chunk), :]
        block = jnp.transpose(sig_turn[...])
        these = slice(lanes * tile, lanes * (tile + 1))
        direct = signal[these, :].astype(jnp.float32)
        gated = post_ref[these, :].astype(jnp.float32) * (block + skip * direct)
        gated_out[these, :] = gated.astype(gated_out.dtype)


def whole(features, pre_gate, gain_row, spec_rows, post_gate, skip_row, tables, chans):
    count = spec_rows.shape[0]
    length, width = features.shape
    pair = width // count
    lanes = 128
    chunk = pair * length // lanes
    vmem = pl.BlockSpec(memory_space=pltpu.VMEM)
    operands = (features, pre_gate, gain_row, spec_rows, post_gate, skip_row) + tuple(tables)
    hbm = pl.BlockSpec(memory_space=pl.ANY)
    return pl.pallas_call(
        whole_kernel,
        out_shape=jax.ShapeDtypeStruct((length, width), jnp.bfloat16),
        in_specs=[hbm] * len(operands),
        out_specs=vmem,
        scratch_shapes=[
            pltpu.VMEM((8, length), jnp.float32),
            pltpu.VMEM((chans, 8, length), jnp.float32),
            pltpu.VMEM((lanes, lanes), jnp.float32),
            pltpu.VMEM((count * chunk, lanes), jnp.float32),
            pltpu.VMEM((count * chunk, lanes), jnp.float32),
            pltpu.VMEM(spec_rows.shape, spec_rows.dtype),
            pltpu.VMEM((pair, count * chunk // pair, lanes), jnp.float32),
            pltpu.VMEM((count * chunk // pair, lanes), jnp.float32),
            pltpu.VMEM((count * chunk, lanes), jnp.float32),
            pltpu.VMEM((count * chunk, lanes), jnp.float32),
            pltpu.SemaphoreType.DMA((2, count)),
            pltpu.SemaphoreType.DMA((2, count)),
            pltpu.SemaphoreType.DMA((2, count)),
            pltpu.SemaphoreType.DMA((2, chans)),
            pltpu.SemaphoreType.DMA((3,)),
            pltpu.SemaphoreType.DMA((len(operands),)),
        ]
        + [pltpu.VMEM(table.shape, table.dtype) for table in operands],
        compiler_params=pltpu.CompilerParams(
            collective_id=0, has_side_effects=True, vmem_limit_bytes=67043328
        ),
    )(*operands)


def dft_tables(seq_count, tok_rows):
    stride = 2 * seq_count
    first_len = stride * ROW_GROUP
    all_bins = stride * tok_rows
    second_len = all_bins // first_len
    half_first = first_len // 2
    row_bins = bin_rows(seq_count).astype(np.int64)
    first_turn = (row_bins[:, None] * np.arange(half_first)[None, :]) % first_len * (2.0 * np.pi / first_len)
    cos_first, sin_first = np.cos(first_turn), np.sin(first_turn)
    twist_turn = (row_bins[:, None] * np.arange(second_len)[None, :]) % all_bins * (2.0 * np.pi / all_bins)
    second_in = np.arange(second_len)
    second_turn = (second_in[:, None] * second_in[None, :]) % second_len * (2.0 * np.pi / second_len)
    cos_second, sin_second = np.cos(second_turn), np.sin(second_turn)

    def pair_of(array):
        array = array.astype(np.float32)
        high = array.astype(jnp.bfloat16)
        return [jnp.asarray(high), jnp.asarray((array - high.astype(np.float32)).astype(jnp.bfloat16))]

    tables = pair_of(np.concatenate([cos_first, sin_first], 0))
    tables += [jnp.asarray(np.cos(twist_turn).astype(np.float32)), jnp.asarray(np.sin(twist_turn).astype(np.float32))]
    tables += pair_of(np.concatenate([cos_second, -sin_second], 1))
    tables += pair_of(np.concatenate([sin_second, cos_second], 1))
    tables += pair_of(np.concatenate([cos_second, sin_second], 1))
    tables += pair_of(np.concatenate([-sin_second, cos_second], 1))
    tables += pair_of(cos_first.T / all_bins)
    tables += pair_of(-sin_first.T / all_bins)
    return tables


def local(features, pre_gate, post_gate, norm_gain, skip_weight, spectrum):
    tok_rows, chan_width = features.shape
    seq_count = lax.axis_size("seq")
    chans = lax.axis_size("chan")
    group = chan_width // seq_count
    second_len = tok_rows // ROW_GROUP
    lanes = 128
    tok_tiles = tok_rows // lanes

    spec_rows = spectrum.reshape(2, 2, second_len, ROW_GROUP, chan_width)
    spec_rows = jnp.transpose(spec_rows, (4, 0, 1, 3, 2)).astype(jnp.bfloat16)
    spec_rows = spec_rows.reshape(seq_count, -1, second_len)
    return whole(
        features, pre_gate, norm_gain.reshape(1, chan_width), spec_rows,
        post_gate, skip_weight.reshape(1, chan_width), dft_tables(seq_count, tok_rows), chans,
    )


def solution(mesh):
    return jax.shard_map(
        local,
        mesh=mesh,
        in_specs=(
            P("seq", "chan"),
            P("seq", "chan"),
            P("seq", "chan"),
            P("chan"),
            P("chan"),
            P(None, "seq", None, "chan"),
        ),
        out_specs=P("seq", "chan"),
        check_vma=False,
    )
```

```python
import math

import jax
import jax.numpy as jnp
import numpy as np
from jax import lax
from jax.experimental import pallas as pl
from jax.experimental.pallas import tpu as pltpu
from jax.sharding import PartitionSpec as P

CHANNELS = 512
ROW_GROUP = 4
TABLE_NAMES = ("st_hi", "st_lo", "tc", "ts", "fa_hi", "fa_lo", "fb_hi", "fb_lo", "ia_hi", "ia_lo", "ib_hi", "ib_lo",
               "lc_hi", "lc_lo", "ls_hi", "ls_lo")
HIGH_DIGIT = 8


PRECISE = lax.Precision.HIGH
FULL_TURN = 2.0 * math.pi


def reversed_digits(count):
    levels = count.bit_length() - 1
    positions = np.arange(count)
    result = np.zeros(count, np.int64)
    for bit_pos in range(levels):
        result = result + ((positions >> bit_pos & 1) << levels - 1 - bit_pos)
    return result


def rotation(numerator, denominator):
    angle = (numerator % denominator).astype(jnp.float32) * (FULL_TURN / denominator)
    return (jnp.cos(angle), jnp.sin(angle))


def mm(spec, left, right):
    return jnp.einsum(spec, left, right, precision=PRECISE, preferred_element_type=jnp.float32)


def bin_rows(seq_count):
    digit_order = reversed_digits(seq_count)
    stride = 2 * seq_count
    slots = np.arange(stride)
    low_bins = 2 * digit_order[slots // 2] + slots % 2
    return (low_bins[:, None] + stride * np.arange(ROW_GROUP)[None, :]).reshape(-1).astype(np.int32)


def split(value):
    high = value.astype(jnp.bfloat16)
    return high, (value - high.astype(jnp.float32)).astype(jnp.bfloat16)


def dot3(left, right):
    if isinstance(left, tuple):
        d_hi, d_lo = split(right)
        out = jnp.dot(left[0], d_hi, preferred_element_type=jnp.float32)
        return out + jnp.dot(left[0], d_lo, preferred_element_type=jnp.float32)
    d_hi, d_lo = split(left)
    out = jnp.dot(d_hi, right[0], preferred_element_type=jnp.float32)
    return out + jnp.dot(d_lo, right[0], preferred_element_type=jnp.float32)


def whole_kernel(*refs):
    table_count = len(TABLE_NAMES) + 6
    held = refs[:table_count]
    gated_out = refs[table_count]
    (sq_mine, sq_recv, sig_turn, sig_send, sig_recv, spec_recv, cols, conv_one, conv_send, res_recv,
     wire_out, wire_in, spec_sems, sig_sems, res_sems, chan_sems, own_sems, table_sems) = refs[table_count + 1:table_count + 19]
    tables = refs[table_count + 19:]
    loads = [pltpu.make_async_copy(held[k], tables[k], table_sems.at[k]) for k in range(table_count)]
    for load in loads:
        load.start()
    inputs = loads[:6]
    loads = loads[6:]
    feat_ref, gate_ref, gain_ref, spec_ref, post_ref, skip_ref = tables[:6]
    tables = tables[6:]
    (st_hi, st_lo, tc_ref, ts_ref, fa_hi, fa_lo, fb_hi, fb_lo, ia_hi, ia_lo, ib_hi, ib_lo,
     lc_hi, lc_lo, ls_hi, ls_lo) = tables
    count = spec_ref.shape[0]
    chans = sq_recv.shape[0]
    me = lax.axis_index("seq")
    mine = lax.axis_index("chan")
    mesh_ids = pl.DeviceIdType.MESH
    barrier = pltpu.get_barrier_semaphore()

    def greet(step, carry):
        peer = lax.rem(me + step, count)
        pl.semaphore_signal(barrier, inc=1, device_id={"seq": peer}, device_id_type=mesh_ids)
        return carry

    lax.fori_loop(1, count, greet, 0)
    for step in range(1, chans):
        peer = lax.rem(mine + step, chans)
        pl.semaphore_signal(barrier, inc=1, device_id={"chan": peer}, device_id_type=mesh_ids)
    inputs[0].wait()
    feat = feat_ref[...].astype(jnp.float32)
    part = jnp.sum(jnp.transpose(feat * feat), axis=0, keepdims=True)
    sq_mine[...] = jnp.broadcast_to(part, sq_mine.shape)
    pl.semaphore_wait(barrier, count + chans - 2)

    def seq_copy(source, target, sems, step):
        peer = lax.rem(me + step, count)
        return pltpu.make_async_remote_copy(
            source(peer), target, sems.at[0, step], sems.at[1, step],
            device_id={"seq": peer}, device_id_type=mesh_ids,
        )

    def start_all(source, target, sems):
        def body(step, carry):
            seq_copy(source, target, sems, step).start()
            return carry
        lax.fori_loop(1, count, body, 0)

    def finish_all(source, target, sems):
        def body(step, carry):
            copy = seq_copy(source, target, sems, step)
            copy.wait_send()
            copy.wait_recv()
            return carry
        lax.fori_loop(1, count, body, 0)


    def chan_copy(step):
        peer = lax.rem(mine + step, chans)
        return pltpu.make_async_remote_copy(
            sq_mine, sq_recv.at[mine], chan_sems.at[0, step], chan_sems.at[1, step],
            device_id={"chan": peer}, device_id_type=mesh_ids,
        )

    for step in range(1, chans):
        chan_copy(step).start()
    inputs[3].wait()
    spec_src = lambda peer: spec_ref.at[peer]
    spec_own = pltpu.make_async_copy(spec_ref.at[me], spec_recv.at[me], own_sems.at[0])
    spec_own.start()
    start_all(spec_src, spec_recv.at[me], spec_sems)
    for step in range(1, chans):
        copy = chan_copy(step)
        copy.wait_send()
        copy.wait_recv()
    total = part
    for step in range(1, chans):
        other = lax.rem(mine + step, chans)
        total = total + sq_recv[other][0:1, :]
    inputs[1].wait()
    inputs[2].wait()
    scale = lax.rsqrt(total / CHANNELS + 1e-06)
    scale = jnp.transpose(jnp.broadcast_to(scale, (8, scale.shape[1])))[:, 0:1]
    signal = (feat * scale * gain_ref[...] * gate_ref[...].astype(jnp.float32)).astype(jnp.bfloat16)
    wide = signal.astype(jnp.float32)
    lanes = wide.shape[1]
    pair = lanes // count
    tiles = wide.shape[0] // lanes
    chunk = pair * tiles
    for tile in range(tiles):
        sig_turn[...] = jnp.transpose(wide[lanes * tile:lanes * (tile + 1), :])
        for chan in range(pair):
            rows = sig_turn[pl.ds(chan, count, stride=pair), :]
            sig_send[pl.ds(tiles * chan + tile, count, stride=chunk), :] = rows

    def rows_of(buffer):
        return lambda peer: buffer.at[pl.ds(pl.multiple_of(peer * chunk, chunk), chunk)]

    wire_out[...] = sig_send[...].astype(wire_out.dtype)
    sig_own = pltpu.make_async_copy(rows_of(wire_out)(me), rows_of(wire_in)(me), own_sems.at[1])
    sig_own.start()
    start_all(rows_of(wire_out), rows_of(wire_in)(me), sig_sems)
    finish_all(rows_of(wire_out), rows_of(wire_in)(me), sig_sems)
    sig_own.wait()
    sig_recv[...] = wire_in[...].astype(jnp.float32)

    for chan in range(pair):
        for tile in range(tiles):
            rows = sig_recv[pl.ds(tiles * chan + tile, count, stride=chunk), :]
            cols[chan, pl.ds(tile, count, stride=tiles), :] = rows

    first_len = tc_ref.shape[0]
    for load in loads:
        load.wait()
    boths = []
    for chan in range(pair):
        signal_cols = cols[chan].astype(jnp.bfloat16)
        boths.append(jnp.dot(st_hi[...], signal_cols, preferred_element_type=jnp.float32))

    cos_twist, sin_twist = tc_ref[...], ts_ref[...]
    own_rows = first_len // count
    freqs = []
    for chan in range(pair):
        p_cos = boths[chan][:first_len]
        p_sin = boths[chan][first_len:]
        twist_re = p_cos * cos_twist - p_sin * sin_twist
        twist_im = -p_sin * cos_twist - p_cos * sin_twist
        freqs.append(dot3(twist_re, (fa_hi[...], fa_lo[...])) + dot3(twist_im, (fb_hi[...], fb_lo[...])))

    finish_all(spec_src, spec_recv.at[me], spec_sems)
    spec_own.wait()

    for chan in range(pair):
        freq = freqs[chan]
        freq_re, freq_im = freq[:, :lanes], freq[:, lanes:]
        filt = []
        for part_of in range(2):
            block = spec_recv[:, pl.ds((2 * chan + part_of) * own_rows, own_rows), :]
            filt.append(block.astype(jnp.float32).reshape(first_len, lanes))
        filt_re, filt_im = filt
        prod_re = freq_re * filt_re - freq_im * filt_im
        prod_im = freq_re * filt_im + freq_im * filt_re
        back = dot3(prod_re, (ia_hi[...], ia_lo[...])) + dot3(prod_im, (ib_hi[...], ib_lo[...]))
        back_re, back_im = back[:, :lanes], back[:, lanes:]
        untwist_re = back_re * cos_twist - back_im * sin_twist
        untwist_im = back_im * cos_twist + back_re * sin_twist
        conv_one[...] = dot3((lc_hi[...], lc_lo[...]), untwist_re) + dot3((ls_hi[...], ls_lo[...]), untwist_im)
        for tile in range(tiles):
            rows = conv_one[pl.ds(tile, count, stride=tiles), :]
            conv_send[pl.ds(tiles * chan + tile, count, stride=chunk), :] = rows

    res_src = rows_of(conv_send)
    res_dst = rows_of(res_recv)(me)
    res_own = pltpu.make_async_copy(res_src(me), res_dst, own_sems.at[2])
    res_own.start()
    start_all(res_src, res_dst, res_sems)
    finish_all(res_src, res_dst, res_sems)
    res_own.wait()

    inputs[4].wait()
    inputs[5].wait()
    skip = skip_ref[...]
    for tile in range(tiles):
        for chan in range(pair):
            sig_turn[pl.ds(chan, count, stride=pair), :] = res_recv[pl.ds(tiles * chan + tile, count, stride=chunk), :]
        block = jnp.transpose(sig_turn[...])
        these = slice(lanes * tile, lanes * (tile + 1))
        direct = signal[these, :].astype(jnp.float32)
        gated = post_ref[these, :].astype(jnp.float32) * (block + skip * direct)
        gated_out[these, :] = gated.astype(gated_out.dtype)


def whole(features, pre_gate, gain_row, spec_rows, post_gate, skip_row, tables, chans):
    count = spec_rows.shape[0]
    length, width = features.shape
    pair = width // count
    lanes = 128
    chunk = pair * length // lanes
    vmem = pl.BlockSpec(memory_space=pltpu.VMEM)
    operands = (features, pre_gate, gain_row, spec_rows, post_gate, skip_row) + tuple(tables)
    hbm = pl.BlockSpec(memory_space=pl.ANY)
    return pl.pallas_call(
        whole_kernel,
        out_shape=jax.ShapeDtypeStruct((length, width), jnp.bfloat16),
        in_specs=[hbm] * len(operands),
        out_specs=vmem,
        scratch_shapes=[
            pltpu.VMEM((8, length), jnp.float32),
            pltpu.VMEM((chans, 8, length), jnp.float32),
            pltpu.VMEM((lanes, lanes), jnp.float32),
            pltpu.VMEM((count * chunk, lanes), jnp.float32),
            pltpu.VMEM((count * chunk, lanes), jnp.float32),
            pltpu.VMEM(spec_rows.shape, spec_rows.dtype),
            pltpu.VMEM((pair, count * chunk // pair, lanes), jnp.float32),
            pltpu.VMEM((count * chunk // pair, lanes), jnp.float32),
            pltpu.VMEM((count * chunk, lanes), jnp.float32),
            pltpu.VMEM((count * chunk, lanes), jnp.float32),
            pltpu.VMEM((count * chunk, lanes), jnp.bfloat16),
            pltpu.VMEM((count * chunk, lanes), jnp.bfloat16),
            pltpu.SemaphoreType.DMA((2, count)),
            pltpu.SemaphoreType.DMA((2, count)),
            pltpu.SemaphoreType.DMA((2, count)),
            pltpu.SemaphoreType.DMA((2, chans)),
            pltpu.SemaphoreType.DMA((3,)),
            pltpu.SemaphoreType.DMA((len(operands),)),
        ]
        + [pltpu.VMEM(table.shape, table.dtype) for table in operands],
        compiler_params=pltpu.CompilerParams(
            collective_id=0, has_side_effects=True, vmem_limit_bytes=67043328
        ),
    )(*operands)


def dft_tables(seq_count, tok_rows):
    stride = 2 * seq_count
    first_len = stride * ROW_GROUP
    all_bins = stride * tok_rows
    second_len = all_bins // first_len
    half_first = first_len // 2
    row_bins = bin_rows(seq_count).astype(np.int64)
    first_turn = (row_bins[:, None] * np.arange(half_first)[None, :]) % first_len * (2.0 * np.pi / first_len)
    cos_first, sin_first = np.cos(first_turn), np.sin(first_turn)
    twist_turn = (row_bins[:, None] * np.arange(second_len)[None, :]) % all_bins * (2.0 * np.pi / all_bins)
    second_in = np.arange(second_len)
    second_turn = (second_in[:, None] * second_in[None, :]) % second_len * (2.0 * np.pi / second_len)
    cos_second, sin_second = np.cos(second_turn), np.sin(second_turn)

    def pair_of(array):
        array = array.astype(np.float32)
        high = array.astype(jnp.bfloat16)
        return [jnp.asarray(high), jnp.asarray((array - high.astype(np.float32)).astype(jnp.bfloat16))]

    tables = pair_of(np.concatenate([cos_first, sin_first], 0))
    tables += [jnp.asarray(np.cos(twist_turn).astype(np.float32)), jnp.asarray(np.sin(twist_turn).astype(np.float32))]
    tables += pair_of(np.concatenate([cos_second, -sin_second], 1))
    tables += pair_of(np.concatenate([sin_second, cos_second], 1))
    tables += pair_of(np.concatenate([cos_second, sin_second], 1))
    tables += pair_of(np.concatenate([-sin_second, cos_second], 1))
    tables += pair_of(cos_first.T / all_bins)
    tables += pair_of(-sin_first.T / all_bins)
    return tables


def local(features, pre_gate, post_gate, norm_gain, skip_weight, spectrum):
    tok_rows, chan_width = features.shape
    seq_count = lax.axis_size("seq")
    chans = lax.axis_size("chan")
    group = chan_width // seq_count
    second_len = tok_rows // ROW_GROUP
    lanes = 128
    tok_tiles = tok_rows // lanes

    spec_rows = spectrum.reshape(2, 2, second_len, ROW_GROUP, chan_width)
    spec_rows = jnp.transpose(spec_rows, (4, 0, 1, 3, 2)).astype(jnp.bfloat16)
    spec_rows = spec_rows.reshape(seq_count, -1, second_len)
    return whole(
        features, pre_gate, norm_gain.reshape(1, chan_width), spec_rows,
        post_gate, skip_weight.reshape(1, chan_width), dft_tables(seq_count, tok_rows), chans,
    )


def solution(mesh):
    return jax.shard_map(
        local,
        mesh=mesh,
        in_specs=(
            P("seq", "chan"),
            P("seq", "chan"),
            P("seq", "chan"),
            P("chan"),
            P("chan"),
            P(None, "seq", None, "chan"),
        ),
        out_specs=P("seq", "chan"),
        check_vma=False,
    )
```

```python
import math

import jax
import jax.numpy as jnp
import numpy as np
from jax import lax
from jax.experimental import pallas as pl
from jax.experimental.pallas import tpu as pltpu
from jax.sharding import PartitionSpec as P

CHANNELS = 512
ROW_GROUP = 4
TABLE_NAMES = ("st_hi", "st_lo", "tc", "ts", "fa_hi", "fa_lo", "fb_hi", "fb_lo", "ia_hi", "ia_lo", "ib_hi", "ib_lo",
               "lc_hi", "lc_lo", "ls_hi", "ls_lo")
HIGH_DIGIT = 8


PRECISE = lax.Precision.HIGH
FULL_TURN = 2.0 * math.pi


def reversed_digits(count):
    levels = count.bit_length() - 1
    positions = np.arange(count)
    result = np.zeros(count, np.int64)
    for bit_pos in range(levels):
        result = result + ((positions >> bit_pos & 1) << levels - 1 - bit_pos)
    return result


def rotation(numerator, denominator):
    angle = (numerator % denominator).astype(jnp.float32) * (FULL_TURN / denominator)
    return (jnp.cos(angle), jnp.sin(angle))


def mm(spec, left, right):
    return jnp.einsum(spec, left, right, precision=PRECISE, preferred_element_type=jnp.float32)


def bin_rows(seq_count):
    digit_order = reversed_digits(seq_count)
    stride = 2 * seq_count
    slots = np.arange(stride)
    low_bins = 2 * digit_order[slots // 2] + slots % 2
    return (low_bins[:, None] + stride * np.arange(ROW_GROUP)[None, :]).reshape(-1).astype(np.int32)


def split(value):
    high = value.astype(jnp.bfloat16)
    return high, (value - high.astype(jnp.float32)).astype(jnp.bfloat16)


def dot3(left, right):
    if isinstance(left, tuple):
        d_hi, d_lo = split(right)
        out = jnp.dot(left[0], d_hi, preferred_element_type=jnp.float32)
        return out + jnp.dot(left[0], d_lo, preferred_element_type=jnp.float32)
    d_hi, d_lo = split(left)
    out = jnp.dot(d_hi, right[0], preferred_element_type=jnp.float32)
    return out + jnp.dot(d_lo, right[0], preferred_element_type=jnp.float32)


def whole_kernel(*refs):
    table_count = len(TABLE_NAMES) + 6
    held = refs[:table_count]
    gated_out = refs[table_count]
    (sq_mine, sq_recv, sig_turn, sig_send, sig_recv, spec_recv, cols, conv_one, conv_send, res_recv,
     wire_out, wire_in, res_out, res_in, spec_sems, sig_sems, res_sems, chan_sems, own_sems, table_sems) = (
        refs[table_count + 1:table_count + 21])
    tables = refs[table_count + 21:]
    loads = [pltpu.make_async_copy(held[k], tables[k], table_sems.at[k]) for k in range(table_count)]
    for load in loads:
        load.start()
    inputs = loads[:6]
    loads = loads[6:]
    feat_ref, gate_ref, gain_ref, spec_ref, post_ref, skip_ref = tables[:6]
    tables = tables[6:]
    (st_hi, st_lo, tc_ref, ts_ref, fa_hi, fa_lo, fb_hi, fb_lo, ia_hi, ia_lo, ib_hi, ib_lo,
     lc_hi, lc_lo, ls_hi, ls_lo) = tables
    count = spec_ref.shape[0]
    chans = sq_recv.shape[0]
    me = lax.axis_index("seq")
    mine = lax.axis_index("chan")
    mesh_ids = pl.DeviceIdType.MESH
    barrier = pltpu.get_barrier_semaphore()

    def greet(step, carry):
        peer = lax.rem(me + step, count)
        pl.semaphore_signal(barrier, inc=1, device_id={"seq": peer}, device_id_type=mesh_ids)
        return carry

    lax.fori_loop(1, count, greet, 0)
    for step in range(1, chans):
        peer = lax.rem(mine + step, chans)
        pl.semaphore_signal(barrier, inc=1, device_id={"chan": peer}, device_id_type=mesh_ids)
    inputs[0].wait()
    feat = feat_ref[...].astype(jnp.float32)
    part = jnp.sum(jnp.transpose(feat * feat), axis=0, keepdims=True)
    sq_mine[...] = jnp.broadcast_to(part, sq_mine.shape)
    pl.semaphore_wait(barrier, count + chans - 2)

    def seq_copy(source, target, sems, step):
        peer = lax.rem(me + step, count)
        return pltpu.make_async_remote_copy(
            source(peer), target, sems.at[0, step], sems.at[1, step],
            device_id={"seq": peer}, device_id_type=mesh_ids,
        )

    def start_all(source, target, sems):
        def body(step, carry):
            seq_copy(source, target, sems, step).start()
            return carry
        lax.fori_loop(1, count, body, 0)

    def finish_all(source, target, sems):
        def body(step, carry):
            copy = seq_copy(source, target, sems, step)
            copy.wait_send()
            copy.wait_recv()
            return carry
        lax.fori_loop(1, count, body, 0)


    def chan_copy(step):
        peer = lax.rem(mine + step, chans)
        return pltpu.make_async_remote_copy(
            sq_mine, sq_recv.at[mine], chan_sems.at[0, step], chan_sems.at[1, step],
            device_id={"chan": peer}, device_id_type=mesh_ids,
        )

    for step in range(1, chans):
        chan_copy(step).start()
    inputs[3].wait()
    spec_src = lambda peer: spec_ref.at[peer]
    spec_own = pltpu.make_async_copy(spec_ref.at[me], spec_recv.at[me], own_sems.at[0])
    spec_own.start()
    start_all(spec_src, spec_recv.at[me], spec_sems)
    for step in range(1, chans):
        copy = chan_copy(step)
        copy.wait_send()
        copy.wait_recv()
    total = part
    for step in range(1, chans):
        other = lax.rem(mine + step, chans)
        total = total + sq_recv[other][0:1, :]
    inputs[1].wait()
    inputs[2].wait()
    scale = lax.rsqrt(total / CHANNELS + 1e-06)
    scale = jnp.transpose(jnp.broadcast_to(scale, (8, scale.shape[1])))[:, 0:1]
    signal = (feat * scale * gain_ref[...] * gate_ref[...].astype(jnp.float32)).astype(jnp.bfloat16)
    wide = signal.astype(jnp.float32)
    lanes = wide.shape[1]
    pair = lanes // count
    tiles = wide.shape[0] // lanes
    chunk = pair * tiles
    for tile in range(tiles):
        sig_turn[...] = jnp.transpose(wide[lanes * tile:lanes * (tile + 1), :])
        for chan in range(pair):
            rows = sig_turn[pl.ds(chan, count, stride=pair), :]
            sig_send[pl.ds(tiles * chan + tile, count, stride=chunk), :] = rows

    def rows_of(buffer):
        return lambda peer: buffer.at[pl.ds(pl.multiple_of(peer * chunk, chunk), chunk)]

    wire_out[...] = sig_send[...].astype(wire_out.dtype)
    sig_own = pltpu.make_async_copy(rows_of(wire_out)(me), rows_of(wire_in)(me), own_sems.at[1])
    sig_own.start()
    start_all(rows_of(wire_out), rows_of(wire_in)(me), sig_sems)
    finish_all(rows_of(wire_out), rows_of(wire_in)(me), sig_sems)
    sig_own.wait()
    sig_recv[...] = wire_in[...].astype(jnp.float32)

    for chan in range(pair):
        for tile in range(tiles):
            rows = sig_recv[pl.ds(tiles * chan + tile, count, stride=chunk), :]
            cols[chan, pl.ds(tile, count, stride=tiles), :] = rows

    first_len = tc_ref.shape[0]
    for load in loads:
        load.wait()
    boths = []
    for chan in range(pair):
        signal_cols = cols[chan].astype(jnp.bfloat16)
        boths.append(jnp.dot(st_hi[...], signal_cols, preferred_element_type=jnp.float32))

    cos_twist, sin_twist = tc_ref[...], ts_ref[...]
    own_rows = first_len // count
    freqs = []
    for chan in range(pair):
        p_cos = boths[chan][:first_len]
        p_sin = boths[chan][first_len:]
        twist_re = p_cos * cos_twist - p_sin * sin_twist
        twist_im = -p_sin * cos_twist - p_cos * sin_twist
        freqs.append(dot3(twist_re, (fa_hi[...], fa_lo[...])) + dot3(twist_im, (fb_hi[...], fb_lo[...])))

    finish_all(spec_src, spec_recv.at[me], spec_sems)
    spec_own.wait()

    for chan in range(pair):
        freq = freqs[chan]
        freq_re, freq_im = freq[:, :lanes], freq[:, lanes:]
        filt = []
        for part_of in range(2):
            block = spec_recv[:, pl.ds((2 * chan + part_of) * own_rows, own_rows), :]
            filt.append(block.astype(jnp.float32).reshape(first_len, lanes))
        filt_re, filt_im = filt
        prod_re = freq_re * filt_re - freq_im * filt_im
        prod_im = freq_re * filt_im + freq_im * filt_re
        back = dot3(prod_re, (ia_hi[...], ia_lo[...])) + dot3(prod_im, (ib_hi[...], ib_lo[...]))
        back_re, back_im = back[:, :lanes], back[:, lanes:]
        untwist_re = back_re * cos_twist - back_im * sin_twist
        untwist_im = back_im * cos_twist + back_re * sin_twist
        conv_one[...] = dot3((lc_hi[...], lc_lo[...]), untwist_re) + dot3((ls_hi[...], ls_lo[...]), untwist_im)
        for tile in range(tiles):
            rows = conv_one[pl.ds(tile, count, stride=tiles), :]
            conv_send[pl.ds(tiles * chan + tile, count, stride=chunk), :] = rows

    res_out[...] = conv_send[...].astype(res_out.dtype)
    res_src = rows_of(res_out)
    res_dst = rows_of(res_in)(me)
    res_own = pltpu.make_async_copy(res_src(me), res_dst, own_sems.at[2])
    res_own.start()
    start_all(res_src, res_dst, res_sems)
    finish_all(res_src, res_dst, res_sems)
    res_own.wait()
    res_recv[...] = res_in[...].astype(jnp.float32)

    inputs[4].wait()
    inputs[5].wait()
    skip = skip_ref[...]
    for tile in range(tiles):
        for chan in range(pair):
            sig_turn[pl.ds(chan, count, stride=pair), :] = res_recv[pl.ds(tiles * chan + tile, count, stride=chunk), :]
        block = jnp.transpose(sig_turn[...])
        these = slice(lanes * tile, lanes * (tile + 1))
        direct = signal[these, :].astype(jnp.float32)
        gated = post_ref[these, :].astype(jnp.float32) * (block + skip * direct)
        gated_out[these, :] = gated.astype(gated_out.dtype)


def whole(features, pre_gate, gain_row, spec_rows, post_gate, skip_row, tables, chans):
    count = spec_rows.shape[0]
    length, width = features.shape
    pair = width // count
    lanes = 128
    chunk = pair * length // lanes
    vmem = pl.BlockSpec(memory_space=pltpu.VMEM)
    operands = (features, pre_gate, gain_row, spec_rows, post_gate, skip_row) + tuple(tables)
    hbm = pl.BlockSpec(memory_space=pl.ANY)
    return pl.pallas_call(
        whole_kernel,
        out_shape=jax.ShapeDtypeStruct((length, width), jnp.bfloat16),
        in_specs=[hbm] * len(operands),
        out_specs=vmem,
        scratch_shapes=[
            pltpu.VMEM((8, length), jnp.float32),
            pltpu.VMEM((chans, 8, length), jnp.float32),
            pltpu.VMEM((lanes, lanes), jnp.float32),
            pltpu.VMEM((count * chunk, lanes), jnp.float32),
            pltpu.VMEM((count * chunk, lanes), jnp.float32),
            pltpu.VMEM(spec_rows.shape, spec_rows.dtype),
            pltpu.VMEM((pair, count * chunk // pair, lanes), jnp.float32),
            pltpu.VMEM((count * chunk // pair, lanes), jnp.float32),
            pltpu.VMEM((count * chunk, lanes), jnp.float32),
            pltpu.VMEM((count * chunk, lanes), jnp.float32),
            pltpu.VMEM((count * chunk, lanes), jnp.bfloat16),
            pltpu.VMEM((count * chunk, lanes), jnp.bfloat16),
            pltpu.VMEM((count * chunk, lanes), jnp.bfloat16),
            pltpu.VMEM((count * chunk, lanes), jnp.bfloat16),
            pltpu.SemaphoreType.DMA((2, count)),
            pltpu.SemaphoreType.DMA((2, count)),
            pltpu.SemaphoreType.DMA((2, count)),
            pltpu.SemaphoreType.DMA((2, chans)),
            pltpu.SemaphoreType.DMA((3,)),
            pltpu.SemaphoreType.DMA((len(operands),)),
        ]
        + [pltpu.VMEM(table.shape, table.dtype) for table in operands],
        compiler_params=pltpu.CompilerParams(
            collective_id=0, has_side_effects=True, vmem_limit_bytes=67043328
        ),
    )(*operands)


def dft_tables(seq_count, tok_rows):
    stride = 2 * seq_count
    first_len = stride * ROW_GROUP
    all_bins = stride * tok_rows
    second_len = all_bins // first_len
    half_first = first_len // 2
    row_bins = bin_rows(seq_count).astype(np.int64)
    first_turn = (row_bins[:, None] * np.arange(half_first)[None, :]) % first_len * (2.0 * np.pi / first_len)
    cos_first, sin_first = np.cos(first_turn), np.sin(first_turn)
    twist_turn = (row_bins[:, None] * np.arange(second_len)[None, :]) % all_bins * (2.0 * np.pi / all_bins)
    second_in = np.arange(second_len)
    second_turn = (second_in[:, None] * second_in[None, :]) % second_len * (2.0 * np.pi / second_len)
    cos_second, sin_second = np.cos(second_turn), np.sin(second_turn)

    def pair_of(array):
        array = array.astype(np.float32)
        high = array.astype(jnp.bfloat16)
        return [jnp.asarray(high), jnp.asarray((array - high.astype(np.float32)).astype(jnp.bfloat16))]

    tables = pair_of(np.concatenate([cos_first, sin_first], 0))
    tables += [jnp.asarray(np.cos(twist_turn).astype(np.float32)), jnp.asarray(np.sin(twist_turn).astype(np.float32))]
    tables += pair_of(np.concatenate([cos_second, -sin_second], 1))
    tables += pair_of(np.concatenate([sin_second, cos_second], 1))
    tables += pair_of(np.concatenate([cos_second, sin_second], 1))
    tables += pair_of(np.concatenate([-sin_second, cos_second], 1))
    tables += pair_of(cos_first.T / all_bins)
    tables += pair_of(-sin_first.T / all_bins)
    return tables


def local(features, pre_gate, post_gate, norm_gain, skip_weight, spectrum):
    tok_rows, chan_width = features.shape
    seq_count = lax.axis_size("seq")
    chans = lax.axis_size("chan")
    group = chan_width // seq_count
    second_len = tok_rows // ROW_GROUP
    lanes = 128
    tok_tiles = tok_rows // lanes

    spec_rows = spectrum.reshape(2, 2, second_len, ROW_GROUP, chan_width)
    spec_rows = jnp.transpose(spec_rows, (4, 0, 1, 3, 2)).astype(jnp.bfloat16)
    spec_rows = spec_rows.reshape(seq_count, -1, second_len)
    return whole(
        features, pre_gate, norm_gain.reshape(1, chan_width), spec_rows,
        post_gate, skip_weight.reshape(1, chan_width), dft_tables(seq_count, tok_rows), chans,
    )


def solution(mesh):
    return jax.shard_map(
        local,
        mesh=mesh,
        in_specs=(
            P("seq", "chan"),
            P("seq", "chan"),
            P("seq", "chan"),
            P("chan"),
            P("chan"),
            P(None, "seq", None, "chan"),
        ),
        out_specs=P("seq", "chan"),
        check_vma=False,
    )
```

```python
import math

import jax
import jax.numpy as jnp
import numpy as np
from jax import lax
from jax.experimental import pallas as pl
from jax.experimental.pallas import tpu as pltpu
from jax.sharding import PartitionSpec as P

CHANNELS = 512
ROW_GROUP = 4
TABLE_NAMES = ("st_hi", "st_lo", "tc", "ts", "fa_hi", "fa_lo", "fb_hi", "fb_lo", "ia_hi", "ia_lo", "ib_hi", "ib_lo",
               "lc_hi", "lc_lo", "ls_hi", "ls_lo")
HIGH_DIGIT = 8


PRECISE = lax.Precision.HIGH
FULL_TURN = 2.0 * math.pi


def reversed_digits(count):
    levels = count.bit_length() - 1
    positions = np.arange(count)
    result = np.zeros(count, np.int64)
    for bit_pos in range(levels):
        result = result + ((positions >> bit_pos & 1) << levels - 1 - bit_pos)
    return result


def rotation(numerator, denominator):
    angle = (numerator % denominator).astype(jnp.float32) * (FULL_TURN / denominator)
    return (jnp.cos(angle), jnp.sin(angle))


def mm(spec, left, right):
    return jnp.einsum(spec, left, right, precision=PRECISE, preferred_element_type=jnp.float32)


def bin_rows(seq_count):
    digit_order = reversed_digits(seq_count)
    stride = 2 * seq_count
    slots = np.arange(stride)
    low_bins = 2 * digit_order[slots // 2] + slots % 2
    return (low_bins[:, None] + stride * np.arange(ROW_GROUP)[None, :]).reshape(-1).astype(np.int32)


def split(value):
    high = value.astype(jnp.bfloat16)
    return high, (value - high.astype(jnp.float32)).astype(jnp.bfloat16)


def dot3(left, right):
    if isinstance(left, tuple):
        return jnp.dot(left[0], right.astype(jnp.bfloat16), preferred_element_type=jnp.float32)
    return jnp.dot(left.astype(jnp.bfloat16), right[0], preferred_element_type=jnp.float32)


def whole_kernel(*refs):
    table_count = len(TABLE_NAMES) + 6
    held = refs[:table_count]
    gated_out = refs[table_count]
    (sq_mine, sq_recv, sig_turn, sig_send, sig_recv, spec_recv, cols, conv_one, conv_send, res_recv,
     wire_out, wire_in, res_out, res_in, spec_sems, sig_sems, res_sems, chan_sems, own_sems, table_sems) = (
        refs[table_count + 1:table_count + 21])
    tables = refs[table_count + 21:]
    loads = [pltpu.make_async_copy(held[k], tables[k], table_sems.at[k]) for k in range(table_count)]
    for load in loads:
        load.start()
    inputs = loads[:6]
    loads = loads[6:]
    feat_ref, gate_ref, gain_ref, spec_ref, post_ref, skip_ref = tables[:6]
    tables = tables[6:]
    (st_hi, st_lo, tc_ref, ts_ref, fa_hi, fa_lo, fb_hi, fb_lo, ia_hi, ia_lo, ib_hi, ib_lo,
     lc_hi, lc_lo, ls_hi, ls_lo) = tables
    count = spec_ref.shape[0]
    chans = sq_recv.shape[0]
    me = lax.axis_index("seq")
    mine = lax.axis_index("chan")
    mesh_ids = pl.DeviceIdType.MESH
    barrier = pltpu.get_barrier_semaphore()

    def greet(step, carry):
        peer = lax.rem(me + step, count)
        pl.semaphore_signal(barrier, inc=1, device_id={"seq": peer}, device_id_type=mesh_ids)
        return carry

    lax.fori_loop(1, count, greet, 0)
    for step in range(1, chans):
        peer = lax.rem(mine + step, chans)
        pl.semaphore_signal(barrier, inc=1, device_id={"chan": peer}, device_id_type=mesh_ids)
    inputs[0].wait()
    feat = feat_ref[...].astype(jnp.float32)
    part = jnp.sum(jnp.transpose(feat * feat), axis=0, keepdims=True)
    sq_mine[...] = jnp.broadcast_to(part, sq_mine.shape)
    pl.semaphore_wait(barrier, count + chans - 2)

    def seq_copy(source, target, sems, step):
        peer = lax.rem(me + step, count)
        return pltpu.make_async_remote_copy(
            source(peer), target, sems.at[0, step], sems.at[1, step],
            device_id={"seq": peer}, device_id_type=mesh_ids,
        )

    def start_all(source, target, sems):
        def body(step, carry):
            seq_copy(source, target, sems, step).start()
            return carry
        lax.fori_loop(1, count, body, 0)

    def finish_all(source, target, sems):
        def body(step, carry):
            copy = seq_copy(source, target, sems, step)
            copy.wait_send()
            copy.wait_recv()
            return carry
        lax.fori_loop(1, count, body, 0)


    def chan_copy(step):
        peer = lax.rem(mine + step, chans)
        return pltpu.make_async_remote_copy(
            sq_mine, sq_recv.at[mine], chan_sems.at[0, step], chan_sems.at[1, step],
            device_id={"chan": peer}, device_id_type=mesh_ids,
        )

    for step in range(1, chans):
        chan_copy(step).start()
    inputs[3].wait()
    spec_src = lambda peer: spec_ref.at[peer]
    spec_own = pltpu.make_async_copy(spec_ref.at[me], spec_recv.at[me], own_sems.at[0])
    spec_own.start()
    start_all(spec_src, spec_recv.at[me], spec_sems)
    for step in range(1, chans):
        copy = chan_copy(step)
        copy.wait_send()
        copy.wait_recv()
    total = part
    for step in range(1, chans):
        other = lax.rem(mine + step, chans)
        total = total + sq_recv[other][0:1, :]
    inputs[1].wait()
    inputs[2].wait()
    scale = lax.rsqrt(total / CHANNELS + 1e-06)
    scale = jnp.transpose(jnp.broadcast_to(scale, (8, scale.shape[1])))[:, 0:1]
    signal = (feat * scale * gain_ref[...] * gate_ref[...].astype(jnp.float32)).astype(jnp.bfloat16)
    wide = signal.astype(jnp.float32)
    lanes = wide.shape[1]
    pair = lanes // count
    tiles = wide.shape[0] // lanes
    chunk = pair * tiles
    for tile in range(tiles):
        sig_turn[...] = jnp.transpose(wide[lanes * tile:lanes * (tile + 1), :])
        for chan in range(pair):
            rows = sig_turn[pl.ds(chan, count, stride=pair), :]
            sig_send[pl.ds(tiles * chan + tile, count, stride=chunk), :] = rows

    def rows_of(buffer):
        return lambda peer: buffer.at[pl.ds(pl.multiple_of(peer * chunk, chunk), chunk)]

    wire_out[...] = sig_send[...].astype(wire_out.dtype)
    sig_own = pltpu.make_async_copy(rows_of(wire_out)(me), rows_of(wire_in)(me), own_sems.at[1])
    sig_own.start()
    start_all(rows_of(wire_out), rows_of(wire_in)(me), sig_sems)
    finish_all(rows_of(wire_out), rows_of(wire_in)(me), sig_sems)
    sig_own.wait()
    sig_recv[...] = wire_in[...].astype(jnp.float32)

    for chan in range(pair):
        for tile in range(tiles):
            rows = sig_recv[pl.ds(tiles * chan + tile, count, stride=chunk), :]
            cols[chan, pl.ds(tile, count, stride=tiles), :] = rows

    first_len = tc_ref.shape[0]
    for load in loads:
        load.wait()
    boths = []
    for chan in range(pair):
        signal_cols = cols[chan].astype(jnp.bfloat16)
        boths.append(jnp.dot(st_hi[...], signal_cols, preferred_element_type=jnp.float32))

    cos_twist, sin_twist = tc_ref[...], ts_ref[...]
    own_rows = first_len // count
    freqs = []
    for chan in range(pair):
        p_cos = boths[chan][:first_len]
        p_sin = boths[chan][first_len:]
        twist_re = p_cos * cos_twist - p_sin * sin_twist
        twist_im = -p_sin * cos_twist - p_cos * sin_twist
        freqs.append(dot3(twist_re, (fa_hi[...], fa_lo[...])) + dot3(twist_im, (fb_hi[...], fb_lo[...])))

    finish_all(spec_src, spec_recv.at[me], spec_sems)
    spec_own.wait()

    for chan in range(pair):
        freq = freqs[chan]
        freq_re, freq_im = freq[:, :lanes], freq[:, lanes:]
        filt = []
        for part_of in range(2):
            block = spec_recv[:, pl.ds((2 * chan + part_of) * own_rows, own_rows), :]
            filt.append(block.astype(jnp.float32).reshape(first_len, lanes))
        filt_re, filt_im = filt
        prod_re = freq_re * filt_re - freq_im * filt_im
        prod_im = freq_re * filt_im + freq_im * filt_re
        back = dot3(prod_re, (ia_hi[...], ia_lo[...])) + dot3(prod_im, (ib_hi[...], ib_lo[...]))
        back_re, back_im = back[:, :lanes], back[:, lanes:]
        untwist_re = back_re * cos_twist - back_im * sin_twist
        untwist_im = back_im * cos_twist + back_re * sin_twist
        conv_one[...] = dot3((lc_hi[...], lc_lo[...]), untwist_re) + dot3((ls_hi[...], ls_lo[...]), untwist_im)
        for tile in range(tiles):
            rows = conv_one[pl.ds(tile, count, stride=tiles), :]
            conv_send[pl.ds(tiles * chan + tile, count, stride=chunk), :] = rows

    res_out[...] = conv_send[...].astype(res_out.dtype)
    res_src = rows_of(res_out)
    res_dst = rows_of(res_in)(me)
    res_own = pltpu.make_async_copy(res_src(me), res_dst, own_sems.at[2])
    res_own.start()
    start_all(res_src, res_dst, res_sems)
    finish_all(res_src, res_dst, res_sems)
    res_own.wait()
    res_recv[...] = res_in[...].astype(jnp.float32)

    inputs[4].wait()
    inputs[5].wait()
    skip = skip_ref[...]
    for tile in range(tiles):
        for chan in range(pair):
            sig_turn[pl.ds(chan, count, stride=pair), :] = res_recv[pl.ds(tiles * chan + tile, count, stride=chunk), :]
        block = jnp.transpose(sig_turn[...])
        these = slice(lanes * tile, lanes * (tile + 1))
        direct = signal[these, :].astype(jnp.float32)
        gated = post_ref[these, :].astype(jnp.float32) * (block + skip * direct)
        gated_out[these, :] = gated.astype(gated_out.dtype)


def whole(features, pre_gate, gain_row, spec_rows, post_gate, skip_row, tables, chans):
    count = spec_rows.shape[0]
    length, width = features.shape
    pair = width // count
    lanes = 128
    chunk = pair * length // lanes
    vmem = pl.BlockSpec(memory_space=pltpu.VMEM)
    operands = (features, pre_gate, gain_row, spec_rows, post_gate, skip_row) + tuple(tables)
    hbm = pl.BlockSpec(memory_space=pl.ANY)
    return pl.pallas_call(
        whole_kernel,
        out_shape=jax.ShapeDtypeStruct((length, width), jnp.bfloat16),
        in_specs=[hbm] * len(operands),
        out_specs=vmem,
        scratch_shapes=[
            pltpu.VMEM((8, length), jnp.float32),
            pltpu.VMEM((chans, 8, length), jnp.float32),
            pltpu.VMEM((lanes, lanes), jnp.float32),
            pltpu.VMEM((count * chunk, lanes), jnp.float32),
            pltpu.VMEM((count * chunk, lanes), jnp.float32),
            pltpu.VMEM(spec_rows.shape, spec_rows.dtype),
            pltpu.VMEM((pair, count * chunk // pair, lanes), jnp.float32),
            pltpu.VMEM((count * chunk // pair, lanes), jnp.float32),
            pltpu.VMEM((count * chunk, lanes), jnp.float32),
            pltpu.VMEM((count * chunk, lanes), jnp.float32),
            pltpu.VMEM((count * chunk, lanes), jnp.bfloat16),
            pltpu.VMEM((count * chunk, lanes), jnp.bfloat16),
            pltpu.VMEM((count * chunk, lanes), jnp.bfloat16),
            pltpu.VMEM((count * chunk, lanes), jnp.bfloat16),
            pltpu.SemaphoreType.DMA((2, count)),
            pltpu.SemaphoreType.DMA((2, count)),
            pltpu.SemaphoreType.DMA((2, count)),
            pltpu.SemaphoreType.DMA((2, chans)),
            pltpu.SemaphoreType.DMA((3,)),
            pltpu.SemaphoreType.DMA((len(operands),)),
        ]
        + [pltpu.VMEM(table.shape, table.dtype) for table in operands],
        compiler_params=pltpu.CompilerParams(
            collective_id=0, has_side_effects=True, vmem_limit_bytes=67043328
        ),
    )(*operands)


def dft_tables(seq_count, tok_rows):
    stride = 2 * seq_count
    first_len = stride * ROW_GROUP
    all_bins = stride * tok_rows
    second_len = all_bins // first_len
    half_first = first_len // 2
    row_bins = bin_rows(seq_count).astype(np.int64)
    first_turn = (row_bins[:, None] * np.arange(half_first)[None, :]) % first_len * (2.0 * np.pi / first_len)
    cos_first, sin_first = np.cos(first_turn), np.sin(first_turn)
    twist_turn = (row_bins[:, None] * np.arange(second_len)[None, :]) % all_bins * (2.0 * np.pi / all_bins)
    second_in = np.arange(second_len)
    second_turn = (second_in[:, None] * second_in[None, :]) % second_len * (2.0 * np.pi / second_len)
    cos_second, sin_second = np.cos(second_turn), np.sin(second_turn)

    def pair_of(array):
        array = array.astype(np.float32)
        high = array.astype(jnp.bfloat16)
        return [jnp.asarray(high), jnp.asarray((array - high.astype(np.float32)).astype(jnp.bfloat16))]

    tables = pair_of(np.concatenate([cos_first, sin_first], 0))
    tables += [jnp.asarray(np.cos(twist_turn).astype(np.float32)), jnp.asarray(np.sin(twist_turn).astype(np.float32))]
    tables += pair_of(np.concatenate([cos_second, -sin_second], 1))
    tables += pair_of(np.concatenate([sin_second, cos_second], 1))
    tables += pair_of(np.concatenate([cos_second, sin_second], 1))
    tables += pair_of(np.concatenate([-sin_second, cos_second], 1))
    tables += pair_of(cos_first.T / all_bins)
    tables += pair_of(-sin_first.T / all_bins)
    return tables


def local(features, pre_gate, post_gate, norm_gain, skip_weight, spectrum):
    tok_rows, chan_width = features.shape
    seq_count = lax.axis_size("seq")
    chans = lax.axis_size("chan")
    group = chan_width // seq_count
    second_len = tok_rows // ROW_GROUP
    lanes = 128
    tok_tiles = tok_rows // lanes

    spec_rows = spectrum.reshape(2, 2, second_len, ROW_GROUP, chan_width)
    spec_rows = jnp.transpose(spec_rows, (4, 0, 1, 3, 2)).astype(jnp.bfloat16)
    spec_rows = spec_rows.reshape(seq_count, -1, second_len)
    return whole(
        features, pre_gate, norm_gain.reshape(1, chan_width), spec_rows,
        post_gate, skip_weight.reshape(1, chan_width), dft_tables(seq_count, tok_rows), chans,
    )


def solution(mesh):
    return jax.shard_map(
        local,
        mesh=mesh,
        in_specs=(
            P("seq", "chan"),
            P("seq", "chan"),
            P("seq", "chan"),
            P("chan"),
            P("chan"),
            P(None, "seq", None, "chan"),
        ),
        out_specs=P("seq", "chan"),
        check_vma=False,
    )
```

```python
import math

import jax
import jax.numpy as jnp
import numpy as np
from jax import lax
from jax.experimental import pallas as pl
from jax.experimental.pallas import tpu as pltpu
from jax.sharding import PartitionSpec as P

CHANNELS = 512
ROW_GROUP = 4
TABLE_NAMES = ("st_hi", "st_lo", "tc", "ts", "fa_hi", "fa_lo", "fb_hi", "fb_lo", "ia_hi", "ia_lo", "ib_hi", "ib_lo",
               "lc_hi", "lc_lo", "ls_hi", "ls_lo")
HIGH_DIGIT = 8


PRECISE = lax.Precision.HIGH
FULL_TURN = 2.0 * math.pi


def reversed_digits(count):
    levels = count.bit_length() - 1
    positions = np.arange(count)
    result = np.zeros(count, np.int64)
    for bit_pos in range(levels):
        result = result + ((positions >> bit_pos & 1) << levels - 1 - bit_pos)
    return result


def rotation(numerator, denominator):
    angle = (numerator % denominator).astype(jnp.float32) * (FULL_TURN / denominator)
    return (jnp.cos(angle), jnp.sin(angle))


def mm(spec, left, right):
    return jnp.einsum(spec, left, right, precision=PRECISE, preferred_element_type=jnp.float32)


def bin_rows(seq_count):
    digit_order = reversed_digits(seq_count)
    stride = 2 * seq_count
    slots = np.arange(stride)
    low_bins = 2 * digit_order[slots // 2] + slots % 2
    return (low_bins[:, None] + stride * np.arange(ROW_GROUP)[None, :]).reshape(-1).astype(np.int32)


def split(value):
    high = value.astype(jnp.bfloat16)
    return high, (value - high.astype(jnp.float32)).astype(jnp.bfloat16)


def dot3(left, right):
    if isinstance(left, tuple):
        return jnp.dot(left[0], right.astype(jnp.bfloat16), preferred_element_type=jnp.float32)
    return jnp.dot(left.astype(jnp.bfloat16), right[0], preferred_element_type=jnp.float32)


def whole_kernel(*refs):
    table_count = len(TABLE_NAMES) + 6
    held = refs[:table_count]
    gated_out = refs[table_count]
    (sq_mine, sq_recv, sig_turn, sig_send, sig_recv, spec_recv, cols, conv_one, conv_send, res_recv,
     wire_out, wire_in, res_out, res_in, spec_send, spec_sems, sig_sems, res_sems, chan_sems, own_sems, table_sems) = (
        refs[table_count + 1:table_count + 22])
    tables = refs[table_count + 22:]
    loads = [pltpu.make_async_copy(held[k], tables[k], table_sems.at[k]) for k in range(table_count)]
    for load in loads:
        load.start()
    inputs = loads[:6]
    loads = loads[6:]
    feat_ref, gate_ref, gain_ref, spec_ref, post_ref, skip_ref = tables[:6]
    tables = tables[6:]
    (st_hi, st_lo, tc_ref, ts_ref, fa_hi, fa_lo, fb_hi, fb_lo, ia_hi, ia_lo, ib_hi, ib_lo,
     lc_hi, lc_lo, ls_hi, ls_lo) = tables
    count = spec_ref.shape[0]
    chans = sq_recv.shape[0]
    me = lax.axis_index("seq")
    mine = lax.axis_index("chan")
    mesh_ids = pl.DeviceIdType.MESH
    barrier = pltpu.get_barrier_semaphore()

    def greet(step, carry):
        peer = lax.rem(me + step, count)
        pl.semaphore_signal(barrier, inc=1, device_id={"seq": peer}, device_id_type=mesh_ids)
        return carry

    lax.fori_loop(1, count, greet, 0)
    for step in range(1, chans):
        peer = lax.rem(mine + step, chans)
        pl.semaphore_signal(barrier, inc=1, device_id={"chan": peer}, device_id_type=mesh_ids)
    inputs[0].wait()
    feat = feat_ref[...].astype(jnp.float32)
    part = jnp.sum(jnp.transpose(feat * feat), axis=0, keepdims=True)
    sq_mine[...] = jnp.broadcast_to(part, sq_mine.shape)
    pl.semaphore_wait(barrier, count + chans - 2)

    def seq_copy(source, target, sems, step):
        peer = lax.rem(me + step, count)
        return pltpu.make_async_remote_copy(
            source(peer), target, sems.at[0, step], sems.at[1, step],
            device_id={"seq": peer}, device_id_type=mesh_ids,
        )

    def start_all(source, target, sems):
        def body(step, carry):
            seq_copy(source, target, sems, step).start()
            return carry
        lax.fori_loop(1, count, body, 0)

    def finish_all(source, target, sems):
        def body(step, carry):
            copy = seq_copy(source, target, sems, step)
            copy.wait_send()
            copy.wait_recv()
            return carry
        lax.fori_loop(1, count, body, 0)


    def chan_copy(step):
        peer = lax.rem(mine + step, chans)
        return pltpu.make_async_remote_copy(
            sq_mine, sq_recv.at[mine], chan_sems.at[0, step], chan_sems.at[1, step],
            device_id={"chan": peer}, device_id_type=mesh_ids,
        )

    for step in range(1, chans):
        chan_copy(step).start()
    inputs[3].wait()
    spec_send[...] = spec_ref[...].astype(spec_send.dtype)
    spec_src = lambda peer: spec_send.at[peer]
    spec_own = pltpu.make_async_copy(spec_send.at[me], spec_recv.at[me], own_sems.at[0])
    spec_own.start()
    start_all(spec_src, spec_recv.at[me], spec_sems)
    for step in range(1, chans):
        copy = chan_copy(step)
        copy.wait_send()
        copy.wait_recv()
    total = part
    for step in range(1, chans):
        other = lax.rem(mine + step, chans)
        total = total + sq_recv[other][0:1, :]
    inputs[1].wait()
    inputs[2].wait()
    scale = lax.rsqrt(total / CHANNELS + 1e-06)
    scale = jnp.transpose(jnp.broadcast_to(scale, (8, scale.shape[1])))[:, 0:1]
    signal = (feat * scale * gain_ref[...] * gate_ref[...].astype(jnp.float32)).astype(jnp.bfloat16)
    wide = signal.astype(jnp.float32)
    lanes = wide.shape[1]
    pair = lanes // count
    tiles = wide.shape[0] // lanes
    chunk = pair * tiles
    for tile in range(tiles):
        sig_turn[...] = jnp.transpose(wide[lanes * tile:lanes * (tile + 1), :])
        for chan in range(pair):
            rows = sig_turn[pl.ds(chan, count, stride=pair), :]
            sig_send[pl.ds(tiles * chan + tile, count, stride=chunk), :] = rows

    def rows_of(buffer):
        return lambda peer: buffer.at[pl.ds(pl.multiple_of(peer * chunk, chunk), chunk)]

    wire_out[...] = sig_send[...].astype(wire_out.dtype)
    sig_own = pltpu.make_async_copy(rows_of(wire_out)(me), rows_of(wire_in)(me), own_sems.at[1])
    sig_own.start()
    start_all(rows_of(wire_out), rows_of(wire_in)(me), sig_sems)
    finish_all(rows_of(wire_out), rows_of(wire_in)(me), sig_sems)
    sig_own.wait()
    sig_recv[...] = wire_in[...].astype(jnp.float32)

    for chan in range(pair):
        for tile in range(tiles):
            rows = sig_recv[pl.ds(tiles * chan + tile, count, stride=chunk), :]
            cols[chan, pl.ds(tile, count, stride=tiles), :] = rows

    first_len = tc_ref.shape[0]
    for load in loads:
        load.wait()
    boths = []
    for chan in range(pair):
        signal_cols = cols[chan].astype(jnp.bfloat16)
        boths.append(jnp.dot(st_hi[...], signal_cols, preferred_element_type=jnp.float32))

    cos_twist, sin_twist = tc_ref[...], ts_ref[...]
    own_rows = first_len // count
    freqs = []
    for chan in range(pair):
        p_cos = boths[chan][:first_len]
        p_sin = boths[chan][first_len:]
        twist_re = p_cos * cos_twist - p_sin * sin_twist
        twist_im = -p_sin * cos_twist - p_cos * sin_twist
        freqs.append(dot3(twist_re, (fa_hi[...], fa_lo[...])) + dot3(twist_im, (fb_hi[...], fb_lo[...])))

    finish_all(spec_src, spec_recv.at[me], spec_sems)
    spec_own.wait()

    for chan in range(pair):
        freq = freqs[chan]
        freq_re, freq_im = freq[:, :lanes], freq[:, lanes:]
        filt = []
        for part_of in range(2):
            block = spec_recv[:, pl.ds((2 * chan + part_of) * own_rows, own_rows), :]
            filt.append(block.astype(jnp.float32).reshape(first_len, lanes))
        filt_re, filt_im = filt
        prod_re = freq_re * filt_re - freq_im * filt_im
        prod_im = freq_re * filt_im + freq_im * filt_re
        back = dot3(prod_re, (ia_hi[...], ia_lo[...])) + dot3(prod_im, (ib_hi[...], ib_lo[...]))
        back_re, back_im = back[:, :lanes], back[:, lanes:]
        untwist_re = back_re * cos_twist - back_im * sin_twist
        untwist_im = back_im * cos_twist + back_re * sin_twist
        conv_one[...] = dot3((lc_hi[...], lc_lo[...]), untwist_re) + dot3((ls_hi[...], ls_lo[...]), untwist_im)
        for tile in range(tiles):
            rows = conv_one[pl.ds(tile, count, stride=tiles), :]
            conv_send[pl.ds(tiles * chan + tile, count, stride=chunk), :] = rows

    res_out[...] = conv_send[...].astype(res_out.dtype)
    res_src = rows_of(res_out)
    res_dst = rows_of(res_in)(me)
    res_own = pltpu.make_async_copy(res_src(me), res_dst, own_sems.at[2])
    res_own.start()
    start_all(res_src, res_dst, res_sems)
    finish_all(res_src, res_dst, res_sems)
    res_own.wait()
    res_recv[...] = res_in[...].astype(jnp.float32)

    inputs[4].wait()
    inputs[5].wait()
    skip = skip_ref[...]
    for tile in range(tiles):
        for chan in range(pair):
            sig_turn[pl.ds(chan, count, stride=pair), :] = res_recv[pl.ds(tiles * chan + tile, count, stride=chunk), :]
        block = jnp.transpose(sig_turn[...])
        these = slice(lanes * tile, lanes * (tile + 1))
        direct = signal[these, :].astype(jnp.float32)
        gated = post_ref[these, :].astype(jnp.float32) * (block + skip * direct)
        gated_out[these, :] = gated.astype(gated_out.dtype)


def whole(features, pre_gate, gain_row, spec_rows, post_gate, skip_row, tables, chans):
    count = spec_rows.shape[0]
    length, width = features.shape
    pair = width // count
    lanes = 128
    chunk = pair * length // lanes
    vmem = pl.BlockSpec(memory_space=pltpu.VMEM)
    operands = (features, pre_gate, gain_row, spec_rows, post_gate, skip_row) + tuple(tables)
    hbm = pl.BlockSpec(memory_space=pl.ANY)
    return pl.pallas_call(
        whole_kernel,
        out_shape=jax.ShapeDtypeStruct((length, width), jnp.bfloat16),
        in_specs=[hbm] * len(operands),
        out_specs=vmem,
        scratch_shapes=[
            pltpu.VMEM((8, length), jnp.float32),
            pltpu.VMEM((chans, 8, length), jnp.float32),
            pltpu.VMEM((lanes, lanes), jnp.float32),
            pltpu.VMEM((count * chunk, lanes), jnp.float32),
            pltpu.VMEM((count * chunk, lanes), jnp.float32),
            pltpu.VMEM(spec_rows.shape, jnp.bfloat16),
            pltpu.VMEM((pair, count * chunk // pair, lanes), jnp.float32),
            pltpu.VMEM((count * chunk // pair, lanes), jnp.float32),
            pltpu.VMEM((count * chunk, lanes), jnp.float32),
            pltpu.VMEM((count * chunk, lanes), jnp.float32),
            pltpu.VMEM((count * chunk, lanes), jnp.bfloat16),
            pltpu.VMEM((count * chunk, lanes), jnp.bfloat16),
            pltpu.VMEM((count * chunk, lanes), jnp.bfloat16),
            pltpu.VMEM((count * chunk, lanes), jnp.bfloat16),
            pltpu.VMEM(spec_rows.shape, jnp.bfloat16),
            pltpu.SemaphoreType.DMA((2, count)),
            pltpu.SemaphoreType.DMA((2, count)),
            pltpu.SemaphoreType.DMA((2, count)),
            pltpu.SemaphoreType.DMA((2, chans)),
            pltpu.SemaphoreType.DMA((3,)),
            pltpu.SemaphoreType.DMA((len(operands),)),
        ]
        + [pltpu.VMEM(table.shape, table.dtype) for table in operands],
        compiler_params=pltpu.CompilerParams(
            collective_id=0, has_side_effects=True, vmem_limit_bytes=67043328
        ),
    )(*operands)


def dft_tables(seq_count, tok_rows):
    stride = 2 * seq_count
    first_len = stride * ROW_GROUP
    all_bins = stride * tok_rows
    second_len = all_bins // first_len
    half_first = first_len // 2
    row_bins = bin_rows(seq_count).astype(np.int64)
    first_turn = (row_bins[:, None] * np.arange(half_first)[None, :]) % first_len * (2.0 * np.pi / first_len)
    cos_first, sin_first = np.cos(first_turn), np.sin(first_turn)
    twist_turn = (row_bins[:, None] * np.arange(second_len)[None, :]) % all_bins * (2.0 * np.pi / all_bins)
    second_in = np.arange(second_len)
    second_turn = (second_in[:, None] * second_in[None, :]) % second_len * (2.0 * np.pi / second_len)
    cos_second, sin_second = np.cos(second_turn), np.sin(second_turn)

    def pair_of(array):
        array = array.astype(np.float32)
        high = array.astype(jnp.bfloat16)
        return [jnp.asarray(high), jnp.asarray((array - high.astype(np.float32)).astype(jnp.bfloat16))]

    tables = pair_of(np.concatenate([cos_first, sin_first], 0))
    tables += [jnp.asarray(np.cos(twist_turn).astype(np.float32)), jnp.asarray(np.sin(twist_turn).astype(np.float32))]
    tables += pair_of(np.concatenate([cos_second, -sin_second], 1))
    tables += pair_of(np.concatenate([sin_second, cos_second], 1))
    tables += pair_of(np.concatenate([cos_second, sin_second], 1))
    tables += pair_of(np.concatenate([-sin_second, cos_second], 1))
    tables += pair_of(cos_first.T / all_bins)
    tables += pair_of(-sin_first.T / all_bins)
    return tables


def local(features, pre_gate, post_gate, norm_gain, skip_weight, spectrum):
    tok_rows, chan_width = features.shape
    seq_count = lax.axis_size("seq")
    chans = lax.axis_size("chan")
    group = chan_width // seq_count
    second_len = tok_rows // ROW_GROUP
    lanes = 128
    tok_tiles = tok_rows // lanes

    spec_rows = spectrum.reshape(2, 2, second_len, ROW_GROUP, chan_width)
    spec_rows = jnp.transpose(spec_rows, (4, 0, 1, 3, 2)).reshape(seq_count, -1, second_len)
    return whole(
        features, pre_gate, norm_gain.reshape(1, chan_width), spec_rows,
        post_gate, skip_weight.reshape(1, chan_width), dft_tables(seq_count, tok_rows), chans,
    )


def solution(mesh):
    return jax.shard_map(
        local,
        mesh=mesh,
        in_specs=(
            P("seq", "chan"),
            P("seq", "chan"),
            P("seq", "chan"),
            P("chan"),
            P("chan"),
            P(None, "seq", None, "chan"),
        ),
        out_specs=P("seq", "chan"),
        check_vma=False,
    )
```

```python
import math

import jax
import jax.numpy as jnp
import numpy as np
from jax import lax
from jax.experimental import pallas as pl
from jax.experimental.pallas import tpu as pltpu
from jax.sharding import PartitionSpec as P

CHANNELS = 512
ROW_GROUP = 4
TABLE_NAMES = ("st_hi", "st_lo", "tc", "ts", "fa_hi", "fa_lo", "fb_hi", "fb_lo", "ia_hi", "ia_lo", "ib_hi", "ib_lo",
               "lc_hi", "lc_lo", "ls_hi", "ls_lo")
HIGH_DIGIT = 8


PRECISE = lax.Precision.HIGH
FULL_TURN = 2.0 * math.pi


def reversed_digits(count):
    levels = count.bit_length() - 1
    positions = np.arange(count)
    result = np.zeros(count, np.int64)
    for bit_pos in range(levels):
        result = result + ((positions >> bit_pos & 1) << levels - 1 - bit_pos)
    return result


def rotation(numerator, denominator):
    angle = (numerator % denominator).astype(jnp.float32) * (FULL_TURN / denominator)
    return (jnp.cos(angle), jnp.sin(angle))


def mm(spec, left, right):
    return jnp.einsum(spec, left, right, precision=PRECISE, preferred_element_type=jnp.float32)


def bin_rows(seq_count):
    digit_order = reversed_digits(seq_count)
    stride = 2 * seq_count
    slots = np.arange(stride)
    low_bins = 2 * digit_order[slots // 2] + slots % 2
    return (low_bins[:, None] + stride * np.arange(ROW_GROUP)[None, :]).reshape(-1).astype(np.int32)


def split(value):
    high = value.astype(jnp.bfloat16)
    return high, (value - high.astype(jnp.float32)).astype(jnp.bfloat16)


def dot3(left, right):
    if isinstance(left, tuple):
        return jnp.dot(left[0], right.astype(jnp.bfloat16), preferred_element_type=jnp.float32)
    return jnp.dot(left.astype(jnp.bfloat16), right[0], preferred_element_type=jnp.float32)


def whole_kernel(*refs):
    table_count = len(TABLE_NAMES) + 6
    held = refs[:table_count]
    gated_out = refs[table_count]
    (sq_mine, sq_recv, sig_turn, sig_send, sig_recv, spec_recv, cols, conv_one, conv_send, res_recv,
     wire_out, wire_in, res_out, res_in, spec_send, spec_sems, sig_sems, res_sems, chan_sems, own_sems, table_sems) = (
        refs[table_count + 1:table_count + 22])
    tables = refs[table_count + 22:]
    loads = [pltpu.make_async_copy(held[k], tables[k], table_sems.at[k]) for k in range(table_count)]
    for load in loads:
        load.start()
    inputs = loads[:6]
    loads = loads[6:]
    feat_ref, gate_ref, gain_ref, spec_ref, post_ref, skip_ref = tables[:6]
    tables = tables[6:]
    (st_hi, st_lo, tc_ref, ts_ref, fa_hi, fa_lo, fb_hi, fb_lo, ia_hi, ia_lo, ib_hi, ib_lo,
     lc_hi, lc_lo, ls_hi, ls_lo) = tables
    count = spec_ref.shape[0]
    chans = sq_recv.shape[0]
    me = lax.axis_index("seq")
    mine = lax.axis_index("chan")
    mesh_ids = pl.DeviceIdType.MESH
    barrier = pltpu.get_barrier_semaphore()

    def greet(step, carry):
        peer = lax.rem(me + step, count)
        pl.semaphore_signal(barrier, inc=1, device_id={"seq": peer}, device_id_type=mesh_ids)
        return carry

    lax.fori_loop(1, count, greet, 0)
    for step in range(1, chans):
        peer = lax.rem(mine + step, chans)
        pl.semaphore_signal(barrier, inc=1, device_id={"chan": peer}, device_id_type=mesh_ids)
    inputs[0].wait()
    feat = feat_ref[...].astype(jnp.float32)
    part = jnp.sum(jnp.transpose(feat * feat), axis=0, keepdims=True)
    sq_mine[...] = jnp.broadcast_to(part, sq_mine.shape)
    inputs[3].wait()
    spec_send[...] = spec_ref[...].astype(spec_send.dtype)
    pl.semaphore_wait(barrier, count + chans - 2)

    def seq_copy(source, target, sems, step):
        peer = lax.rem(me + step, count)
        return pltpu.make_async_remote_copy(
            source(peer), target, sems.at[0, step], sems.at[1, step],
            device_id={"seq": peer}, device_id_type=mesh_ids,
        )

    def start_all(source, target, sems):
        def body(step, carry):
            seq_copy(source, target, sems, step).start()
            return carry
        lax.fori_loop(1, count, body, 0)

    def finish_all(source, target, sems):
        def body(step, carry):
            copy = seq_copy(source, target, sems, step)
            copy.wait_send()
            copy.wait_recv()
            return carry
        lax.fori_loop(1, count, body, 0)


    def chan_copy(step):
        peer = lax.rem(mine + step, chans)
        return pltpu.make_async_remote_copy(
            sq_mine, sq_recv.at[mine], chan_sems.at[0, step], chan_sems.at[1, step],
            device_id={"chan": peer}, device_id_type=mesh_ids,
        )

    for step in range(1, chans):
        chan_copy(step).start()
    spec_src = lambda peer: spec_send.at[peer]
    spec_own = pltpu.make_async_copy(spec_send.at[me], spec_recv.at[me], own_sems.at[0])
    spec_own.start()
    start_all(spec_src, spec_recv.at[me], spec_sems)
    for step in range(1, chans):
        copy = chan_copy(step)
        copy.wait_send()
        copy.wait_recv()
    total = part
    for step in range(1, chans):
        other = lax.rem(mine + step, chans)
        total = total + sq_recv[other][0:1, :]
    inputs[1].wait()
    inputs[2].wait()
    scale = lax.rsqrt(total / CHANNELS + 1e-06)
    scale = jnp.transpose(jnp.broadcast_to(scale, (8, scale.shape[1])))[:, 0:1]
    signal = (feat * scale * gain_ref[...] * gate_ref[...].astype(jnp.float32)).astype(jnp.bfloat16)
    wide = signal.astype(jnp.float32)
    lanes = wide.shape[1]
    pair = lanes // count
    tiles = wide.shape[0] // lanes
    chunk = pair * tiles
    for tile in range(tiles):
        sig_turn[...] = jnp.transpose(wide[lanes * tile:lanes * (tile + 1), :])
        for chan in range(pair):
            rows = sig_turn[pl.ds(chan, count, stride=pair), :]
            sig_send[pl.ds(tiles * chan + tile, count, stride=chunk), :] = rows

    def rows_of(buffer):
        return lambda peer: buffer.at[pl.ds(pl.multiple_of(peer * chunk, chunk), chunk)]

    wire_out[...] = sig_send[...].astype(wire_out.dtype)
    sig_own = pltpu.make_async_copy(rows_of(wire_out)(me), rows_of(wire_in)(me), own_sems.at[1])
    sig_own.start()
    start_all(rows_of(wire_out), rows_of(wire_in)(me), sig_sems)
    finish_all(rows_of(wire_out), rows_of(wire_in)(me), sig_sems)
    sig_own.wait()
    sig_recv[...] = wire_in[...].astype(jnp.float32)

    for chan in range(pair):
        for tile in range(tiles):
            rows = sig_recv[pl.ds(tiles * chan + tile, count, stride=chunk), :]
            cols[chan, pl.ds(tile, count, stride=tiles), :] = rows

    first_len = tc_ref.shape[0]
    for load in loads:
        load.wait()
    boths = []
    for chan in range(pair):
        signal_cols = cols[chan].astype(jnp.bfloat16)
        boths.append(jnp.dot(st_hi[...], signal_cols, preferred_element_type=jnp.float32))

    cos_twist, sin_twist = tc_ref[...], ts_ref[...]
    own_rows = first_len // count
    freqs = []
    for chan in range(pair):
        p_cos = boths[chan][:first_len]
        p_sin = boths[chan][first_len:]
        twist_re = p_cos * cos_twist - p_sin * sin_twist
        twist_im = -p_sin * cos_twist - p_cos * sin_twist
        freqs.append(dot3(twist_re, (fa_hi[...], fa_lo[...])) + dot3(twist_im, (fb_hi[...], fb_lo[...])))

    finish_all(spec_src, spec_recv.at[me], spec_sems)
    spec_own.wait()

    for chan in range(pair):
        freq = freqs[chan]
        freq_re, freq_im = freq[:, :lanes], freq[:, lanes:]
        filt = []
        for part_of in range(2):
            block = spec_recv[:, pl.ds((2 * chan + part_of) * own_rows, own_rows), :]
            filt.append(block.astype(jnp.float32).reshape(first_len, lanes))
        filt_re, filt_im = filt
        prod_re = freq_re * filt_re - freq_im * filt_im
        prod_im = freq_re * filt_im + freq_im * filt_re
        back = dot3(prod_re, (ia_hi[...], ia_lo[...])) + dot3(prod_im, (ib_hi[...], ib_lo[...]))
        back_re, back_im = back[:, :lanes], back[:, lanes:]
        untwist_re = back_re * cos_twist - back_im * sin_twist
        untwist_im = back_im * cos_twist + back_re * sin_twist
        conv_one[...] = dot3((lc_hi[...], lc_lo[...]), untwist_re) + dot3((ls_hi[...], ls_lo[...]), untwist_im)
        for tile in range(tiles):
            rows = conv_one[pl.ds(tile, count, stride=tiles), :]
            conv_send[pl.ds(tiles * chan + tile, count, stride=chunk), :] = rows

    res_out[...] = conv_send[...].astype(res_out.dtype)
    res_src = rows_of(res_out)
    res_dst = rows_of(res_in)(me)
    res_own = pltpu.make_async_copy(res_src(me), res_dst, own_sems.at[2])
    res_own.start()
    start_all(res_src, res_dst, res_sems)
    finish_all(res_src, res_dst, res_sems)
    res_own.wait()
    res_recv[...] = res_in[...].astype(jnp.float32)

    inputs[4].wait()
    inputs[5].wait()
    skip = skip_ref[...]
    for tile in range(tiles):
        for chan in range(pair):
            sig_turn[pl.ds(chan, count, stride=pair), :] = res_recv[pl.ds(tiles * chan + tile, count, stride=chunk), :]
        block = jnp.transpose(sig_turn[...])
        these = slice(lanes * tile, lanes * (tile + 1))
        direct = signal[these, :].astype(jnp.float32)
        gated = post_ref[these, :].astype(jnp.float32) * (block + skip * direct)
        gated_out[these, :] = gated.astype(gated_out.dtype)


def whole(features, pre_gate, gain_row, spec_rows, post_gate, skip_row, tables, chans):
    count = spec_rows.shape[0]
    length, width = features.shape
    pair = width // count
    lanes = 128
    chunk = pair * length // lanes
    vmem = pl.BlockSpec(memory_space=pltpu.VMEM)
    operands = (features, pre_gate, gain_row, spec_rows, post_gate, skip_row) + tuple(tables)
    hbm = pl.BlockSpec(memory_space=pl.ANY)
    return pl.pallas_call(
        whole_kernel,
        out_shape=jax.ShapeDtypeStruct((length, width), jnp.bfloat16),
        in_specs=[hbm] * len(operands),
        out_specs=vmem,
        scratch_shapes=[
            pltpu.VMEM((8, length), jnp.float32),
            pltpu.VMEM((chans, 8, length), jnp.float32),
            pltpu.VMEM((lanes, lanes), jnp.float32),
            pltpu.VMEM((count * chunk, lanes), jnp.float32),
            pltpu.VMEM((count * chunk, lanes), jnp.float32),
            pltpu.VMEM(spec_rows.shape, jnp.bfloat16),
            pltpu.VMEM((pair, count * chunk // pair, lanes), jnp.float32),
            pltpu.VMEM((count * chunk // pair, lanes), jnp.float32),
            pltpu.VMEM((count * chunk, lanes), jnp.float32),
            pltpu.VMEM((count * chunk, lanes), jnp.float32),
            pltpu.VMEM((count * chunk, lanes), jnp.bfloat16),
            pltpu.VMEM((count * chunk, lanes), jnp.bfloat16),
            pltpu.VMEM((count * chunk, lanes), jnp.bfloat16),
            pltpu.VMEM((count * chunk, lanes), jnp.bfloat16),
            pltpu.VMEM(spec_rows.shape, jnp.bfloat16),
            pltpu.SemaphoreType.DMA((2, count)),
            pltpu.SemaphoreType.DMA((2, count)),
            pltpu.SemaphoreType.DMA((2, count)),
            pltpu.SemaphoreType.DMA((2, chans)),
            pltpu.SemaphoreType.DMA((3,)),
            pltpu.SemaphoreType.DMA((len(operands),)),
        ]
        + [pltpu.VMEM(table.shape, table.dtype) for table in operands],
        compiler_params=pltpu.CompilerParams(
            collective_id=0, has_side_effects=True, vmem_limit_bytes=67043328
        ),
    )(*operands)


def dft_tables(seq_count, tok_rows):
    stride = 2 * seq_count
    first_len = stride * ROW_GROUP
    all_bins = stride * tok_rows
    second_len = all_bins // first_len
    half_first = first_len // 2
    row_bins = bin_rows(seq_count).astype(np.int64)
    first_turn = (row_bins[:, None] * np.arange(half_first)[None, :]) % first_len * (2.0 * np.pi / first_len)
    cos_first, sin_first = np.cos(first_turn), np.sin(first_turn)
    twist_turn = (row_bins[:, None] * np.arange(second_len)[None, :]) % all_bins * (2.0 * np.pi / all_bins)
    second_in = np.arange(second_len)
    second_turn = (second_in[:, None] * second_in[None, :]) % second_len * (2.0 * np.pi / second_len)
    cos_second, sin_second = np.cos(second_turn), np.sin(second_turn)

    def pair_of(array):
        array = array.astype(np.float32)
        high = array.astype(jnp.bfloat16)
        return [jnp.asarray(high), jnp.asarray((array - high.astype(np.float32)).astype(jnp.bfloat16))]

    tables = pair_of(np.concatenate([cos_first, sin_first], 0))
    tables += [jnp.asarray(np.cos(twist_turn).astype(np.float32)), jnp.asarray(np.sin(twist_turn).astype(np.float32))]
    tables += pair_of(np.concatenate([cos_second, -sin_second], 1))
    tables += pair_of(np.concatenate([sin_second, cos_second], 1))
    tables += pair_of(np.concatenate([cos_second, sin_second], 1))
    tables += pair_of(np.concatenate([-sin_second, cos_second], 1))
    tables += pair_of(cos_first.T / all_bins)
    tables += pair_of(-sin_first.T / all_bins)
    return tables


def local(features, pre_gate, post_gate, norm_gain, skip_weight, spectrum):
    tok_rows, chan_width = features.shape
    seq_count = lax.axis_size("seq")
    chans = lax.axis_size("chan")
    group = chan_width // seq_count
    second_len = tok_rows // ROW_GROUP
    lanes = 128
    tok_tiles = tok_rows // lanes

    spec_rows = spectrum.reshape(2, 2, second_len, ROW_GROUP, chan_width)
    spec_rows = jnp.transpose(spec_rows, (4, 0, 1, 3, 2)).reshape(seq_count, -1, second_len)
    return whole(
        features, pre_gate, norm_gain.reshape(1, chan_width), spec_rows,
        post_gate, skip_weight.reshape(1, chan_width), dft_tables(seq_count, tok_rows), chans,
    )


def solution(mesh):
    return jax.shard_map(
        local,
        mesh=mesh,
        in_specs=(
            P("seq", "chan"),
            P("seq", "chan"),
            P("seq", "chan"),
            P("chan"),
            P("chan"),
            P(None, "seq", None, "chan"),
        ),
        out_specs=P("seq", "chan"),
        check_vma=False,
    )
```

```python
import math

import jax
import jax.numpy as jnp
import numpy as np
from jax import lax
from jax.experimental import pallas as pl
from jax.experimental.pallas import tpu as pltpu
from jax.sharding import PartitionSpec as P

CHANNELS = 512
ROW_GROUP = 4
TABLE_NAMES = ("st", "tc", "ts", "fa", "fb", "ia", "ib", "lc", "ls")
HIGH_DIGIT = 8


PRECISE = lax.Precision.HIGH
FULL_TURN = 2.0 * math.pi


def reversed_digits(count):
    levels = count.bit_length() - 1
    positions = np.arange(count)
    result = np.zeros(count, np.int64)
    for bit_pos in range(levels):
        result = result + ((positions >> bit_pos & 1) << levels - 1 - bit_pos)
    return result


def rotation(numerator, denominator):
    angle = (numerator % denominator).astype(jnp.float32) * (FULL_TURN / denominator)
    return (jnp.cos(angle), jnp.sin(angle))


def mm(spec, left, right):
    return jnp.einsum(spec, left, right, precision=PRECISE, preferred_element_type=jnp.float32)


def bin_rows(seq_count):
    digit_order = reversed_digits(seq_count)
    stride = 2 * seq_count
    slots = np.arange(stride)
    low_bins = 2 * digit_order[slots // 2] + slots % 2
    return (low_bins[:, None] + stride * np.arange(ROW_GROUP)[None, :]).reshape(-1).astype(np.int32)


def split(value):
    high = value.astype(jnp.bfloat16)
    return high, (value - high.astype(jnp.float32)).astype(jnp.bfloat16)


def dot3(left, right):
    if isinstance(left, tuple):
        return jnp.dot(left[0], right.astype(jnp.bfloat16), preferred_element_type=jnp.float32)
    return jnp.dot(left.astype(jnp.bfloat16), right[0], preferred_element_type=jnp.float32)


def whole_kernel(*refs):
    table_count = len(TABLE_NAMES) + 6
    held = refs[:table_count]
    gated_out = refs[table_count]
    (sq_mine, sq_recv, sig_turn, sig_send, sig_recv, spec_recv, cols, conv_one, conv_send, res_recv,
     wire_out, wire_in, res_out, res_in, spec_send, spec_sems, sig_sems, res_sems, chan_sems, own_sems, table_sems) = (
        refs[table_count + 1:table_count + 22])
    tables = refs[table_count + 22:]
    loads = [pltpu.make_async_copy(held[k], tables[k], table_sems.at[k]) for k in range(table_count)]
    for load in loads:
        load.start()
    inputs = loads[:6]
    loads = loads[6:]
    feat_ref, gate_ref, gain_ref, spec_ref, post_ref, skip_ref = tables[:6]
    tables = tables[6:]
    (st_hi, tc_ref, ts_ref, fa_hi, fb_hi, ia_hi, ib_hi, lc_hi, ls_hi) = tables
    count = spec_ref.shape[0]
    chans = sq_recv.shape[0]
    me = lax.axis_index("seq")
    mine = lax.axis_index("chan")
    mesh_ids = pl.DeviceIdType.MESH
    barrier = pltpu.get_barrier_semaphore()

    def greet(step, carry):
        peer = lax.rem(me + step, count)
        pl.semaphore_signal(barrier, inc=1, device_id={"seq": peer}, device_id_type=mesh_ids)
        return carry

    lax.fori_loop(1, count, greet, 0)
    for step in range(1, chans):
        peer = lax.rem(mine + step, chans)
        pl.semaphore_signal(barrier, inc=1, device_id={"chan": peer}, device_id_type=mesh_ids)
    inputs[0].wait()
    feat = feat_ref[...].astype(jnp.float32)
    part = jnp.sum(jnp.transpose(feat * feat), axis=0, keepdims=True)
    sq_mine[...] = jnp.broadcast_to(part, sq_mine.shape)
    inputs[3].wait()
    spec_send[...] = spec_ref[...].astype(spec_send.dtype)
    pl.semaphore_wait(barrier, count + chans - 2)

    def seq_copy(source, target, sems, step):
        peer = lax.rem(me + step, count)
        return pltpu.make_async_remote_copy(
            source(peer), target, sems.at[0, step], sems.at[1, step],
            device_id={"seq": peer}, device_id_type=mesh_ids,
        )

    def start_all(source, target, sems):
        def body(step, carry):
            seq_copy(source, target, sems, step).start()
            return carry
        lax.fori_loop(1, count, body, 0)

    def finish_all(source, target, sems):
        def body(step, carry):
            copy = seq_copy(source, target, sems, step)
            copy.wait_send()
            copy.wait_recv()
            return carry
        lax.fori_loop(1, count, body, 0)


    def chan_copy(step):
        peer = lax.rem(mine + step, chans)
        return pltpu.make_async_remote_copy(
            sq_mine, sq_recv.at[mine], chan_sems.at[0, step], chan_sems.at[1, step],
            device_id={"chan": peer}, device_id_type=mesh_ids,
        )

    for step in range(1, chans):
        chan_copy(step).start()
    spec_src = lambda peer: spec_send.at[peer]
    spec_own = pltpu.make_async_copy(spec_send.at[me], spec_recv.at[me], own_sems.at[0])
    spec_own.start()
    start_all(spec_src, spec_recv.at[me], spec_sems)
    for step in range(1, chans):
        copy = chan_copy(step)
        copy.wait_send()
        copy.wait_recv()
    total = part
    for step in range(1, chans):
        other = lax.rem(mine + step, chans)
        total = total + sq_recv[other][0:1, :]
    inputs[1].wait()
    inputs[2].wait()
    scale = lax.rsqrt(total / CHANNELS + 1e-06)
    scale = jnp.transpose(jnp.broadcast_to(scale, (8, scale.shape[1])))[:, 0:1]
    signal = (feat * scale * gain_ref[...] * gate_ref[...].astype(jnp.float32)).astype(jnp.bfloat16)
    wide = signal.astype(jnp.float32)
    lanes = wide.shape[1]
    pair = lanes // count
    tiles = wide.shape[0] // lanes
    chunk = pair * tiles
    for tile in range(tiles):
        sig_turn[...] = jnp.transpose(wide[lanes * tile:lanes * (tile + 1), :])
        for chan in range(pair):
            rows = sig_turn[pl.ds(chan, count, stride=pair), :]
            sig_send[pl.ds(tiles * chan + tile, count, stride=chunk), :] = rows

    def rows_of(buffer):
        return lambda peer: buffer.at[pl.ds(pl.multiple_of(peer * chunk, chunk), chunk)]

    wire_out[...] = sig_send[...].astype(wire_out.dtype)
    sig_own = pltpu.make_async_copy(rows_of(wire_out)(me), rows_of(wire_in)(me), own_sems.at[1])
    sig_own.start()
    start_all(rows_of(wire_out), rows_of(wire_in)(me), sig_sems)
    finish_all(rows_of(wire_out), rows_of(wire_in)(me), sig_sems)
    sig_own.wait()
    sig_recv[...] = wire_in[...].astype(jnp.float32)

    for chan in range(pair):
        for tile in range(tiles):
            rows = sig_recv[pl.ds(tiles * chan + tile, count, stride=chunk), :]
            cols[chan, pl.ds(tile, count, stride=tiles), :] = rows

    first_len = tc_ref.shape[0]
    for load in loads:
        load.wait()
    boths = []
    for chan in range(pair):
        signal_cols = cols[chan].astype(jnp.bfloat16)
        boths.append(jnp.dot(st_hi[...], signal_cols, preferred_element_type=jnp.float32))

    cos_twist, sin_twist = tc_ref[...], ts_ref[...]
    own_rows = first_len // count
    freqs = []
    for chan in range(pair):
        p_cos = boths[chan][:first_len]
        p_sin = boths[chan][first_len:]
        twist_re = p_cos * cos_twist - p_sin * sin_twist
        twist_im = -p_sin * cos_twist - p_cos * sin_twist
        freqs.append(dot3(twist_re, (fa_hi[...],)) + dot3(twist_im, (fb_hi[...],)))

    finish_all(spec_src, spec_recv.at[me], spec_sems)
    spec_own.wait()

    for chan in range(pair):
        freq = freqs[chan]
        freq_re, freq_im = freq[:, :lanes], freq[:, lanes:]
        filt = []
        for part_of in range(2):
            block = spec_recv[:, pl.ds((2 * chan + part_of) * own_rows, own_rows), :]
            filt.append(block.astype(jnp.float32).reshape(first_len, lanes))
        filt_re, filt_im = filt
        prod_re = freq_re * filt_re - freq_im * filt_im
        prod_im = freq_re * filt_im + freq_im * filt_re
        back = dot3(prod_re, (ia_hi[...],)) + dot3(prod_im, (ib_hi[...],))
        back_re, back_im = back[:, :lanes], back[:, lanes:]
        untwist_re = back_re * cos_twist - back_im * sin_twist
        untwist_im = back_im * cos_twist + back_re * sin_twist
        conv_one[...] = dot3((lc_hi[...],), untwist_re) + dot3((ls_hi[...],), untwist_im)
        for tile in range(tiles):
            rows = conv_one[pl.ds(tile, count, stride=tiles), :]
            conv_send[pl.ds(tiles * chan + tile, count, stride=chunk), :] = rows

    res_out[...] = conv_send[...].astype(res_out.dtype)
    res_src = rows_of(res_out)
    res_dst = rows_of(res_in)(me)
    res_own = pltpu.make_async_copy(res_src(me), res_dst, own_sems.at[2])
    res_own.start()
    start_all(res_src, res_dst, res_sems)
    finish_all(res_src, res_dst, res_sems)
    res_own.wait()
    res_recv[...] = res_in[...].astype(jnp.float32)

    inputs[4].wait()
    inputs[5].wait()
    skip = skip_ref[...]
    for tile in range(tiles):
        for chan in range(pair):
            sig_turn[pl.ds(chan, count, stride=pair), :] = res_recv[pl.ds(tiles * chan + tile, count, stride=chunk), :]
        block = jnp.transpose(sig_turn[...])
        these = slice(lanes * tile, lanes * (tile + 1))
        direct = signal[these, :].astype(jnp.float32)
        gated = post_ref[these, :].astype(jnp.float32) * (block + skip * direct)
        gated_out[these, :] = gated.astype(gated_out.dtype)


def whole(features, pre_gate, gain_row, spec_rows, post_gate, skip_row, tables, chans):
    count = spec_rows.shape[0]
    length, width = features.shape
    pair = width // count
    lanes = 128
    chunk = pair * length // lanes
    vmem = pl.BlockSpec(memory_space=pltpu.VMEM)
    operands = (features, pre_gate, gain_row, spec_rows, post_gate, skip_row) + tuple(tables)
    hbm = pl.BlockSpec(memory_space=pl.ANY)
    return pl.pallas_call(
        whole_kernel,
        out_shape=jax.ShapeDtypeStruct((length, width), jnp.bfloat16),
        in_specs=[hbm] * len(operands),
        out_specs=vmem,
        scratch_shapes=[
            pltpu.VMEM((8, length), jnp.float32),
            pltpu.VMEM((chans, 8, length), jnp.float32),
            pltpu.VMEM((lanes, lanes), jnp.float32),
            pltpu.VMEM((count * chunk, lanes), jnp.float32),
            pltpu.VMEM((count * chunk, lanes), jnp.float32),
            pltpu.VMEM(spec_rows.shape, jnp.bfloat16),
            pltpu.VMEM((pair, count * chunk // pair, lanes), jnp.float32),
            pltpu.VMEM((count * chunk // pair, lanes), jnp.float32),
            pltpu.VMEM((count * chunk, lanes), jnp.float32),
            pltpu.VMEM((count * chunk, lanes), jnp.float32),
            pltpu.VMEM((count * chunk, lanes), jnp.bfloat16),
            pltpu.VMEM((count * chunk, lanes), jnp.bfloat16),
            pltpu.VMEM((count * chunk, lanes), jnp.bfloat16),
            pltpu.VMEM((count * chunk, lanes), jnp.bfloat16),
            pltpu.VMEM(spec_rows.shape, jnp.bfloat16),
            pltpu.SemaphoreType.DMA((2, count)),
            pltpu.SemaphoreType.DMA((2, count)),
            pltpu.SemaphoreType.DMA((2, count)),
            pltpu.SemaphoreType.DMA((2, chans)),
            pltpu.SemaphoreType.DMA((3,)),
            pltpu.SemaphoreType.DMA((len(operands),)),
        ]
        + [pltpu.VMEM(table.shape, table.dtype) for table in operands],
        compiler_params=pltpu.CompilerParams(
            collective_id=0, has_side_effects=True, vmem_limit_bytes=67043328
        ),
    )(*operands)


def dft_tables(seq_count, tok_rows):
    stride = 2 * seq_count
    first_len = stride * ROW_GROUP
    all_bins = stride * tok_rows
    second_len = all_bins // first_len
    half_first = first_len // 2
    row_bins = bin_rows(seq_count).astype(np.int64)
    first_turn = (row_bins[:, None] * np.arange(half_first)[None, :]) % first_len * (2.0 * np.pi / first_len)
    cos_first, sin_first = np.cos(first_turn), np.sin(first_turn)
    twist_turn = (row_bins[:, None] * np.arange(second_len)[None, :]) % all_bins * (2.0 * np.pi / all_bins)
    second_in = np.arange(second_len)
    second_turn = (second_in[:, None] * second_in[None, :]) % second_len * (2.0 * np.pi / second_len)
    cos_second, sin_second = np.cos(second_turn), np.sin(second_turn)

    def pair_of(array):
        return [jnp.asarray(array.astype(np.float32).astype(jnp.bfloat16))]

    tables = pair_of(np.concatenate([cos_first, sin_first], 0))
    tables += [jnp.asarray(np.cos(twist_turn).astype(np.float32)), jnp.asarray(np.sin(twist_turn).astype(np.float32))]
    tables += pair_of(np.concatenate([cos_second, -sin_second], 1))
    tables += pair_of(np.concatenate([sin_second, cos_second], 1))
    tables += pair_of(np.concatenate([cos_second, sin_second], 1))
    tables += pair_of(np.concatenate([-sin_second, cos_second], 1))
    tables += pair_of(cos_first.T / all_bins)
    tables += pair_of(-sin_first.T / all_bins)
    return tables


def local(features, pre_gate, post_gate, norm_gain, skip_weight, spectrum):
    tok_rows, chan_width = features.shape
    seq_count = lax.axis_size("seq")
    chans = lax.axis_size("chan")
    group = chan_width // seq_count
    second_len = tok_rows // ROW_GROUP
    lanes = 128
    tok_tiles = tok_rows // lanes

    spec_rows = spectrum.reshape(2, 2, second_len, ROW_GROUP, chan_width)
    spec_rows = jnp.transpose(spec_rows, (4, 0, 1, 3, 2)).reshape(seq_count, -1, second_len)
    return whole(
        features, pre_gate, norm_gain.reshape(1, chan_width), spec_rows,
        post_gate, skip_weight.reshape(1, chan_width), dft_tables(seq_count, tok_rows), chans,
    )


def solution(mesh):
    return jax.shard_map(
        local,
        mesh=mesh,
        in_specs=(
            P("seq", "chan"),
            P("seq", "chan"),
            P("seq", "chan"),
            P("chan"),
            P("chan"),
            P(None, "seq", None, "chan"),
        ),
        out_specs=P("seq", "chan"),
        check_vma=False,
    )
```

```python
import math

import jax
import jax.numpy as jnp
import numpy as np
from jax import lax
from jax.experimental import pallas as pl
from jax.experimental.pallas import tpu as pltpu
from jax.sharding import PartitionSpec as P

CHANNELS = 512
ROW_GROUP = 4
TABLE_NAMES = ("st", "tc", "ts", "fa", "fb", "ia", "ib", "lc", "ls")
HIGH_DIGIT = 8


PRECISE = lax.Precision.HIGH
FULL_TURN = 2.0 * math.pi


def reversed_digits(count):
    levels = count.bit_length() - 1
    positions = np.arange(count)
    result = np.zeros(count, np.int64)
    for bit_pos in range(levels):
        result = result + ((positions >> bit_pos & 1) << levels - 1 - bit_pos)
    return result


def rotation(numerator, denominator):
    angle = (numerator % denominator).astype(jnp.float32) * (FULL_TURN / denominator)
    return (jnp.cos(angle), jnp.sin(angle))


def mm(spec, left, right):
    return jnp.einsum(spec, left, right, precision=PRECISE, preferred_element_type=jnp.float32)


def bin_rows(seq_count):
    digit_order = reversed_digits(seq_count)
    stride = 2 * seq_count
    slots = np.arange(stride)
    low_bins = 2 * digit_order[slots // 2] + slots % 2
    return (low_bins[:, None] + stride * np.arange(ROW_GROUP)[None, :]).reshape(-1).astype(np.int32)


def split(value):
    high = value.astype(jnp.bfloat16)
    return high, (value - high.astype(jnp.float32)).astype(jnp.bfloat16)


def dot3(left, right):
    if isinstance(left, tuple):
        return jnp.dot(left[0], right.astype(jnp.bfloat16), preferred_element_type=jnp.float32)
    return jnp.dot(left.astype(jnp.bfloat16), right[0], preferred_element_type=jnp.float32)


def whole_kernel(*refs):
    table_count = len(TABLE_NAMES) + 6
    held = refs[:table_count]
    gated_out = refs[table_count]
    (sq_mine, sq_recv, sig_turn, sig_send, sig_recv, spec_recv, cols, conv_one, conv_send, res_recv,
     wire_out, wire_in, res_out, res_in, spec_send, spec_sems, sig_sems, res_sems, chan_sems, own_sems, table_sems) = (
        refs[table_count + 1:table_count + 22])
    tables = refs[table_count + 22:]
    loads = [pltpu.make_async_copy(held[k], tables[k], table_sems.at[k]) for k in range(table_count)]
    for load in loads:
        load.start()
    inputs = loads[:6]
    loads = loads[6:]
    feat_ref, gate_ref, gain_ref, spec_ref, post_ref, skip_ref = tables[:6]
    tables = tables[6:]
    (st_hi, tc_ref, ts_ref, fa_hi, fb_hi, ia_hi, ib_hi, lc_hi, ls_hi) = tables
    count = spec_ref.shape[0]
    chans = sq_recv.shape[0]
    me = lax.axis_index("seq")
    mine = lax.axis_index("chan")
    mesh_ids = pl.DeviceIdType.MESH
    barrier = pltpu.get_barrier_semaphore()

    def greet(step, carry):
        peer = lax.rem(me + step, count)
        pl.semaphore_signal(barrier, inc=1, device_id={"seq": peer}, device_id_type=mesh_ids)
        return carry

    lax.fori_loop(1, count, greet, 0)
    for step in range(1, chans):
        peer = lax.rem(mine + step, chans)
        pl.semaphore_signal(barrier, inc=1, device_id={"chan": peer}, device_id_type=mesh_ids)
    inputs[0].wait()
    feat = feat_ref[...].astype(jnp.float32)
    part = jnp.sum(jnp.transpose(feat * feat), axis=0, keepdims=True)
    sq_mine[...] = jnp.broadcast_to(part, sq_mine.shape)
    inputs[3].wait()
    spec_send[...] = spec_ref[...].astype(spec_send.dtype)
    pl.semaphore_wait(barrier, count + chans - 2)

    def seq_copy(source, target, sems, step):
        peer = lax.rem(me + step, count)
        return pltpu.make_async_remote_copy(
            source(peer), target, sems.at[0, step], sems.at[1, step],
            device_id={"seq": peer}, device_id_type=mesh_ids,
        )

    def start_all(source, target, sems):
        def body(step, carry):
            seq_copy(source, target, sems, step).start()
            return carry
        lax.fori_loop(1, count, body, 0)

    def finish_all(source, target, sems):
        def body(step, carry):
            copy = seq_copy(source, target, sems, step)
            copy.wait_send()
            copy.wait_recv()
            return carry
        lax.fori_loop(1, count, body, 0)


    def chan_copy(step):
        peer = lax.rem(mine + step, chans)
        return pltpu.make_async_remote_copy(
            sq_mine, sq_recv.at[mine], chan_sems.at[0, step], chan_sems.at[1, step],
            device_id={"chan": peer}, device_id_type=mesh_ids,
        )

    for step in range(1, chans):
        chan_copy(step).start()
    spec_src = lambda peer: spec_send.at[peer]
    spec_own = pltpu.make_async_copy(spec_send.at[me], spec_recv.at[me], own_sems.at[0])
    spec_own.start()
    z_step = HIGH_DIGIT
    z_count = count // z_step
    far_first = sorted(range(1, count), key=lambda s: -min(s // z_step, z_count - s // z_step))
    for step in far_first:
        seq_copy(spec_src, spec_recv.at[me], spec_sems, step).start()
    for step in range(1, chans):
        copy = chan_copy(step)
        copy.wait_send()
        copy.wait_recv()
    total = part
    for step in range(1, chans):
        other = lax.rem(mine + step, chans)
        total = total + sq_recv[other][0:1, :]
    inputs[1].wait()
    inputs[2].wait()
    scale = lax.rsqrt(total / CHANNELS + 1e-06)
    scale = jnp.transpose(jnp.broadcast_to(scale, (8, scale.shape[1])))[:, 0:1]
    signal = (feat * scale * gain_ref[...] * gate_ref[...].astype(jnp.float32)).astype(jnp.bfloat16)
    wide = signal.astype(jnp.float32)
    lanes = wide.shape[1]
    pair = lanes // count
    tiles = wide.shape[0] // lanes
    chunk = pair * tiles
    for tile in range(tiles):
        sig_turn[...] = jnp.transpose(wide[lanes * tile:lanes * (tile + 1), :])
        for chan in range(pair):
            rows = sig_turn[pl.ds(chan, count, stride=pair), :]
            sig_send[pl.ds(tiles * chan + tile, count, stride=chunk), :] = rows

    def rows_of(buffer):
        return lambda peer: buffer.at[pl.ds(pl.multiple_of(peer * chunk, chunk), chunk)]

    wire_out[...] = sig_send[...].astype(wire_out.dtype)
    sig_own = pltpu.make_async_copy(rows_of(wire_out)(me), rows_of(wire_in)(me), own_sems.at[1])
    sig_own.start()
    start_all(rows_of(wire_out), rows_of(wire_in)(me), sig_sems)
    finish_all(rows_of(wire_out), rows_of(wire_in)(me), sig_sems)
    sig_own.wait()
    sig_recv[...] = wire_in[...].astype(jnp.float32)

    for chan in range(pair):
        for tile in range(tiles):
            rows = sig_recv[pl.ds(tiles * chan + tile, count, stride=chunk), :]
            cols[chan, pl.ds(tile, count, stride=tiles), :] = rows

    first_len = tc_ref.shape[0]
    for load in loads:
        load.wait()
    boths = []
    for chan in range(pair):
        signal_cols = cols[chan].astype(jnp.bfloat16)
        boths.append(jnp.dot(st_hi[...], signal_cols, preferred_element_type=jnp.float32))

    cos_twist, sin_twist = tc_ref[...], ts_ref[...]
    own_rows = first_len // count
    freqs = []
    for chan in range(pair):
        p_cos = boths[chan][:first_len]
        p_sin = boths[chan][first_len:]
        twist_re = p_cos * cos_twist - p_sin * sin_twist
        twist_im = -p_sin * cos_twist - p_cos * sin_twist
        freqs.append(dot3(twist_re, (fa_hi[...],)) + dot3(twist_im, (fb_hi[...],)))

    finish_all(spec_src, spec_recv.at[me], spec_sems)
    spec_own.wait()

    for chan in range(pair):
        freq = freqs[chan]
        freq_re, freq_im = freq[:, :lanes], freq[:, lanes:]
        filt = []
        for part_of in range(2):
            block = spec_recv[:, pl.ds((2 * chan + part_of) * own_rows, own_rows), :]
            filt.append(block.astype(jnp.float32).reshape(first_len, lanes))
        filt_re, filt_im = filt
        prod_re = freq_re * filt_re - freq_im * filt_im
        prod_im = freq_re * filt_im + freq_im * filt_re
        back = dot3(prod_re, (ia_hi[...],)) + dot3(prod_im, (ib_hi[...],))
        back_re, back_im = back[:, :lanes], back[:, lanes:]
        untwist_re = back_re * cos_twist - back_im * sin_twist
        untwist_im = back_im * cos_twist + back_re * sin_twist
        conv_one[...] = dot3((lc_hi[...],), untwist_re) + dot3((ls_hi[...],), untwist_im)
        for tile in range(tiles):
            rows = conv_one[pl.ds(tile, count, stride=tiles), :]
            conv_send[pl.ds(tiles * chan + tile, count, stride=chunk), :] = rows

    res_out[...] = conv_send[...].astype(res_out.dtype)
    res_src = rows_of(res_out)
    res_dst = rows_of(res_in)(me)
    res_own = pltpu.make_async_copy(res_src(me), res_dst, own_sems.at[2])
    res_own.start()
    start_all(res_src, res_dst, res_sems)
    finish_all(res_src, res_dst, res_sems)
    res_own.wait()
    res_recv[...] = res_in[...].astype(jnp.float32)

    inputs[4].wait()
    inputs[5].wait()
    skip = skip_ref[...]
    for tile in range(tiles):
        for chan in range(pair):
            sig_turn[pl.ds(chan, count, stride=pair), :] = res_recv[pl.ds(tiles * chan + tile, count, stride=chunk), :]
        block = jnp.transpose(sig_turn[...])
        these = slice(lanes * tile, lanes * (tile + 1))
        direct = signal[these, :].astype(jnp.float32)
        gated = post_ref[these, :].astype(jnp.float32) * (block + skip * direct)
        gated_out[these, :] = gated.astype(gated_out.dtype)


def whole(features, pre_gate, gain_row, spec_rows, post_gate, skip_row, tables, chans):
    count = spec_rows.shape[0]
    length, width = features.shape
    pair = width // count
    lanes = 128
    chunk = pair * length // lanes
    vmem = pl.BlockSpec(memory_space=pltpu.VMEM)
    operands = (features, pre_gate, gain_row, spec_rows, post_gate, skip_row) + tuple(tables)
    hbm = pl.BlockSpec(memory_space=pl.ANY)
    return pl.pallas_call(
        whole_kernel,
        out_shape=jax.ShapeDtypeStruct((length, width), jnp.bfloat16),
        in_specs=[hbm] * len(operands),
        out_specs=vmem,
        scratch_shapes=[
            pltpu.VMEM((8, length), jnp.float32),
            pltpu.VMEM((chans, 8, length), jnp.float32),
            pltpu.VMEM((lanes, lanes), jnp.float32),
            pltpu.VMEM((count * chunk, lanes), jnp.float32),
            pltpu.VMEM((count * chunk, lanes), jnp.float32),
            pltpu.VMEM(spec_rows.shape, jnp.bfloat16),
            pltpu.VMEM((pair, count * chunk // pair, lanes), jnp.float32),
            pltpu.VMEM((count * chunk // pair, lanes), jnp.float32),
            pltpu.VMEM((count * chunk, lanes), jnp.float32),
            pltpu.VMEM((count * chunk, lanes), jnp.float32),
            pltpu.VMEM((count * chunk, lanes), jnp.bfloat16),
            pltpu.VMEM((count * chunk, lanes), jnp.bfloat16),
            pltpu.VMEM((count * chunk, lanes), jnp.bfloat16),
            pltpu.VMEM((count * chunk, lanes), jnp.bfloat16),
            pltpu.VMEM(spec_rows.shape, jnp.bfloat16),
            pltpu.SemaphoreType.DMA((2, count)),
            pltpu.SemaphoreType.DMA((2, count)),
            pltpu.SemaphoreType.DMA((2, count)),
            pltpu.SemaphoreType.DMA((2, chans)),
            pltpu.SemaphoreType.DMA((3,)),
            pltpu.SemaphoreType.DMA((len(operands),)),
        ]
        + [pltpu.VMEM(table.shape, table.dtype) for table in operands],
        compiler_params=pltpu.CompilerParams(
            collective_id=0, has_side_effects=True, vmem_limit_bytes=67043328
        ),
    )(*operands)


def dft_tables(seq_count, tok_rows):
    stride = 2 * seq_count
    first_len = stride * ROW_GROUP
    all_bins = stride * tok_rows
    second_len = all_bins // first_len
    half_first = first_len // 2
    row_bins = bin_rows(seq_count).astype(np.int64)
    first_turn = (row_bins[:, None] * np.arange(half_first)[None, :]) % first_len * (2.0 * np.pi / first_len)
    cos_first, sin_first = np.cos(first_turn), np.sin(first_turn)
    twist_turn = (row_bins[:, None] * np.arange(second_len)[None, :]) % all_bins * (2.0 * np.pi / all_bins)
    second_in = np.arange(second_len)
    second_turn = (second_in[:, None] * second_in[None, :]) % second_len * (2.0 * np.pi / second_len)
    cos_second, sin_second = np.cos(second_turn), np.sin(second_turn)

    def pair_of(array):
        return [jnp.asarray(array.astype(np.float32).astype(jnp.bfloat16))]

    tables = pair_of(np.concatenate([cos_first, sin_first], 0))
    tables += [jnp.asarray(np.cos(twist_turn).astype(np.float32)), jnp.asarray(np.sin(twist_turn).astype(np.float32))]
    tables += pair_of(np.concatenate([cos_second, -sin_second], 1))
    tables += pair_of(np.concatenate([sin_second, cos_second], 1))
    tables += pair_of(np.concatenate([cos_second, sin_second], 1))
    tables += pair_of(np.concatenate([-sin_second, cos_second], 1))
    tables += pair_of(cos_first.T / all_bins)
    tables += pair_of(-sin_first.T / all_bins)
    return tables


def local(features, pre_gate, post_gate, norm_gain, skip_weight, spectrum):
    tok_rows, chan_width = features.shape
    seq_count = lax.axis_size("seq")
    chans = lax.axis_size("chan")
    group = chan_width // seq_count
    second_len = tok_rows // ROW_GROUP
    lanes = 128
    tok_tiles = tok_rows // lanes

    spec_rows = spectrum.reshape(2, 2, second_len, ROW_GROUP, chan_width)
    spec_rows = jnp.transpose(spec_rows, (4, 0, 1, 3, 2)).reshape(seq_count, -1, second_len)
    return whole(
        features, pre_gate, norm_gain.reshape(1, chan_width), spec_rows,
        post_gate, skip_weight.reshape(1, chan_width), dft_tables(seq_count, tok_rows), chans,
    )


def solution(mesh):
    return jax.shard_map(
        local,
        mesh=mesh,
        in_specs=(
            P("seq", "chan"),
            P("seq", "chan"),
            P("seq", "chan"),
            P("chan"),
            P("chan"),
            P(None, "seq", None, "chan"),
        ),
        out_specs=P("seq", "chan"),
        check_vma=False,
    )
```

```python
import math

import jax
import jax.numpy as jnp
import numpy as np
from jax import lax
from jax.experimental import pallas as pl
from jax.experimental.pallas import tpu as pltpu
from jax.sharding import PartitionSpec as P

CHANNELS = 512
ROW_GROUP = 4
TABLE_NAMES = ("st", "tc", "ts", "fab", "iab", "lc", "ls")
HIGH_DIGIT = 8


PRECISE = lax.Precision.HIGH
FULL_TURN = 2.0 * math.pi


def reversed_digits(count):
    levels = count.bit_length() - 1
    positions = np.arange(count)
    result = np.zeros(count, np.int64)
    for bit_pos in range(levels):
        result = result + ((positions >> bit_pos & 1) << levels - 1 - bit_pos)
    return result


def rotation(numerator, denominator):
    angle = (numerator % denominator).astype(jnp.float32) * (FULL_TURN / denominator)
    return (jnp.cos(angle), jnp.sin(angle))


def mm(spec, left, right):
    return jnp.einsum(spec, left, right, precision=PRECISE, preferred_element_type=jnp.float32)


def bin_rows(seq_count):
    digit_order = reversed_digits(seq_count)
    stride = 2 * seq_count
    slots = np.arange(stride)
    low_bins = 2 * digit_order[slots // 2] + slots % 2
    return (low_bins[:, None] + stride * np.arange(ROW_GROUP)[None, :]).reshape(-1).astype(np.int32)


def split(value):
    high = value.astype(jnp.bfloat16)
    return high, (value - high.astype(jnp.float32)).astype(jnp.bfloat16)


def dot3(left, right):
    if isinstance(left, tuple):
        return jnp.dot(left[0], right.astype(jnp.bfloat16), preferred_element_type=jnp.float32)
    return jnp.dot(left.astype(jnp.bfloat16), right[0], preferred_element_type=jnp.float32)


def whole_kernel(*refs):
    table_count = len(TABLE_NAMES) + 6
    held = refs[:table_count]
    gated_out = refs[table_count]
    (sq_mine, sq_recv, sig_turn, sig_send, sig_recv, spec_recv, cols, conv_one, conv_send, res_recv,
     wire_out, wire_in, res_out, res_in, spec_send, spec_sems, sig_sems, res_sems, chan_sems, own_sems, table_sems) = (
        refs[table_count + 1:table_count + 22])
    tables = refs[table_count + 22:]
    loads = [pltpu.make_async_copy(held[k], tables[k], table_sems.at[k]) for k in range(table_count)]
    for load in loads:
        load.start()
    inputs = loads[:6]
    loads = loads[6:]
    feat_ref, gate_ref, gain_ref, spec_ref, post_ref, skip_ref = tables[:6]
    tables = tables[6:]
    (st_hi, tc_ref, ts_ref, fab_hi, iab_hi, lc_hi, ls_hi) = tables
    count = spec_ref.shape[0]
    chans = sq_recv.shape[0]
    me = lax.axis_index("seq")
    mine = lax.axis_index("chan")
    mesh_ids = pl.DeviceIdType.MESH
    barrier = pltpu.get_barrier_semaphore()

    def greet(step, carry):
        peer = lax.rem(me + step, count)
        pl.semaphore_signal(barrier, inc=1, device_id={"seq": peer}, device_id_type=mesh_ids)
        return carry

    lax.fori_loop(1, count, greet, 0)
    for step in range(1, chans):
        peer = lax.rem(mine + step, chans)
        pl.semaphore_signal(barrier, inc=1, device_id={"chan": peer}, device_id_type=mesh_ids)
    inputs[0].wait()
    feat = feat_ref[...].astype(jnp.float32)
    part = jnp.sum(jnp.transpose(feat * feat), axis=0, keepdims=True)
    sq_mine[...] = jnp.broadcast_to(part, sq_mine.shape)
    inputs[3].wait()
    spec_send[...] = spec_ref[...].astype(spec_send.dtype)
    pl.semaphore_wait(barrier, count + chans - 2)

    def seq_copy(source, target, sems, step):
        peer = lax.rem(me + step, count)
        return pltpu.make_async_remote_copy(
            source(peer), target, sems.at[0, step], sems.at[1, step],
            device_id={"seq": peer}, device_id_type=mesh_ids,
        )

    def start_all(source, target, sems):
        def body(step, carry):
            seq_copy(source, target, sems, step).start()
            return carry
        lax.fori_loop(1, count, body, 0)

    def finish_all(source, target, sems):
        def body(step, carry):
            copy = seq_copy(source, target, sems, step)
            copy.wait_send()
            copy.wait_recv()
            return carry
        lax.fori_loop(1, count, body, 0)


    def chan_copy(step):
        peer = lax.rem(mine + step, chans)
        return pltpu.make_async_remote_copy(
            sq_mine, sq_recv.at[mine], chan_sems.at[0, step], chan_sems.at[1, step],
            device_id={"chan": peer}, device_id_type=mesh_ids,
        )

    for step in range(1, chans):
        chan_copy(step).start()
    spec_src = lambda peer: spec_send.at[peer]
    spec_own = pltpu.make_async_copy(spec_send.at[me], spec_recv.at[me], own_sems.at[0])
    spec_own.start()
    start_all(spec_src, spec_recv.at[me], spec_sems)
    for step in range(1, chans):
        copy = chan_copy(step)
        copy.wait_send()
        copy.wait_recv()
    total = part
    for step in range(1, chans):
        other = lax.rem(mine + step, chans)
        total = total + sq_recv[other][0:1, :]
    inputs[1].wait()
    inputs[2].wait()
    scale = lax.rsqrt(total / CHANNELS + 1e-06)
    scale = jnp.transpose(jnp.broadcast_to(scale, (8, scale.shape[1])))[:, 0:1]
    signal = (feat * scale * gain_ref[...] * gate_ref[...].astype(jnp.float32)).astype(jnp.bfloat16)
    wide = signal.astype(jnp.float32)
    lanes = wide.shape[1]
    pair = lanes // count
    tiles = wide.shape[0] // lanes
    chunk = pair * tiles
    for tile in range(tiles):
        sig_turn[...] = jnp.transpose(wide[lanes * tile:lanes * (tile + 1), :])
        for chan in range(pair):
            rows = sig_turn[pl.ds(chan, count, stride=pair), :]
            sig_send[pl.ds(tiles * chan + tile, count, stride=chunk), :] = rows

    def rows_of(buffer):
        return lambda peer: buffer.at[pl.ds(pl.multiple_of(peer * chunk, chunk), chunk)]

    wire_out[...] = sig_send[...].astype(wire_out.dtype)
    sig_own = pltpu.make_async_copy(rows_of(wire_out)(me), rows_of(wire_in)(me), own_sems.at[1])
    sig_own.start()
    start_all(rows_of(wire_out), rows_of(wire_in)(me), sig_sems)
    finish_all(rows_of(wire_out), rows_of(wire_in)(me), sig_sems)
    sig_own.wait()
    sig_recv[...] = wire_in[...].astype(jnp.float32)

    for chan in range(pair):
        for tile in range(tiles):
            rows = sig_recv[pl.ds(tiles * chan + tile, count, stride=chunk), :]
            cols[chan, pl.ds(tile, count, stride=tiles), :] = rows

    first_len = tc_ref.shape[0]
    for load in loads:
        load.wait()
    boths = []
    for chan in range(pair):
        signal_cols = cols[chan].astype(jnp.bfloat16)
        boths.append(jnp.dot(st_hi[...], signal_cols, preferred_element_type=jnp.float32))

    cos_twist, sin_twist = tc_ref[...], ts_ref[...]
    own_rows = first_len // count
    freqs = []
    for chan in range(pair):
        p_cos = boths[chan][:first_len]
        p_sin = boths[chan][first_len:]
        twist_re = p_cos * cos_twist - p_sin * sin_twist
        twist_im = -p_sin * cos_twist - p_cos * sin_twist
        freqs.append(dot3(jnp.concatenate([twist_re, twist_im], axis=1), (fab_hi[...],)))

    finish_all(spec_src, spec_recv.at[me], spec_sems)
    spec_own.wait()

    for chan in range(pair):
        freq = freqs[chan]
        freq_re, freq_im = freq[:, :lanes], freq[:, lanes:]
        filt = []
        for part_of in range(2):
            block = spec_recv[:, pl.ds((2 * chan + part_of) * own_rows, own_rows), :]
            filt.append(block.astype(jnp.float32).reshape(first_len, lanes))
        filt_re, filt_im = filt
        prod_re = freq_re * filt_re - freq_im * filt_im
        prod_im = freq_re * filt_im + freq_im * filt_re
        back = dot3(jnp.concatenate([prod_re, prod_im], axis=1), (iab_hi[...],))
        back_re, back_im = back[:, :lanes], back[:, lanes:]
        untwist_re = back_re * cos_twist - back_im * sin_twist
        untwist_im = back_im * cos_twist + back_re * sin_twist
        conv_one[...] = dot3((lc_hi[...],), untwist_re) + dot3((ls_hi[...],), untwist_im)
        for tile in range(tiles):
            rows = conv_one[pl.ds(tile, count, stride=tiles), :]
            conv_send[pl.ds(tiles * chan + tile, count, stride=chunk), :] = rows

    res_out[...] = conv_send[...].astype(res_out.dtype)
    res_src = rows_of(res_out)
    res_dst = rows_of(res_in)(me)
    res_own = pltpu.make_async_copy(res_src(me), res_dst, own_sems.at[2])
    res_own.start()
    start_all(res_src, res_dst, res_sems)
    finish_all(res_src, res_dst, res_sems)
    res_own.wait()
    res_recv[...] = res_in[...].astype(jnp.float32)

    inputs[4].wait()
    inputs[5].wait()
    skip = skip_ref[...]
    for tile in range(tiles):
        for chan in range(pair):
            sig_turn[pl.ds(chan, count, stride=pair), :] = res_recv[pl.ds(tiles * chan + tile, count, stride=chunk), :]
        block = jnp.transpose(sig_turn[...])
        these = slice(lanes * tile, lanes * (tile + 1))
        direct = signal[these, :].astype(jnp.float32)
        gated = post_ref[these, :].astype(jnp.float32) * (block + skip * direct)
        gated_out[these, :] = gated.astype(gated_out.dtype)


def whole(features, pre_gate, gain_row, spec_rows, post_gate, skip_row, tables, chans):
    count = spec_rows.shape[0]
    length, width = features.shape
    pair = width // count
    lanes = 128
    chunk = pair * length // lanes
    vmem = pl.BlockSpec(memory_space=pltpu.VMEM)
    operands = (features, pre_gate, gain_row, spec_rows, post_gate, skip_row) + tuple(tables)
    hbm = pl.BlockSpec(memory_space=pl.ANY)
    return pl.pallas_call(
        whole_kernel,
        out_shape=jax.ShapeDtypeStruct((length, width), jnp.bfloat16),
        in_specs=[hbm] * len(operands),
        out_specs=vmem,
        scratch_shapes=[
            pltpu.VMEM((8, length), jnp.float32),
            pltpu.VMEM((chans, 8, length), jnp.float32),
            pltpu.VMEM((lanes, lanes), jnp.float32),
            pltpu.VMEM((count * chunk, lanes), jnp.float32),
            pltpu.VMEM((count * chunk, lanes), jnp.float32),
            pltpu.VMEM(spec_rows.shape, jnp.bfloat16),
            pltpu.VMEM((pair, count * chunk // pair, lanes), jnp.float32),
            pltpu.VMEM((count * chunk // pair, lanes), jnp.float32),
            pltpu.VMEM((count * chunk, lanes), jnp.float32),
            pltpu.VMEM((count * chunk, lanes), jnp.float32),
            pltpu.VMEM((count * chunk, lanes), jnp.bfloat16),
            pltpu.VMEM((count * chunk, lanes), jnp.bfloat16),
            pltpu.VMEM((count * chunk, lanes), jnp.bfloat16),
            pltpu.VMEM((count * chunk, lanes), jnp.bfloat16),
            pltpu.VMEM(spec_rows.shape, jnp.bfloat16),
            pltpu.SemaphoreType.DMA((2, count)),
            pltpu.SemaphoreType.DMA((2, count)),
            pltpu.SemaphoreType.DMA((2, count)),
            pltpu.SemaphoreType.DMA((2, chans)),
            pltpu.SemaphoreType.DMA((3,)),
            pltpu.SemaphoreType.DMA((len(operands),)),
        ]
        + [pltpu.VMEM(table.shape, table.dtype) for table in operands],
        compiler_params=pltpu.CompilerParams(
            collective_id=0, has_side_effects=True, vmem_limit_bytes=67043328
        ),
    )(*operands)


def dft_tables(seq_count, tok_rows):
    stride = 2 * seq_count
    first_len = stride * ROW_GROUP
    all_bins = stride * tok_rows
    second_len = all_bins // first_len
    half_first = first_len // 2
    row_bins = bin_rows(seq_count).astype(np.int64)
    first_turn = (row_bins[:, None] * np.arange(half_first)[None, :]) % first_len * (2.0 * np.pi / first_len)
    cos_first, sin_first = np.cos(first_turn), np.sin(first_turn)
    twist_turn = (row_bins[:, None] * np.arange(second_len)[None, :]) % all_bins * (2.0 * np.pi / all_bins)
    second_in = np.arange(second_len)
    second_turn = (second_in[:, None] * second_in[None, :]) % second_len * (2.0 * np.pi / second_len)
    cos_second, sin_second = np.cos(second_turn), np.sin(second_turn)

    def pair_of(array):
        return [jnp.asarray(array.astype(np.float32).astype(jnp.bfloat16))]

    tables = pair_of(np.concatenate([cos_first, sin_first], 0))
    tables += [jnp.asarray(np.cos(twist_turn).astype(np.float32)), jnp.asarray(np.sin(twist_turn).astype(np.float32))]
    fwd_a = np.concatenate([cos_second, -sin_second], 1)
    fwd_b = np.concatenate([sin_second, cos_second], 1)
    tables += pair_of(np.concatenate([fwd_a, fwd_b], 0))
    inv_a = np.concatenate([cos_second, sin_second], 1)
    inv_b = np.concatenate([-sin_second, cos_second], 1)
    tables += pair_of(np.concatenate([inv_a, inv_b], 0))
    tables += pair_of(cos_first.T / all_bins)
    tables += pair_of(-sin_first.T / all_bins)
    return tables


def local(features, pre_gate, post_gate, norm_gain, skip_weight, spectrum):
    tok_rows, chan_width = features.shape
    seq_count = lax.axis_size("seq")
    chans = lax.axis_size("chan")
    group = chan_width // seq_count
    second_len = tok_rows // ROW_GROUP
    lanes = 128
    tok_tiles = tok_rows // lanes

    spec_rows = spectrum.reshape(2, 2, second_len, ROW_GROUP, chan_width)
    spec_rows = jnp.transpose(spec_rows, (4, 0, 1, 3, 2)).reshape(seq_count, -1, second_len)
    return whole(
        features, pre_gate, norm_gain.reshape(1, chan_width), spec_rows,
        post_gate, skip_weight.reshape(1, chan_width), dft_tables(seq_count, tok_rows), chans,
    )


def solution(mesh):
    return jax.shard_map(
        local,
        mesh=mesh,
        in_specs=(
            P("seq", "chan"),
            P("seq", "chan"),
            P("seq", "chan"),
            P("chan"),
            P("chan"),
            P(None, "seq", None, "chan"),
        ),
        out_specs=P("seq", "chan"),
        check_vma=False,
    )
```
